32 devices in a mesh: fsdp: 8 (over y, x, core), tensor: 4 (over z).
Axes of the slice: x: 2, y: 2, z: 4, core: 2. Of those that a mesh axis runs over, the one named last changes fastest.
Arguments:
- latents: bfloat16 [16, 1024, 1152], P('fsdp', 'tensor'), may hold values from -6 to 6
- conditioning: bfloat16 [16, 1152], P('fsdp'), may hold values from -6 to 6
- mod_weight: bfloat16 [1152, 6, 1152], P('fsdp', None, 'tensor'), may hold values from -0.1875 to 0.1875
- mod_bias: bfloat16 [6, 1152], P(None, 'tensor'), may hold values from -3 to 3
- in_weight: bfloat16 [3, 1152, 1152], P(None, 'fsdp', 'tensor'), may hold values from -0.1875 to 0.1875
- query_value_bias: bfloat16 [2, 1152], P(None, 'tensor'), may hold values from -3 to 3
- out_weight: bfloat16 [1152, 1152], P('tensor', 'fsdp'), may hold values from -1.5 to 1.5
- branch_bias: bfloat16 [2, 1152], replicated, may hold values from -3 to 3
- up_weight: bfloat16 [1152, 4608], P('fsdp', 'tensor'), may hold values from -0.1875 to 0.1875
- up_bias: bfloat16 [4608], P('tensor'), may hold values from -3 to 3
- down_weight: bfloat16 [4608, 1152], P('tensor', 'fsdp'), may hold values from -0.1875 to 0.1875
- cotangent: bfloat16 [16, 1024, 1152], P('fsdp', 'tensor'), may hold values from -6 to 6
Outputs:
- block_out: bfloat16 [16, 1024, 1152], P('fsdp', 'tensor')
- latent_grad: bfloat16 [16, 1024, 1152], P('fsdp', 'tensor')
- cond_grad: float32 [16, 1152], P('fsdp')
- mod_weight_grad: float32 [1152, 6, 1152], P('fsdp', None, 'tensor')
- mod_bias_grad: float32 [6, 1152], P(None, 'tensor')
- in_weight_grad: float32 [3, 1152, 1152], P(None, 'fsdp', 'tensor')
- query_value_bias_grad: float32 [2, 1152], P(None, 'tensor')
- out_weight_grad: float32 [1152, 1152], P('tensor', 'fsdp')
- branch_bias_grad: float32 [2, 1152], replicated
- up_weight_grad: float32 [1152, 4608], P('fsdp', 'tensor')
- up_bias_grad: float32 [4608], P('tensor')
- down_weight_grad: float32 [4608, 1152], P('tensor', 'fsdp')
The draws below stay inside these ranges and needn't reach their ends.
All inputs are finite; a program needn't handle non-finite values.
Results may differ from the reference program's by a relative error of at most 0.02.
Values may be sent and summed in bfloat16 or wider, within the bound.
No kernel may reach another device: no remote copies, remote signals or barrier semaphores. Data moves between devices by JAX's collectives and lax.ppermute only.
A program may use at most 256 MiB of HBM per device.

```python
import jax
import jax.numpy as jnp
from jax import lax

D = 1152
HEADS = 16
HEAD_DIM = 72
FF = 4608
SEQ = 1024
BATCH = 16
N_TENSOR = 4


def shard_levels(key, dims, shards, low, high):
    factor_of, own = 1.0, jax.random.fold_in(key, 6)
    for axis_at, parts in shards:
        draws = jnp.exp(jax.random.uniform(jax.random.fold_in(own, axis_at), (parts,), jnp.float32, low / len(shards), high / len(shards)))
        factor_of = factor_of * jnp.repeat(draws, dims[axis_at] // parts).reshape([-1 if axis == axis_at else 1 for axis in range(len(dims))])
    return factor_of


def bell_draw(key, dims, scale, reach, shards=(), dtype=jnp.bfloat16):
    array = jax.random.normal(key, dims, jnp.float32) * scale
    if len(shards) > 0:
        array = shard_levels(key, dims, shards, -0.22, 0.18) * array
    return jnp.clip(array, min=-reach, max=reach).astype(dtype)


def setup_inputs(seed: int = 0) -> dict:
    streams_of = jax.random.split(jax.random.key(seed), 13)
    latents = bell_draw(streams_of[0], (BATCH, SEQ, D), 1.0, 6.0, ((0, 8), (1, 4)))
    conditioning = bell_draw(streams_of[1], (BATCH, D), 1.0, 6.0, ((0, 8),))
    mod_weight = bell_draw(streams_of[2], (D, 6, D), D ** -0.5, 0.1875, ((0, 8), (2, 4)))
    mod_bias = bell_draw(streams_of[3], (6, D), 0.5, 3.0, ((1, 4),))
    in_weight = bell_draw(streams_of[4], (3, D, D), D ** -0.5, 0.1875, ((1, 8), (2, 4)))
    query_value_bias = bell_draw(streams_of[5], (2, D), 0.5, 3.0, ((1, 4),))
    out_weight = bell_draw(streams_of[6], (D, D), (max(1, D * 16 // SEQ)) ** -0.5, 1.5, ((0, 4), (1, 8)))
    branch_bias = bell_draw(streams_of[7], (2, D), 0.5, 3.0)
    up_weight = bell_draw(streams_of[8], (D, FF), D ** -0.5, 0.1875, ((0, 8), (1, 4)))
    up_bias = bell_draw(streams_of[9], (FF,), 0.5, 3.0, ((0, 4),))
    down_weight = bell_draw(streams_of[10], (FF, D), (FF // 4) ** -0.5, 0.1875, ((0, 4), (1, 8)))
    cotangent = bell_draw(streams_of[11], (BATCH, SEQ, D), 1.0, 6.0, ((0, 8), (1, 4)))
    return {"latents": latents, "conditioning": conditioning, "mod_weight": mod_weight, "mod_bias": mod_bias, "in_weight": in_weight, "query_value_bias": query_value_bias, "out_weight": out_weight, "branch_bias": branch_bias, "up_weight": up_weight, "up_bias": up_bias, "down_weight": down_weight, "cotangent": cotangent}


@jax.custom_vjp
def low(v):
    return lax.optimization_barrier(v.astype(jnp.bfloat16)).astype(jnp.float32)

@jax.custom_vjp
def low_back(v):
    return v

def low_keep(v):
    return (low(v), None)

def low_pass(kept, grad):
    return (grad,)

def back_keep(v):
    return (v, None)

def back_low(kept, grad):
    return (low(grad),)
low.defvjp(low_keep, low_pass)
low_back.defvjp(back_keep, back_low)
eps_norm = 1e-06
tanh_coeff = 0.7978845608028654
cubic_coeff = 0.044715

def gelu_tanh(inputs):
    inner = tanh_coeff * (inputs + cubic_coeff * inputs * inputs * inputs)
    return 0.5 * inputs * (1.0 + jnp.tanh(inner))

def normalize(values):
    centre = values - lax.optimization_barrier(jnp.mean(values, axis=-1, keepdims=True))
    spread = lax.optimization_barrier(jnp.mean(centre * centre, axis=-1, keepdims=True))
    return centre * lax.rsqrt(spread + eps_norm)

def group_copies(values):
    return low_back(jnp.broadcast_to(values[None], (N_TENSOR,) + values.shape))

def image_block(latent, cond_vec, mod_weight, mod_bias, in_weight, query_value_bias, out_weight, branch_bias, up_weight, up_bias, down_weight):
    highest = lax.Precision.HIGHEST
    col_group = D // N_TENSOR
    unit_group = FF // N_TENSOR
    silu_cond = low(jax.nn.silu(cond_vec))
    modulation = jnp.einsum('d,dcj->cj', silu_cond, mod_weight, precision=highest) + mod_bias
    h_first = low(normalize(latent) * (1.0 + modulation[1]) + modulation[0])
    first_copies = group_copies(h_first)
    in_groups = in_weight.reshape(3, D, N_TENSOR, col_group)
    triple = jnp.einsum('gsd,cdge->scge', first_copies, in_groups, precision=highest).reshape(SEQ, 3, D)
    triple_bias = jnp.stack([query_value_bias[0], jnp.zeros_like(query_value_bias[0]), query_value_bias[1]])
    triple = low(low_back(triple + triple_bias))
    queries = triple[:, 0].reshape(SEQ, HEADS, HEAD_DIM)
    key_rows = triple[:, 1].reshape(SEQ, HEADS, HEAD_DIM)
    value_rows = triple[:, 2].reshape(SEQ, HEADS, HEAD_DIM)
    scores = low_back(jnp.einsum('qhe,khe->hqk', queries, key_rows, precision=highest) * HEAD_DIM ** (-0.5))
    probs = jax.nn.softmax(scores, axis=-1)
    mixed = jnp.einsum('hqk,khe->qhe', low(probs), value_rows, precision=highest).reshape(SEQ, D)
    mixed = low(low_back(mixed))
    attn_parts = jnp.einsum('sgc,gcd->gsd', mixed.reshape(SEQ, N_TENSOR, col_group), out_weight.reshape(N_TENSOR, col_group, D), precision=highest)
    attn_branch = low_back(lax.optimization_barrier(jnp.sum(low(attn_parts), axis=0)) + branch_bias[0])
    resid = latent + modulation[2] * attn_branch
    h_second = low(normalize(resid) * (1.0 + modulation[4]) + modulation[3])
    second_copies = group_copies(h_second)
    pre_act = jnp.einsum('gsd,dgf->sgf', second_copies, up_weight.reshape(D, N_TENSOR, unit_group), precision=highest).reshape(SEQ, FF)
    pre_act = low_back(pre_act + up_bias)
    hidden = low(gelu_tanh(pre_act))
    ffn_parts = jnp.einsum('sgf,gfd->gsd', hidden.reshape(SEQ, N_TENSOR, unit_group), down_weight.reshape(N_TENSOR, unit_group, D), precision=highest)
    ffn_branch = low_back(lax.optimization_barrier(jnp.sum(low(ffn_parts), axis=0)) + branch_bias[1])
    return resid + modulation[5] * ffn_branch

def reference(latents, conditioning, mod_weight, mod_bias, in_weight, query_value_bias, out_weight, branch_bias, up_weight, up_bias, down_weight, cotangent):
    params = tuple((item.astype(jnp.float32) for item in (mod_weight, mod_bias, in_weight, query_value_bias, out_weight, branch_bias, up_weight, up_bias, down_weight)))
    zero_grads = tuple((jnp.zeros_like(item) for item in params))

    def one_image(totals, item):
        latent_rows, cond_row, grad_rows = item
        result, backward = jax.vjp(image_block, latent_rows.astype(jnp.float32), cond_row.astype(jnp.float32), *params)
        grads = backward(grad_rows.astype(jnp.float32))
        totals = tuple((total + grad for total, grad in zip(totals, grads[2:])))
        return (totals, (result.astype(jnp.bfloat16), grads[0].astype(jnp.bfloat16), grads[1]))
    totals, outputs = lax.scan(one_image, zero_grads, (latents, conditioning, cotangent))
    return (outputs[0], outputs[1], outputs[2], totals[0], totals[1], totals[2], totals[3], totals[4], totals[5], totals[6], totals[7], totals[8])
```

```python
import functools

import jax
import jax.numpy as jnp
from jax import lax
from jax.experimental import pallas as pl
from jax.experimental.pallas import tpu as pltpu
from jax.sharding import PartitionSpec as P

HEAD_DIM = 72
EPS = 1e-06
TANH_C = 0.7978845608028654
CUBIC = 0.044715
LOG2E = 1.4426950408889634
VMEM_BYTES = 56 << 20
ROWS = 16
BF = jnp.bfloat16
F32 = jnp.float32
BOTH = ("fsdp", "tensor")


def dotg(a, b, ca, cb):
    return lax.dot_general(a, b, (((ca,), (cb,)), ((), ())), preferred_element_type=F32)


class Geo:
    def __init__(self, fsdp, tensor, dim):
        self.F, self.T, self.P = fsdp, tensor, fsdp // 2
        self.Th = tensor // 2
        self.D = dim
        self.R = dim // fsdp
        self.bits = [1 << b for b in range((self.P - 1).bit_length())]
        self.order = (self.orders(self.bits[::-1]), self.orders(self.bits))
        self.direct = self.R % 16 == 0

    @staticmethod
    def orders(msb_first):
        vals = [0]
        for bit in reversed(msb_first):
            vals = vals + [v | bit for v in vals]
        return vals


def reorder(x, index, axis=0):
    return jnp.stack([lax.dynamic_index_in_dim(x, i, axis, keepdims=False) for i in index], axis)


def flip_pair(x, bit, geo):
    return lax.ppermute(x, "fsdp", [(i, i ^ (2 * bit)) for i in range(geo.F)])


def flip_core(x, geo):
    return lax.ppermute(x, "fsdp", [(i, i ^ 1) for i in range(geo.F)])


def flip_tensor(x, k, geo):
    return lax.ppermute(x, "tensor", [(i, i ^ k) for i in range(geo.T)])


def gather_weight(shard, geo):
    parts = [shard] + [flip_tensor(shard, k, geo) for k in range(1, geo.T)]
    halves = []
    for half in range(2):
        buf = jnp.stack(parts[half * geo.Th : (half + 1) * geo.Th])[None]
        bits = geo.bits if half == 0 else geo.bits[::-1]
        for bit in bits[:-1]:
            buf = jnp.concatenate([buf, flip_pair(buf, bit, geo)])
        own = [buf, flip_pair(buf, bits[-1], geo)]
        other = [flip_core(a, geo) for a in own]
        halves.append(own + other)
    return halves


class Gathered:
    def __init__(self, halves, geo, scal):
        self.geo = geo
        if not geo.direct:
            fixed = []
            for half, arrays in enumerate(halves):
                at = [geo.order[half].index(rel) for rel in range(geo.P)]
                lookup = jnp.array(at, jnp.int32)
                blocks = jnp.concatenate(arrays)
                blocks = reorder(
                    blocks,
                    [
                        lookup[(f // 2) ^ scal[0]] + geo.P * ((f % 2) ^ scal[1])
                        for f in range(geo.F)
                    ],
                )
                _, th, k, r, w = blocks.shape
                fixed.append([blocks.transpose(1, 2, 0, 3, 4).reshape(1, th, k, geo.D, w)])
            halves = fixed
        self.arrays = halves[0] + halves[1]
        self.n = len(halves[0])
        self.width = self.arrays[0].shape[-1]

    def specs(self, plane, count):
        th = self.geo.Th
        out = []
        for idx, a in enumerate(self.arrays):
            block = (a.shape[0], 1, count, a.shape[3], a.shape[4])
            if idx < self.n:
                out.append(pl.BlockSpec(block, lambda j, s: (0, jnp.minimum(j, th - 1), plane, 0, 0)))
            else:
                out.append(pl.BlockSpec(block, lambda j, s: (0, jnp.maximum(j - th, 0), plane, 0, 0)))
        return out

    def assemble(self, j, s_ref, refs, dst):
        geo = self.geo
        for half in range(2):

            @pl.when((j < geo.Th) if half == 0 else (j >= geo.Th))
            def _():
                for at in range(self.n):
                    ref = refs[half * self.n + at]
                    n, _, count, rows, _ = ref.shape
                    for i in range(n):
                        if geo.direct:
                            rel = geo.order[half][(at % 2) * n + i]
                            place = 2 * (s_ref[0] ^ rel) + (s_ref[1] ^ (at // 2))
                            place = pl.multiple_of(place * rows, rows)
                        else:
                            place = 0
                        for q in range(count):
                            dst[q, pl.ds(place, rows), :] = ref[i, 0, q]


def scatter_grad(pieces, geo):
    def add(a, b):
        return a.astype(F32) + b.astype(F32)

    halves = []
    for half in range(2):
        keep, send = pieces[2 * half], pieces[2 * half + 1]
        bits = geo.bits[::-1] if half == 0 else geo.bits
        for at, bit in enumerate(bits):
            got = flip_pair(send, bit, geo)
            if at == len(bits) - 1:
                halves.append(add(keep, got)[0].astype(BF))
            else:
                m = keep.shape[0] // 2
                send = add(keep[m:], got[m:]).astype(BF)
                keep = add(keep[:m], got[:m]).astype(BF)
    keep, send = halves
    size = geo.Th
    while True:
        got = flip_tensor(send, size, geo)
        if size == 1:
            return add(keep, got)[0]
        size //= 2
        send = add(keep[size:], got[size:]).astype(BF)
        keep = add(keep[:size], got[:size]).astype(BF)


def params():
    return pltpu.CompilerParams(vmem_limit_bytes=VMEM_BYTES)


def cost(flops, size):
    return pl.CostEstimate(flops=int(flops), bytes_accessed=int(size), transcendentals=0)


def whole(shape):
    zeros = (0,) * len(shape)
    return pl.BlockSpec(shape, lambda j, s: zeros)


def chunked(total, want):
    return want if total % want == 0 else total


def norm_of(v):
    centre = v - jnp.mean(v, axis=-1, keepdims=True)
    inv = lax.rsqrt(jnp.mean(centre * centre, axis=-1, keepdims=True) + EPS)
    return centre * inv, inv


def norm_back(norm, inv, g):
    return (
        g
        - jnp.mean(g, axis=-1, keepdims=True)
        - norm * jnp.mean(g * norm, axis=-1, keepdims=True)
    ) * inv


def fold_rows(v):
    return v.reshape(v.shape[0] // 8, 8, v.shape[1]).sum(axis=0)


def in_proj(scal, x, mod, wt, bias, geo):
    n, d = x.shape
    w = wt.width
    nw = len(wt.arrays)

    def kernel(s, x_ref, m_ref, b_ref, *refs):
        w_refs, (h_ref, q_ref, kv_ref, wbuf) = refs[:nw], refs[nw:]
        j = pl.program_id(0)

        @pl.when(j == 0)
        def _():
            @pl.loop(0, n // ROWS)
            def _(i):
                at = pl.ds(pl.multiple_of(i * ROWS, ROWS), ROWS)
                norm, _ = norm_of(x_ref[at, :].astype(F32))
                h_ref[at, :] = (norm * (1.0 + m_ref[1:2, :]) + m_ref[0:1, :]).astype(BF)

        wt.assemble(j, s, w_refs, wbuf)
        for q in range(3):
            y = dotg(h_ref[...], wbuf[q], 1, 0) + b_ref[0, q]
            if q == 0:
                q_ref[0] = y.astype(BF)
            else:
                kv_ref[0, q - 1] = y.astype(BF)

    return pl.pallas_call(
        kernel,
        grid_spec=pltpu.PrefetchScalarGridSpec(
            num_scalar_prefetch=1,
            grid=(geo.T,),
            in_specs=[
                whole((n, d)),
                whole(mod.shape),
                pl.BlockSpec((1, 3, 1, w), lambda j, s: (s[2] ^ j, 0, 0, 0)),
                *wt.specs(0, 3),
            ],
            out_specs=[
                whole((n, d)),
                pl.BlockSpec((1, n, w), lambda j, s: (j, 0, 0)),
                pl.BlockSpec((1, 2, n, w), lambda j, s: (j, 0, 0, 0)),
            ],
            scratch_shapes=[pltpu.VMEM((3, d, w), BF)],
        ),
        out_shape=[
            jax.ShapeDtypeStruct((n, d), BF),
            jax.ShapeDtypeStruct((geo.T, n, w), BF),
            jax.ShapeDtypeStruct((geo.T, 2, n, w), BF),
        ],
        compiler_params=params(),
        cost_estimate=cost(6 * n * d * d, 6 * d * d + 8 * n * d),
        name="in_proj",
    )(scal, x, mod, bias, *wt.arrays)


def attn_fwd(q, kv, kvo):
    z, n, w = q.shape
    heads = w // HEAD_DIM
    c = HEAD_DIM**-0.5 * LOG2E

    def kernel(q_ref, kv_ref, kvo_ref, o_ref, lse_ref):
        outs = []
        for h in range(heads):
            sl = slice(h * HEAD_DIM, (h + 1) * HEAD_DIM)
            qh = q_ref[0, :, sl]
            sa = dotg(kv_ref[0, 0, :, sl], qh, 1, 1) * c
            sb = dotg(kvo_ref[0, 0, :, sl], qh, 1, 1) * c
            top = jnp.maximum(
                jnp.max(sa, axis=0, keepdims=True), jnp.max(sb, axis=0, keepdims=True)
            )
            pa, pb = jnp.exp2(sa - top), jnp.exp2(sb - top)
            total = jnp.sum(pa, axis=0, keepdims=True) + jnp.sum(pb, axis=0, keepdims=True)
            o = dotg(kv_ref[0, 1, :, sl], pa.astype(BF), 0, 0)
            o = o + dotg(kvo_ref[0, 1, :, sl], pb.astype(BF), 0, 0)
            outs.append(o / total)
            lse_ref[0, h : h + 1, :] = top + jnp.log2(total)
        o_ref[0] = jnp.concatenate(outs, axis=0).T.astype(BF)

    s3 = pl.BlockSpec((1, n, w), lambda j: (j, 0, 0))
    s4 = pl.BlockSpec((1, 2, n, w), lambda j: (j, 0, 0, 0))
    sl = pl.BlockSpec((1, heads, n), lambda j: (j, 0, 0))
    return pl.pallas_call(
        kernel,
        grid=(z,),
        in_specs=[s3, s4, s4],
        out_specs=[s3, sl],
        out_shape=[
            jax.ShapeDtypeStruct((z, n, w), BF),
            jax.ShapeDtypeStruct((z, heads, n), F32),
        ],
        compiler_params=params(),
        cost_estimate=cost(30 * 1e9, 14 * z * n * w),
        name="attn_fwd",
    )(q, kv, kvo)


def attn_bwd(q, kv, kvo, o, do, lse):
    z, n, w = q.shape
    heads = w // HEAD_DIM
    scale = HEAD_DIM**-0.5
    c = scale * LOG2E

    def kernel(q_ref, kv_ref, kvo_ref, o_ref, do_ref, lse_ref, dq_ref, dkv_ref, dkvo_ref, sum_ref):
        both = (do_ref[0].astype(F32) * o_ref[0].astype(F32)).T
        dqs, parts = [], [[[], []], [[], []]]
        for h in range(heads):
            sl = slice(h * HEAD_DIM, (h + 1) * HEAD_DIM)
            qh, doh = q_ref[0, :, sl], do_ref[0, :, sl]
            delta = jnp.sum(both[sl], axis=0, keepdims=True)
            lse_h = lse_ref[0, h : h + 1, :]
            dq = None
            for i, ref in enumerate((kv_ref, kvo_ref)):
                k, v = ref[0, 0, :, sl], ref[0, 1, :, sl]
                p = jnp.exp2(dotg(k, qh, 1, 1) * c - lse_h)
                ds = (p * (dotg(v, doh, 1, 1) - delta)).astype(BF)
                parts[i][1].append(dotg(doh, p.astype(BF), 0, 1))
                parts[i][0].append(dotg(qh, ds, 0, 1) * scale)
                got = dotg(k, ds, 0, 0)
                dq = got if dq is None else dq + got
            dqs.append(dq * scale)
        dq = jnp.concatenate(dqs, axis=0).T
        dq_ref[0] = dq.astype(BF)
        sum_ref[0, 0:1, :] = jnp.sum(dq, axis=0, keepdims=True)
        dv_sum = None
        for i, ref in enumerate((dkv_ref, dkvo_ref)):
            for at in range(2):
                full = jnp.concatenate(parts[i][at], axis=0).T
                ref[0, at] = full.astype(BF)
                if at == 1:
                    now = jnp.sum(full, axis=0, keepdims=True)
                    dv_sum = now if dv_sum is None else dv_sum + now
        sum_ref[0, 1:2, :] = dv_sum

    s3 = pl.BlockSpec((1, n, w), lambda j: (j, 0, 0))
    s4 = pl.BlockSpec((1, 2, n, w), lambda j: (j, 0, 0, 0))
    sl = pl.BlockSpec((1, heads, n), lambda j: (j, 0, 0))
    return pl.pallas_call(
        kernel,
        grid=(z,),
        in_specs=[s3, s4, s4, s3, s3, sl],
        out_specs=[s3, s4, s4, pl.BlockSpec((1, 2, w), lambda j: (j, 0, 0))],
        out_shape=[
            jax.ShapeDtypeStruct((z, n, w), BF),
            jax.ShapeDtypeStruct((z, 2, n, w), BF),
            jax.ShapeDtypeStruct((z, 2, n, w), BF),
            jax.ShapeDtypeStruct((z, 2, w), F32),
        ],
        compiler_params=params(),
        cost_estimate=cost(50 * 1e9, 24 * z * n * w),
        name="attn_bwd",
    )(q, kv, kvo, o, do, lse)


def out_proj(scal, mixed, x, mod, bias, wt, geo):
    _, n, w = mixed.shape
    d = geo.D
    nw = len(wt.arrays)

    def kernel(s, y_ref, x_ref, m_ref, b_ref, *refs):
        w_refs, (attn_ref, resid_ref, h_ref, wbuf) = refs[:nw], refs[nw:]
        j = pl.program_id(0)
        wt.assemble(j, s, w_refs, wbuf)
        part = dotg(y_ref[0], wbuf[0], 1, 1)

        @pl.when(j == 0)
        def _():
            attn_ref[...] = part

        @pl.when(j > 0)
        def _():
            attn_ref[...] += part

        @pl.when(j == geo.T - 1)
        def _():
            @pl.loop(0, n // ROWS)
            def _(i):
                at = pl.ds(pl.multiple_of(i * ROWS, ROWS), ROWS)
                attn = attn_ref[at, :] + b_ref[...]
                attn_ref[at, :] = attn
                resid = x_ref[at, :].astype(F32) + m_ref[2:3, :] * attn
                resid_ref[at, :] = resid
                norm, _ = norm_of(resid)
                h_ref[at, :] = (norm * (1.0 + m_ref[4:5, :]) + m_ref[3:4, :]).astype(BF)

    return pl.pallas_call(
        kernel,
        grid_spec=pltpu.PrefetchScalarGridSpec(
            num_scalar_prefetch=1,
            grid=(geo.T,),
            in_specs=[
                pl.BlockSpec((1, n, w), lambda j, s: (j, 0, 0)),
                whole((n, d)),
                whole(mod.shape),
                whole((1, d)),
                *wt.specs(3, 1),
            ],
            out_specs=[whole((n, d))] * 3,
            scratch_shapes=[pltpu.VMEM((1, d, w), BF)],
        ),
        out_shape=[
            jax.ShapeDtypeStruct((n, d), F32),
            jax.ShapeDtypeStruct((n, d), F32),
            jax.ShapeDtypeStruct((n, d), BF),
        ],
        compiler_params=params(),
        cost_estimate=cost(2 * n * d * d, 2 * d * d + 14 * n * d),
        name="out_proj",
    )(scal, mixed, x, mod, bias, *wt.arrays)


def up_proj(scal, h, bias, wt, geo):
    n, d = h.shape
    w = wt.width
    nw = len(wt.arrays)
    step = chunked(w, 384)

    def kernel(s, h_ref, b_ref, *refs):
        w_refs, (hid_ref, gp_ref, wbuf) = refs[:nw], refs[nw:]
        j = pl.program_id(0)
        wt.assemble(j, s, w_refs, wbuf)
        for at in range(0, w, step):
            cols = slice(at, at + step)
            u = dotg(h_ref[...], wbuf[0, :, cols], 1, 0) + b_ref[0, :, cols]
            sq = u * u
            t = jnp.tanh(TANH_C * (u + CUBIC * sq * u))
            half = 0.5 * (1.0 + t)
            hid_ref[0, :, cols] = (u * half).astype(BF)
            slope = TANH_C * (1.0 + 3.0 * CUBIC * sq)
            gp_ref[0, :, cols] = (half + 0.5 * u * (1.0 - t * t) * slope).astype(BF)

    out = pl.BlockSpec((1, n, w), lambda j, s: (j, 0, 0))
    return pl.pallas_call(
        kernel,
        grid_spec=pltpu.PrefetchScalarGridSpec(
            num_scalar_prefetch=1,
            grid=(geo.T,),
            in_specs=[
                whole((n, d)),
                pl.BlockSpec((1, 1, w), lambda j, s: (s[2] ^ j, 0, 0)),
                *wt.specs(0, 1),
            ],
            out_specs=[out, out],
            scratch_shapes=[pltpu.VMEM((1, d, w), BF)],
        ),
        out_shape=[jax.ShapeDtypeStruct((geo.T, n, w), BF)] * 2,
        compiler_params=params(),
        cost_estimate=cost(2 * n * d * w * geo.T, 2 * geo.T * w * (d + 2 * n)),
        name="up_proj",
    )(scal, h, bias, *wt.arrays)


def down_proj(scal, hidden, resid, cot, mod, bias, wt, geo):
    _, n, w = hidden.shape
    d = geo.D
    nw = len(wt.arrays)

    def kernel(s, y_ref, r_ref, c_ref, m_ref, b_ref, *refs):
        w_refs, (out_ref, sum_ref, wbuf, acc) = refs[:nw], refs[nw:]
        j = pl.program_id(0)
        wt.assemble(j, s, w_refs, wbuf)
        part = dotg(y_ref[0], wbuf[0], 1, 1)

        @pl.when(j == 0)
        def _():
            acc[...] = part
            sum_ref[...] = jnp.zeros_like(sum_ref)

        @pl.when(j > 0)
        def _():
            acc[...] += part

        @pl.when(j == geo.T - 1)
        def _():
            @pl.loop(0, n // ROWS)
            def _(i):
                at = pl.ds(pl.multiple_of(i * ROWS, ROWS), ROWS)
                ffn = acc[at, :] + b_ref[...]
                out_ref[at, :] = (r_ref[at, :] + m_ref[5:6, :] * ffn).astype(BF)
                sum_ref[...] += fold_rows(c_ref[at, :].astype(F32) * ffn)

    return pl.pallas_call(
        kernel,
        grid_spec=pltpu.PrefetchScalarGridSpec(
            num_scalar_prefetch=1,
            grid=(geo.T,),
            in_specs=[
                pl.BlockSpec((1, n, w), lambda j, s: (j, 0, 0)),
                whole((n, d)),
                whole((n, d)),
                whole(mod.shape),
                whole((1, d)),
                *wt.specs(0, 1),
            ],
            out_specs=[whole((n, d)), whole((8, d))],
            scratch_shapes=[pltpu.VMEM((1, d, w), BF), pltpu.VMEM((n, d), F32)],
        ),
        out_shape=[jax.ShapeDtypeStruct((n, d), BF), jax.ShapeDtypeStruct((8, d), F32)],
        compiler_params=params(),
        cost_estimate=cost(2 * n * d * w * geo.T, 2 * geo.T * w * (d + n) + 8 * n * d),
        name="down_proj",
    )(scal, hidden, resid, cot, mod, bias, *wt.arrays)


def pre_back(scal, g, gp, wt, geo):
    n, d = g.shape
    w = wt.width
    nw = len(wt.arrays)
    step = chunked(w, 384)

    def kernel(s, g_ref, gp_ref, *refs):
        w_refs, (out_ref, sum_ref, wbuf) = refs[:nw], refs[nw:]
        j = pl.program_id(0)
        wt.assemble(j, s, w_refs, wbuf)
        for at in range(0, w, step):
            cols = slice(at, at + step)
            y = dotg(g_ref[...], wbuf[0, :, cols], 1, 0) * gp_ref[0, :, cols].astype(F32)
            out_ref[0, :, cols] = y.astype(BF)
            sum_ref[0, :, cols] = jnp.sum(y, axis=0, keepdims=True)

    out = pl.BlockSpec((1, n, w), lambda j, s: (j, 0, 0))
    return pl.pallas_call(
        kernel,
        grid_spec=pltpu.PrefetchScalarGridSpec(
            num_scalar_prefetch=1,
            grid=(geo.T,),
            in_specs=[whole((n, d)), out, *wt.specs(0, 1)],
            out_specs=[out, pl.BlockSpec((1, 1, w), lambda j, s: (j, 0, 0))],
            scratch_shapes=[pltpu.VMEM((1, d, w), BF)],
        ),
        out_shape=[
            jax.ShapeDtypeStruct((geo.T, n, w), BF),
            jax.ShapeDtypeStruct((geo.T, 1, w), F32),
        ],
        compiler_params=params(),
        cost_estimate=cost(2 * n * d * w * geo.T, 2 * geo.T * w * (d + 2 * n)),
        name="pre_back",
    )(scal, g, gp, *wt.arrays)


def second_back(scal, pre, resid, attn, cot, mod, wt, geo):
    _, n, w = pre.shape
    d = geo.D
    nw = len(wt.arrays)

    def kernel(s, y_ref, r_ref, a_ref, c_ref, m_ref, *refs):
        w_refs, (rg_ref, ag_ref, sum_ref, wbuf, acc) = refs[:nw], refs[nw:]
        j = pl.program_id(0)
        wt.assemble(j, s, w_refs, wbuf)
        part = dotg(y_ref[0], wbuf[0], 1, 1)

        @pl.when(j == 0)
        def _():
            acc[...] = part
            sum_ref[...] = jnp.zeros_like(sum_ref)

        @pl.when(j > 0)
        def _():
            acc[...] += part

        @pl.when(j == geo.T - 1)
        def _():
            @pl.loop(0, n // ROWS)
            def _(i):
                at = pl.ds(pl.multiple_of(i * ROWS, ROWS), ROWS)
                g = acc[at, :]
                norm, inv = norm_of(r_ref[at, :])
                rg = c_ref[at, :].astype(F32) + norm_back(norm, inv, g * (1.0 + m_ref[4:5, :]))
                rg_ref[at, :] = rg
                ag = rg * m_ref[2:3, :]
                ag_ref[at, :] = ag.astype(BF)
                sum_ref[0] += fold_rows(rg * a_ref[at, :])
                sum_ref[1] += fold_rows(g)
                sum_ref[2] += fold_rows(g * norm)
                sum_ref[3] += fold_rows(ag)

    return pl.pallas_call(
        kernel,
        grid_spec=pltpu.PrefetchScalarGridSpec(
            num_scalar_prefetch=1,
            grid=(geo.T,),
            in_specs=[
                pl.BlockSpec((1, n, w), lambda j, s: (j, 0, 0)),
                whole((n, d)),
                whole((n, d)),
                whole((n, d)),
                whole(mod.shape),
                *wt.specs(0, 1),
            ],
            out_specs=[whole((n, d)), whole((n, d)), whole((4, 8, d))],
            scratch_shapes=[pltpu.VMEM((1, d, w), BF), pltpu.VMEM((n, d), F32)],
        ),
        out_shape=[
            jax.ShapeDtypeStruct((n, d), F32),
            jax.ShapeDtypeStruct((n, d), BF),
            jax.ShapeDtypeStruct((4, 8, d), F32),
        ],
        compiler_params=params(),
        cost_estimate=cost(2 * n * d * w * geo.T, 2 * geo.T * w * (d + n) + 18 * n * d),
        name="second_back",
    )(scal, pre, resid, attn, cot, mod, *wt.arrays)


def mixed_back(scal, g, wt, geo):
    n, d = g.shape
    w = wt.width
    nw = len(wt.arrays)

    def kernel(s, g_ref, *refs):
        w_refs, (out_ref, wbuf) = refs[:nw], refs[nw:]
        wt.assemble(pl.program_id(0), s, w_refs, wbuf)
        out_ref[0] = dotg(g_ref[...], wbuf[0], 1, 0).astype(BF)

    return pl.pallas_call(
        kernel,
        grid_spec=pltpu.PrefetchScalarGridSpec(
            num_scalar_prefetch=1,
            grid=(geo.T,),
            in_specs=[whole((n, d)), *wt.specs(3, 1)],
            out_specs=pl.BlockSpec((1, n, w), lambda j, s: (j, 0, 0)),
            scratch_shapes=[pltpu.VMEM((1, d, w), BF)],
        ),
        out_shape=jax.ShapeDtypeStruct((geo.T, n, w), BF),
        compiler_params=params(),
        cost_estimate=cost(2 * n * d * d, 2 * d * d + 4 * n * d),
        name="mixed_back",
    )(scal, g, *wt.arrays)


def first_back(scal, dq, dkv, x, rg, mod, wt, geo):
    _, n, w = dq.shape
    d = geo.D
    nw = len(wt.arrays)

    def kernel(s, q_ref, kv_ref, x_ref, r_ref, m_ref, *refs):
        w_refs, (out_ref, sum_ref, wbuf, acc) = refs[:nw], refs[nw:]
        j = pl.program_id(0)
        wt.assemble(j, s, w_refs, wbuf)
        part = dotg(q_ref[0], wbuf[0], 1, 1)
        part += dotg(kv_ref[0, 0], wbuf[1], 1, 1)
        part += dotg(kv_ref[0, 1], wbuf[2], 1, 1)

        @pl.when(j == 0)
        def _():
            acc[...] = part
            sum_ref[...] = jnp.zeros_like(sum_ref)

        @pl.when(j > 0)
        def _():
            acc[...] += part

        @pl.when(j == geo.T - 1)
        def _():
            @pl.loop(0, n // ROWS)
            def _(i):
                at = pl.ds(pl.multiple_of(i * ROWS, ROWS), ROWS)
                g = acc[at, :]
                norm, inv = norm_of(x_ref[at, :].astype(F32))
                back = norm_back(norm, inv, g * (1.0 + m_ref[1:2, :]))
                out_ref[at, :] = (r_ref[at, :] + back).astype(BF)
                sum_ref[0] += fold_rows(g)
                sum_ref[1] += fold_rows(g * norm)

    return pl.pallas_call(
        kernel,
        grid_spec=pltpu.PrefetchScalarGridSpec(
            num_scalar_prefetch=1,
            grid=(geo.T,),
            in_specs=[
                pl.BlockSpec((1, n, w), lambda j, s: (j, 0, 0)),
                pl.BlockSpec((1, 2, n, w), lambda j, s: (j, 0, 0, 0)),
                whole((n, d)),
                whole((n, d)),
                whole(mod.shape),
                *wt.specs(0, 3),
            ],
            out_specs=[whole((n, d)), whole((2, 8, d))],
            scratch_shapes=[pltpu.VMEM((3, d, w), BF), pltpu.VMEM((n, d), F32)],
        ),
        out_shape=[jax.ShapeDtypeStruct((n, d), BF), jax.ShapeDtypeStruct((2, 8, d), F32)],
        compiler_params=params(),
        cost_estimate=cost(6 * n * d * d, 6 * d * d + 16 * n * d),
        name="first_back",
    )(scal, dq, dkv, x, rg, mod, *wt.arrays)


def weight_grad(scal, a_own, a_other, bs, geo, name):
    w = bs[0][0].shape[-1]
    n = a_own.shape[0]
    pr = geo.P * geo.R
    th = geo.Th
    planes = sum(b[0].shape[1] for b in bs)
    flat = [part for pair in bs for part in pair]
    nb = len(flat)
    half_n = geo.P // 2
    if not geo.direct:

        def pick(a):
            cols = a.reshape(n, geo.P, 2, geo.R)
            cols = jnp.where(scal[1] == 0, cols[:, :, 0], cols[:, :, 1])
            return cols.reshape(n, pr).T

        a_own, a_other = pick(a_own), pick(a_other)

    def kernel(s, a_ref, ao_ref, *refs):
        b_refs, outs = refs[:nb], refs[nb:]
        if geo.direct:
            outs, ats = outs[:-2], outs[-2:]
        else:
            ats = (a_ref, ao_ref)
        j = pl.program_id(0)

        if geo.direct:

            @pl.when(j == 0)
            def _():
                for ref, at in ((a_ref, ats[0]), (ao_ref, ats[1])):
                    flip = ref[...].T
                    for p in range(geo.P):
                        even = flip[2 * p * geo.R : (2 * p + 1) * geo.R]
                        odd = flip[(2 * p + 1) * geo.R : (2 * p + 2) * geo.R]
                        at[p * geo.R : (p + 1) * geo.R, :] = jnp.where(s[1] == 0, even, odd)

        plane = 0
        for at in range(nb // 2):
            own, other = b_refs[2 * at], b_refs[2 * at + 1]
            for q in range(own.shape[1]):
                full = dotg(ats[0][...], own[0, q], 1, 0) + dotg(ats[1][...], other[0, q], 1, 0)
                full = full.astype(BF)
                if not geo.direct:
                    outs[0][0, plane] = full
                else:
                    for half in range(2):

                        @pl.when((j < th) if half == 0 else (j >= th))
                        def _():
                            for i, rel in enumerate(geo.order[half]):
                                src = s[0] ^ rel
                                ref = outs[2 * half + i // half_n]
                                for p in range(geo.P):

                                    @pl.when(src == p)
                                    def _():
                                        ref[i % half_n, 0, plane] = full[
                                            p * geo.R : (p + 1) * geo.R
                                        ]

                plane += 1

    if geo.direct:
        a_block = (half_n, 1, planes, geo.R, w)
        specs = [
            pl.BlockSpec(a_block, lambda j, s: (0, jnp.minimum(j, th - 1), 0, 0, 0)),
            pl.BlockSpec(a_block, lambda j, s: (0, jnp.minimum(j, th - 1), 0, 0, 0)),
            pl.BlockSpec(a_block, lambda j, s: (0, jnp.maximum(j - th, 0), 0, 0, 0)),
            pl.BlockSpec(a_block, lambda j, s: (0, jnp.maximum(j - th, 0), 0, 0, 0)),
        ]
        shapes = [jax.ShapeDtypeStruct((half_n, th, planes, geo.R, w), BF)] * 4
        scratch = [pltpu.VMEM((pr, n), BF)] * 2
    else:
        specs = [pl.BlockSpec((1, planes, pr, w), lambda j, s: (j, 0, 0, 0))]
        shapes = [jax.ShapeDtypeStruct((geo.T, planes, pr, w), BF)]
        scratch = []

    got = pl.pallas_call(
        kernel,
        grid_spec=pltpu.PrefetchScalarGridSpec(
            num_scalar_prefetch=1,
            grid=(geo.T,),
            in_specs=[
                whole(a_own.shape),
                whole(a_other.shape),
                *[
                    pl.BlockSpec((1,) + b.shape[1:], lambda j, s: (j, 0, 0, 0))
                    for b in flat
                ],
            ],
            out_specs=specs,
            scratch_shapes=scratch,
        ),
        out_shape=shapes,
        compiler_params=params(),
        cost_estimate=cost(
            4 * pr * n * w * planes * geo.T, 2 * geo.T * planes * w * (pr + 2 * n)
        ),
        name=name,
    )(scal, a_own, a_other, *flat)
    if geo.direct:
        return got
    blocks = got[0].reshape(geo.T, planes, geo.P, geo.R, w)
    out = []
    for half in range(2):
        part = blocks[half * th : (half + 1) * th]
        part = reorder(part, [scal[0] ^ rel for rel in geo.order[half]], 2)
        part = part.transpose(2, 0, 1, 3, 4)
        out += [part[:half_n], part[half_n:]]
    return out


def body(
    latents,
    conditioning,
    mod_weight,
    mod_bias,
    in_weight,
    query_value_bias,
    out_weight,
    branch_bias,
    up_weight,
    up_bias,
    down_weight,
    cotangent,
):
    images, row_count, width = latents.shape
    geo = Geo(lax.axis_size("fsdp"), lax.axis_size("tensor"), width)
    F, T = geo.F, geo.T
    assert 2 * images == T
    highest = lax.Precision.HIGHEST
    fi = lax.axis_index("fsdp")
    ti = lax.axis_index("tensor")
    pair, core = fi // 2, fi % 2
    scal = jnp.stack([pair, core, ti]).astype(jnp.int32)
    cols = in_weight.shape[2]
    units = up_weight.shape[1]

    def places(k):
        return [
            ((2 * p + c) * T + t, (2 * p + t // images) * T + c * images + (t % images + k) % images)
            for p in range(geo.P)
            for c in range(2)
            for t in range(T)
        ]

    def to_chip(arr):
        got = []
        for k in range(images):
            item = lax.dynamic_index_in_dim(arr, (ti + k) % images, 0, keepdims=False)
            got.append(lax.ppermute(item, BOTH, places(k)))
        return jnp.concatenate(got)

    def from_chip(arr):
        got = []
        for k in range(images):
            back = [(dst, src) for src, dst in places(k)]
            got.append(lax.ppermute(arr[k * row_count : (k + 1) * row_count], BOTH, back))
        return reorder(jnp.stack(got), [(i - ti) % images for i in range(images)])

    attn_shard = jnp.concatenate([in_weight, out_weight.T[None]])
    attn_halves = gather_weight(attn_shard, geo)
    x = to_chip(latents)
    up_halves = gather_weight(up_weight[None], geo)
    down_halves = gather_weight(down_weight.T[None], geo)
    cot = to_chip(cotangent)

    info = jnp.concatenate([conditioning.reshape(-1), query_value_bias.reshape(-1), up_bias])
    info = lax.all_gather(info, BOTH, axis=0).reshape(F, T, -1)
    cond_all = info[:, 0, : images * width].reshape(F * images, width)
    qv_bias = info[0, :, images * width : images * width + 2 * cols].reshape(T, 2, 1, cols)
    unit_bias = info[0, :, images * width + 2 * cols :].reshape(T, 1, units).astype(F32)
    triple_bias = jnp.stack(
        [qv_bias[:, 0], jnp.zeros_like(qv_bias[:, 0]), qv_bias[:, 1]], axis=1
    ).astype(F32)
    silu_low = jax.nn.silu(cond_all.astype(F32)).astype(BF)
    silu_own = lax.dynamic_slice_in_dim(silu_low, fi * geo.R, geo.R, 1)
    mod_part = jnp.einsum("bd,dcj->bcj", silu_own, mod_weight, preferred_element_type=F32)
    mod_part += jnp.where(fi == 0, mod_bias.astype(F32), 0.0)
    mod_part = mod_part.reshape(geo.P, 1, T, 6, cols)
    mod_part = jnp.broadcast_to(mod_part, (geo.P, 2, T, 6, cols)).reshape(F * T, 6, cols)
    mod_part = lax.all_to_all(mod_part, BOTH, 0, 0, tiled=True)
    mod = mod_part.reshape(F, T, 6, cols).sum(axis=0).transpose(1, 0, 2).reshape(6, width)

    w_attn = Gathered(attn_halves, geo, scal)
    w_up = Gathered(up_halves, geo, scal)
    w_down = Gathered(down_halves, geo, scal)
    bias_rows = branch_bias.astype(F32)

    h1, q, kv = in_proj(scal, x, mod, w_attn, triple_bias, geo)
    kvo = flip_core(kv, geo)
    h1o = flip_core(h1, geo)
    mixed, lse = attn_fwd(q, kv, kvo)
    mixed_o = flip_core(mixed, geo)
    attn, resid, h2 = out_proj(scal, mixed, x, mod, bias_rows[0:1], w_attn, geo)
    h2o = flip_core(h2, geo)
    hidden, gp = up_proj(scal, h2, unit_bias, w_up, geo)
    hidden_o = flip_core(hidden, geo)
    ffn_grad = (cot.astype(F32) * mod[5]).astype(BF)
    ffn_sum = jnp.sum(ffn_grad.astype(F32), axis=0)
    ffn_o = flip_core(ffn_grad, geo)
    block_rows, ffn_sums = down_proj(scal, hidden, resid, cot, mod, bias_rows[1:2], w_down, geo)
    block_out = from_chip(block_rows)

    down_grad = scatter_grad(
        weight_grad(scal, ffn_grad, ffn_o, [(hidden[:, None], hidden_o[:, None])], geo, "w_down"),
        geo,
    )
    pre, unit_sum = pre_back(scal, ffn_grad, gp, w_down, geo)
    pre_o = flip_core(pre, geo)
    up_grad = scatter_grad(
        weight_grad(scal, h2, h2o, [(pre[:, None], pre_o[:, None])], geo, "w_up"), geo
    )
    rg, ag, mid_sums = second_back(scal, pre, resid, attn, cot, mod, w_up, geo)
    ag_o = flip_core(ag, geo)
    out_grad = scatter_grad(
        weight_grad(scal, ag, ag_o, [(mixed[:, None], mixed_o[:, None])], geo, "w_out"), geo
    )
    mg = mixed_back(scal, ag, w_attn, geo)
    dq, dkv, dkv_send, tri_sums = attn_bwd(q, kv, kvo, mixed, mg, lse)
    dq_o = flip_core(dq, geo)
    dkv = (dkv.astype(F32) + flip_core(dkv_send, geo).astype(F32)).astype(BF)
    dkv_o = flip_core(dkv, geo)
    in_grad = scatter_grad(
        weight_grad(scal, h1, h1o, [(dq[:, None], dq_o[:, None]), (dkv, dkv_o)], geo, "w_in"), geo
    )
    latent_rows, first_sums = first_back(scal, dq, dkv, x, rg, mod, w_attn, geo)
    latent_grad = from_chip(latent_rows)

    mine = [i ^ ti for i in range(T)]
    bias_pack = jnp.concatenate(
        [
            mid_sums[3].sum(axis=0),
            ffn_sum,
            reorder(unit_sum, mine).reshape(-1),
            reorder(tri_sums, mine).reshape(-1),
        ]
    )
    bias_total = lax.psum(bias_pack, BOTH)
    branch_grad = bias_total[: 2 * width].reshape(2, width)
    unit_grad = lax.dynamic_index_in_dim(
        bias_total[2 * width : 2 * width + T * units].reshape(T, units), ti, 0, keepdims=False
    )
    pair_grad = lax.dynamic_index_in_dim(
        bias_total[2 * width + T * units :].reshape(T, 2, cols), ti, 0, keepdims=False
    )

    rows = jnp.concatenate(
        [first_sums.sum(axis=1), mid_sums[:3].sum(axis=1), ffn_sums.sum(axis=0, keepdims=True)]
    )
    rows = lax.all_gather(rows, BOTH, axis=0)
    rows = rows.reshape(geo.P, 2, T, 6, width).sum(axis=1).reshape(F * images, 6, width)
    mine_rows = lax.dynamic_slice_in_dim(rows, ti * cols, cols, 2)
    mod_weight_grad = jnp.einsum(
        "bd,bcj->dcj", silu_own.astype(F32), mine_rows, precision=highest
    )
    mod_bias_grad = mine_rows.sum(axis=0)
    cond_part = jnp.einsum("bcj,dcj->bd", mine_rows, mod_weight.astype(F32), precision=highest)
    cond_all_parts = lax.all_gather(cond_part, BOTH, axis=0).reshape(F, T, F * images, geo.R)
    cond_mine = lax.dynamic_slice_in_dim(cond_all_parts.sum(axis=1), fi * images, images, 1)
    silu_grad = cond_mine.transpose(1, 0, 2).reshape(images, width)
    cond_f = conditioning.astype(F32)
    sig = jax.nn.sigmoid(cond_f)
    cond_grad = silu_grad * (sig * (1.0 + cond_f * (1.0 - sig)))

    return (
        block_out,
        latent_grad,
        cond_grad,
        mod_weight_grad,
        mod_bias_grad,
        in_grad,
        pair_grad,
        out_grad[0].T,
        branch_grad,
        up_grad[0],
        unit_grad,
        down_grad[0].T,
    )


def solution(mesh):
    in_specs = (
        P("fsdp", "tensor", None),
        P("fsdp", None),
        P("fsdp", None, "tensor"),
        P(None, "tensor"),
        P(None, "fsdp", "tensor"),
        P(None, "tensor"),
        P("tensor", "fsdp"),
        P(),
        P("fsdp", "tensor"),
        P("tensor"),
        P("tensor", "fsdp"),
        P("fsdp", "tensor", None),
    )
    out_specs = (
        P("fsdp", "tensor", None),
        P("fsdp", "tensor", None),
        P("fsdp", None),
        P("fsdp", None, "tensor"),
        P(None, "tensor"),
        P(None, "fsdp", "tensor"),
        P(None, "tensor"),
        P("tensor", "fsdp"),
        P(),
        P("fsdp", "tensor"),
        P("tensor"),
        P("tensor", "fsdp"),
    )
    return jax.shard_map(body, mesh=mesh, in_specs=in_specs, out_specs=out_specs, check_vma=False)
```

```python
import functools

import jax
import jax.numpy as jnp
from jax import lax
from jax.experimental import pallas as pl
from jax.experimental.pallas import tpu as pltpu
from jax.sharding import PartitionSpec as P

HEAD_DIM = 72
EPS = 1e-06
TANH_C = 0.7978845608028654
CUBIC = 0.044715
LOG2E = 1.4426950408889634
VMEM_BYTES = 56 << 20
ROWS = 16
BF = jnp.bfloat16
F32 = jnp.float32
BOTH = ("fsdp", "tensor")


def dotg(a, b, ca, cb):
    return lax.dot_general(a, b, (((ca,), (cb,)), ((), ())), preferred_element_type=F32)


class Geo:
    def __init__(self, fsdp, tensor, dim):
        self.F, self.T, self.P = fsdp, tensor, fsdp // 2
        self.Th = tensor // 2
        self.D = dim
        self.R = dim // fsdp
        self.bits = [1 << b for b in range((self.P - 1).bit_length())]
        self.order = (self.orders(self.bits[::-1]), self.orders(self.bits))
        self.direct = self.R % 16 == 0

    @staticmethod
    def orders(msb_first):
        vals = [0]
        for bit in reversed(msb_first):
            vals = vals + [v | bit for v in vals]
        return vals


def reorder(x, index, axis=0):
    return jnp.stack([lax.dynamic_index_in_dim(x, i, axis, keepdims=False) for i in index], axis)


def flip_pair(x, bit, geo):
    return lax.ppermute(x, "fsdp", [(i, i ^ (2 * bit)) for i in range(geo.F)])


def flip_core(x, geo):
    return lax.ppermute(x, "fsdp", [(i, i ^ 1) for i in range(geo.F)])


def flip_tensor(x, k, geo):
    return lax.ppermute(x, "tensor", [(i, i ^ k) for i in range(geo.T)])


def after(value, *done):
    return lax.optimization_barrier((value, done))[0] if done else value


class Chain:
    def __init__(self, steps):
        self.steps = steps
        self.flight = next(steps)
        self.result = None

    def advance(self, *done):
        if self.result is not None:
            return []
        try:
            self.flight = self.steps.send(after(self.flight, *done))
        except StopIteration as end:
            self.flight, self.result = [], end.value
        return self.flight

    def finish(self, *done):
        while self.result is None:
            self.advance(*done)
        return self.result


def gather_steps(shard, geo):
    got = yield [flip_tensor(shard, k, geo) for k in range(1, geo.T)]
    parts = [shard] + got
    bufs = [jnp.stack(parts[h * geo.Th : (h + 1) * geo.Th])[None] for h in range(2)]
    for at in range(len(geo.bits)):
        bits = (geo.bits[at], geo.bits[-1 - at])
        got = yield [flip_pair(bufs[h], bits[h], geo) for h in range(2)]
        bufs = [jnp.concatenate(pair) for pair in zip(bufs, got)]
    got = yield [flip_core(b, geo) for b in bufs]
    return [[bufs[h], got[h]] for h in range(2)]


class Gathered:
    def __init__(self, halves, geo, scal):
        self.geo = geo
        if not geo.direct:
            fixed = []
            for half, arrays in enumerate(halves):
                at = [geo.order[half].index(rel) for rel in range(geo.P)]
                lookup = jnp.array(at, jnp.int32)
                blocks = jnp.concatenate(arrays)
                blocks = reorder(
                    blocks,
                    [
                        lookup[(f // 2) ^ scal[0]] + geo.P * ((f % 2) ^ scal[1])
                        for f in range(geo.F)
                    ],
                )
                _, th, r, w = blocks.shape
                fixed.append([blocks.transpose(1, 0, 2, 3).reshape(1, th, geo.D, w)])
            halves = fixed
        self.halves = halves
        self.arrays = halves[0] + halves[1]
        self.n = len(halves[0])
        self.width = self.arrays[0].shape[-1]

    def specs(self, half=None):
        th = self.geo.Th
        out = []
        for idx, a in enumerate(self.arrays if half is None else self.halves[half]):
            block = (a.shape[0], 1, a.shape[2], a.shape[3])
            if half is not None:
                out.append(pl.BlockSpec(block, lambda j, s: (0, j, 0, 0)))
            elif idx < self.n:
                out.append(pl.BlockSpec(block, lambda j, s: (0, jnp.minimum(j, th - 1), 0, 0)))
            else:
                out.append(pl.BlockSpec(block, lambda j, s: (0, jnp.maximum(j - th, 0), 0, 0)))
        return out

    def place(self, half, s_ref, refs, dst):
        geo = self.geo
        for at, ref in enumerate(refs):
            n, _, rows, _ = ref.shape
            for i in range(n):
                if geo.direct:
                    rel = geo.order[half][i]
                    row = 2 * (s_ref[0] ^ rel) + (s_ref[1] ^ at)
                    row = pl.multiple_of(row * rows, rows)
                else:
                    row = 0
                dst[pl.ds(row, rows), :] = ref[i, 0]

    def assemble(self, j, s_ref, refs, dst):
        for half in range(2):

            @pl.when((j < self.geo.Th) if half == 0 else (j >= self.geo.Th))
            def _():
                self.place(half, s_ref, refs[half * self.n : (half + 1) * self.n], dst)


def scatter_steps(pieces, geo):
    def add(a, b):
        return a.astype(F32) + b.astype(F32)

    keeps, sends = [pieces[0], pieces[2]], [pieces[1], pieces[3]]
    for at in range(len(geo.bits)):
        bits = (geo.bits[-1 - at], geo.bits[at])
        got = yield [flip_pair(sends[h], bits[h], geo) for h in range(2)]
        m = max(1, keeps[0].shape[0] // 2)
        if at < len(geo.bits) - 1:
            sends = [add(keeps[h][m:], got[h][m:]).astype(BF) for h in range(2)]
        keeps = [add(keeps[h][:m], got[h][:m]).astype(BF) for h in range(2)]
    units = [keep[0, k] for keep in keeps for k in range(geo.Th)]
    got = yield [flip_tensor(units[k], k, geo) for k in range(1, geo.T)]
    total = units[0].astype(F32)
    for part in got:
        total = total + part.astype(F32)
    return total


def params():
    return pltpu.CompilerParams(vmem_limit_bytes=VMEM_BYTES)


def cost(flops, size):
    return pl.CostEstimate(flops=int(flops), bytes_accessed=int(size), transcendentals=0)


def whole(shape):
    zeros = (0,) * len(shape)
    return pl.BlockSpec(shape, lambda j, s: zeros)


def padded(w):
    return -(-w // 128) * 128


def chunked(total, want):
    return want if total % want == 0 else total


def norm_of(v):
    centre = v - jnp.mean(v, axis=-1, keepdims=True)
    inv = lax.rsqrt(jnp.mean(centre * centre, axis=-1, keepdims=True) + EPS)
    return centre * inv, inv


def norm_back(norm, inv, g):
    return (
        g
        - jnp.mean(g, axis=-1, keepdims=True)
        - norm * jnp.mean(g * norm, axis=-1, keepdims=True)
    ) * inv


def fold_rows(v):
    return v.reshape(v.shape[0] // 8, 8, v.shape[1]).sum(axis=0)


def two_halves(block, th, tail):
    return [
        pl.BlockSpec(block, lambda j, s: (jnp.minimum(j, th - 1),) + tail),
        pl.BlockSpec(block, lambda j, s: (jnp.maximum(j - th, 0),) + tail),
    ]


def norm_mod(x, mod):
    n, d = x.shape

    def kernel(x_ref, m_ref, h_ref):
        @pl.loop(0, n // ROWS, unroll=4)
        def _(i):
            at = pl.ds(pl.multiple_of(i * ROWS, ROWS), ROWS)
            norm, _ = norm_of(x_ref[at, :].astype(F32))
            h_ref[at, :] = (norm * (1.0 + m_ref[1:2, :]) + m_ref[0:1, :]).astype(BF)

    return pl.pallas_call(
        kernel,
        out_shape=jax.ShapeDtypeStruct((n, d), BF),
        compiler_params=params(),
        cost_estimate=cost(20 * n * d, 4 * n * d),
        name="norm_mod",
    )(x, mod)


def in_proj(scal, h, wt, bias, w, half, geo):
    n, d = h.shape
    wp = padded(w)
    nw = wt.n

    def kernel(s, h_ref, b_ref, *refs):
        w_refs, (q_ref, kv_ref, wbuf) = refs[:nw], refs[nw:]
        wt.place(half, s, w_refs, wbuf)
        y = dotg(h_ref[...], wbuf[:, : 3 * w], 1, 0) + b_ref[0]
        y = y.astype(BF)
        q_ref[0, :, :w] = y[:, :w]
        kv_ref[0, 0, :, :w] = y[:, w : 2 * w]
        kv_ref[0, 1, :, :w] = y[:, 2 * w :]

    first = half * geo.Th
    return pl.pallas_call(
        kernel,
        grid_spec=pltpu.PrefetchScalarGridSpec(
            num_scalar_prefetch=1,
            grid=(geo.Th,),
            in_specs=[
                whole((n, d)),
                pl.BlockSpec((1, 1, 3 * w), lambda j, s: (s[2] ^ (j + first), 0, 0)),
                *wt.specs(half),
            ],
            out_specs=[
                pl.BlockSpec((1, n, wp), lambda j, s: (j, 0, 0)),
                pl.BlockSpec((1, 2, n, wp), lambda j, s: (j, 0, 0, 0)),
            ],
            scratch_shapes=[pltpu.VMEM((d, wt.width), BF)],
        ),
        out_shape=[
            jax.ShapeDtypeStruct((geo.Th, n, wp), BF),
            jax.ShapeDtypeStruct((geo.Th, 2, n, wp), BF),
        ],
        compiler_params=params(),
        cost_estimate=cost(6 * n * d * w * geo.Th, 8 * d * w * geo.Th + 8 * n * d),
        name="in_proj",
    )(scal, h, bias, *wt.halves[half])


def attn_fwd(q, kv, kvo, heads):
    z, n, w = q.shape
    used = heads * HEAD_DIM
    c = HEAD_DIM**-0.5 * LOG2E

    def kernel(q_ref, kv_ref, kvo_ref, o_ref, lse_ref):
        outs = []
        for h in range(heads):
            sl = slice(h * HEAD_DIM, (h + 1) * HEAD_DIM)
            qh = q_ref[0, :, sl]
            sa = dotg(kv_ref[0, 0, :, sl], qh, 1, 1) * c
            sb = dotg(kvo_ref[0, 0, :, sl], qh, 1, 1) * c
            top = jnp.maximum(
                jnp.max(sa, axis=0, keepdims=True), jnp.max(sb, axis=0, keepdims=True)
            )
            pa, pb = jnp.exp2(sa - top), jnp.exp2(sb - top)
            total = jnp.sum(pa, axis=0, keepdims=True) + jnp.sum(pb, axis=0, keepdims=True)
            o = dotg(kv_ref[0, 1, :, sl], pa.astype(BF), 0, 0)
            o = o + dotg(kvo_ref[0, 1, :, sl], pb.astype(BF), 0, 0)
            outs.append(o / total)
            lse_ref[0, h : h + 1, :] = top + jnp.log2(total)
        o_ref[0, :, :used] = jnp.concatenate(outs, axis=0).T.astype(BF)

    s3 = pl.BlockSpec((1, n, w), lambda j: (j, 0, 0))
    s4 = pl.BlockSpec((1, 2, n, w), lambda j: (j, 0, 0, 0))
    sl = pl.BlockSpec((1, heads, n), lambda j: (j, 0, 0))
    return pl.pallas_call(
        kernel,
        grid=(z,),
        in_specs=[s3, s4, s4],
        out_specs=[s3, sl],
        out_shape=[
            jax.ShapeDtypeStruct((z, n, w), BF),
            jax.ShapeDtypeStruct((z, heads, n), F32),
        ],
        compiler_params=params(),
        cost_estimate=cost(3e9 * z, 14 * z * n * w),
        name="attn_fwd",
    )(q, kv, kvo)


def attn_bwd(q, kv, kvo, o, do, lse, first):
    z, n, w = q.shape
    heads = lse.shape[1]
    used = heads * HEAD_DIM
    scale = HEAD_DIM**-0.5
    c = scale * LOG2E

    def kernel(q_ref, kv_ref, kvo_ref, o_ref, do_ref, lse_ref, dq_ref, dkv_ref, dkvo_ref, sum_ref):
        both = (do_ref[0, :, :used].astype(F32) * o_ref[0, :, :used].astype(F32)).T
        dqs, parts = [], [[[], []], [[], []]]
        for h in range(heads):
            sl = slice(h * HEAD_DIM, (h + 1) * HEAD_DIM)
            qh, doh = q_ref[0, :, sl], do_ref[0, :, sl]
            delta = jnp.sum(both[sl], axis=0, keepdims=True)
            lse_h = lse_ref[0, h : h + 1, :]
            dq = None
            for i, ref in enumerate((kv_ref, kvo_ref)):
                k, v = ref[0, 0, :, sl], ref[0, 1, :, sl]
                p = jnp.exp2(dotg(k, qh, 1, 1) * c - lse_h)
                ds = (p * (dotg(v, doh, 1, 1) - delta)).astype(BF)
                parts[i][1].append(dotg(doh, p.astype(BF), 0, 1))
                parts[i][0].append(dotg(qh, ds, 0, 1) * scale)
                got = dotg(k, ds, 0, 0)
                dq = got if dq is None else dq + got
            dqs.append(dq * scale)
        dq = jnp.concatenate(dqs, axis=0).T
        dq_ref[0, :, :used] = dq.astype(BF)
        sum_ref[0, 0:1, :] = jnp.sum(dq, axis=0, keepdims=True)
        dv_sum = None
        for i, ref in enumerate((dkv_ref, dkvo_ref)):
            for at in range(2):
                full = jnp.concatenate(parts[i][at], axis=0).T
                ref[0, at, :, :used] = full.astype(BF)
                if at == 1:
                    now = jnp.sum(full, axis=0, keepdims=True)
                    dv_sum = now if dv_sum is None else dv_sum + now
        sum_ref[0, 1:2, :] = dv_sum

    s3 = pl.BlockSpec((1, n, w), lambda j: (j, 0, 0))
    s4 = pl.BlockSpec((1, 2, n, w), lambda j: (j, 0, 0, 0))
    sl = pl.BlockSpec((1, heads, n), lambda j: (j, 0, 0))
    return pl.pallas_call(
        kernel,
        grid=(z,),
        in_specs=[s3, s4, s4, s3, pl.BlockSpec((1, n, w), lambda j: (j + first, 0, 0)), sl],
        out_specs=[s3, s4, s4, pl.BlockSpec((1, 2, used), lambda j: (j, 0, 0))],
        out_shape=[
            jax.ShapeDtypeStruct((z, n, w), BF),
            jax.ShapeDtypeStruct((z, 2, n, w), BF),
            jax.ShapeDtypeStruct((z, 2, n, w), BF),
            jax.ShapeDtypeStruct((z, 2, used), F32),
        ],
        compiler_params=params(),
        cost_estimate=cost(5e9 * z, 24 * z * n * w),
        name="attn_bwd",
    )(q, kv, kvo, o, do, lse)


def out_proj(scal, mixed, x, mod, bias, wt, geo):
    _, n, wp = mixed[0].shape
    w = wt.width // 4
    d = geo.D
    nw = len(wt.arrays)
    th = geo.Th

    def kernel(s, ya_ref, yb_ref, x_ref, m_ref, b_ref, *refs):
        w_refs, (attn_ref, resid_ref, h_ref, wbuf) = refs[:nw], refs[nw:]
        j = pl.program_id(0)
        wt.assemble(j, s, w_refs, wbuf)
        y = jnp.where(j < th, ya_ref[0, :, :w], yb_ref[0, :, :w])
        part = dotg(y, wbuf[:, 3 * w :], 1, 1)

        @pl.when(j == 0)
        def _():
            attn_ref[...] = part

        @pl.when(j > 0)
        def _():
            attn_ref[...] += part

        @pl.when(j == geo.T - 1)
        def _():
            @pl.loop(0, n // ROWS, unroll=4)
            def _(i):
                at = pl.ds(pl.multiple_of(i * ROWS, ROWS), ROWS)
                attn = attn_ref[at, :] + b_ref[...]
                attn_ref[at, :] = attn
                resid = x_ref[at, :].astype(F32) + m_ref[2:3, :] * attn
                resid_ref[at, :] = resid
                norm, _ = norm_of(resid)
                h_ref[at, :] = (norm * (1.0 + m_ref[4:5, :]) + m_ref[3:4, :]).astype(BF)

    return pl.pallas_call(
        kernel,
        grid_spec=pltpu.PrefetchScalarGridSpec(
            num_scalar_prefetch=1,
            grid=(geo.T,),
            in_specs=[
                *two_halves((1, n, wp), th, (0, 0)),
                whole((n, d)),
                whole(mod.shape),
                whole((1, d)),
                *wt.specs(),
            ],
            out_specs=[whole((n, d))] * 3,
            scratch_shapes=[pltpu.VMEM((d, wt.width), BF)],
        ),
        out_shape=[
            jax.ShapeDtypeStruct((n, d), F32),
            jax.ShapeDtypeStruct((n, d), F32),
            jax.ShapeDtypeStruct((n, d), BF),
        ],
        compiler_params=params(),
        cost_estimate=cost(2 * n * d * d, 8 * d * d + 14 * n * d),
        name="out_proj",
    )(scal, *mixed, x, mod, bias, *wt.arrays)


def up_proj(scal, h, bias, wt, geo):
    n, d = h.shape
    w = wt.width
    nw = len(wt.arrays)
    step = chunked(w, 384)

    def kernel(s, h_ref, b_ref, *refs):
        w_refs, (hid_ref, gp_ref, wbuf) = refs[:nw], refs[nw:]
        j = pl.program_id(0)
        wt.assemble(j, s, w_refs, wbuf)
        for at in range(0, w, step):
            cols = slice(at, at + step)
            u = dotg(h_ref[...], wbuf[:, cols], 1, 0) + b_ref[0, :, cols]
            sq = u * u
            t = jnp.tanh(TANH_C * (u + CUBIC * sq * u))
            half = 0.5 * (1.0 + t)
            hid_ref[0, :, cols] = (u * half).astype(BF)
            slope = TANH_C * (1.0 + 3.0 * CUBIC * sq)
            gp_ref[0, :, cols] = (half + 0.5 * u * (1.0 - t * t) * slope).astype(BF)

    out = pl.BlockSpec((1, n, w), lambda j, s: (j, 0, 0))
    return pl.pallas_call(
        kernel,
        grid_spec=pltpu.PrefetchScalarGridSpec(
            num_scalar_prefetch=1,
            grid=(geo.T,),
            in_specs=[
                whole((n, d)),
                pl.BlockSpec((1, 1, w), lambda j, s: (s[2] ^ j, 0, 0)),
                *wt.specs(),
            ],
            out_specs=[out, out],
            scratch_shapes=[pltpu.VMEM((d, w), BF)],
        ),
        out_shape=[jax.ShapeDtypeStruct((geo.T, n, w), BF)] * 2,
        compiler_params=params(),
        cost_estimate=cost(2 * n * d * w * geo.T, 2 * geo.T * w * (d + 2 * n)),
        name="up_proj",
    )(scal, h, bias, *wt.arrays)


def down_proj(scal, hidden, resid, cot, mod, bias, wt, geo):
    _, n, w = hidden.shape
    d = geo.D
    nw = len(wt.arrays)

    def kernel(s, y_ref, r_ref, c_ref, m_ref, b_ref, *refs):
        w_refs, (out_ref, sum_ref, wbuf, acc) = refs[:nw], refs[nw:]
        j = pl.program_id(0)
        wt.assemble(j, s, w_refs, wbuf)
        part = dotg(y_ref[0], wbuf[...], 1, 1)

        @pl.when(j == 0)
        def _():
            acc[...] = part
            sum_ref[...] = jnp.zeros_like(sum_ref)

        @pl.when(j > 0)
        def _():
            acc[...] += part

        @pl.when(j == geo.T - 1)
        def _():
            @pl.loop(0, n // ROWS, unroll=4)
            def _(i):
                at = pl.ds(pl.multiple_of(i * ROWS, ROWS), ROWS)
                ffn = acc[at, :] + b_ref[...]
                out_ref[at, :] = (r_ref[at, :] + m_ref[5:6, :] * ffn).astype(BF)
                sum_ref[...] += fold_rows(c_ref[at, :].astype(F32) * ffn)

    return pl.pallas_call(
        kernel,
        grid_spec=pltpu.PrefetchScalarGridSpec(
            num_scalar_prefetch=1,
            grid=(geo.T,),
            in_specs=[
                pl.BlockSpec((1, n, w), lambda j, s: (j, 0, 0)),
                whole((n, d)),
                whole((n, d)),
                whole(mod.shape),
                whole((1, d)),
                *wt.specs(),
            ],
            out_specs=[whole((n, d)), whole((8, d))],
            scratch_shapes=[pltpu.VMEM((d, w), BF), pltpu.VMEM((n, d), F32)],
        ),
        out_shape=[jax.ShapeDtypeStruct((n, d), BF), jax.ShapeDtypeStruct((8, d), F32)],
        compiler_params=params(),
        cost_estimate=cost(2 * n * d * w * geo.T, 2 * geo.T * w * (d + n) + 8 * n * d),
        name="down_proj",
    )(scal, hidden, resid, cot, mod, bias, *wt.arrays)


def pre_back(scal, g, gp, wt, geo):
    n, d = g.shape
    w = wt.width
    nw = len(wt.arrays)
    step = chunked(w, 384)

    def kernel(s, g_ref, gp_ref, *refs):
        w_refs, (out_ref, sum_ref, wbuf) = refs[:nw], refs[nw:]
        j = pl.program_id(0)
        wt.assemble(j, s, w_refs, wbuf)
        for at in range(0, w, step):
            cols = slice(at, at + step)
            y = dotg(g_ref[...], wbuf[:, cols], 1, 0) * gp_ref[0, :, cols].astype(F32)
            out_ref[0, :, cols] = y.astype(BF)
            sum_ref[0, :, cols] = jnp.sum(y, axis=0, keepdims=True)

    out = pl.BlockSpec((1, n, w), lambda j, s: (j, 0, 0))
    return pl.pallas_call(
        kernel,
        grid_spec=pltpu.PrefetchScalarGridSpec(
            num_scalar_prefetch=1,
            grid=(geo.T,),
            in_specs=[whole((n, d)), out, *wt.specs()],
            out_specs=[out, pl.BlockSpec((1, 1, w), lambda j, s: (j, 0, 0))],
            scratch_shapes=[pltpu.VMEM((d, w), BF)],
        ),
        out_shape=[
            jax.ShapeDtypeStruct((geo.T, n, w), BF),
            jax.ShapeDtypeStruct((geo.T, 1, w), F32),
        ],
        compiler_params=params(),
        cost_estimate=cost(2 * n * d * w * geo.T, 2 * geo.T * w * (d + 2 * n)),
        name="pre_back",
    )(scal, g, gp, *wt.arrays)


def second_back(scal, pre, resid, attn, cot, mod, wt, geo):
    _, n, w = pre.shape
    d = geo.D
    nw = len(wt.arrays)

    def kernel(s, y_ref, r_ref, a_ref, c_ref, m_ref, *refs):
        w_refs, (rg_ref, ag_ref, sum_ref, wbuf, acc) = refs[:nw], refs[nw:]
        j = pl.program_id(0)
        wt.assemble(j, s, w_refs, wbuf)
        part = dotg(y_ref[0], wbuf[...], 1, 1)

        @pl.when(j == 0)
        def _():
            acc[...] = part
            sum_ref[...] = jnp.zeros_like(sum_ref)

        @pl.when(j > 0)
        def _():
            acc[...] += part

        @pl.when(j == geo.T - 1)
        def _():
            @pl.loop(0, n // ROWS, unroll=4)
            def _(i):
                at = pl.ds(pl.multiple_of(i * ROWS, ROWS), ROWS)
                g = acc[at, :]
                norm, inv = norm_of(r_ref[at, :])
                rg = c_ref[at, :].astype(F32) + norm_back(norm, inv, g * (1.0 + m_ref[4:5, :]))
                rg_ref[at, :] = rg
                ag = rg * m_ref[2:3, :]
                ag_ref[at, :] = ag.astype(BF)
                sum_ref[0] += fold_rows(rg * a_ref[at, :])
                sum_ref[1] += fold_rows(g)
                sum_ref[2] += fold_rows(g * norm)
                sum_ref[3] += fold_rows(ag)

    return pl.pallas_call(
        kernel,
        grid_spec=pltpu.PrefetchScalarGridSpec(
            num_scalar_prefetch=1,
            grid=(geo.T,),
            in_specs=[
                pl.BlockSpec((1, n, w), lambda j, s: (j, 0, 0)),
                whole((n, d)),
                whole((n, d)),
                whole((n, d)),
                whole(mod.shape),
                *wt.specs(),
            ],
            out_specs=[whole((n, d)), whole((n, d)), whole((4, 8, d))],
            scratch_shapes=[pltpu.VMEM((d, w), BF), pltpu.VMEM((n, d), F32)],
        ),
        out_shape=[
            jax.ShapeDtypeStruct((n, d), F32),
            jax.ShapeDtypeStruct((n, d), BF),
            jax.ShapeDtypeStruct((4, 8, d), F32),
        ],
        compiler_params=params(),
        cost_estimate=cost(2 * n * d * w * geo.T, 2 * geo.T * w * (d + n) + 18 * n * d),
        name="second_back",
    )(scal, pre, resid, attn, cot, mod, *wt.arrays)


def mixed_back(scal, g, wt, geo):
    n, d = g.shape
    w = wt.width // 4
    nw = len(wt.arrays)

    def kernel(s, g_ref, *refs):
        w_refs, (out_ref, wbuf) = refs[:nw], refs[nw:]
        wt.assemble(pl.program_id(0), s, w_refs, wbuf)
        out_ref[0, :, :w] = dotg(g_ref[...], wbuf[:, 3 * w :], 1, 0).astype(BF)

    return pl.pallas_call(
        kernel,
        grid_spec=pltpu.PrefetchScalarGridSpec(
            num_scalar_prefetch=1,
            grid=(geo.T,),
            in_specs=[whole((n, d)), *wt.specs()],
            out_specs=pl.BlockSpec((1, n, padded(w)), lambda j, s: (j, 0, 0)),
            scratch_shapes=[pltpu.VMEM((d, wt.width), BF)],
        ),
        out_shape=jax.ShapeDtypeStruct((geo.T, n, padded(w)), BF),
        compiler_params=params(),
        cost_estimate=cost(2 * n * d * d, 8 * d * d + 4 * n * d),
        name="mixed_back",
    )(scal, g, *wt.arrays)


def first_back(scal, dq, dkv, got, x, rg, mod, wt, geo):
    _, n, wp = dq[0].shape
    w = wt.width // 4
    d = geo.D
    nw = len(wt.arrays)
    th = geo.Th

    def kernel(s, qa, qb, kva, kvb, ga, gb, x_ref, r_ref, m_ref, *refs):
        w_refs, (out_ref, sum_ref, wbuf, lhs, acc) = refs[:nw], refs[nw:]
        j = pl.program_id(0)
        wt.assemble(j, s, w_refs, wbuf)
        for half, (q, kv, g) in enumerate(((qa, kva, ga), (qb, kvb, gb))):

            @pl.when((j < th) if half == 0 else (j >= th))
            def _():
                lhs[:, :w] = q[0, :, :w]
                for at in range(2):
                    both = kv[0, at, :, :w].astype(F32) + g[0, at, :, :w].astype(F32)
                    lhs[:, (at + 1) * w : (at + 2) * w] = both.astype(BF)

        part = dotg(lhs[...], wbuf[:, : 3 * w], 1, 1)

        @pl.when(j == 0)
        def _():
            acc[...] = part
            sum_ref[...] = jnp.zeros_like(sum_ref)

        @pl.when(j > 0)
        def _():
            acc[...] += part

        @pl.when(j == geo.T - 1)
        def _():
            @pl.loop(0, n // ROWS, unroll=4)
            def _(i):
                at = pl.ds(pl.multiple_of(i * ROWS, ROWS), ROWS)
                g = acc[at, :]
                norm, inv = norm_of(x_ref[at, :].astype(F32))
                back = norm_back(norm, inv, g * (1.0 + m_ref[1:2, :]))
                out_ref[at, :] = (r_ref[at, :] + back).astype(BF)
                sum_ref[0] += fold_rows(g)
                sum_ref[1] += fold_rows(g * norm)

    return pl.pallas_call(
        kernel,
        grid_spec=pltpu.PrefetchScalarGridSpec(
            num_scalar_prefetch=1,
            grid=(geo.T,),
            in_specs=[
                *two_halves((1, n, wp), th, (0, 0)),
                *two_halves((1, 2, n, wp), th, (0, 0, 0)),
                *two_halves((1, 2, n, wp), th, (0, 0, 0)),
                whole((n, d)),
                whole((n, d)),
                whole(mod.shape),
                *wt.specs(),
            ],
            out_specs=[whole((n, d)), whole((2, 8, d))],
            scratch_shapes=[
                pltpu.VMEM((d, wt.width), BF),
                pltpu.VMEM((n, 3 * w), BF),
                pltpu.VMEM((n, d), F32),
            ],
        ),
        out_shape=[jax.ShapeDtypeStruct((n, d), BF), jax.ShapeDtypeStruct((2, 8, d), F32)],
        compiler_params=params(),
        cost_estimate=cost(6 * n * d * d, 8 * d * d + 16 * n * d),
        name="first_back",
    )(scal, *dq, *dkv, *got, x, rg, mod, *wt.arrays)


def weight_grad(scal, terms, w, mine, geo, name, partial=None):
    n = terms[0][0].shape[0]
    pr = geo.P * geo.R
    th = geo.Th
    half_n = geo.P // 2
    want = scal[1] if mine else 1 - scal[1]
    lefts = [term[0] for term in terms]
    if not geo.direct:

        def pick(a):
            cols = a.reshape(n, geo.P, 2, geo.R)
            cols = jnp.where(want == 0, cols[:, :, 0], cols[:, :, 1])
            return cols.reshape(n, pr).T

        lefts = [pick(a) for a in lefts]
    ops, op_specs, counts = [], [], []
    for _, operands, _, _ in terms:
        counts.append(len(operands))
        for pair in operands:
            if isinstance(pair, tuple):
                tail = (0,) * (pair[0].ndim - 1)
                op_specs += two_halves((1,) + pair[0].shape[1:], th, tail)
                ops += pair
            else:
                op_specs.append(pl.BlockSpec((1,) + pair.shape[1:], lambda j, s: (j, 0, 0)))
                ops.append(pair)
    na, nb = len(lefts), len(ops)

    def kernel(s, *refs):
        a_refs, b_refs = refs[:na], refs[na : na + nb]
        rest = refs[na + nb :]
        got_ref = None
        if mine:
            got_ref, rest = rest[0], rest[1:]
        n_out = 4 if (mine and geo.direct) else 1
        outs, ats = rest[:n_out], rest[n_out:]
        j = pl.program_id(0)
        if geo.direct:

            @pl.when(j == 0)
            def _():
                pick_odd = (s[1] == 1) if mine else (s[1] == 0)
                for ref, at in zip(a_refs, ats):
                    flip = ref[...].T
                    for p in range(geo.P):
                        even = flip[2 * p * geo.R : (2 * p + 1) * geo.R]
                        odd = flip[(2 * p + 1) * geo.R : (2 * p + 2) * geo.R]
                        at[p * geo.R : (p + 1) * geo.R, :] = jnp.where(pick_odd, odd, even)
        else:
            ats = a_refs

        def store(half):
            at_op, parts = 0, []
            for at, (_, operands, build, _) in zip(ats, terms):
                blocks = []
                for pair in operands:
                    if isinstance(pair, tuple):
                        blocks.append(b_refs[at_op + half])
                        at_op += 2
                    else:
                        blocks.append(b_refs[at_op])
                        at_op += 1
                parts.append(dotg(at[...], build(*blocks), 1, 0))
            full = parts[0] if len(parts) == 1 else jnp.concatenate(parts, axis=1)
            if not geo.direct:
                if mine:
                    full = full + got_ref[0, 0].astype(F32)
                outs[0][0, 0] = full.astype(BF)
                return
            for p in range(geo.P):
                part = full[p * geo.R : (p + 1) * geo.R]
                rel = s[0] ^ p
                if not mine:
                    outs[0][0, rel] = part.astype(BF)
                    continue
                part = (part + got_ref[0, rel].astype(F32)).astype(BF)
                for i, here in enumerate(geo.order[half]):

                    @pl.when(rel == here)
                    def _():
                        outs[2 * half + i // half_n][i % half_n, 0] = part

        for half in range(2):

            @pl.when((j < th) if half == 0 else (j >= th))
            def _():
                store(half)

    in_specs = [whole(a.shape) for a in lefts] + op_specs
    rel_block = (1, geo.P, geo.R, w) if geo.direct else (1, 1, pr, w)
    rel_spec = pl.BlockSpec(rel_block, lambda j, s: (j, 0, 0, 0))
    rel_shape = jax.ShapeDtypeStruct((geo.T,) + rel_block[1:], BF)
    args = [*lefts, *ops]
    out_specs, shapes = [rel_spec], [rel_shape]
    if mine:
        in_specs.append(rel_spec)
        args.append(partial)
        if geo.direct:
            block = (half_n, 1, geo.R, w)
            first = pl.BlockSpec(block, lambda j, s: (0, jnp.minimum(j, th - 1), 0, 0))
            second = pl.BlockSpec(block, lambda j, s: (0, jnp.maximum(j - th, 0), 0, 0))
            out_specs = [first, first, second, second]
            shapes = [jax.ShapeDtypeStruct((half_n, th, geo.R, w), BF)] * 4
    got = pl.pallas_call(
        kernel,
        grid_spec=pltpu.PrefetchScalarGridSpec(
            num_scalar_prefetch=1,
            grid=(geo.T,),
            in_specs=in_specs,
            out_specs=out_specs,
            scratch_shapes=[pltpu.VMEM((pr, n), BF)] * (na if geo.direct else 0),
        ),
        out_shape=shapes,
        compiler_params=params(),
        cost_estimate=cost(2 * pr * n * w * geo.T, 2 * geo.T * w * (2 * pr + n)),
        name=name,
    )(scal, *args)
    if not mine:
        return got[0]
    if geo.direct:
        return got
    blocks = got[0].reshape(geo.T, geo.P, geo.R, w)
    out = []
    for half in range(2):
        part = blocks[half * th : (half + 1) * th]
        part = reorder(part, [scal[0] ^ rel for rel in geo.order[half]], 1)
        part = part.transpose(1, 0, 2, 3)
        out += [part[:half_n], part[half_n:]]
    return out


def body(
    latents,
    conditioning,
    mod_weight,
    mod_bias,
    in_weight,
    query_value_bias,
    out_weight,
    branch_bias,
    up_weight,
    up_bias,
    down_weight,
    cotangent,
):
    images, row_count, width = latents.shape
    geo = Geo(lax.axis_size("fsdp"), lax.axis_size("tensor"), width)
    F, T = geo.F, geo.T
    assert 2 * images == T
    highest = lax.Precision.HIGHEST
    fi = lax.axis_index("fsdp")
    ti = lax.axis_index("tensor")
    pair, core = fi // 2, fi % 2
    scal = jnp.stack([pair, core, ti]).astype(jnp.int32)
    cols = in_weight.shape[2]
    units = up_weight.shape[1]

    def places(k):
        return [
            ((2 * p + c) * T + t, (2 * p + t // images) * T + c * images + (t % images + k) % images)
            for p in range(geo.P)
            for c in range(2)
            for t in range(T)
        ]

    def to_chip(arr):
        got = []
        for k in range(images):
            item = lax.dynamic_index_in_dim(arr, (ti + k) % images, 0, keepdims=False)
            got.append(lax.ppermute(item, BOTH, places(k)))
        return got

    def from_chip(arr):
        got = []
        for k in range(images):
            back = [(dst, src) for src, dst in places(k)]
            got.append(lax.ppermute(arr[k * row_count : (k + 1) * row_count], BOTH, back))
        return got

    def home(parts):
        return reorder(jnp.stack(parts), [(i - ti) % images for i in range(images)])

    def share(arr):
        sent = jnp.broadcast_to(arr[None], (F * T,) + arr.shape)
        return lax.all_to_all(sent, BOTH, 0, 0, tiled=True)

    now, opened = (), []

    def tie(value):
        return after(value, *now)

    def start(*chains):
        for way in chains:
            opened.extend(way.advance(*now))

    def begin(shard, make):
        way = Chain(make(tie(shard), geo))
        opened.extend(way.flight)
        return way

    def across(value):
        got = flip_core(tie(value), geo)
        opened.append(got)
        return got

    def close(*made):
        nonlocal now
        now = (*opened, *made)
        opened.clear()

    heads = cols // HEAD_DIM
    attn_shard = jnp.concatenate([in_weight[0], in_weight[1], in_weight[2], out_weight.T], axis=1)
    attn_way = begin(attn_shard, gather_steps)
    info = jnp.concatenate([conditioning.reshape(-1), query_value_bias.reshape(-1), up_bias])
    info = share(info)
    close(info)
    start(attn_way)
    x_parts = to_chip(tie(latents))
    opened.extend(x_parts)
    info = info.reshape(F, T, -1)
    cond_all = info[:, 0, : images * width].reshape(F * images, width)
    qv_bias = info[0, :, images * width : images * width + 2 * cols].reshape(T, 2, 1, cols)
    unit_bias = info[0, :, images * width + 2 * cols :].reshape(T, 1, units).astype(F32)
    triple_bias = jnp.concatenate(
        [qv_bias[:, 0], jnp.zeros_like(qv_bias[:, 0]), qv_bias[:, 1]], axis=2
    ).astype(F32)
    silu_low = jax.nn.silu(cond_all.astype(F32)).astype(BF)
    silu_own = lax.dynamic_slice_in_dim(silu_low, fi * geo.R, geo.R, 1)
    mod_part = jnp.einsum("bd,dcj->bcj", silu_own, mod_weight, preferred_element_type=F32)
    mod_part += jnp.where(fi == 0, mod_bias.astype(F32), 0.0)
    mod_part = mod_part.reshape(geo.P, 1, T, 6, cols)
    mod_part = jnp.broadcast_to(mod_part, (geo.P, 2, T, 6, cols)).reshape(F * T, 6, cols)
    mod_part = lax.all_to_all(mod_part, BOTH, 0, 0, tiled=True)
    mod = mod_part.reshape(F, T, 6, cols).sum(axis=0).transpose(1, 0, 2).reshape(6, width)
    bias_rows = branch_bias.astype(F32)
    close(mod)
    x = jnp.concatenate(x_parts)
    start(attn_way)
    up_way = begin(up_weight, gather_steps)
    close()
    start(attn_way, up_way)
    h1 = norm_mod(tie(x), mod)
    close(h1)
    start(attn_way)
    w_attn = Gathered(attn_way.finish(*now), geo, scal)

    start(up_way)
    down_way = begin(down_weight.T, gather_steps)
    q, kv, kvo = [None] * 2, [None] * 2, [None] * 2
    mixed, lse = [None] * 2, [None] * 2
    for half in range(2):
        q[half], kv[half] = in_proj(tie(scal), h1, w_attn, triple_bias, cols, half, geo)
    close(q[0], q[1])
    kvo = [across(kv[0]), across(kv[1])]
    start(up_way)
    close()
    start(down_way, up_way)
    cot_parts = to_chip(tie(cotangent))
    opened.extend(cot_parts)
    w_up = Gathered(up_way.finish(*now), geo, scal)
    for half in range(2):
        mixed[half], lse[half] = attn_fwd(tie(q[half]), kv[half], kvo[half], heads)
    close(lse[0], lse[1])
    start(down_way)
    cot = jnp.concatenate(cot_parts)
    attn, resid, h2 = out_proj(tie(scal), mixed, x, mod, bias_rows[0:1], w_attn, geo)
    hidden, gp = up_proj(tie(scal), h2, unit_bias, w_up, geo)
    ffn_grad = (cot.astype(F32) * mod[5]).astype(BF)
    ffn_sum = jnp.sum(ffn_grad.astype(F32), axis=0)
    close(hidden)
    start(down_way)
    down_terms = [(ffn_grad, [hidden], lambda ref: ref[0], units)]
    down_half = weight_grad(tie(scal), down_terms, units, False, geo, "w_down_send")
    close(down_half)
    start(down_way)
    w_down = Gathered(down_way.finish(*now), geo, scal)
    down_got = across(down_half)
    block_rows, ffn_sums = down_proj(
        tie(scal), hidden, resid, cot, mod, bias_rows[1:2], w_down, geo
    )
    close(ffn_sums)

    down_parts = weight_grad(tie(scal), down_terms, units, True, geo, "w_down", down_got)
    close(*down_parts)
    down_back = begin(down_parts, scatter_steps)
    block_back = from_chip(tie(block_rows))
    opened.extend(block_back)
    pre, unit_sum = pre_back(tie(scal), ffn_grad, gp, w_down, geo)
    up_terms = [(h2, [pre], lambda ref: ref[0], units)]
    up_half = weight_grad(tie(scal), up_terms, units, False, geo, "w_up_send")
    close(up_half)
    start(down_back)
    up_got = across(up_half)
    rg, ag, mid_sums = second_back(tie(scal), pre, resid, attn, cot, mod, w_up, geo)
    close(ag)
    start(down_back)
    up_parts = weight_grad(tie(scal), up_terms, units, True, geo, "w_up", up_got)
    mg = mixed_back(tie(scal), ag, w_attn, geo)
    close(mg, *up_parts)
    start(down_back)
    up_back = begin(up_parts, scatter_steps)
    dq, dkv, dkv_got, tri_sums = [None] * 2, [None] * 2, [None] * 2, [None] * 2
    dkv_send = [None] * 2
    for half in range(2):
        dq[half], dkv[half], dkv_send[half], tri_sums[half] = attn_bwd(
            tie(q[half]), kv[half], kvo[half], mixed[half], mg, lse[half], half * geo.Th
        )
    dkv_got[0] = across(dkv_send[0])
    close(*tri_sums)
    dkv_got[1] = across(dkv_send[1])
    tri_sums = jnp.concatenate(tri_sums)
    close()
    start(up_back)

    def triple(q_ref, kv_ref, got_ref):
        parts = [q_ref[0, :, :cols]]
        for at in range(2):
            both = kv_ref[0, at, :, :cols].astype(F32) + got_ref[0, at, :, :cols].astype(F32)
            parts.append(both.astype(BF))
        return jnp.concatenate(parts, axis=1)

    attn_terms = [
        (h1, [tuple(dq), tuple(dkv), tuple(dkv_got)], triple, 3 * cols),
        (ag, [tuple(mixed)], lambda ref: ref[0, :, :cols], cols),
    ]
    attn_half = weight_grad(tie(scal), attn_terms, 4 * cols, False, geo, "w_attn_send")
    close(attn_half)
    start(up_back)
    attn_got = across(attn_half)
    latent_rows, first_sums = first_back(tie(scal), dq, dkv, dkv_got, x, rg, mod, w_attn, geo)
    close(first_sums)
    attn_parts = weight_grad(tie(scal), attn_terms, 4 * cols, True, geo, "w_attn", attn_got)
    close(*attn_parts)
    start(up_back)
    attn_back = begin(attn_parts, scatter_steps)
    latent_back = from_chip(tie(latent_rows))
    opened.extend(latent_back)
    close()
    start(attn_back)
    close()
    start(attn_back)
    close()
    start(attn_back)
    block_out, latent_grad = home(block_back), home(latent_back)
    down_grad, up_grad = down_back.finish(*now), up_back.finish(*now)
    attn_grad = attn_back.finish(*now)
    in_grad = attn_grad[:, : 3 * cols].reshape(geo.R, 3, cols).transpose(1, 0, 2)

    mine = [i ^ ti for i in range(T)]
    branch_sums = jnp.stack([mid_sums[3].sum(axis=0), ffn_sum]).reshape(1, 2 * width)
    bias_pack = jnp.concatenate(
        [
            jnp.broadcast_to(branch_sums, (T, 2 * width)),
            reorder(unit_sum, mine).reshape(T, units),
            reorder(tri_sums, mine).reshape(T, 2 * cols),
        ],
        axis=1,
    )
    bias_pack = jnp.broadcast_to(bias_pack[None], (F,) + bias_pack.shape).reshape(F * T, -1)
    bias_total = lax.all_to_all(bias_pack, BOTH, 0, 0, tiled=True).sum(axis=0)
    branch_grad = bias_total[: 2 * width].reshape(2, width)
    unit_grad = bias_total[2 * width : 2 * width + units]
    pair_grad = bias_total[2 * width + units :].reshape(2, cols)

    rows = jnp.concatenate(
        [first_sums.sum(axis=1), mid_sums[:3].sum(axis=1), ffn_sums.sum(axis=0, keepdims=True)]
    )
    rows = rows.reshape(6, T, cols).transpose(1, 0, 2)
    rows = jnp.broadcast_to(rows[None], (F, T, 6, cols)).reshape(F * T, 6, cols)
    rows = lax.all_to_all(rows, BOTH, 0, 0, tiled=True)
    mine_rows = rows.reshape(geo.P, 2, T, 6, cols).sum(axis=1).reshape(F * images, 6, cols)
    mod_weight_grad = jnp.einsum(
        "bd,bcj->dcj", silu_own.astype(F32), mine_rows, precision=highest
    )
    mod_bias_grad = mine_rows.sum(axis=0)
    cond_part = jnp.einsum("bcj,dcj->bd", mine_rows, mod_weight.astype(F32), precision=highest)
    cond_part = cond_part.reshape(F, 1, images, geo.R)
    cond_part = jnp.broadcast_to(cond_part, (F, T, images, geo.R)).reshape(F * T, images, geo.R)
    cond_part = lax.all_to_all(cond_part, BOTH, 0, 0, tiled=True)
    cond_mine = cond_part.reshape(F, T, images, geo.R).sum(axis=1)
    silu_grad = cond_mine.transpose(1, 0, 2).reshape(images, width)
    cond_f = conditioning.astype(F32)
    sig = jax.nn.sigmoid(cond_f)
    cond_grad = silu_grad * (sig * (1.0 + cond_f * (1.0 - sig)))

    return (
        block_out,
        latent_grad,
        cond_grad,
        mod_weight_grad,
        mod_bias_grad,
        in_grad,
        pair_grad,
        attn_grad[:, 3 * cols :].T,
        branch_grad,
        up_grad,
        unit_grad,
        down_grad.T,
    )


def solution(mesh):
    in_specs = (
        P("fsdp", "tensor", None),
        P("fsdp", None),
        P("fsdp", None, "tensor"),
        P(None, "tensor"),
        P(None, "fsdp", "tensor"),
        P(None, "tensor"),
        P("tensor", "fsdp"),
        P(),
        P("fsdp", "tensor"),
        P("tensor"),
        P("tensor", "fsdp"),
        P("fsdp", "tensor", None),
    )
    out_specs = (
        P("fsdp", "tensor", None),
        P("fsdp", "tensor", None),
        P("fsdp", None),
        P("fsdp", None, "tensor"),
        P(None, "tensor"),
        P(None, "fsdp", "tensor"),
        P(None, "tensor"),
        P("tensor", "fsdp"),
        P(),
        P("fsdp", "tensor"),
        P("tensor"),
        P("tensor", "fsdp"),
    )
    return jax.shard_map(body, mesh=mesh, in_specs=in_specs, out_specs=out_specs, check_vma=False)
```

```python
import functools

import jax
import jax.numpy as jnp
from jax import lax
from jax.experimental import pallas as pl
from jax.experimental.pallas import tpu as pltpu
from jax.sharding import PartitionSpec as P

HEAD_DIM = 72
EPS = 1e-06
TANH_C = 0.7978845608028654
CUBIC = 0.044715
LOG2E = 1.4426950408889634
VMEM_BYTES = 56 << 20
ROWS = 16
BF = jnp.bfloat16
F32 = jnp.float32
BOTH = ("fsdp", "tensor")


def dotg(a, b, ca, cb):
    return lax.dot_general(a, b, (((ca,), (cb,)), ((), ())), preferred_element_type=F32)


class Geo:
    def __init__(self, fsdp, tensor, dim):
        self.F, self.T, self.P = fsdp, tensor, fsdp // 2
        self.Th = tensor // 2
        self.D = dim
        self.R = dim // fsdp
        self.bits = [1 << b for b in range((self.P - 1).bit_length())]
        self.order = (self.orders(self.bits[::-1]), self.orders(self.bits))
        self.direct = self.R % 16 == 0

    def windows(self, w):
        self.w = w
        self.n3 = min(padded(3 * w), 4 * w)
        self.kbase = w // 128 * 128
        self.koff = w - self.kbase
        self.kvw = self.n3 - self.kbase
        self.base = 3 * w // 128 * 128
        self.off = 3 * w - self.base
        self.win = 4 * w - self.base

    @staticmethod
    def orders(msb_first):
        vals = [0]
        for bit in reversed(msb_first):
            vals = vals + [v | bit for v in vals]
        return vals


def reorder(x, index, axis=0):
    return jnp.stack([lax.dynamic_index_in_dim(x, i, axis, keepdims=False) for i in index], axis)


def flip_pair(x, bit, geo):
    return lax.ppermute(x, "fsdp", [(i, i ^ (2 * bit)) for i in range(geo.F)])


def flip_core(x, geo):
    return lax.ppermute(x, "fsdp", [(i, i ^ 1) for i in range(geo.F)])


def flip_tensor(x, k, geo):
    return lax.ppermute(x, "tensor", [(i, i ^ k) for i in range(geo.T)])


def after(value, *done):
    return lax.optimization_barrier((value, done))[0] if done else value


class Chain:
    def __init__(self, steps):
        self.steps = steps
        self.flight = next(steps)
        self.result = None

    def advance(self, *done):
        if self.result is not None:
            return []
        try:
            self.flight = self.steps.send(after(self.flight, *done))
        except StopIteration as end:
            self.flight, self.result = [], end.value
        return self.flight

    def finish(self, *done):
        while self.result is None:
            self.advance(*done)
        return self.result


def gather_steps(shard, geo, parted=True, joined=False):
    if parted:
        far = yield [flip_tensor(shard, k, geo) for k in range(geo.Th + 1, geo.T)]
        near = yield [flip_tensor(shard, k, geo) for k in range(1, geo.Th)]
        mid = yield [flip_tensor(shard, geo.Th, geo)]
        parts = [shard] + near + mid + far
    else:
        got = yield [flip_tensor(shard, k, geo) for k in range(1, geo.T)]
        parts = [shard] + got
    bufs = [jnp.stack(parts[h * geo.Th : (h + 1) * geo.Th])[None] for h in range(2)]
    for at in range(len(geo.bits)):
        bits = (geo.bits[at], geo.bits[-1 - at])
        got = yield [flip_pair(bufs[h], bits[h], geo) for h in range(2)]
        if joined or at < len(geo.bits) - 1:
            bufs = [jnp.concatenate(pair) for pair in zip(bufs, got)]
    owns = [[buf] for buf in bufs] if joined else [list(pair) for pair in zip(bufs, got)]
    count = len(owns[0])
    others = yield [flip_core(a, geo) for own in owns for a in own]
    return [owns[h] + others[h * count : (h + 1) * count] for h in range(2)]


class Gathered:
    def __init__(self, halves, geo, scal):
        self.geo = geo
        if not geo.direct:
            fixed = []
            for half, arrays in enumerate(halves):
                at = [geo.order[half].index(rel) for rel in range(geo.P)]
                lookup = jnp.array(at, jnp.int32)
                blocks = jnp.concatenate(arrays)
                blocks = reorder(
                    blocks,
                    [
                        lookup[(f // 2) ^ scal[0]] + geo.P * ((f % 2) ^ scal[1])
                        for f in range(geo.F)
                    ],
                )
                _, th, r, w = blocks.shape
                fixed.append([blocks.transpose(1, 0, 2, 3).reshape(1, th, geo.D, w)])
            halves = fixed
        self.halves = halves
        self.arrays = halves[0] + halves[1]
        self.n = len(halves[0])
        self.width = self.arrays[0].shape[-1]

    def operands(self, half=None):
        return self.arrays if half is None else self.halves[half]

    def specs(self, half=None):
        return [pl.BlockSpec(memory_space=pl.ANY)] * len(self.operands(half))

    def scratch(self, lo=0, hi=None):
        hi = self.width if hi is None else hi
        if lo % 128 or hi % 128:
            lo, hi = 0, self.width
        self.lo, self.hi = lo, hi
        count = self.n * self.arrays[0].shape[0]
        return [
            pltpu.VMEM((2, self.geo.D, hi - lo), BF),
            pltpu.SemaphoreType.DMA((2, count)),
        ]

    def copies(self, group, slot, half, s_ref, refs, buf, sem):
        geo, out = self.geo, []
        for at, ref in enumerate(refs):
            n, _, rows, _ = ref.shape
            for i in range(n):
                row = 0
                if geo.direct:
                    place = at * n + i
                    rel = geo.order[half][place % geo.P]
                    row = 2 * (s_ref[0] ^ rel) + (s_ref[1] ^ (place // geo.P))
                    row = pl.multiple_of(row * rows, rows)
                out.append(
                    pltpu.make_async_copy(
                        ref.at[i, group, :, pl.ds(self.lo, self.hi - self.lo)],
                        buf.at[slot, pl.ds(row, rows), :],
                        sem.at[slot, at * n + i],
                    )
                )
        return out

    def stream(self, j, s_ref, refs, buf, sem, half=None):
        th = self.geo.Th

        def each(step, act):
            if half is not None:
                for copy in self.copies(step, step % 2, half, s_ref, refs, buf, sem):
                    act(copy)
                return
            for part in range(2):

                @pl.when((step < th) if part == 0 else (step >= th))
                def _():
                    mine = refs[part * self.n : (part + 1) * self.n]
                    for copy in self.copies(
                        step - part * th, step % 2, part, s_ref, mine, buf, sem
                    ):
                        act(copy)

        @pl.when(j == 0)
        def _():
            each(j, lambda copy: copy.start())

        @pl.when(j + 1 < (self.geo.T if half is None else th))
        def _():
            each(j + 1, lambda copy: copy.start())

        each(j, lambda copy: copy.wait())
        return buf.at[j % 2]


def scatter_steps(pieces, geo, parted=True):
    def add(a, b):
        return a.astype(F32) + b.astype(F32)

    keeps, sends = [pieces[0], pieces[2]], [pieces[1], pieces[3]]
    for at in range(len(geo.bits)):
        bits = (geo.bits[-1 - at], geo.bits[at])
        got = yield [flip_pair(sends[h], bits[h], geo) for h in range(2)]
        m = max(1, keeps[0].shape[0] // 2)
        if at < len(geo.bits) - 1:
            sends = [add(keeps[h][m:], got[h][m:]).astype(BF) for h in range(2)]
        keeps = [add(keeps[h][:m], got[h][:m]).astype(BF) for h in range(2)]
    units = [keep[0, k] for keep in keeps for k in range(geo.Th)]
    if parted:
        rest = [k for k in range(1, geo.T) if k != geo.Th]
        got = yield [flip_tensor(units[k], k, geo) for k in rest]
        got += yield [flip_tensor(units[geo.Th], geo.Th, geo)]
    else:
        got = yield [flip_tensor(units[k], k, geo) for k in range(1, geo.T)]
    total = units[0].astype(F32)
    for part in got:
        total = total + part.astype(F32)
    return total


def params():
    return pltpu.CompilerParams(vmem_limit_bytes=VMEM_BYTES)


def cost(flops, size):
    return pl.CostEstimate(flops=int(flops), bytes_accessed=int(size), transcendentals=0)


def whole(shape):
    zeros = (0,) * len(shape)
    return pl.BlockSpec(shape, lambda j, s: zeros)


def padded(w):
    return -(-w // 128) * 128


def chunked(total, want):
    return want if total % want == 0 else total


def norm_of(v):
    centre = v - jnp.mean(v, axis=-1, keepdims=True)
    inv = lax.rsqrt(jnp.mean(centre * centre, axis=-1, keepdims=True) + EPS)
    return centre * inv, inv


def norm_back(norm, inv, g):
    return (
        g
        - jnp.mean(g, axis=-1, keepdims=True)
        - norm * jnp.mean(g * norm, axis=-1, keepdims=True)
    ) * inv


def fold_rows(v):
    return v.reshape(v.shape[0] // 8, 8, v.shape[1]).sum(axis=0)


def two_halves(block, th, tail):
    return [
        pl.BlockSpec(block, lambda j, s: (jnp.minimum(j, th - 1),) + tail),
        pl.BlockSpec(block, lambda j, s: (jnp.maximum(j - th, 0),) + tail),
    ]


def norm_mod(x, mod):
    n, d = x.shape

    def kernel(x_ref, m_ref, h_ref):
        @pl.loop(0, n // ROWS, unroll=4)
        def _(i):
            at = pl.ds(pl.multiple_of(i * ROWS, ROWS), ROWS)
            norm, _ = norm_of(x_ref[at, :].astype(F32))
            h_ref[at, :] = (norm * (1.0 + m_ref[1:2, :]) + m_ref[0:1, :]).astype(BF)

    return pl.pallas_call(
        kernel,
        out_shape=jax.ShapeDtypeStruct((n, d), BF),
        compiler_params=params(),
        cost_estimate=cost(20 * n * d, 4 * n * d),
        name="norm_mod",
    )(x, mod)


def in_proj(scal, h, wt, bias, half, geo):
    n, d = h.shape
    n3, wp = geo.n3, padded(geo.w)
    nw = wt.n

    def kernel(s, h_ref, b_ref, *refs):
        w_refs, (q_ref, kv_ref, wbuf, sem) = refs[:nw], refs[nw:]
        now = wt.stream(pl.program_id(0), s, w_refs, wbuf, sem, half)
        y = dotg(h_ref[...], now[:, :n3], 1, 0) + b_ref[0]
        y = y.astype(BF)
        q_ref[0] = y[:, :wp]
        kv_ref[0] = y[:, geo.kbase :]

    first = half * geo.Th
    return pl.pallas_call(
        kernel,
        grid_spec=pltpu.PrefetchScalarGridSpec(
            num_scalar_prefetch=1,
            grid=(geo.Th,),
            in_specs=[
                whole((n, d)),
                pl.BlockSpec((1, 1, n3), lambda j, s: (s[2] ^ (j + first), 0, 0)),
                *wt.specs(half),
            ],
            out_specs=[
                pl.BlockSpec((1, n, wp), lambda j, s: (j, 0, 0)),
                pl.BlockSpec((1, n, geo.kvw), lambda j, s: (j, 0, 0)),
            ],
            scratch_shapes=wt.scratch(0, n3),
        ),
        out_shape=[
            jax.ShapeDtypeStruct((geo.Th, n, wp), BF),
            jax.ShapeDtypeStruct((geo.Th, n, geo.kvw), BF),
        ],
        compiler_params=params(),
        cost_estimate=cost(2 * n * d * n3 * geo.Th, 8 * d * geo.w * geo.Th + 8 * n * d),
        name="in_proj",
    )(scal, h, bias, *wt.operands(half))


def head_lanes(geo, h):
    at = h * HEAD_DIM
    return [
        slice(start + at, start + at + HEAD_DIM)
        for start in (0, geo.koff, geo.koff + geo.w, geo.off)
    ]


def attn_fwd(q, kv, kvo, geo):
    z, n, wp = q.shape
    heads = geo.w // HEAD_DIM
    c = HEAD_DIM**-0.5 * LOG2E

    def kernel(q_ref, kv_ref, kvo_ref, o_ref, lse_ref):
        outs = [jnp.zeros((geo.off, n), F32)] if geo.off else []
        for h in range(heads):
            lq, lk, lv, _ = head_lanes(geo, h)
            qh = q_ref[0, :, lq]
            sa = dotg(kv_ref[0, :, lk], qh, 1, 1) * c
            sb = dotg(kvo_ref[0, :, lk], qh, 1, 1) * c
            top = jnp.maximum(
                jnp.max(sa, axis=0, keepdims=True), jnp.max(sb, axis=0, keepdims=True)
            )
            pa, pb = jnp.exp2(sa - top), jnp.exp2(sb - top)
            total = jnp.sum(pa, axis=0, keepdims=True) + jnp.sum(pb, axis=0, keepdims=True)
            o = dotg(kv_ref[0, :, lv], pa.astype(BF), 0, 0)
            o = o + dotg(kvo_ref[0, :, lv], pb.astype(BF), 0, 0)
            outs.append(o / total)
            lse_ref[0, h : h + 1, :] = top + jnp.log2(total)
        o_ref[0] = jnp.concatenate(outs, axis=0).T.astype(BF)

    def spec(width):
        return pl.BlockSpec((1, n, width), lambda j: (j, 0, 0))

    return pl.pallas_call(
        kernel,
        grid=(z,),
        in_specs=[spec(wp), spec(geo.kvw), spec(geo.kvw)],
        out_specs=[spec(geo.win), pl.BlockSpec((1, heads, n), lambda j: (j, 0, 0))],
        out_shape=[
            jax.ShapeDtypeStruct((z, n, geo.win), BF),
            jax.ShapeDtypeStruct((z, heads, n), F32),
        ],
        compiler_params=params(),
        cost_estimate=cost(3e9 * z, 10 * z * n * wp),
        name="attn_fwd",
    )(q, kv, kvo)


def attn_bwd(q, kv, kvo, o, do, lse, first, geo):
    z, n, wp = q.shape
    heads = lse.shape[1]
    scale = HEAD_DIM**-0.5
    c = scale * LOG2E

    def kernel(q_ref, kv_ref, kvo_ref, o_ref, do_ref, lse_ref, tri_ref, send_ref, ts_ref, ss_ref):
        both = (do_ref[0].astype(F32) * o_ref[0].astype(F32)).T
        dqs, parts = [], [[[], []], [[], []]]
        for h in range(heads):
            lq, lk, lv, lm = head_lanes(geo, h)
            qh, doh = q_ref[0, :, lq], do_ref[0, :, lm]
            delta = jnp.sum(both[lm], axis=0, keepdims=True)
            lse_h = lse_ref[0, h : h + 1, :]
            dq = None
            for i, ref in enumerate((kv_ref, kvo_ref)):
                k, v = ref[0, :, lk], ref[0, :, lv]
                p = jnp.exp2(dotg(k, qh, 1, 1) * c - lse_h)
                ds = (p * (dotg(v, doh, 1, 1) - delta)).astype(BF)
                parts[i][1].append(dotg(doh, p.astype(BF), 0, 1))
                parts[i][0].append(dotg(qh, ds, 0, 1) * scale)
                got = dotg(k, ds, 0, 0)
                dq = got if dq is None else dq + got
            dqs.append(dq * scale)

        def rows(count):
            return [jnp.zeros((count, n), F32)] if count else []

        pad = rows(geo.n3 - 3 * geo.w)
        own = jnp.concatenate(dqs + parts[0][0] + parts[0][1] + pad, axis=0).T
        other = jnp.concatenate(rows(geo.koff) + parts[1][0] + parts[1][1] + pad, axis=0).T
        tri_ref[0] = own.astype(BF)
        send_ref[0] = other.astype(BF)
        ts_ref[0] = jnp.sum(own, axis=0, keepdims=True)
        ss_ref[0] = jnp.sum(other, axis=0, keepdims=True)

    def spec(width, at=0, count=n):
        return pl.BlockSpec((1, count, width), lambda j: (j + at, 0, 0))

    return pl.pallas_call(
        kernel,
        grid=(z,),
        in_specs=[
            spec(wp),
            spec(geo.kvw),
            spec(geo.kvw),
            spec(geo.win),
            spec(geo.win, first),
            spec(n, 0, heads),
        ],
        out_specs=[spec(geo.n3), spec(geo.kvw), spec(geo.n3, 0, 1), spec(geo.kvw, 0, 1)],
        out_shape=[
            jax.ShapeDtypeStruct((z, n, geo.n3), BF),
            jax.ShapeDtypeStruct((z, n, geo.kvw), BF),
            jax.ShapeDtypeStruct((z, 1, geo.n3), F32),
            jax.ShapeDtypeStruct((z, 1, geo.kvw), F32),
        ],
        compiler_params=params(),
        cost_estimate=cost(5e9 * z, 16 * z * n * wp),
        name="attn_bwd",
    )(q, kv, kvo, o, do, lse)


def triple_grad(tri_ref, got_ref, geo):
    late = tri_ref[0, :, geo.kbase :].astype(F32) + got_ref[0].astype(F32)
    if not geo.kbase:
        return late.astype(BF)
    return jnp.concatenate([tri_ref[0, :, : geo.kbase], late.astype(BF)], axis=1)


def out_proj(scal, mixed, x, mod, bias, wt, geo):
    _, n, win = mixed[0].shape
    d = geo.D
    nw = len(wt.arrays)
    th = geo.Th

    def kernel(s, ya_ref, yb_ref, x_ref, m_ref, b_ref, *refs):
        w_refs, (attn_ref, resid_ref, h_ref, wbuf, sem) = refs[:nw], refs[nw:]
        j = pl.program_id(0)
        now = wt.stream(j, s, w_refs, wbuf, sem)
        y = jnp.where(j < th, ya_ref[0], yb_ref[0])
        part = dotg(y, now[:, -win:], 1, 1)

        @pl.when(j == 0)
        def _():
            attn_ref[...] = part

        @pl.when(j > 0)
        def _():
            attn_ref[...] += part

        @pl.when(j == geo.T - 1)
        def _():
            @pl.loop(0, n // ROWS, unroll=4)
            def _(i):
                at = pl.ds(pl.multiple_of(i * ROWS, ROWS), ROWS)
                attn = attn_ref[at, :] + b_ref[...]
                attn_ref[at, :] = attn
                resid = x_ref[at, :].astype(F32) + m_ref[2:3, :] * attn
                resid_ref[at, :] = resid
                norm, _ = norm_of(resid)
                h_ref[at, :] = (norm * (1.0 + m_ref[4:5, :]) + m_ref[3:4, :]).astype(BF)

    return pl.pallas_call(
        kernel,
        grid_spec=pltpu.PrefetchScalarGridSpec(
            num_scalar_prefetch=1,
            grid=(geo.T,),
            in_specs=[
                *two_halves((1, n, win), th, (0, 0)),
                whole((n, d)),
                whole(mod.shape),
                whole((1, d)),
                *wt.specs(),
            ],
            out_specs=[whole((n, d))] * 3,
            scratch_shapes=wt.scratch(geo.base, 4 * geo.w),
        ),
        out_shape=[
            jax.ShapeDtypeStruct((n, d), F32),
            jax.ShapeDtypeStruct((n, d), F32),
            jax.ShapeDtypeStruct((n, d), BF),
        ],
        compiler_params=params(),
        cost_estimate=cost(2 * n * d * d, 8 * d * d + 14 * n * d),
        name="out_proj",
    )(scal, *mixed, x, mod, bias, *wt.arrays)


def up_proj(scal, h, bias, wt, geo):
    n, d = h.shape
    w = wt.width
    nw = len(wt.arrays)
    step = chunked(w, 384)

    def kernel(s, h_ref, b_ref, *refs):
        w_refs, (hid_ref, gp_ref, wbuf, sem) = refs[:nw], refs[nw:]
        j = pl.program_id(0)
        now = wt.stream(j, s, w_refs, wbuf, sem)
        for at in range(0, w, step):
            cols = slice(at, at + step)
            u = dotg(h_ref[...], now[:, cols], 1, 0) + b_ref[0, :, cols]
            sq = u * u
            t = jnp.tanh(TANH_C * (u + CUBIC * sq * u))
            half = 0.5 * (1.0 + t)
            hid_ref[0, :, cols] = (u * half).astype(BF)
            slope = TANH_C * (1.0 + 3.0 * CUBIC * sq)
            gp_ref[0, :, cols] = (half + 0.5 * u * (1.0 - t * t) * slope).astype(BF)

    out = pl.BlockSpec((1, n, w), lambda j, s: (j, 0, 0))
    return pl.pallas_call(
        kernel,
        grid_spec=pltpu.PrefetchScalarGridSpec(
            num_scalar_prefetch=1,
            grid=(geo.T,),
            in_specs=[
                whole((n, d)),
                pl.BlockSpec((1, 1, w), lambda j, s: (s[2] ^ j, 0, 0)),
                *wt.specs(),
            ],
            out_specs=[out, out],
            scratch_shapes=wt.scratch(),
        ),
        out_shape=[jax.ShapeDtypeStruct((geo.T, n, w), BF)] * 2,
        compiler_params=params(),
        cost_estimate=cost(2 * n * d * w * geo.T, 2 * geo.T * w * (d + 2 * n)),
        name="up_proj",
    )(scal, h, bias, *wt.arrays)


def down_proj(scal, hidden, resid, cot, mod, bias, wt, geo):
    _, n, w = hidden.shape
    d = geo.D
    nw = len(wt.arrays)

    def kernel(s, y_ref, r_ref, c_ref, m_ref, b_ref, *refs):
        w_refs, (out_ref, sum_ref, wbuf, sem, acc) = refs[:nw], refs[nw:]
        j = pl.program_id(0)
        now = wt.stream(j, s, w_refs, wbuf, sem)
        part = dotg(y_ref[0], now[...], 1, 1)

        @pl.when(j == 0)
        def _():
            acc[...] = part
            sum_ref[...] = jnp.zeros_like(sum_ref)

        @pl.when(j > 0)
        def _():
            acc[...] += part

        @pl.when(j == geo.T - 1)
        def _():
            @pl.loop(0, n // ROWS, unroll=4)
            def _(i):
                at = pl.ds(pl.multiple_of(i * ROWS, ROWS), ROWS)
                ffn = acc[at, :] + b_ref[...]
                out_ref[at, :] = (r_ref[at, :] + m_ref[5:6, :] * ffn).astype(BF)
                sum_ref[...] += fold_rows(c_ref[at, :].astype(F32) * ffn)

    return pl.pallas_call(
        kernel,
        grid_spec=pltpu.PrefetchScalarGridSpec(
            num_scalar_prefetch=1,
            grid=(geo.T,),
            in_specs=[
                pl.BlockSpec((1, n, w), lambda j, s: (j, 0, 0)),
                whole((n, d)),
                whole((n, d)),
                whole(mod.shape),
                whole((1, d)),
                *wt.specs(),
            ],
            out_specs=[whole((n, d)), whole((8, d))],
            scratch_shapes=[*wt.scratch(), pltpu.VMEM((n, d), F32)],
        ),
        out_shape=[jax.ShapeDtypeStruct((n, d), BF), jax.ShapeDtypeStruct((8, d), F32)],
        compiler_params=params(),
        cost_estimate=cost(2 * n * d * w * geo.T, 2 * geo.T * w * (d + n) + 8 * n * d),
        name="down_proj",
    )(scal, hidden, resid, cot, mod, bias, *wt.arrays)


def pre_back(scal, g, gp, wt, geo):
    n, d = g.shape
    w = wt.width
    nw = len(wt.arrays)
    step = chunked(w, 384)

    def kernel(s, g_ref, gp_ref, *refs):
        w_refs, (out_ref, sum_ref, wbuf, sem) = refs[:nw], refs[nw:]
        j = pl.program_id(0)
        now = wt.stream(j, s, w_refs, wbuf, sem)
        for at in range(0, w, step):
            cols = slice(at, at + step)
            y = dotg(g_ref[...], now[:, cols], 1, 0) * gp_ref[0, :, cols].astype(F32)
            out_ref[0, :, cols] = y.astype(BF)
            sum_ref[0, :, cols] = jnp.sum(y, axis=0, keepdims=True)

    out = pl.BlockSpec((1, n, w), lambda j, s: (j, 0, 0))
    return pl.pallas_call(
        kernel,
        grid_spec=pltpu.PrefetchScalarGridSpec(
            num_scalar_prefetch=1,
            grid=(geo.T,),
            in_specs=[whole((n, d)), out, *wt.specs()],
            out_specs=[out, pl.BlockSpec((1, 1, w), lambda j, s: (j, 0, 0))],
            scratch_shapes=wt.scratch(),
        ),
        out_shape=[
            jax.ShapeDtypeStruct((geo.T, n, w), BF),
            jax.ShapeDtypeStruct((geo.T, 1, w), F32),
        ],
        compiler_params=params(),
        cost_estimate=cost(2 * n * d * w * geo.T, 2 * geo.T * w * (d + 2 * n)),
        name="pre_back",
    )(scal, g, gp, *wt.arrays)


def second_back(scal, pre, resid, attn, cot, mod, wt, geo):
    _, n, w = pre.shape
    d = geo.D
    nw = len(wt.arrays)

    def kernel(s, y_ref, r_ref, a_ref, c_ref, m_ref, *refs):
        w_refs, (rg_ref, ag_ref, sum_ref, wbuf, sem, acc) = refs[:nw], refs[nw:]
        j = pl.program_id(0)
        now = wt.stream(j, s, w_refs, wbuf, sem)
        part = dotg(y_ref[0], now[...], 1, 1)

        @pl.when(j == 0)
        def _():
            acc[...] = part
            sum_ref[...] = jnp.zeros_like(sum_ref)

        @pl.when(j > 0)
        def _():
            acc[...] += part

        @pl.when(j == geo.T - 1)
        def _():
            @pl.loop(0, n // ROWS, unroll=4)
            def _(i):
                at = pl.ds(pl.multiple_of(i * ROWS, ROWS), ROWS)
                g = acc[at, :]
                norm, inv = norm_of(r_ref[at, :])
                rg = c_ref[at, :].astype(F32) + norm_back(norm, inv, g * (1.0 + m_ref[4:5, :]))
                rg_ref[at, :] = rg
                ag = rg * m_ref[2:3, :]
                ag_ref[at, :] = ag.astype(BF)
                sum_ref[0] += fold_rows(rg * a_ref[at, :])
                sum_ref[1] += fold_rows(g)
                sum_ref[2] += fold_rows(g * norm)
                sum_ref[3] += fold_rows(ag)

    return pl.pallas_call(
        kernel,
        grid_spec=pltpu.PrefetchScalarGridSpec(
            num_scalar_prefetch=1,
            grid=(geo.T,),
            in_specs=[
                pl.BlockSpec((1, n, w), lambda j, s: (j, 0, 0)),
                whole((n, d)),
                whole((n, d)),
                whole((n, d)),
                whole(mod.shape),
                *wt.specs(),
            ],
            out_specs=[whole((n, d)), whole((n, d)), whole((4, 8, d))],
            scratch_shapes=[*wt.scratch(), pltpu.VMEM((n, d), F32)],
        ),
        out_shape=[
            jax.ShapeDtypeStruct((n, d), F32),
            jax.ShapeDtypeStruct((n, d), BF),
            jax.ShapeDtypeStruct((4, 8, d), F32),
        ],
        compiler_params=params(),
        cost_estimate=cost(2 * n * d * w * geo.T, 2 * geo.T * w * (d + n) + 18 * n * d),
        name="second_back",
    )(scal, pre, resid, attn, cot, mod, *wt.arrays)


def mixed_back(scal, g, wt, geo):
    n, d = g.shape
    win = geo.win
    nw = len(wt.arrays)

    def kernel(s, g_ref, *refs):
        w_refs, (out_ref, wbuf, sem) = refs[:nw], refs[nw:]
        now = wt.stream(pl.program_id(0), s, w_refs, wbuf, sem)
        out_ref[0] = dotg(g_ref[...], now[:, -win:], 1, 0).astype(BF)

    return pl.pallas_call(
        kernel,
        grid_spec=pltpu.PrefetchScalarGridSpec(
            num_scalar_prefetch=1,
            grid=(geo.T,),
            in_specs=[whole((n, d)), *wt.specs()],
            out_specs=pl.BlockSpec((1, n, win), lambda j, s: (j, 0, 0)),
            scratch_shapes=wt.scratch(geo.base, 4 * geo.w),
        ),
        out_shape=jax.ShapeDtypeStruct((geo.T, n, win), BF),
        compiler_params=params(),
        cost_estimate=cost(2 * n * d * d, 8 * d * d + 4 * n * d),
        name="mixed_back",
    )(scal, g, *wt.arrays)


def first_back(scal, tri, got, x, rg, mod, wt, geo):
    _, n, n3 = tri[0].shape
    d = geo.D
    nw = len(wt.arrays)
    th = geo.Th

    def kernel(s, ta, tb, ga, gb, x_ref, r_ref, m_ref, *refs):
        w_refs, (out_ref, sum_ref, wbuf, sem, lhs, acc) = refs[:nw], refs[nw:]
        j = pl.program_id(0)
        now = wt.stream(j, s, w_refs, wbuf, sem)
        for half, (tri_ref, got_ref) in enumerate(((ta, ga), (tb, gb))):

            @pl.when((j < th) if half == 0 else (j >= th))
            def _():
                lhs[...] = triple_grad(tri_ref, got_ref, geo)

        part = dotg(lhs[...], now[:, :n3], 1, 1)

        @pl.when(j == 0)
        def _():
            acc[...] = part
            sum_ref[...] = jnp.zeros_like(sum_ref)

        @pl.when(j > 0)
        def _():
            acc[...] += part

        @pl.when(j == geo.T - 1)
        def _():
            @pl.loop(0, n // ROWS, unroll=4)
            def _(i):
                at = pl.ds(pl.multiple_of(i * ROWS, ROWS), ROWS)
                g = acc[at, :]
                norm, inv = norm_of(x_ref[at, :].astype(F32))
                back = norm_back(norm, inv, g * (1.0 + m_ref[1:2, :]))
                out_ref[at, :] = (r_ref[at, :] + back).astype(BF)
                sum_ref[0] += fold_rows(g)
                sum_ref[1] += fold_rows(g * norm)

    return pl.pallas_call(
        kernel,
        grid_spec=pltpu.PrefetchScalarGridSpec(
            num_scalar_prefetch=1,
            grid=(geo.T,),
            in_specs=[
                *two_halves((1, n, n3), th, (0, 0)),
                *two_halves((1, n, geo.kvw), th, (0, 0)),
                whole((n, d)),
                whole((n, d)),
                whole(mod.shape),
                *wt.specs(),
            ],
            out_specs=[whole((n, d)), whole((2, 8, d))],
            scratch_shapes=[
                *wt.scratch(0, n3),
                pltpu.VMEM((n, n3), BF),
                pltpu.VMEM((n, d), F32),
            ],
        ),
        out_shape=[jax.ShapeDtypeStruct((n, d), BF), jax.ShapeDtypeStruct((2, 8, d), F32)],
        compiler_params=params(),
        cost_estimate=cost(6 * n * d * d, 8 * d * d + 16 * n * d),
        name="first_back",
    )(scal, *tri, *got, x, rg, mod, *wt.arrays)


def weight_grad(scal, terms, join, w, mine, geo, name, partial=None):
    n = terms[0][0].shape[0]
    pr = geo.P * geo.R
    th = geo.Th
    half_n = geo.P // 2
    want = scal[1] if mine else 1 - scal[1]
    lefts = [term[0] for term in terms]
    if not geo.direct:

        def pick(a):
            cols = a.reshape(n, geo.P, 2, geo.R)
            cols = jnp.where(want == 0, cols[:, :, 0], cols[:, :, 1])
            return cols.reshape(n, pr).T

        lefts = [pick(a) for a in lefts]
    ops, op_specs, counts = [], [], []
    for _, operands, _ in terms:
        counts.append(len(operands))
        for pair in operands:
            if isinstance(pair, tuple):
                tail = (0,) * (pair[0].ndim - 1)
                op_specs += two_halves((1,) + pair[0].shape[1:], th, tail)
                ops += pair
            else:
                op_specs.append(pl.BlockSpec((1,) + pair.shape[1:], lambda j, s: (j, 0, 0)))
                ops.append(pair)
    na, nb = len(lefts), len(ops)

    def kernel(s, *refs):
        a_refs, b_refs = refs[:na], refs[na : na + nb]
        rest = refs[na + nb :]
        got_ref = None
        if mine:
            got_ref, rest = rest[0], rest[1:]
        n_out = 4 if (mine and geo.direct) else 1
        outs, ats = rest[:n_out], rest[n_out:]
        j = pl.program_id(0)
        if geo.direct:

            @pl.when(j == 0)
            def _():
                pick_odd = (s[1] == 1) if mine else (s[1] == 0)
                for ref, at in zip(a_refs, ats):
                    flip = ref[...].T
                    for p in range(geo.P):
                        even = flip[2 * p * geo.R : (2 * p + 1) * geo.R]
                        odd = flip[(2 * p + 1) * geo.R : (2 * p + 2) * geo.R]
                        at[p * geo.R : (p + 1) * geo.R, :] = jnp.where(pick_odd, odd, even)
        else:
            ats = a_refs

        def store(half):
            at_op, parts = 0, []
            for at, (_, operands, build) in zip(ats, terms):
                blocks = []
                for pair in operands:
                    if isinstance(pair, tuple):
                        blocks.append(b_refs[at_op + half])
                        at_op += 2
                    else:
                        blocks.append(b_refs[at_op])
                        at_op += 1
                parts.append(dotg(at[...], build(*blocks), 1, 0))
            full = join(*parts)
            if not geo.direct:
                if mine:
                    full = full + got_ref[0, 0].astype(F32)
                outs[0][0, 0] = full.astype(BF)
                return
            for p in range(geo.P):
                part = full[p * geo.R : (p + 1) * geo.R]
                rel = s[0] ^ p
                if not mine:
                    outs[0][0, rel] = part.astype(BF)
                    continue
                part = (part + got_ref[0, rel].astype(F32)).astype(BF)
                for i, here in enumerate(geo.order[half]):

                    @pl.when(rel == here)
                    def _():
                        outs[2 * half + i // half_n][i % half_n, 0] = part

        for half in range(2):

            @pl.when((j < th) if half == 0 else (j >= th))
            def _():
                store(half)

    in_specs = [whole(a.shape) for a in lefts] + op_specs
    rel_block = (1, geo.P, geo.R, w) if geo.direct else (1, 1, pr, w)
    rel_spec = pl.BlockSpec(rel_block, lambda j, s: (j, 0, 0, 0))
    rel_shape = jax.ShapeDtypeStruct((geo.T,) + rel_block[1:], BF)
    args = [*lefts, *ops]
    out_specs, shapes = [rel_spec], [rel_shape]
    if mine:
        in_specs.append(rel_spec)
        args.append(partial)
        if geo.direct:
            block = (half_n, 1, geo.R, w)
            first = pl.BlockSpec(block, lambda j, s: (0, jnp.minimum(j, th - 1), 0, 0))
            second = pl.BlockSpec(block, lambda j, s: (0, jnp.maximum(j - th, 0), 0, 0))
            out_specs = [first, first, second, second]
            shapes = [jax.ShapeDtypeStruct((half_n, th, geo.R, w), BF)] * 4
    got = pl.pallas_call(
        kernel,
        grid_spec=pltpu.PrefetchScalarGridSpec(
            num_scalar_prefetch=1,
            grid=(geo.T,),
            in_specs=in_specs,
            out_specs=out_specs,
            scratch_shapes=[pltpu.VMEM((pr, n), BF)] * (na if geo.direct else 0),
        ),
        out_shape=shapes,
        compiler_params=params(),
        cost_estimate=cost(2 * pr * n * w * geo.T, 2 * geo.T * w * (2 * pr + n)),
        name=name,
    )(scal, *args)
    if not mine:
        return got[0]
    if geo.direct:
        return got
    blocks = got[0].reshape(geo.T, geo.P, geo.R, w)
    out = []
    for half in range(2):
        part = blocks[half * th : (half + 1) * th]
        part = reorder(part, [scal[0] ^ rel for rel in geo.order[half]], 1)
        part = part.transpose(1, 0, 2, 3)
        out += [part[:half_n], part[half_n:]]
    return out


def body(
    latents,
    conditioning,
    mod_weight,
    mod_bias,
    in_weight,
    query_value_bias,
    out_weight,
    branch_bias,
    up_weight,
    up_bias,
    down_weight,
    cotangent,
):
    images, row_count, width = latents.shape
    geo = Geo(lax.axis_size("fsdp"), lax.axis_size("tensor"), width)
    F, T = geo.F, geo.T
    assert 2 * images == T
    highest = lax.Precision.HIGHEST
    fi = lax.axis_index("fsdp")
    ti = lax.axis_index("tensor")
    pair, core = fi // 2, fi % 2
    scal = jnp.stack([pair, core, ti]).astype(jnp.int32)
    cols = in_weight.shape[2]
    units = up_weight.shape[1]
    geo.windows(cols)

    def places(k):
        return [
            ((2 * p + c) * T + t, (2 * p + t // images) * T + c * images + (t % images + k) % images)
            for p in range(geo.P)
            for c in range(2)
            for t in range(T)
        ]

    def to_chip(arr):
        got = []
        for k in range(images):
            item = lax.dynamic_index_in_dim(arr, (ti + k) % images, 0, keepdims=False)
            got.append(lax.ppermute(item, BOTH, places(k)))
        return got

    def from_chip(arr):
        got = []
        for k in range(images):
            back = [(dst, src) for src, dst in places(k)]
            got.append(lax.ppermute(arr[k * row_count : (k + 1) * row_count], BOTH, back))
        return got

    def home(parts):
        return reorder(jnp.stack(parts), [(i - ti) % images for i in range(images)])

    def share(arr):
        sent = jnp.broadcast_to(arr[None], (F * T,) + arr.shape)
        return lax.all_to_all(sent, BOTH, 0, 0, tiled=True)

    now, opened = (), []

    def tie(value):
        return after(value, *now)

    def start(*chains):
        for way in chains:
            opened.extend(way.advance(*now))

    def begin(shard, make, *how):
        way = Chain(make(tie(shard), geo, *how))
        opened.extend(way.flight)
        return way

    def across(value):
        got = flip_core(tie(value), geo)
        opened.append(got)
        return got

    def close(*made):
        nonlocal now
        now = (*opened, *made)
        opened.clear()

    heads = cols // HEAD_DIM
    attn_shard = jnp.concatenate([in_weight[0], in_weight[1], in_weight[2], out_weight.T], axis=1)
    attn_way = begin(attn_shard, gather_steps, False)
    info = jnp.concatenate([conditioning.reshape(-1), query_value_bias.reshape(-1), up_bias])
    count = info.shape[0]
    info = jnp.pad(info, (0, -count % 2048)).reshape(-1, 128)
    info = share(info)
    close()
    start(attn_way)
    up_way = begin(up_weight, gather_steps, True, True)
    info = info.reshape(F, T, -1)[:, :, :count]
    cond_all = info[:, 0, : images * width].reshape(F * images, width)
    qv_bias = info[0, :, images * width : images * width + 2 * cols].reshape(T, 2, 1, cols)
    unit_bias = info[0, :, images * width + 2 * cols :].reshape(T, 1, units).astype(F32)
    triple_bias = jnp.concatenate(
        [
            qv_bias[:, 0],
            jnp.zeros_like(qv_bias[:, 0]),
            qv_bias[:, 1],
            jnp.zeros((T, 1, geo.n3 - 3 * cols), BF),
        ],
        axis=2,
    ).astype(F32)
    silu_low = jax.nn.silu(cond_all.astype(F32)).astype(BF)
    silu_own = lax.dynamic_slice_in_dim(silu_low, fi * geo.R, geo.R, 1)
    mod_part = jnp.einsum("bd,dcj->bcj", silu_own, mod_weight, preferred_element_type=F32)
    mod_part += jnp.where(fi == 0, mod_bias.astype(F32), 0.0)
    mod_part = mod_part.reshape(geo.P, 1, T, 6, cols)
    mod_part = jnp.broadcast_to(mod_part, (geo.P, 2, T, 6, cols)).reshape(F * T, 6, cols)
    mod_part = lax.all_to_all(after(mod_part, *up_way.flight), BOTH, 0, 0, tiled=True)
    mod = mod_part.reshape(F, T, 6, cols).sum(axis=0).transpose(1, 0, 2).reshape(6, width)
    bias_rows = branch_bias.astype(F32)
    close(mod)
    start(attn_way)
    start(up_way)
    x_parts = to_chip(tie(latents))
    opened.extend(x_parts)
    close()
    x = jnp.concatenate(x_parts)
    start(attn_way, up_way)
    h1 = norm_mod(tie(x), mod)
    close(h1)
    w_attn = Gathered(attn_way.finish(*now), geo, scal)
    start(up_way)

    q, kv, kvo = [None] * 2, [None] * 2, [None] * 2
    mixed, lse = [None] * 2, [None] * 2
    down_way = begin(down_weight.T, gather_steps)
    for half in range(2):
        q[half], kv[half] = in_proj(tie(scal), h1, w_attn, triple_bias, half, geo)
    close(q[0], q[1])
    kvo = [across(kv[0]), across(kv[1])]
    start(down_way)
    close()
    start(up_way, down_way)
    for half in range(2):
        mixed[half], lse[half] = attn_fwd(tie(q[half]), kv[half], kvo[half], geo)
    attn, resid, h2 = out_proj(tie(scal), mixed, x, mod, bias_rows[0:1], w_attn, geo)
    close(h2)
    start(up_way, down_way)
    close()
    w_up = Gathered(up_way.finish(*now), geo, scal)
    start(down_way)
    cot_parts = to_chip(tie(cotangent))
    opened.extend(cot_parts)
    hidden, gp = up_proj(tie(scal), h2, unit_bias, w_up, geo)
    close(hidden)
    start(down_way)
    cot = jnp.concatenate(cot_parts)
    ffn_grad = (cot.astype(F32) * mod[5]).astype(BF)
    ffn_sum = jnp.sum(ffn_grad.astype(F32), axis=0)

    def block(ref):
        return ref[0]

    def alone(part):
        return part

    down_terms = [(ffn_grad, [hidden], block)]
    down_half = weight_grad(tie(scal), down_terms, alone, units, False, geo, "w_down_send")
    close(down_half)
    w_down = Gathered(down_way.finish(*now), geo, scal)
    down_got = across(down_half)
    block_rows, ffn_sums = down_proj(
        tie(scal), hidden, resid, cot, mod, bias_rows[1:2], w_down, geo
    )
    close(ffn_sums)

    down_parts = weight_grad(tie(scal), down_terms, alone, units, True, geo, "w_down", down_got)
    close(*down_parts)
    down_back = begin(down_parts, scatter_steps)
    block_back = from_chip(tie(block_rows))
    opened.extend(block_back)
    pre, unit_sum = pre_back(tie(scal), ffn_grad, gp, w_down, geo)
    up_terms = [(h2, [pre], block)]
    up_half = weight_grad(tie(scal), up_terms, alone, units, False, geo, "w_up_send")
    close(up_half)
    start(down_back)
    up_got = across(up_half)
    rg, ag, mid_sums = second_back(tie(scal), pre, resid, attn, cot, mod, w_up, geo)
    close(ag)
    start(down_back)
    up_parts = weight_grad(tie(scal), up_terms, alone, units, True, geo, "w_up", up_got)
    mg = mixed_back(tie(scal), ag, w_attn, geo)
    close(mg, *up_parts)
    start(down_back)
    up_back = begin(up_parts, scatter_steps, False)
    tri, tri_send, tri_sums, send_sums = [None] * 2, [None] * 2, [None] * 2, [None] * 2
    for half in range(2):
        tri[half], tri_send[half], tri_sums[half], send_sums[half] = attn_bwd(
            tie(q[half]), kv[half], kvo[half], mixed[half], mg, lse[half], half * geo.Th, geo
        )
    close(*tri_sums)
    tri_got = [across(tri_send[0]), across(tri_send[1])]
    tri_sum, send_sum = jnp.concatenate(tri_sums), jnp.concatenate(send_sums)
    pair_sums = jnp.concatenate(
        [
            tri_sum[:, :, :cols],
            tri_sum[:, :, 2 * cols : 3 * cols]
            + send_sum[:, :, geo.koff + cols : geo.koff + 2 * cols],
        ],
        axis=1,
    )
    close()
    start(up_back)
    down_back.finish(*now)

    def beside(first, second):
        shared = geo.n3 - geo.base
        middle = first[:, geo.base :] + second[:, :shared]
        return jnp.concatenate([first[:, : geo.base], middle, second[:, shared:]], axis=1)

    attn_terms = [
        (h1, [tuple(tri), tuple(tri_got)], lambda a, b: triple_grad(a, b, geo)),
        (ag, [tuple(mixed)], block),
    ]
    attn_half = weight_grad(tie(scal), attn_terms, beside, 4 * cols, False, geo, "w_attn_send")
    close(attn_half)
    start(up_back)
    attn_got = across(attn_half)
    latent_rows, first_sums = first_back(tie(scal), tri, tri_got, x, rg, mod, w_attn, geo)
    close(first_sums)
    mine = [i ^ ti for i in range(T)]
    rows = jnp.concatenate(
        [first_sums.sum(axis=1), mid_sums[:3].sum(axis=1), ffn_sums.sum(axis=0, keepdims=True)]
    )
    rows = rows.reshape(6, T, cols).transpose(1, 0, 2).reshape(T, 6 * cols)
    branch_sums = jnp.stack([mid_sums[3].sum(axis=0), ffn_sum]).reshape(1, 2 * width)
    rows = tie(rows)
    pack = jnp.concatenate(
        [
            rows,
            jnp.broadcast_to(branch_sums, (T, 2 * width)),
            reorder(unit_sum, mine).reshape(T, units),
            reorder(pair_sums, mine).reshape(T, 2 * cols),
        ],
        axis=1,
    )
    pack = jnp.pad(pack, ((0, 0), (0, -pack.shape[1] % 1024)))
    pack = jnp.broadcast_to(pack[None], (F,) + pack.shape).reshape(F * T, -1, 128)
    pack = lax.all_to_all(pack, BOTH, 0, 0, tiled=True)
    attn_parts = weight_grad(
        tie(scal), attn_terms, beside, 4 * cols, True, geo, "w_attn", attn_got
    )
    close(pack, *attn_parts)
    attn_back = begin(attn_parts, scatter_steps, False)
    pack = tie(pack).reshape(F, T, -1)
    mine_rows = pack[:, :, : 6 * cols].reshape(geo.P, 2, T, 6, cols).sum(axis=1)
    mine_rows = mine_rows.reshape(F * images, 6, cols)
    cond_part = jnp.einsum("bcj,dcj->bd", mine_rows, mod_weight.astype(F32), precision=highest)
    cond_part = cond_part.reshape(F, 1, images, geo.R)
    cond_part = jnp.broadcast_to(cond_part, (F, T, images, geo.R)).reshape(F * T, images, geo.R)
    cond_part = lax.all_to_all(cond_part, BOTH, 0, 0, tiled=True)
    latent_back = from_chip(tie(latent_rows))
    opened.extend(latent_back)
    close()
    start(attn_back)
    close()
    start(attn_back)
    block_out, latent_grad = home(block_back), home(latent_back)
    down_grad, up_grad = down_back.finish(*now), up_back.finish(*now)
    attn_grad = attn_back.finish(*now)
    in_grad = attn_grad[:, : 3 * cols].reshape(geo.R, 3, cols).transpose(1, 0, 2)

    bias_total = pack[:, :, 6 * cols :].sum(axis=(0, 1))
    branch_grad = bias_total[: 2 * width].reshape(2, width)
    unit_grad = bias_total[2 * width : 2 * width + units]
    pair_grad = bias_total[2 * width + units :][: 2 * cols].reshape(2, cols)
    mod_weight_grad = jnp.einsum("bd,bcj->dcj", silu_own.astype(F32), mine_rows, precision=highest)
    mod_bias_grad = mine_rows.sum(axis=0)
    cond_mine = cond_part.reshape(F, T, images, geo.R).sum(axis=1)
    silu_grad = cond_mine.transpose(1, 0, 2).reshape(images, width)
    cond_f = conditioning.astype(F32)
    sig = jax.nn.sigmoid(cond_f)
    cond_grad = silu_grad * (sig * (1.0 + cond_f * (1.0 - sig)))

    return (
        block_out,
        latent_grad,
        cond_grad,
        mod_weight_grad,
        mod_bias_grad,
        in_grad,
        pair_grad,
        attn_grad[:, 3 * cols :].T,
        branch_grad,
        up_grad,
        unit_grad,
        down_grad.T,
    )


def solution(mesh):
    in_specs = (
        P("fsdp", "tensor", None),
        P("fsdp", None),
        P("fsdp", None, "tensor"),
        P(None, "tensor"),
        P(None, "fsdp", "tensor"),
        P(None, "tensor"),
        P("tensor", "fsdp"),
        P(),
        P("fsdp", "tensor"),
        P("tensor"),
        P("tensor", "fsdp"),
        P("fsdp", "tensor", None),
    )
    out_specs = (
        P("fsdp", "tensor", None),
        P("fsdp", "tensor", None),
        P("fsdp", None),
        P("fsdp", None, "tensor"),
        P(None, "tensor"),
        P(None, "fsdp", "tensor"),
        P(None, "tensor"),
        P("tensor", "fsdp"),
        P(),
        P("fsdp", "tensor"),
        P("tensor"),
        P("tensor", "fsdp"),
    )
    return jax.shard_map(body, mesh=mesh, in_specs=in_specs, out_specs=out_specs, check_vma=False)
```

```python
import functools

import jax
import jax.numpy as jnp
from jax import lax
from jax.experimental import pallas as pl
from jax.experimental.pallas import tpu as pltpu
from jax.sharding import PartitionSpec as P

HEAD_DIM = 72
EPS = 1e-06
TANH_C = 0.7978845608028654
CUBIC = 0.044715
LOG2E = 1.4426950408889634
VMEM_BYTES = 56 << 20
ROWS = 32
BF = jnp.bfloat16
F32 = jnp.float32
BOTH = ("fsdp", "tensor")


def dotg(a, b, ca, cb):
    return lax.dot_general(a, b, (((ca,), (cb,)), ((), ())), preferred_element_type=F32)


class Geo:
    def __init__(self, fsdp, tensor, dim):
        self.F, self.T, self.P = fsdp, tensor, fsdp // 2
        self.Th = tensor // 2
        self.D = dim
        self.R = dim // fsdp
        self.bits = [1 << b for b in range((self.P - 1).bit_length())]
        self.order = (self.orders(self.bits[::-1]), self.orders(self.bits))
        self.direct = self.R % 16 == 0

    def windows(self, w):
        self.w = w
        self.n3 = min(padded(3 * w), 4 * w)
        self.kbase = w // 128 * 128
        self.koff = w - self.kbase
        self.kvw = self.n3 - self.kbase
        self.base = 3 * w // 128 * 128
        self.off = 3 * w - self.base
        self.win = 4 * w - self.base

    @staticmethod
    def orders(msb_first):
        vals = [0]
        for bit in reversed(msb_first):
            vals = vals + [v | bit for v in vals]
        return vals


def reorder(x, index, axis=0):
    return jnp.stack([lax.dynamic_index_in_dim(x, i, axis, keepdims=False) for i in index], axis)


def flip_pair(x, bit, geo):
    return lax.ppermute(x, "fsdp", [(i, i ^ (2 * bit)) for i in range(geo.F)])


def flip_core(x, geo):
    return lax.ppermute(x, "fsdp", [(i, i ^ 1) for i in range(geo.F)])


def flip_tensor(x, k, geo):
    return lax.ppermute(x, "tensor", [(i, i ^ k) for i in range(geo.T)])


def after(value, *done):
    return lax.optimization_barrier((value, done))[0] if done else value


class Chain:
    def __init__(self, steps):
        self.steps = steps
        self.flight = next(steps)
        self.result = None

    def advance(self, *done):
        if self.result is not None:
            return []
        try:
            self.flight = self.steps.send(after(self.flight, *done))
        except StopIteration as end:
            self.flight, self.result = [], end.value
        return self.flight

    def finish(self, *done):
        while self.result is None:
            self.advance(*done)
        return self.result


def gather_steps(shard, geo, parted=True, joined=False, extras=None):
    if parted:
        most = [k for k in range(1, geo.T) if k != geo.Th]
        got = yield [flip_tensor(shard, k, geo) for k in most]
        mid = yield [flip_tensor(shard, geo.Th, geo)]
        parts = [shard] + got[: geo.Th - 1] + mid + got[geo.Th - 1 :]
    else:
        got = yield [flip_tensor(shard, k, geo) for k in range(1, geo.T)]
        parts = [shard] + got
    if extras is not None:
        extras += [part[geo.R :] for part in parts]
        parts = [part[: geo.R] for part in parts]
    bufs = [jnp.stack(parts[h * geo.Th : (h + 1) * geo.Th])[None] for h in range(2)]
    for at in range(len(geo.bits)):
        bits = (geo.bits[at], geo.bits[-1 - at])
        got = yield [flip_pair(bufs[h], bits[h], geo) for h in range(2)]
        if joined or at < len(geo.bits) - 1:
            bufs = [jnp.concatenate(pair) for pair in zip(bufs, got)]
    owns = [[buf] for buf in bufs] if joined else [list(pair) for pair in zip(bufs, got)]
    count = len(owns[0])
    others = yield [flip_core(a, geo) for own in owns for a in own]
    return [owns[h] + others[h * count : (h + 1) * count] for h in range(2)]


class Gathered:
    def __init__(self, halves, geo, scal):
        self.geo = geo
        if not geo.direct:
            fixed = []
            for half, arrays in enumerate(halves):
                at = [geo.order[half].index(rel) for rel in range(geo.P)]
                lookup = jnp.array(at, jnp.int32)
                blocks = jnp.concatenate(arrays)
                blocks = reorder(
                    blocks,
                    [
                        lookup[(f // 2) ^ scal[0]] + geo.P * ((f % 2) ^ scal[1])
                        for f in range(geo.F)
                    ],
                )
                _, th, r, w = blocks.shape
                fixed.append([blocks.transpose(1, 0, 2, 3).reshape(1, th, geo.D, w)])
            halves = fixed
        self.halves = halves
        self.arrays = halves[0] + halves[1]
        self.n = len(halves[0])
        self.width = self.arrays[0].shape[-1]

    def operands(self, half=None):
        return self.arrays if half is None else self.halves[half]

    def specs(self, half=None):
        return [pl.BlockSpec(memory_space=pl.ANY)] * len(self.operands(half))

    def scratch(self, lo=0, hi=None):
        hi = self.width if hi is None else hi
        if lo % 128 or hi % 128:
            lo, hi = 0, self.width
        self.lo, self.hi = lo, hi
        count = self.n * self.arrays[0].shape[0]
        return [
            pltpu.VMEM((2, self.geo.D, hi - lo), BF),
            pltpu.SemaphoreType.DMA((2, count)),
        ]

    def copies(self, group, slot, half, s_ref, refs, buf, sem):
        geo, out = self.geo, []
        for at, ref in enumerate(refs):
            n, _, rows, _ = ref.shape
            for i in range(n):
                row = 0
                if geo.direct:
                    place = at * n + i
                    rel = geo.order[half][place % geo.P]
                    row = 2 * (s_ref[0] ^ rel) + (s_ref[1] ^ (place // geo.P))
                    row = pl.multiple_of(row * rows, rows)
                out.append(
                    pltpu.make_async_copy(
                        ref.at[i, group, :, pl.ds(self.lo, self.hi - self.lo)],
                        buf.at[slot, pl.ds(row, rows), :],
                        sem.at[slot, at * n + i],
                    )
                )
        return out

    def stream(self, j, s_ref, refs, buf, sem, half=None):
        th = self.geo.Th

        def each(step, act):
            if half is not None:
                for copy in self.copies(step, step % 2, half, s_ref, refs, buf, sem):
                    act(copy)
                return
            for part in range(2):

                @pl.when((step < th) if part == 0 else (step >= th))
                def _():
                    mine = refs[part * self.n : (part + 1) * self.n]
                    for copy in self.copies(
                        step - part * th, step % 2, part, s_ref, mine, buf, sem
                    ):
                        act(copy)

        @pl.when(j == 0)
        def _():
            each(j, lambda copy: copy.start(priority=1))

        @pl.when(j + 1 < (self.geo.T if half is None else th))
        def _():
            each(j + 1, lambda copy: copy.start(priority=1))

        each(j, lambda copy: copy.wait())
        return buf.at[j % 2]


def scatter_steps(pieces, geo, parted=True):
    def add(a, b):
        return a.astype(F32) + b.astype(F32)

    keeps, sends = [pieces[0], pieces[2]], [pieces[1], pieces[3]]
    for at in range(len(geo.bits)):
        bits = (geo.bits[-1 - at], geo.bits[at])
        got = yield [flip_pair(sends[h], bits[h], geo) for h in range(2)]
        m = max(1, keeps[0].shape[0] // 2)
        if at < len(geo.bits) - 1:
            sends = [add(keeps[h][m:], got[h][m:]).astype(BF) for h in range(2)]
        keeps = [add(keeps[h][:m], got[h][:m]).astype(BF) for h in range(2)]
    units = [keep[0, k] for keep in keeps for k in range(geo.Th)]
    if parted:
        rest = [k for k in range(1, geo.T) if k != geo.Th]
        got = yield [flip_tensor(units[k], k, geo) for k in rest]
        got += yield [flip_tensor(units[geo.Th], geo.Th, geo)]
    else:
        got = yield [flip_tensor(units[k], k, geo) for k in range(1, geo.T)]
    total = units[0].astype(F32)
    for part in got:
        total = total + part.astype(F32)
    return total


def params(size=VMEM_BYTES):
    return pltpu.CompilerParams(vmem_limit_bytes=size)


def cost(flops, size):
    return pl.CostEstimate(flops=int(flops), bytes_accessed=int(size), transcendentals=0)


def whole(shape):
    zeros = (0,) * len(shape)
    return pl.BlockSpec(shape, lambda j, s: zeros)


def padded(w):
    return -(-w // 128) * 128


def chunked(total, want):
    return want if total % want == 0 else total


def norm_of(v):
    centre = v - jnp.mean(v, axis=-1, keepdims=True)
    inv = lax.rsqrt(jnp.mean(centre * centre, axis=-1, keepdims=True) + EPS)
    return centre * inv, inv


def norm_back(norm, inv, g):
    return (
        g
        - jnp.mean(g, axis=-1, keepdims=True)
        - norm * jnp.mean(g * norm, axis=-1, keepdims=True)
    ) * inv


def fold_rows(v):
    return v.reshape(v.shape[0] // 8, 8, v.shape[1]).sum(axis=0)


class Late:
    def __init__(self, *arrays):
        self.arrays = arrays
        self.specs = [pl.BlockSpec(memory_space=pl.ANY)] * len(arrays)
        self.scratch = [pltpu.VMEM(a.shape, a.dtype) for a in arrays]
        self.scratch.append(pltpu.SemaphoreType.DMA((len(arrays),)))

    def copies(self, refs, scratch):
        sem = scratch[-1]
        return [
            pltpu.make_async_copy(ref, scratch[i], sem.at[i]) for i, ref in enumerate(refs)
        ]

    def start(self, j, refs, scratch):
        @pl.when(j == 0)
        def _():
            for copy in self.copies(refs, scratch):
                copy.start(priority=1)

    def wait(self, refs, scratch):
        for copy in self.copies(refs, scratch):
            copy.wait()
        return scratch[:-1]


def two_halves(block, th, tail):
    return [
        pl.BlockSpec(block, lambda j, s: (jnp.minimum(j, th - 1),) + tail),
        pl.BlockSpec(block, lambda j, s: (jnp.maximum(j - th, 0),) + tail),
    ]


def norm_mod(x, mod):
    n, d = x.shape[0] - ROWS, x.shape[1]

    def kernel(x_ref, m_ref, h_ref):
        @pl.loop(0, n // ROWS, unroll=4)
        def _(i):
            at = pl.ds(pl.multiple_of(i * ROWS, ROWS), ROWS)
            norm, _ = norm_of(x_ref[at, :].astype(F32))
            h_ref[at, :] = (norm * (1.0 + m_ref[1:2, :]) + m_ref[0:1, :]).astype(BF)

    return pl.pallas_call(
        kernel,
        out_shape=jax.ShapeDtypeStruct((n, d), BF),
        compiler_params=params(),
        cost_estimate=cost(20 * n * d, 4 * n * d),
        name="norm_mod",
    )(x, mod)


def in_proj(scal, h, wt, bias, half, geo):
    n, d = h.shape
    n3, wp = geo.n3, padded(geo.w)
    nw = wt.n

    def kernel(s, h_ref, b_ref, *refs):
        w_refs, (q_ref, kv_ref, wbuf, sem) = refs[:nw], refs[nw:]
        now = wt.stream(pl.program_id(0), s, w_refs, wbuf, sem, half)
        y = dotg(h_ref[...], now[:, :n3], 1, 0) + b_ref[0]
        y = y.astype(BF)
        q_ref[0] = y[:, :wp]
        kv_ref[0] = y[:, geo.kbase :]

    first = half * geo.Th
    return pl.pallas_call(
        kernel,
        grid_spec=pltpu.PrefetchScalarGridSpec(
            num_scalar_prefetch=1,
            grid=(geo.Th,),
            in_specs=[
                whole((n, d)),
                pl.BlockSpec((1, 1, n3), lambda j, s: (s[2] ^ (j + first), 0, 0)),
                *wt.specs(half),
            ],
            out_specs=[
                pl.BlockSpec((1, n, wp), lambda j, s: (j, 0, 0)),
                pl.BlockSpec((1, n, geo.kvw), lambda j, s: (j, 0, 0)),
            ],
            scratch_shapes=wt.scratch(0, n3),
        ),
        out_shape=[
            jax.ShapeDtypeStruct((geo.Th, n, wp), BF),
            jax.ShapeDtypeStruct((geo.Th, n, geo.kvw), BF),
        ],
        compiler_params=params(),
        cost_estimate=cost(2 * n * d * n3 * geo.Th, 8 * d * geo.w * geo.Th + 8 * n * d),
        name="in_proj",
    )(scal, h, bias, *wt.operands(half))


def head_lanes(geo, h):
    at = h * HEAD_DIM
    return [
        slice(start + at, start + at + HEAD_DIM)
        for start in (0, geo.koff, geo.koff + geo.w, geo.off)
    ]


def attn_fwd(q, kv, kvo, geo):
    z, n, wp = q.shape
    heads = geo.w // HEAD_DIM
    c = HEAD_DIM**-0.5 * LOG2E

    def kernel(q_ref, kv_ref, kvo_ref, o_ref, lse_ref):
        outs = [jnp.zeros((geo.off, n), F32)] if geo.off else []
        for h in range(heads):
            lq, lk, lv, _ = head_lanes(geo, h)
            qh = q_ref[0, :, lq]
            sa = dotg(kv_ref[0, :, lk], qh, 1, 1) * c
            sb = dotg(kvo_ref[0, :, lk], qh, 1, 1) * c
            top = jnp.maximum(
                jnp.max(sa, axis=0, keepdims=True), jnp.max(sb, axis=0, keepdims=True)
            )
            pa, pb = jnp.exp2(sa - top), jnp.exp2(sb - top)
            total = jnp.sum(pa, axis=0, keepdims=True) + jnp.sum(pb, axis=0, keepdims=True)
            o = dotg(kv_ref[0, :, lv], pa.astype(BF), 0, 0)
            o = o + dotg(kvo_ref[0, :, lv], pb.astype(BF), 0, 0)
            outs.append(o / total)
            lse_ref[0, h : h + 1, :] = top + jnp.log2(total)
        o_ref[0] = jnp.concatenate(outs, axis=0).T.astype(BF)

    def spec(width):
        return pl.BlockSpec((1, n, width), lambda j: (j, 0, 0))

    return pl.pallas_call(
        kernel,
        grid=(z,),
        in_specs=[spec(wp), spec(geo.kvw), spec(geo.kvw)],
        out_specs=[spec(geo.win), pl.BlockSpec((1, heads, n), lambda j: (j, 0, 0))],
        out_shape=[
            jax.ShapeDtypeStruct((z, n, geo.win), BF),
            jax.ShapeDtypeStruct((z, heads, n), F32),
        ],
        compiler_params=params(),
        cost_estimate=cost(3e9 * z, 10 * z * n * wp),
        name="attn_fwd",
    )(q, kv, kvo)


def attn_bwd(q, kv, kvo, o, do, lse, first, geo):
    z, n, wp = q.shape
    heads = lse.shape[1]
    scale = HEAD_DIM**-0.5
    c = scale * LOG2E

    def kernel(q_ref, kv_ref, kvo_ref, o_ref, do_ref, lse_ref, tri_ref, send_ref, ts_ref, ss_ref):
        both = (do_ref[0].astype(F32) * o_ref[0].astype(F32)).T
        dqs, parts = [], [[[], []], [[], []]]
        for h in range(heads):
            lq, lk, lv, lm = head_lanes(geo, h)
            qh, doh = q_ref[0, :, lq], do_ref[0, :, lm]
            delta = jnp.sum(both[lm], axis=0, keepdims=True)
            lse_h = lse_ref[0, h : h + 1, :]
            dq = None
            for i, ref in enumerate((kv_ref, kvo_ref)):
                k, v = ref[0, :, lk], ref[0, :, lv]
                p = jnp.exp2(dotg(k, qh, 1, 1) * c - lse_h)
                ds = (p * (dotg(v, doh, 1, 1) - delta)).astype(BF)
                parts[i][1].append(dotg(doh, p.astype(BF), 0, 1))
                parts[i][0].append(dotg(qh, ds, 0, 1) * scale)
                got = dotg(k, ds, 0, 0)
                dq = got if dq is None else dq + got
            dqs.append(dq * scale)

        def rows(count):
            return [jnp.zeros((count, n), F32)] if count else []

        pad = rows(geo.n3 - 3 * geo.w)
        own = jnp.concatenate(dqs + parts[0][0] + parts[0][1] + pad, axis=0).T
        other = jnp.concatenate(rows(geo.koff) + parts[1][0] + parts[1][1] + pad, axis=0).T
        tri_ref[0] = own.astype(BF)
        send_ref[0] = other.astype(BF)
        ts_ref[0] = jnp.sum(own, axis=0, keepdims=True)
        ss_ref[0] = jnp.sum(other, axis=0, keepdims=True)

    def spec(width, at=0, count=n):
        return pl.BlockSpec((1, count, width), lambda j: (j + at, 0, 0))

    return pl.pallas_call(
        kernel,
        grid=(z,),
        in_specs=[
            spec(wp),
            spec(geo.kvw),
            spec(geo.kvw),
            spec(geo.win),
            spec(geo.win, first),
            spec(n, 0, heads),
        ],
        out_specs=[spec(geo.n3), spec(geo.kvw), spec(geo.n3, 0, 1), spec(geo.kvw, 0, 1)],
        out_shape=[
            jax.ShapeDtypeStruct((z, n, geo.n3), BF),
            jax.ShapeDtypeStruct((z, n, geo.kvw), BF),
            jax.ShapeDtypeStruct((z, 1, geo.n3), F32),
            jax.ShapeDtypeStruct((z, 1, geo.kvw), F32),
        ],
        compiler_params=params(),
        cost_estimate=cost(5e9 * z, 16 * z * n * wp),
        name="attn_bwd",
    )(q, kv, kvo, o, do, lse)


def triple_grad(tri_ref, got_ref, geo):
    late = tri_ref[0, :, geo.kbase :].astype(F32) + got_ref[0].astype(F32)
    if not geo.kbase:
        return late.astype(BF)
    return jnp.concatenate([tri_ref[0, :, : geo.kbase], late.astype(BF)], axis=1)


def out_proj(scal, mixed, x, mod, bias, wt, geo):
    _, n, win = mixed[0].shape
    d = geo.D
    nw = len(wt.arrays)
    th = geo.Th

    late = Late(x)

    def kernel(s, ya_ref, yb_ref, m_ref, b_ref, *refs):
        late_in, refs = refs[:1], refs[1:]
        w_refs, (attn_out, resid_ref, h_ref, wbuf, sem, attn_ref, *late_buf) = refs[:nw], refs[nw:]
        j = pl.program_id(0)
        late.start(j, late_in, late_buf)
        now = wt.stream(j, s, w_refs, wbuf, sem)
        y = jnp.where(j < th, ya_ref[0], yb_ref[0])
        part = dotg(y, now[:, -win:], 1, 1)

        @pl.when(j == 0)
        def _():
            attn_ref[...] = part

        @pl.when(j > 0)
        def _():
            attn_ref[...] += part

        @pl.when(j == geo.T - 1)
        def _():
            (x_ref,) = late.wait(late_in, late_buf)

            @pl.loop(0, n // ROWS, unroll=4)
            def _(i):
                at = pl.ds(pl.multiple_of(i * ROWS, ROWS), ROWS)
                attn = attn_ref[at, :] + b_ref[...]
                attn_out[at, :] = attn.astype(BF)
                resid = x_ref[at, :].astype(F32) + m_ref[2:3, :] * attn
                resid_ref[at, :] = resid
                norm, _ = norm_of(resid)
                h_ref[at, :] = (norm * (1.0 + m_ref[4:5, :]) + m_ref[3:4, :]).astype(BF)

    return pl.pallas_call(
        kernel,
        grid_spec=pltpu.PrefetchScalarGridSpec(
            num_scalar_prefetch=1,
            grid=(geo.T,),
            in_specs=[
                *two_halves((1, n, win), th, (0, 0)),
                whole(mod.shape),
                whole((1, d)),
                *late.specs,
                *wt.specs(),
            ],
            out_specs=[whole((n, d))] * 3,
            scratch_shapes=[
                *wt.scratch(geo.base, 4 * geo.w),
                pltpu.VMEM((n, d), F32),
                *late.scratch,
            ],
        ),
        out_shape=[
            jax.ShapeDtypeStruct((n + ROWS, d), BF),
            jax.ShapeDtypeStruct((n, d), F32),
            jax.ShapeDtypeStruct((n + ROWS, d), BF),
        ],
        compiler_params=params(),
        cost_estimate=cost(2 * n * d * d, 8 * d * d + 14 * n * d),
        name="out_proj",
    )(scal, *mixed, mod, bias, *late.arrays, *wt.arrays)


def up_proj(scal, h, bias, wt, geo):
    n, d = h.shape[0] - ROWS, h.shape[1]
    w = wt.width
    nw = len(wt.arrays)
    step = chunked(w, 384)

    def kernel(s, h_ref, b_ref, *refs):
        w_refs, (hid_ref, gp_ref, wbuf, sem) = refs[:nw], refs[nw:]
        j = pl.program_id(0)
        now = wt.stream(j, s, w_refs, wbuf, sem)
        for at in range(0, w, step):
            cols = slice(at, at + step)
            u = dotg(h_ref[...], now[:, cols], 1, 0) + b_ref[0, :, cols]
            sq = u * u
            t = jnp.tanh(TANH_C * (u + CUBIC * sq * u))
            half = 0.5 * (1.0 + t)
            hid_ref[0, :, cols] = (u * half).astype(BF)
            slope = TANH_C * (1.0 + 3.0 * CUBIC * sq)
            gp_ref[0, :, cols] = (half + 0.5 * u * (1.0 - t * t) * slope).astype(BF)

    out = pl.BlockSpec((1, n, w), lambda j, s: (j, 0, 0))
    return pl.pallas_call(
        kernel,
        grid_spec=pltpu.PrefetchScalarGridSpec(
            num_scalar_prefetch=1,
            grid=(geo.T,),
            in_specs=[
                whole((n, d)),
                pl.BlockSpec((1, 1, w), lambda j, s: (j, 0, 0)),
                *wt.specs(),
            ],
            out_specs=[out, out],
            scratch_shapes=wt.scratch(),
        ),
        out_shape=[jax.ShapeDtypeStruct((geo.T, n, w), BF)] * 2,
        compiler_params=params(),
        cost_estimate=cost(2 * n * d * w * geo.T, 2 * geo.T * w * (d + 2 * n)),
        name="up_proj",
    )(scal, h, bias, *wt.arrays)


def down_proj(scal, hidden, resid, cot, mod, bias, wt, geo):
    _, n, w = hidden.shape
    d = geo.D
    nw = len(wt.arrays)

    late = Late(resid, cot)

    def kernel(s, y_ref, m_ref, b_ref, *refs):
        late_in, refs = refs[:2], refs[2:]
        w_refs, (out_ref, sum_ref, wbuf, sem, acc, *late_buf) = refs[:nw], refs[nw:]
        j = pl.program_id(0)
        late.start(j, late_in, late_buf)
        now = wt.stream(j, s, w_refs, wbuf, sem)
        part = dotg(y_ref[0], now[...], 1, 1)

        @pl.when(j == 0)
        def _():
            acc[...] = part
            sum_ref[...] = jnp.zeros_like(sum_ref)

        @pl.when(j > 0)
        def _():
            acc[...] += part

        @pl.when(j == geo.T - 1)
        def _():
            r_ref, c_ref = late.wait(late_in, late_buf)

            @pl.loop(0, n // ROWS, unroll=4)
            def _(i):
                at = pl.ds(pl.multiple_of(i * ROWS, ROWS), ROWS)
                ffn = acc[at, :] + b_ref[...]
                out_ref[at, :] = (r_ref[at, :] + m_ref[5:6, :] * ffn).astype(BF)
                sum_ref[...] += fold_rows(c_ref[at, :].astype(F32) * ffn)

    return pl.pallas_call(
        kernel,
        grid_spec=pltpu.PrefetchScalarGridSpec(
            num_scalar_prefetch=1,
            grid=(geo.T,),
            in_specs=[
                pl.BlockSpec((1, n, w), lambda j, s: (j, 0, 0)),
                whole(mod.shape),
                whole((1, d)),
                *late.specs,
                *wt.specs(),
            ],
            out_specs=[whole((n, d)), whole((8, d))],
            scratch_shapes=[*wt.scratch(), pltpu.VMEM((n, d), F32), *late.scratch],
        ),
        out_shape=[jax.ShapeDtypeStruct((n, d), BF), jax.ShapeDtypeStruct((8, d), F32)],
        compiler_params=params(),
        cost_estimate=cost(2 * n * d * w * geo.T, 2 * geo.T * w * (d + n) + 8 * n * d),
        name="down_proj",
    )(scal, hidden, mod, bias, *late.arrays, *wt.arrays)


def pre_back(scal, g, gp, wt, geo):
    n, d = g.shape
    w = wt.width
    nw = len(wt.arrays)
    step = chunked(w, 384)

    def kernel(s, g_ref, gp_ref, *refs):
        w_refs, (out_ref, sum_ref, wbuf, sem) = refs[:nw], refs[nw:]
        j = pl.program_id(0)
        now = wt.stream(j, s, w_refs, wbuf, sem)
        for at in range(0, w, step):
            cols = slice(at, at + step)
            y = dotg(g_ref[...], now[:, cols], 1, 0) * gp_ref[0, :, cols].astype(F32)
            out_ref[0, :, cols] = y.astype(BF)
            sum_ref[0, :, cols] = jnp.sum(y, axis=0, keepdims=True)

    out = pl.BlockSpec((1, n, w), lambda j, s: (j, 0, 0))
    return pl.pallas_call(
        kernel,
        grid_spec=pltpu.PrefetchScalarGridSpec(
            num_scalar_prefetch=1,
            grid=(geo.T,),
            in_specs=[whole((n, d)), out, *wt.specs()],
            out_specs=[out, pl.BlockSpec((1, 1, w), lambda j, s: (j, 0, 0))],
            scratch_shapes=wt.scratch(),
        ),
        out_shape=[
            jax.ShapeDtypeStruct((geo.T, n, w), BF),
            jax.ShapeDtypeStruct((geo.T, 1, w), F32),
        ],
        compiler_params=params(),
        cost_estimate=cost(2 * n * d * w * geo.T, 2 * geo.T * w * (d + 2 * n)),
        name="pre_back",
    )(scal, g, gp, *wt.arrays)


def second_back(scal, pre, resid, attn, cot, mod, wt, geo):
    _, n, w = pre.shape
    d = geo.D
    nw = len(wt.arrays)

    late = Late(resid, attn, cot)

    def kernel(s, y_ref, m_ref, *refs):
        late_in, refs = refs[:3], refs[3:]
        w_refs, (rg_ref, ag_ref, sum_ref, wbuf, sem, acc, *late_buf) = refs[:nw], refs[nw:]
        j = pl.program_id(0)
        late.start(j, late_in, late_buf)
        now = wt.stream(j, s, w_refs, wbuf, sem)
        part = dotg(y_ref[0], now[...], 1, 1)

        @pl.when(j == 0)
        def _():
            acc[...] = part
            sum_ref[...] = jnp.zeros_like(sum_ref)

        @pl.when(j > 0)
        def _():
            acc[...] += part

        @pl.when(j == geo.T - 1)
        def _():
            r_ref, a_ref, c_ref = late.wait(late_in, late_buf)

            @pl.loop(0, n // ROWS, unroll=4)
            def _(i):
                at = pl.ds(pl.multiple_of(i * ROWS, ROWS), ROWS)
                g = acc[at, :]
                norm, inv = norm_of(r_ref[at, :])
                rg = c_ref[at, :].astype(F32) + norm_back(norm, inv, g * (1.0 + m_ref[4:5, :]))
                rg_ref[at, :] = rg
                ag = rg * m_ref[2:3, :]
                ag_ref[at, :] = ag.astype(BF)
                sum_ref[0] += fold_rows(rg * a_ref[at, :].astype(F32))
                sum_ref[1] += fold_rows(g)
                sum_ref[2] += fold_rows(g * norm)
                sum_ref[3] += fold_rows(ag)

    return pl.pallas_call(
        kernel,
        grid_spec=pltpu.PrefetchScalarGridSpec(
            num_scalar_prefetch=1,
            grid=(geo.T,),
            in_specs=[
                pl.BlockSpec((1, n, w), lambda j, s: (j, 0, 0)),
                whole(mod.shape),
                *late.specs,
                *wt.specs(),
            ],
            out_specs=[whole((n, d)), whole((n, d)), whole((4, 8, d))],
            scratch_shapes=[*wt.scratch(), pltpu.VMEM((n, d), F32), *late.scratch],
        ),
        out_shape=[
            jax.ShapeDtypeStruct((n, d), F32),
            jax.ShapeDtypeStruct((n, d), BF),
            jax.ShapeDtypeStruct((4, 8, d), F32),
        ],
        compiler_params=params(),
        cost_estimate=cost(2 * n * d * w * geo.T, 2 * geo.T * w * (d + n) + 18 * n * d),
        name="second_back",
    )(scal, pre, mod, *late.arrays, *wt.arrays)


def mixed_back(scal, g, wt, geo):
    n, d = g.shape
    win = geo.win
    nw = len(wt.arrays)

    def kernel(s, g_ref, *refs):
        w_refs, (out_ref, wbuf, sem) = refs[:nw], refs[nw:]
        now = wt.stream(pl.program_id(0), s, w_refs, wbuf, sem)
        out_ref[0] = dotg(g_ref[...], now[:, -win:], 1, 0).astype(BF)

    return pl.pallas_call(
        kernel,
        grid_spec=pltpu.PrefetchScalarGridSpec(
            num_scalar_prefetch=1,
            grid=(geo.T,),
            in_specs=[whole((n, d)), *wt.specs()],
            out_specs=pl.BlockSpec((1, n, win), lambda j, s: (j, 0, 0)),
            scratch_shapes=wt.scratch(geo.base, 4 * geo.w),
        ),
        out_shape=jax.ShapeDtypeStruct((geo.T, n, win), BF),
        compiler_params=params(),
        cost_estimate=cost(2 * n * d * d, 8 * d * d + 4 * n * d),
        name="mixed_back",
    )(scal, g, *wt.arrays)


def first_back(scal, tri, got, x, rg, mod, wt, geo):
    _, n, n3 = tri[0].shape
    d = geo.D
    nw = len(wt.arrays)
    th = geo.Th

    late = Late(x, rg)

    def kernel(s, ta, tb, ga, gb, m_ref, *refs):
        late_in, refs = refs[:2], refs[2:]
        w_refs, (out_ref, sum_ref, wbuf, sem, lhs, acc, *late_buf) = refs[:nw], refs[nw:]
        j = pl.program_id(0)
        late.start(j, late_in, late_buf)
        now = wt.stream(j, s, w_refs, wbuf, sem)
        for half, (tri_ref, got_ref) in enumerate(((ta, ga), (tb, gb))):

            @pl.when((j < th) if half == 0 else (j >= th))
            def _():
                lhs[...] = triple_grad(tri_ref, got_ref, geo)

        part = dotg(lhs[...], now[:, :n3], 1, 1)

        @pl.when(j == 0)
        def _():
            acc[...] = part
            sum_ref[...] = jnp.zeros_like(sum_ref)

        @pl.when(j > 0)
        def _():
            acc[...] += part

        @pl.when(j == geo.T - 1)
        def _():
            x_ref, r_ref = late.wait(late_in, late_buf)

            @pl.loop(0, n // ROWS, unroll=4)
            def _(i):
                at = pl.ds(pl.multiple_of(i * ROWS, ROWS), ROWS)
                g = acc[at, :]
                norm, inv = norm_of(x_ref[at, :].astype(F32))
                back = norm_back(norm, inv, g * (1.0 + m_ref[1:2, :]))
                out_ref[at, :] = (r_ref[at, :] + back).astype(BF)
                sum_ref[0] += fold_rows(g)
                sum_ref[1] += fold_rows(g * norm)

    return pl.pallas_call(
        kernel,
        grid_spec=pltpu.PrefetchScalarGridSpec(
            num_scalar_prefetch=1,
            grid=(geo.T,),
            in_specs=[
                *two_halves((1, n, n3), th, (0, 0)),
                *two_halves((1, n, geo.kvw), th, (0, 0)),
                whole(mod.shape),
                *late.specs,
                *wt.specs(),
            ],
            out_specs=[whole((n, d)), whole((2, 8, d))],
            scratch_shapes=[
                *wt.scratch(0, n3),
                pltpu.VMEM((n, n3), BF),
                pltpu.VMEM((n, d), F32),
                *late.scratch,
            ],
        ),
        out_shape=[jax.ShapeDtypeStruct((n, d), BF), jax.ShapeDtypeStruct((2, 8, d), F32)],
        compiler_params=params(),
        cost_estimate=cost(6 * n * d * d, 8 * d * d + 16 * n * d),
        name="first_back",
    )(scal, *tri, *got, mod, *late.arrays, *wt.arrays)


def weight_grad(scal, terms, join, w, mine, geo, name, partial=None):
    n = terms[0][1][0].shape[-2] if not isinstance(terms[0][1][0], tuple) else terms[0][1][0][0].shape[-2]
    pr = geo.P * geo.R
    th = geo.Th
    half_n = geo.P // 2
    want = scal[1] if mine else 1 - scal[1]
    lefts = [term[0] for term in terms]
    if not geo.direct:
        lefts = [a[:n] for a in lefts]
    if not geo.direct:

        def pick(a):
            cols = a.reshape(n, geo.P, 2, geo.R)
            cols = jnp.where(want == 0, cols[:, :, 0], cols[:, :, 1])
            return cols.reshape(n, pr).T

        lefts = [pick(a) for a in lefts]
    ops, op_specs, counts = [], [], []
    for _, operands, _ in terms:
        counts.append(len(operands))
        for pair in operands:
            if isinstance(pair, tuple):
                tail = (0,) * (pair[0].ndim - 1)
                op_specs += two_halves((1,) + pair[0].shape[1:], th, tail)
                ops += pair
            else:
                op_specs.append(pl.BlockSpec((1,) + pair.shape[1:], lambda j, s: (j, 0, 0)))
                ops.append(pair)
    na, nb = len(lefts), len(ops)

    def kernel(s, *refs):
        a_refs, b_refs = refs[:na], refs[na : na + nb]
        rest = refs[na + nb :]
        got_ref = None
        if mine:
            got_ref, rest = rest[0], rest[1:]
        n_out = 4 if (mine and geo.direct) else 1
        outs, ats = rest[:n_out], rest[n_out:]
        if mine and geo.direct:
            total, ats = ats[-1], ats[:-1]
        j = pl.program_id(0)
        if geo.direct:

            @pl.when(j == 0)
            def _():
                pick_odd = (s[1] == 1) if mine else (s[1] == 0)
                for ref, at in zip(a_refs, ats):
                    flip = ref[...].T
                    for p in range(geo.P):
                        even = flip[2 * p * geo.R : (2 * p + 1) * geo.R]
                        odd = flip[(2 * p + 1) * geo.R : (2 * p + 2) * geo.R]
                        at[p * geo.R : (p + 1) * geo.R, :] = jnp.where(pick_odd, odd, even)
        else:
            ats = a_refs

        def store(half):
            at_op, parts = 0, []
            for at, (_, operands, build) in zip(ats, terms):
                blocks = []
                for pair in operands:
                    if isinstance(pair, tuple):
                        blocks.append(b_refs[at_op + half])
                        at_op += 2
                    else:
                        blocks.append(b_refs[at_op])
                        at_op += 1
                parts.append(dotg(at[...], build(*blocks), 1, 0))
            full = join(*parts)
            if not geo.direct:
                if mine:
                    full = full + got_ref[0, 0].astype(F32)
                outs[0][0, 0] = full.astype(BF)
                return
            if not mine:
                for p in range(geo.P):
                    outs[0][0, s[0] ^ p] = full[p * geo.R : (p + 1) * geo.R].astype(BF)
                return
            total[...] = full
            for i, here in enumerate(geo.order[half]):
                row = pl.multiple_of((s[0] ^ here) * geo.R, geo.R)
                part = total[pl.ds(row, geo.R), :] + got_ref[0, here].astype(F32)
                outs[2 * half + i // half_n][i % half_n, 0] = part.astype(BF)

        for half in range(2):

            @pl.when((j < th) if half == 0 else (j >= th))
            def _():
                store(half)

    in_specs = [whole((n, a.shape[1])) if geo.direct else whole(a.shape) for a in lefts] + op_specs
    rel_block = (1, geo.P, geo.R, w) if geo.direct else (1, 1, pr, w)
    rel_spec = pl.BlockSpec(rel_block, lambda j, s: (j, 0, 0, 0))
    rel_shape = jax.ShapeDtypeStruct((geo.T,) + rel_block[1:], BF)
    args = [*lefts, *ops]
    out_specs, shapes = [rel_spec], [rel_shape]
    if mine:
        in_specs.append(rel_spec)
        args.append(partial)
        if geo.direct:
            block = (half_n, 1, geo.R, w)
            first = pl.BlockSpec(block, lambda j, s: (0, jnp.minimum(j, th - 1), 0, 0))
            second = pl.BlockSpec(block, lambda j, s: (0, jnp.maximum(j - th, 0), 0, 0))
            out_specs = [first, first, second, second]
            shapes = [jax.ShapeDtypeStruct((half_n, th, geo.R, w), BF)] * 4
    scratch = [pltpu.VMEM((pr, n), BF)] * na if geo.direct else []
    if mine and geo.direct:
        scratch.append(pltpu.VMEM((pr, w), F32))
    got = pl.pallas_call(
        kernel,
        grid_spec=pltpu.PrefetchScalarGridSpec(
            num_scalar_prefetch=1,
            grid=(geo.T,),
            in_specs=in_specs,
            out_specs=out_specs,
            scratch_shapes=scratch,
        ),
        out_shape=shapes,
        compiler_params=params(62 << 20),
        cost_estimate=cost(2 * pr * n * w * geo.T, 2 * geo.T * w * (2 * pr + n)),
        name=name,
    )(scal, *args)
    if not mine:
        return got[0]
    if geo.direct:
        return got
    blocks = got[0].reshape(geo.T, geo.P, geo.R, w)
    out = []
    for half in range(2):
        part = blocks[half * th : (half + 1) * th]
        part = reorder(part, [scal[0] ^ rel for rel in geo.order[half]], 1)
        part = part.transpose(1, 0, 2, 3)
        out += [part[:half_n], part[half_n:]]
    return out


def body(
    latents,
    conditioning,
    mod_weight,
    mod_bias,
    in_weight,
    query_value_bias,
    out_weight,
    branch_bias,
    up_weight,
    up_bias,
    down_weight,
    cotangent,
):
    images, row_count, width = latents.shape
    geo = Geo(lax.axis_size("fsdp"), lax.axis_size("tensor"), width)
    F, T = geo.F, geo.T
    assert 2 * images == T
    highest = lax.Precision.HIGHEST
    fi = lax.axis_index("fsdp")
    ti = lax.axis_index("tensor")
    pair, core = fi // 2, fi % 2
    scal = jnp.stack([pair, core, ti]).astype(jnp.int32)
    cols = in_weight.shape[2]
    units = up_weight.shape[1]
    geo.windows(cols)

    def places(k):
        return [
            ((2 * p + c) * T + t, (2 * p + t // images) * T + c * images + (t % images + k) % images)
            for p in range(geo.P)
            for c in range(2)
            for t in range(T)
        ]

    def to_chip(arr):
        got = []
        for k in range(images):
            item = lax.dynamic_index_in_dim(arr, (ti + k) % images, 0, keepdims=False)
            got.append(lax.ppermute(item, BOTH, places(k)))
        return got

    def from_chip(arr):
        got = []
        for k in range(images):
            back = [(dst, src) for src, dst in places(k)]
            got.append(lax.ppermute(arr[k * row_count : (k + 1) * row_count], BOTH, back))
        return got

    def home(parts):
        return reorder(jnp.stack(parts), [(i - ti) % images for i in range(images)])

    def share(arr):
        sent = jnp.broadcast_to(arr[None], (F * T,) + arr.shape)
        return lax.all_to_all(sent, BOTH, 0, 0, tiled=True)

    now, opened = (), []

    def tie(value):
        return after(value, *now)

    def start(*chains):
        for way in chains:
            opened.extend(way.advance(*now))

    def begin(shard, make, *how):
        way = Chain(make(tie(shard), geo, *how))
        opened.extend(way.flight)
        return way

    def across(value):
        got = flip_core(tie(value), geo)
        opened.append(got)
        return got

    def close(*made):
        nonlocal now
        now = (*opened, *made)
        opened.clear()

    heads = cols // HEAD_DIM
    attn_shard = jnp.concatenate([in_weight[0], in_weight[1], in_weight[2], out_weight.T], axis=1)
    attn_way = begin(attn_shard, gather_steps, False)
    cond_all = conditioning[None]
    bit = 1
    while bit < F:
        got = lax.ppermute(cond_all, "fsdp", [(i, i ^ bit) for i in range(F)])
        cond_all = jnp.concatenate([cond_all, got])
        bit *= 2
    cond_all = reorder(cond_all, [fi ^ f for f in range(F)]).reshape(F * images, width)
    silu_low = jax.nn.silu(cond_all.astype(F32)).astype(BF)
    silu_own = lax.dynamic_slice_in_dim(silu_low, fi * geo.R, geo.R, 1)
    mod_part = jnp.einsum("bd,dcj->bcj", silu_own, mod_weight, preferred_element_type=F32)
    bias_rows = jnp.concatenate([mod_bias, query_value_bias]).astype(F32)
    bias_rows = jnp.where(fi == 0, bias_rows, 0.0)
    mod_part = jnp.pad(mod_part, ((0, 0), (0, 2), (0, 0))) + bias_rows
    mod_part = mod_part.reshape(geo.P, 1, T, 8, cols)
    mod_part = jnp.broadcast_to(mod_part, (geo.P, 2, T, 8, cols)).reshape(F * T, 8, cols)
    close()
    start(attn_way)
    up_way = begin(up_weight, gather_steps, True, True)
    mod_part = lax.all_to_all(mod_part, BOTH, 0, 0, tiled=True)
    mod_part = mod_part.reshape(F, T, 8, cols).sum(axis=0)
    mod = mod_part[:, :6].transpose(1, 0, 2).reshape(6, width)
    qv_bias = mod_part[:, 6:]
    triple_bias = jnp.concatenate(
        [
            qv_bias[:, :1],
            jnp.zeros_like(qv_bias[:, :1]),
            qv_bias[:, 1:],
            jnp.zeros((T, 1, geo.n3 - 3 * cols), F32),
        ],
        axis=2,
    )
    bias_rows = branch_bias.astype(F32)
    close(mod)
    start(attn_way)
    x_parts = to_chip(tie(latents))
    opened.extend(x_parts)
    close()
    x = jnp.concatenate([*x_parts, jnp.zeros((ROWS, width), BF)])
    start(attn_way, up_way)
    h1 = norm_mod(tie(x), mod)
    close(h1)
    w_attn = Gathered(attn_way.finish(*now), geo, scal)
    start(up_way)

    q, kv, kvo = [None] * 2, [None] * 2, [None] * 2
    mixed, lse = [None] * 2, [None] * 2
    extras = []
    down_shard = jnp.concatenate(
        [down_weight.T, jnp.broadcast_to(up_bias, (16, units))]
    )
    down_way = begin(down_shard, gather_steps, True, False, extras)
    for half in range(2):
        q[half], kv[half] = in_proj(tie(scal), h1, w_attn, triple_bias, half, geo)
    close(q[0], q[1])
    kvo = [across(kv[0]), across(kv[1])]
    close()
    start(up_way, down_way)
    for half in range(2):
        mixed[half], lse[half] = attn_fwd(tie(q[half]), kv[half], kvo[half], geo)
    attn, resid, h2 = out_proj(tie(scal), mixed, x, mod, bias_rows[0:1], w_attn, geo)
    close(h2)
    start(up_way, down_way)
    close()
    w_up = Gathered(up_way.finish(*now), geo, scal)
    start(down_way)
    cot_parts = to_chip(tie(cotangent))
    opened.extend(cot_parts)
    unit_bias = jnp.stack([part[:1] for part in extras]).astype(F32)
    hidden, gp = up_proj(tie(scal), h2, unit_bias, w_up, geo)
    close(hidden)
    start(down_way)
    cot = jnp.concatenate(cot_parts)
    ffn_grad = (cot.astype(F32) * mod[5]).astype(BF)
    ffn_sum = jnp.sum(ffn_grad.astype(F32), axis=0)

    def block(ref):
        return ref[0]

    def alone(part):
        return part

    down_terms = [(ffn_grad, [hidden], block)]
    down_half = weight_grad(tie(scal), down_terms, alone, units, False, geo, "w_down_send")
    close(down_half)
    w_down = Gathered(down_way.finish(*now), geo, scal)
    down_got = across(down_half)
    block_rows, ffn_sums = down_proj(
        tie(scal), hidden, resid, cot, mod, bias_rows[1:2], w_down, geo
    )
    close(ffn_sums)

    down_parts = weight_grad(tie(scal), down_terms, alone, units, True, geo, "w_down", down_got)
    close(*down_parts)
    down_back = begin(down_parts, scatter_steps)
    block_back = from_chip(tie(block_rows))
    opened.extend(block_back)
    pre, unit_sum = pre_back(tie(scal), ffn_grad, gp, w_down, geo)
    up_terms = [(h2, [pre], block)]
    up_half = weight_grad(tie(scal), up_terms, alone, units, False, geo, "w_up_send")
    close(up_half)
    start(down_back)
    up_got = across(up_half)
    rg, ag, mid_sums = second_back(tie(scal), pre, resid, attn, cot, mod, w_up, geo)
    close(ag)
    start(down_back)
    up_parts = weight_grad(tie(scal), up_terms, alone, units, True, geo, "w_up", up_got)
    mg = mixed_back(tie(scal), ag, w_attn, geo)
    close(mg, *up_parts)
    start(down_back)
    up_back = begin(up_parts, scatter_steps)
    tri, tri_send, tri_sums, send_sums = [None] * 2, [None] * 2, [None] * 2, [None] * 2
    for half in range(2):
        tri[half], tri_send[half], tri_sums[half], send_sums[half] = attn_bwd(
            tie(q[half]), kv[half], kvo[half], mixed[half], mg, lse[half], half * geo.Th, geo
        )
    close(*tri_sums)
    tri_got = [across(tri_send[0]), across(tri_send[1])]
    tri_sum, send_sum = jnp.concatenate(tri_sums), jnp.concatenate(send_sums)
    pair_sums = jnp.concatenate(
        [
            tri_sum[:, :, :cols],
            tri_sum[:, :, 2 * cols : 3 * cols]
            + send_sum[:, :, geo.koff + cols : geo.koff + 2 * cols],
        ],
        axis=1,
    )
    close()
    start(up_back)
    down_back.finish(*now)

    def beside(first, second):
        shared = geo.n3 - geo.base
        middle = first[:, geo.base :] + second[:, :shared]
        return jnp.concatenate([first[:, : geo.base], middle, second[:, shared:]], axis=1)

    attn_terms = [
        (h1, [tuple(tri), tuple(tri_got)], lambda a, b: triple_grad(a, b, geo)),
        (ag, [tuple(mixed)], block),
    ]
    attn_half = weight_grad(tie(scal), attn_terms, beside, 4 * cols, False, geo, "w_attn_send")
    close(attn_half)
    start(up_back)
    attn_got = across(attn_half)
    latent_rows, first_sums = first_back(tie(scal), tri, tri_got, x, rg, mod, w_attn, geo)
    close(first_sums)
    start(up_back)
    mine = [i ^ ti for i in range(T)]
    rows = jnp.concatenate(
        [first_sums.sum(axis=1), mid_sums[:3].sum(axis=1), ffn_sums.sum(axis=0, keepdims=True)]
    )
    rows = tie(rows).reshape(6, T, cols).transpose(1, 0, 2).reshape(T, 6 * cols)
    branch_sums = jnp.stack([mid_sums[3].sum(axis=0), ffn_sum]).reshape(F, T, -1)
    unit_sums = reorder(unit_sum, mine).reshape(T, F, units // F).transpose(1, 0, 2)
    pair_sums = reorder(pair_sums, mine).reshape(T, F, 2 * cols // F).transpose(1, 0, 2)
    rows = jnp.broadcast_to(rows[None], (F,) + rows.shape)
    pack = jnp.concatenate([rows, branch_sums, unit_sums, pair_sums], axis=2)
    count = pack.shape[2]
    pack = jnp.pad(pack, ((0, 0), (0, 0), (0, -count % 1024))).reshape(F * T, -1, 128)
    pack = lax.all_to_all(pack, BOTH, 0, 0, tiled=True)
    attn_parts = weight_grad(
        tie(scal), attn_terms, beside, 4 * cols, True, geo, "w_attn", attn_got
    )
    close(pack, *attn_parts)
    attn_back = begin(attn_parts, scatter_steps, False)
    latent_back = from_chip(tie(latent_rows))
    opened.extend(latent_back)
    pack = tie(pack)
    slices = pack.sum(axis=0).reshape(-1)[6 * cols : count]
    tiles = -(-6 * cols // 128)
    mine_rows = pack[:, :tiles].reshape(geo.P, 2, T, tiles, 128).sum(axis=1)
    mine_rows = mine_rows.reshape(F * images, -1)[:, : 6 * cols].reshape(F * images, 6, cols)
    cond_part = jnp.einsum("bcj,dcj->bd", mine_rows, mod_weight.astype(F32), precision=highest)
    cond_part = cond_part.reshape(F, 1, images * geo.R)
    cond_part = jnp.broadcast_to(cond_part, (F, T, images * geo.R))
    kept = jnp.broadcast_to(slices[None, None], (F, T) + slices.shape)
    final = jnp.concatenate([cond_part, kept], axis=2).reshape(F * T, -1)
    final = jnp.pad(final, ((0, 0), (0, -final.shape[1] % 1024))).reshape(F * T, -1, 128)
    final = lax.all_to_all(final, BOTH, 0, 0, tiled=True)
    close(final)
    start(attn_back)
    close()
    start(attn_back)
    block_out, latent_grad = home(block_back), home(latent_back)
    down_grad, up_grad = down_back.finish(*now), up_back.finish(*now)
    attn_grad = attn_back.finish(*now)
    in_grad = attn_grad[:, : 3 * cols].reshape(geo.R, 3, cols).transpose(1, 0, 2)

    final = final.reshape(F, T, -1)
    at = images * geo.R
    cond_mine = final[:, :, :at].sum(axis=1).reshape(F, images, geo.R)
    step = 2 * width // (F * T)
    branch_grad = final[:, :, at : at + step].reshape(2, width)
    own = lax.dynamic_index_in_dim(final, ti, 1, keepdims=False)
    at += step
    unit_grad = own[:, at : at + units // F].reshape(units)
    at += units // F
    pair_grad = own[:, at : at + 2 * cols // F].reshape(2, cols)
    mod_weight_grad = jnp.einsum("bd,bcj->dcj", silu_own.astype(F32), mine_rows, precision=highest)
    mod_bias_grad = mine_rows.sum(axis=0)
    silu_grad = cond_mine.transpose(1, 0, 2).reshape(images, width)
    cond_f = conditioning.astype(F32)
    sig = jax.nn.sigmoid(cond_f)
    cond_grad = silu_grad * (sig * (1.0 + cond_f * (1.0 - sig)))

    return (
        block_out,
        latent_grad,
        cond_grad,
        mod_weight_grad,
        mod_bias_grad,
        in_grad,
        pair_grad,
        attn_grad[:, 3 * cols :].T,
        branch_grad,
        up_grad,
        unit_grad,
        down_grad.T,
    )


def solution(mesh):
    in_specs = (
        P("fsdp", "tensor", None),
        P("fsdp", None),
        P("fsdp", None, "tensor"),
        P(None, "tensor"),
        P(None, "fsdp", "tensor"),
        P(None, "tensor"),
        P("tensor", "fsdp"),
        P(),
        P("fsdp", "tensor"),
        P("tensor"),
        P("tensor", "fsdp"),
        P("fsdp", "tensor", None),
    )
    out_specs = (
        P("fsdp", "tensor", None),
        P("fsdp", "tensor", None),
        P("fsdp", None),
        P("fsdp", None, "tensor"),
        P(None, "tensor"),
        P(None, "fsdp", "tensor"),
        P(None, "tensor"),
        P("tensor", "fsdp"),
        P(),
        P("fsdp", "tensor"),
        P("tensor"),
        P("tensor", "fsdp"),
    )
    return jax.shard_map(body, mesh=mesh, in_specs=in_specs, out_specs=out_specs, check_vma=False)
```

```python
import functools

import jax
import jax.numpy as jnp
from jax import lax
from jax.experimental import pallas as pl
from jax.experimental.pallas import tpu as pltpu
from jax.sharding import PartitionSpec as P

HEAD_DIM = 72
EPS = 1e-06
TANH_C = 0.7978845608028654
CUBIC = 0.044715
LOG2E = 1.4426950408889634
VMEM_BYTES = 56 << 20
ROWS = 32
BF = jnp.bfloat16
F32 = jnp.float32
BOTH = ("fsdp", "tensor")


def dotg(a, b, ca, cb):
    return lax.dot_general(a, b, (((ca,), (cb,)), ((), ())), preferred_element_type=F32)


class Geo:
    def __init__(self, fsdp, tensor, dim):
        self.F, self.T, self.P = fsdp, tensor, fsdp // 2
        self.Th = tensor // 2
        self.D = dim
        self.R = dim // fsdp
        self.bits = [1 << b for b in range((self.P - 1).bit_length())]
        self.order = (self.orders(self.bits[::-1]), self.orders(self.bits))
        self.direct = self.R % 16 == 0

    def windows(self, w):
        self.w = w
        self.n3 = min(padded(3 * w), 4 * w)
        self.kbase = w // 128 * 128
        self.koff = w - self.kbase
        self.kvw = self.n3 - self.kbase
        self.base = 3 * w // 128 * 128
        self.off = 3 * w - self.base
        self.win = 4 * w - self.base

    @staticmethod
    def orders(msb_first):
        vals = [0]
        for bit in reversed(msb_first):
            vals = vals + [v | bit for v in vals]
        return vals


def reorder(x, index, axis=0):
    return jnp.stack([lax.dynamic_index_in_dim(x, i, axis, keepdims=False) for i in index], axis)


def flip_pair(x, bit, geo):
    return lax.ppermute(x, "fsdp", [(i, i ^ (2 * bit)) for i in range(geo.F)])


def flip_core(x, geo):
    return lax.ppermute(x, "fsdp", [(i, i ^ 1) for i in range(geo.F)])


def flip_tensor(x, k, geo):
    return lax.ppermute(x, "tensor", [(i, i ^ k) for i in range(geo.T)])


def after(value, *done):
    return lax.optimization_barrier((value, done))[0] if done else value


class Chain:
    def __init__(self, steps):
        self.steps = steps
        self.flight = next(steps)
        self.result = None

    def advance(self, *done):
        if self.result is not None:
            return []
        try:
            self.flight = self.steps.send(after(self.flight, *done))
        except StopIteration as end:
            self.flight, self.result = [], end.value
        return self.flight

    def finish(self, *done):
        while self.result is None:
            self.advance(*done)
        return self.result


def gather_steps(shard, geo, parted=True, joined=False, extras=None):
    if parted:
        late = [geo.Th] if extras is None else list(range(1, geo.Th + 1))
        most = [k for k in range(1, geo.T) if k not in late]
        got = dict(zip(most, (yield [flip_tensor(shard, k, geo) for k in most])))
        got.update(zip(late, (yield [flip_tensor(shard, k, geo) for k in late])))
        parts = [shard] + [got[k] for k in range(1, geo.T)]
    else:
        got = yield [flip_tensor(shard, k, geo) for k in range(1, geo.T)]
        parts = [shard] + got
    if extras is not None:
        extras += [part[geo.R :] for part in parts]
        parts = [part[: geo.R] for part in parts]
    bufs = [jnp.stack(parts[h * geo.Th : (h + 1) * geo.Th])[None] for h in range(2)]
    for at in range(len(geo.bits)):
        bits = (geo.bits[at], geo.bits[-1 - at])
        got = yield [flip_pair(bufs[h], bits[h], geo) for h in range(2)]
        if joined or at < len(geo.bits) - 1:
            bufs = [jnp.concatenate(pair) for pair in zip(bufs, got)]
    owns = [[buf] for buf in bufs] if joined else [list(pair) for pair in zip(bufs, got)]
    count = len(owns[0])
    others = yield [flip_core(a, geo) for own in owns for a in own]
    return [owns[h] + others[h * count : (h + 1) * count] for h in range(2)]


class Gathered:
    def __init__(self, halves, geo, scal):
        self.geo = geo
        if not geo.direct:
            fixed = []
            for half, arrays in enumerate(halves):
                at = [geo.order[half].index(rel) for rel in range(geo.P)]
                lookup = jnp.array(at, jnp.int32)
                blocks = jnp.concatenate(arrays)
                blocks = reorder(
                    blocks,
                    [
                        lookup[(f // 2) ^ scal[0]] + geo.P * ((f % 2) ^ scal[1])
                        for f in range(geo.F)
                    ],
                )
                _, th, r, w = blocks.shape
                fixed.append([blocks.transpose(1, 0, 2, 3).reshape(1, th, geo.D, w)])
            halves = fixed
        self.halves = halves
        self.arrays = halves[0] + halves[1]
        self.n = len(halves[0])
        self.width = self.arrays[0].shape[-1]

    def operands(self, half=None):
        return self.arrays if half is None else self.halves[half]

    def specs(self, half=None):
        return [pl.BlockSpec(memory_space=pl.ANY)] * len(self.operands(half))

    def scratch(self, lo=0, hi=None):
        hi = self.width if hi is None else hi
        if lo % 128 or hi % 128:
            lo, hi = 0, self.width
        self.lo, self.hi = lo, hi
        count = self.n * self.arrays[0].shape[0]
        return [
            pltpu.VMEM((2, self.geo.D, hi - lo), BF),
            pltpu.SemaphoreType.DMA((2, count)),
        ]

    def copies(self, group, slot, half, s_ref, refs, buf, sem):
        geo, out = self.geo, []
        for at, ref in enumerate(refs):
            n, _, rows, _ = ref.shape
            for i in range(n):
                row = 0
                if geo.direct:
                    place = at * n + i
                    rel = geo.order[half][place % geo.P]
                    row = 2 * (s_ref[0] ^ rel) + (s_ref[1] ^ (place // geo.P))
                    row = pl.multiple_of(row * rows, rows)
                out.append(
                    pltpu.make_async_copy(
                        ref.at[i, group, :, pl.ds(self.lo, self.hi - self.lo)],
                        buf.at[slot, pl.ds(row, rows), :],
                        sem.at[slot, at * n + i],
                    )
                )
        return out

    def stream(self, j, s_ref, refs, buf, sem, half=None):
        th = self.geo.Th

        def each(step, act):
            if half is not None:
                for copy in self.copies(step, step % 2, half, s_ref, refs, buf, sem):
                    act(copy)
                return
            for part in range(2):

                @pl.when((step < th) if part == 0 else (step >= th))
                def _():
                    mine = refs[part * self.n : (part + 1) * self.n]
                    for copy in self.copies(
                        step - part * th, step % 2, part, s_ref, mine, buf, sem
                    ):
                        act(copy)

        @pl.when(j == 0)
        def _():
            each(j, lambda copy: copy.start(priority=1))

        @pl.when(j + 1 < (self.geo.T if half is None else th))
        def _():
            each(j + 1, lambda copy: copy.start(priority=1))

        each(j, lambda copy: copy.wait())
        return buf.at[j % 2]


def scatter_steps(pieces, geo, parted=True):
    def add(a, b):
        return a.astype(F32) + b.astype(F32)

    keeps, sends = [pieces[0], pieces[2]], [pieces[1], pieces[3]]
    for at in range(len(geo.bits)):
        bits = (geo.bits[-1 - at], geo.bits[at])
        got = yield [flip_pair(sends[h], bits[h], geo) for h in range(2)]
        m = max(1, keeps[0].shape[0] // 2)
        if at < len(geo.bits) - 1:
            sends = [add(keeps[h][m:], got[h][m:]).astype(BF) for h in range(2)]
        keeps = [add(keeps[h][:m], got[h][:m]).astype(BF) for h in range(2)]
    units = [keep[0, k] for keep in keeps for k in range(geo.Th)]
    if parted:
        rest = [k for k in range(1, geo.T) if k != geo.Th]
        got = yield [flip_tensor(units[k], k, geo) for k in rest]
        got += yield [flip_tensor(units[geo.Th], geo.Th, geo)]
    else:
        got = yield [flip_tensor(units[k], k, geo) for k in range(1, geo.T)]
    total = units[0].astype(F32)
    for part in got:
        total = total + part.astype(F32)
    return total


def params(size=VMEM_BYTES):
    return pltpu.CompilerParams(vmem_limit_bytes=size)


def cost(flops, size):
    return pl.CostEstimate(flops=int(flops), bytes_accessed=int(size), transcendentals=0)


def whole(shape):
    zeros = (0,) * len(shape)
    return pl.BlockSpec(shape, lambda j, s: zeros)


def padded(w):
    return -(-w // 128) * 128


def chunked(total, want):
    return want if total % want == 0 else total


def norm_of(v):
    centre = v - jnp.mean(v, axis=-1, keepdims=True)
    inv = lax.rsqrt(jnp.mean(centre * centre, axis=-1, keepdims=True) + EPS)
    return centre * inv, inv


def norm_back(norm, inv, g):
    return (
        g
        - jnp.mean(g, axis=-1, keepdims=True)
        - norm * jnp.mean(g * norm, axis=-1, keepdims=True)
    ) * inv


def fold_rows(v):
    return v.reshape(v.shape[0] // 8, 8, v.shape[1]).sum(axis=0)


class Late:
    def __init__(self, *arrays):
        self.arrays = arrays
        self.specs = [pl.BlockSpec(memory_space=pl.ANY)] * len(arrays)
        self.scratch = [pltpu.VMEM(a.shape, a.dtype) for a in arrays]
        self.scratch.append(pltpu.SemaphoreType.DMA((len(arrays),)))

    def copies(self, refs, scratch):
        sem = scratch[-1]
        return [
            pltpu.make_async_copy(ref, scratch[i], sem.at[i]) for i, ref in enumerate(refs)
        ]

    def start(self, j, refs, scratch):
        @pl.when(j == 0)
        def _():
            for copy in self.copies(refs, scratch):
                copy.start(priority=1)

    def wait(self, refs, scratch):
        for copy in self.copies(refs, scratch):
            copy.wait()
        return scratch[:-1]


def two_halves(block, th, tail):
    return [
        pl.BlockSpec(block, lambda j, s: (jnp.minimum(j, th - 1),) + tail),
        pl.BlockSpec(block, lambda j, s: (jnp.maximum(j - th, 0),) + tail),
    ]


def norm_mod(x, mod):
    n, d = x.shape[0] - ROWS, x.shape[1]

    def kernel(x_ref, m_ref, h_ref):
        @pl.loop(0, n // ROWS, unroll=4)
        def _(i):
            at = pl.ds(pl.multiple_of(i * ROWS, ROWS), ROWS)
            norm, _ = norm_of(x_ref[at, :].astype(F32))
            h_ref[at, :] = (norm * (1.0 + m_ref[1:2, :]) + m_ref[0:1, :]).astype(BF)

    return pl.pallas_call(
        kernel,
        out_shape=jax.ShapeDtypeStruct((n, d), BF),
        compiler_params=params(),
        cost_estimate=cost(20 * n * d, 4 * n * d),
        name="norm_mod",
    )(x, mod)


def in_proj(scal, h, wt, bias, half, geo):
    n, d = h.shape
    n3, wp = geo.n3, padded(geo.w)
    nw = wt.n

    def kernel(s, h_ref, b_ref, *refs):
        w_refs, (q_ref, kv_ref, wbuf, sem) = refs[:nw], refs[nw:]
        now = wt.stream(pl.program_id(0), s, w_refs, wbuf, sem, half)
        y = dotg(h_ref[...], now[:, :n3], 1, 0) + b_ref[0]
        y = y.astype(BF)
        q_ref[0] = y[:, :wp]
        kv_ref[0] = y[:, geo.kbase :]

    first = half * geo.Th
    return pl.pallas_call(
        kernel,
        grid_spec=pltpu.PrefetchScalarGridSpec(
            num_scalar_prefetch=1,
            grid=(geo.Th,),
            in_specs=[
                whole((n, d)),
                pl.BlockSpec((1, 1, n3), lambda j, s: (s[2] ^ (j + first), 0, 0)),
                *wt.specs(half),
            ],
            out_specs=[
                pl.BlockSpec((1, n, wp), lambda j, s: (j, 0, 0)),
                pl.BlockSpec((1, n, geo.kvw), lambda j, s: (j, 0, 0)),
            ],
            scratch_shapes=wt.scratch(0, n3),
        ),
        out_shape=[
            jax.ShapeDtypeStruct((geo.Th, n, wp), BF),
            jax.ShapeDtypeStruct((geo.Th, n, geo.kvw), BF),
        ],
        compiler_params=params(),
        cost_estimate=cost(2 * n * d * n3 * geo.Th, 8 * d * geo.w * geo.Th + 8 * n * d),
        name="in_proj",
    )(scal, h, bias, *wt.operands(half))


def head_lanes(geo, h):
    at = h * HEAD_DIM
    return [
        slice(start + at, start + at + HEAD_DIM)
        for start in (0, geo.koff, geo.koff + geo.w, geo.off)
    ]


def attn_fwd(q, kv, kvo, geo):
    z, n, wp = q.shape
    heads = geo.w // HEAD_DIM
    c = HEAD_DIM**-0.5 * LOG2E

    def kernel(q_ref, kv_ref, kvo_ref, o_ref, lse_ref):
        outs = [jnp.zeros((geo.off, n), F32)] if geo.off else []
        for h in range(heads):
            lq, lk, lv, _ = head_lanes(geo, h)
            qh = q_ref[0, :, lq]
            sa = dotg(kv_ref[0, :, lk], qh, 1, 1) * c
            sb = dotg(kvo_ref[0, :, lk], qh, 1, 1) * c
            top = jnp.maximum(
                jnp.max(sa, axis=0, keepdims=True), jnp.max(sb, axis=0, keepdims=True)
            )
            pa, pb = jnp.exp2(sa - top), jnp.exp2(sb - top)
            total = jnp.sum(pa, axis=0, keepdims=True) + jnp.sum(pb, axis=0, keepdims=True)
            o = dotg(kv_ref[0, :, lv], pa.astype(BF), 0, 0)
            o = o + dotg(kvo_ref[0, :, lv], pb.astype(BF), 0, 0)
            outs.append(o / total)
            lse_ref[0, h : h + 1, :] = top + jnp.log2(total)
        o_ref[0] = jnp.concatenate(outs, axis=0).T.astype(BF)

    def spec(width):
        return pl.BlockSpec((1, n, width), lambda j: (j, 0, 0))

    return pl.pallas_call(
        kernel,
        grid=(z,),
        in_specs=[spec(wp), spec(geo.kvw), spec(geo.kvw)],
        out_specs=[spec(geo.win), pl.BlockSpec((1, heads, n), lambda j: (j, 0, 0))],
        out_shape=[
            jax.ShapeDtypeStruct((z, n, geo.win), BF),
            jax.ShapeDtypeStruct((z, heads, n), F32),
        ],
        compiler_params=params(),
        cost_estimate=cost(3e9 * z, 10 * z * n * wp),
        name="attn_fwd",
    )(q, kv, kvo)


def attn_bwd(q, kv, kvo, o, do, lse, first, geo):
    z, n, wp = q.shape
    heads = lse.shape[1]
    scale = HEAD_DIM**-0.5
    c = scale * LOG2E

    def kernel(q_ref, kv_ref, kvo_ref, o_ref, do_ref, lse_ref, tri_ref, send_ref, ts_ref, ss_ref):
        both = (do_ref[0].astype(F32) * o_ref[0].astype(F32)).T
        dqs, parts = [], [[[], []], [[], []]]
        for h in range(heads):
            lq, lk, lv, lm = head_lanes(geo, h)
            qh, doh = q_ref[0, :, lq], do_ref[0, :, lm]
            delta = jnp.sum(both[lm], axis=0, keepdims=True)
            lse_h = lse_ref[0, h : h + 1, :]
            dq = None
            for i, ref in enumerate((kv_ref, kvo_ref)):
                k, v = ref[0, :, lk], ref[0, :, lv]
                p = jnp.exp2(dotg(k, qh, 1, 1) * c - lse_h)
                ds = (p * (dotg(v, doh, 1, 1) - delta)).astype(BF)
                parts[i][1].append(dotg(doh, p.astype(BF), 0, 1))
                parts[i][0].append(dotg(qh, ds, 0, 1) * scale)
                got = dotg(k, ds, 0, 0)
                dq = got if dq is None else dq + got
            dqs.append(dq * scale)

        def rows(count):
            return [jnp.zeros((count, n), F32)] if count else []

        pad = rows(geo.n3 - 3 * geo.w)
        own = jnp.concatenate(dqs + parts[0][0] + parts[0][1] + pad, axis=0).T
        other = jnp.concatenate(rows(geo.koff) + parts[1][0] + parts[1][1] + pad, axis=0).T
        tri_ref[0] = own.astype(BF)
        send_ref[0] = other.astype(BF)
        ts_ref[0] = jnp.sum(own, axis=0, keepdims=True)
        ss_ref[0] = jnp.sum(other, axis=0, keepdims=True)

    def spec(width, at=0, count=n):
        return pl.BlockSpec((1, count, width), lambda j: (j + at, 0, 0))

    return pl.pallas_call(
        kernel,
        grid=(z,),
        in_specs=[
            spec(wp),
            spec(geo.kvw),
            spec(geo.kvw),
            spec(geo.win),
            spec(geo.win, first),
            spec(n, 0, heads),
        ],
        out_specs=[spec(geo.n3), spec(geo.kvw), spec(geo.n3, 0, 1), spec(geo.kvw, 0, 1)],
        out_shape=[
            jax.ShapeDtypeStruct((z, n, geo.n3), BF),
            jax.ShapeDtypeStruct((z, n, geo.kvw), BF),
            jax.ShapeDtypeStruct((z, 1, geo.n3), F32),
            jax.ShapeDtypeStruct((z, 1, geo.kvw), F32),
        ],
        compiler_params=params(),
        cost_estimate=cost(5e9 * z, 16 * z * n * wp),
        name="attn_bwd",
    )(q, kv, kvo, o, do, lse)


def triple_grad(tri_ref, got_ref, geo):
    late = tri_ref[0, :, geo.kbase :].astype(F32) + got_ref[0].astype(F32)
    if not geo.kbase:
        return late.astype(BF)
    return jnp.concatenate([tri_ref[0, :, : geo.kbase], late.astype(BF)], axis=1)


def out_proj(scal, mixed, x, mod, bias, wt, geo):
    _, n, win = mixed[0].shape
    d = geo.D
    nw = len(wt.arrays)
    th = geo.Th

    late = Late(x)

    def kernel(s, ya_ref, yb_ref, m_ref, b_ref, *refs):
        late_in, refs = refs[:1], refs[1:]
        w_refs, (attn_out, resid_ref, h_ref, wbuf, sem, attn_ref, *late_buf) = refs[:nw], refs[nw:]
        j = pl.program_id(0)
        late.start(j, late_in, late_buf)
        now = wt.stream(j, s, w_refs, wbuf, sem)
        y = jnp.where(j < th, ya_ref[0], yb_ref[0])
        part = dotg(y, now[:, -win:], 1, 1)

        @pl.when(j == 0)
        def _():
            attn_ref[...] = part

        @pl.when(j > 0)
        def _():
            attn_ref[...] += part

        @pl.when(j == geo.T - 1)
        def _():
            (x_ref,) = late.wait(late_in, late_buf)

            @pl.loop(0, n // ROWS, unroll=4)
            def _(i):
                at = pl.ds(pl.multiple_of(i * ROWS, ROWS), ROWS)
                attn = attn_ref[at, :] + b_ref[...]
                attn_out[at, :] = attn.astype(BF)
                resid = x_ref[at, :].astype(F32) + m_ref[2:3, :] * attn
                resid_ref[at, :] = resid
                norm, _ = norm_of(resid)
                h_ref[at, :] = (norm * (1.0 + m_ref[4:5, :]) + m_ref[3:4, :]).astype(BF)

    return pl.pallas_call(
        kernel,
        grid_spec=pltpu.PrefetchScalarGridSpec(
            num_scalar_prefetch=1,
            grid=(geo.T,),
            in_specs=[
                *two_halves((1, n, win), th, (0, 0)),
                whole(mod.shape),
                whole((1, d)),
                *late.specs,
                *wt.specs(),
            ],
            out_specs=[whole((n, d))] * 3,
            scratch_shapes=[
                *wt.scratch(geo.base, 4 * geo.w),
                pltpu.VMEM((n, d), F32),
                *late.scratch,
            ],
        ),
        out_shape=[
            jax.ShapeDtypeStruct((n + ROWS, d), BF),
            jax.ShapeDtypeStruct((n, d), F32),
            jax.ShapeDtypeStruct((n + ROWS, d), BF),
        ],
        compiler_params=params(),
        cost_estimate=cost(2 * n * d * d, 8 * d * d + 14 * n * d),
        name="out_proj",
    )(scal, *mixed, mod, bias, *late.arrays, *wt.arrays)


def up_proj(scal, h, bias, wt, geo):
    n, d = h.shape[0] - ROWS, h.shape[1]
    w = wt.width
    nw = len(wt.arrays)
    step = chunked(w, 384)

    def kernel(s, h_ref, b_ref, *refs):
        w_refs, (hid_ref, gp_ref, wbuf, sem) = refs[:nw], refs[nw:]
        j = pl.program_id(0)
        now = wt.stream(j, s, w_refs, wbuf, sem)
        for at in range(0, w, step):
            cols = slice(at, at + step)
            u = dotg(h_ref[...], now[:, cols], 1, 0) + b_ref[0, :, cols]
            sq = u * u
            t = jnp.tanh(TANH_C * (u + CUBIC * sq * u))
            half = 0.5 * (1.0 + t)
            hid_ref[0, :, cols] = (u * half).astype(BF)
            slope = TANH_C * (1.0 + 3.0 * CUBIC * sq)
            gp_ref[0, :, cols] = (half + 0.5 * u * (1.0 - t * t) * slope).astype(BF)

    out = pl.BlockSpec((1, n, w), lambda j, s: (j, 0, 0))
    return pl.pallas_call(
        kernel,
        grid_spec=pltpu.PrefetchScalarGridSpec(
            num_scalar_prefetch=1,
            grid=(geo.T,),
            in_specs=[
                whole((n, d)),
                pl.BlockSpec((1, 1, w), lambda j, s: (j, 0, 0)),
                *wt.specs(),
            ],
            out_specs=[out, out],
            scratch_shapes=wt.scratch(),
        ),
        out_shape=[jax.ShapeDtypeStruct((geo.T, n, w), BF)] * 2,
        compiler_params=params(),
        cost_estimate=cost(2 * n * d * w * geo.T, 2 * geo.T * w * (d + 2 * n)),
        name="up_proj",
    )(scal, h, bias, *wt.arrays)


def down_proj(scal, hidden, resid, cot, mod, bias, wt, geo):
    _, n, w = hidden.shape
    d = geo.D
    nw = len(wt.arrays)

    late = Late(resid, cot)

    def kernel(s, y_ref, m_ref, b_ref, *refs):
        late_in, refs = refs[:2], refs[2:]
        w_refs, (out_ref, sum_ref, wbuf, sem, acc, *late_buf) = refs[:nw], refs[nw:]
        j = pl.program_id(0)
        late.start(j, late_in, late_buf)
        now = wt.stream(j, s, w_refs, wbuf, sem)
        part = dotg(y_ref[0], now[...], 1, 1)

        @pl.when(j == 0)
        def _():
            acc[...] = part
            sum_ref[...] = jnp.zeros_like(sum_ref)

        @pl.when(j > 0)
        def _():
            acc[...] += part

        @pl.when(j == geo.T - 1)
        def _():
            r_ref, c_ref = late.wait(late_in, late_buf)

            @pl.loop(0, n // ROWS, unroll=4)
            def _(i):
                at = pl.ds(pl.multiple_of(i * ROWS, ROWS), ROWS)
                ffn = acc[at, :] + b_ref[...]
                out_ref[at, :] = (r_ref[at, :] + m_ref[5:6, :] * ffn).astype(BF)
                sum_ref[...] += fold_rows(c_ref[at, :].astype(F32) * ffn)

    return pl.pallas_call(
        kernel,
        grid_spec=pltpu.PrefetchScalarGridSpec(
            num_scalar_prefetch=1,
            grid=(geo.T,),
            in_specs=[
                pl.BlockSpec((1, n, w), lambda j, s: (j, 0, 0)),
                whole(mod.shape),
                whole((1, d)),
                *late.specs,
                *wt.specs(),
            ],
            out_specs=[whole((n, d)), whole((8, d))],
            scratch_shapes=[*wt.scratch(), pltpu.VMEM((n, d), F32), *late.scratch],
        ),
        out_shape=[jax.ShapeDtypeStruct((n, d), BF), jax.ShapeDtypeStruct((8, d), F32)],
        compiler_params=params(),
        cost_estimate=cost(2 * n * d * w * geo.T, 2 * geo.T * w * (d + n) + 8 * n * d),
        name="down_proj",
    )(scal, hidden, mod, bias, *late.arrays, *wt.arrays)


def pre_back(scal, g, gp, wt, geo):
    n, d = g.shape
    w = wt.width
    nw = len(wt.arrays)
    step = chunked(w, 384)

    def kernel(s, g_ref, gp_ref, *refs):
        w_refs, (out_ref, sum_ref, wbuf, sem) = refs[:nw], refs[nw:]
        j = pl.program_id(0)
        now = wt.stream(j, s, w_refs, wbuf, sem)
        for at in range(0, w, step):
            cols = slice(at, at + step)
            y = dotg(g_ref[...], now[:, cols], 1, 0) * gp_ref[0, :, cols].astype(F32)
            out_ref[0, :, cols] = y.astype(BF)
            sum_ref[0, :, cols] = jnp.sum(y, axis=0, keepdims=True)

    out = pl.BlockSpec((1, n, w), lambda j, s: (j, 0, 0))
    return pl.pallas_call(
        kernel,
        grid_spec=pltpu.PrefetchScalarGridSpec(
            num_scalar_prefetch=1,
            grid=(geo.T,),
            in_specs=[whole((n, d)), out, *wt.specs()],
            out_specs=[out, pl.BlockSpec((1, 1, w), lambda j, s: (j, 0, 0))],
            scratch_shapes=wt.scratch(),
        ),
        out_shape=[
            jax.ShapeDtypeStruct((geo.T, n, w), BF),
            jax.ShapeDtypeStruct((geo.T, 1, w), F32),
        ],
        compiler_params=params(),
        cost_estimate=cost(2 * n * d * w * geo.T, 2 * geo.T * w * (d + 2 * n)),
        name="pre_back",
    )(scal, g, gp, *wt.arrays)


def second_back(scal, pre, resid, attn, cot, mod, wt, geo):
    _, n, w = pre.shape
    d = geo.D
    nw = len(wt.arrays)

    late = Late(resid, attn, cot)

    def kernel(s, y_ref, m_ref, *refs):
        late_in, refs = refs[:3], refs[3:]
        w_refs, (rg_ref, ag_ref, sum_ref, wbuf, sem, acc, *late_buf) = refs[:nw], refs[nw:]
        j = pl.program_id(0)
        late.start(j, late_in, late_buf)
        now = wt.stream(j, s, w_refs, wbuf, sem)
        part = dotg(y_ref[0], now[...], 1, 1)

        @pl.when(j == 0)
        def _():
            acc[...] = part
            sum_ref[...] = jnp.zeros_like(sum_ref)

        @pl.when(j > 0)
        def _():
            acc[...] += part

        @pl.when(j == geo.T - 1)
        def _():
            r_ref, a_ref, c_ref = late.wait(late_in, late_buf)

            @pl.loop(0, n // ROWS, unroll=4)
            def _(i):
                at = pl.ds(pl.multiple_of(i * ROWS, ROWS), ROWS)
                g = acc[at, :]
                norm, inv = norm_of(r_ref[at, :])
                rg = c_ref[at, :].astype(F32) + norm_back(norm, inv, g * (1.0 + m_ref[4:5, :]))
                rg_ref[at, :] = rg
                ag = rg * m_ref[2:3, :]
                ag_ref[at, :] = ag.astype(BF)
                sum_ref[0] += fold_rows(rg * a_ref[at, :].astype(F32))
                sum_ref[1] += fold_rows(g)
                sum_ref[2] += fold_rows(g * norm)
                sum_ref[3] += fold_rows(ag)

    return pl.pallas_call(
        kernel,
        grid_spec=pltpu.PrefetchScalarGridSpec(
            num_scalar_prefetch=1,
            grid=(geo.T,),
            in_specs=[
                pl.BlockSpec((1, n, w), lambda j, s: (j, 0, 0)),
                whole(mod.shape),
                *late.specs,
                *wt.specs(),
            ],
            out_specs=[whole((n, d)), whole((n, d)), whole((4, 8, d))],
            scratch_shapes=[*wt.scratch(), pltpu.VMEM((n, d), F32), *late.scratch],
        ),
        out_shape=[
            jax.ShapeDtypeStruct((n, d), F32),
            jax.ShapeDtypeStruct((n, d), BF),
            jax.ShapeDtypeStruct((4, 8, d), F32),
        ],
        compiler_params=params(),
        cost_estimate=cost(2 * n * d * w * geo.T, 2 * geo.T * w * (d + n) + 18 * n * d),
        name="second_back",
    )(scal, pre, mod, *late.arrays, *wt.arrays)


def mixed_back(scal, g, wt, geo):
    n, d = g.shape
    win = geo.win
    nw = len(wt.arrays)

    def kernel(s, g_ref, *refs):
        w_refs, (out_ref, wbuf, sem) = refs[:nw], refs[nw:]
        now = wt.stream(pl.program_id(0), s, w_refs, wbuf, sem)
        out_ref[0] = dotg(g_ref[...], now[:, -win:], 1, 0).astype(BF)

    return pl.pallas_call(
        kernel,
        grid_spec=pltpu.PrefetchScalarGridSpec(
            num_scalar_prefetch=1,
            grid=(geo.T,),
            in_specs=[whole((n, d)), *wt.specs()],
            out_specs=pl.BlockSpec((1, n, win), lambda j, s: (j, 0, 0)),
            scratch_shapes=wt.scratch(geo.base, 4 * geo.w),
        ),
        out_shape=jax.ShapeDtypeStruct((geo.T, n, win), BF),
        compiler_params=params(),
        cost_estimate=cost(2 * n * d * d, 8 * d * d + 4 * n * d),
        name="mixed_back",
    )(scal, g, *wt.arrays)


def first_back(scal, tri, got, x, rg, mod, wt, geo):
    _, n, n3 = tri[0].shape
    d = geo.D
    nw = len(wt.arrays)
    th = geo.Th

    late = Late(x, rg)

    def kernel(s, ta, tb, ga, gb, m_ref, *refs):
        late_in, refs = refs[:2], refs[2:]
        w_refs, (out_ref, sum_ref, wbuf, sem, lhs, acc, *late_buf) = refs[:nw], refs[nw:]
        j = pl.program_id(0)
        late.start(j, late_in, late_buf)
        now = wt.stream(j, s, w_refs, wbuf, sem)
        for half, (tri_ref, got_ref) in enumerate(((ta, ga), (tb, gb))):

            @pl.when((j < th) if half == 0 else (j >= th))
            def _():
                lhs[...] = triple_grad(tri_ref, got_ref, geo)

        part = dotg(lhs[...], now[:, :n3], 1, 1)

        @pl.when(j == 0)
        def _():
            acc[...] = part
            sum_ref[...] = jnp.zeros_like(sum_ref)

        @pl.when(j > 0)
        def _():
            acc[...] += part

        @pl.when(j == geo.T - 1)
        def _():
            x_ref, r_ref = late.wait(late_in, late_buf)

            @pl.loop(0, n // ROWS, unroll=4)
            def _(i):
                at = pl.ds(pl.multiple_of(i * ROWS, ROWS), ROWS)
                g = acc[at, :]
                norm, inv = norm_of(x_ref[at, :].astype(F32))
                back = norm_back(norm, inv, g * (1.0 + m_ref[1:2, :]))
                out_ref[at, :] = (r_ref[at, :] + back).astype(BF)
                sum_ref[0] += fold_rows(g)
                sum_ref[1] += fold_rows(g * norm)

    return pl.pallas_call(
        kernel,
        grid_spec=pltpu.PrefetchScalarGridSpec(
            num_scalar_prefetch=1,
            grid=(geo.T,),
            in_specs=[
                *two_halves((1, n, n3), th, (0, 0)),
                *two_halves((1, n, geo.kvw), th, (0, 0)),
                whole(mod.shape),
                *late.specs,
                *wt.specs(),
            ],
            out_specs=[whole((n, d)), whole((2, 8, d))],
            scratch_shapes=[
                *wt.scratch(0, n3),
                pltpu.VMEM((n, n3), BF),
                pltpu.VMEM((n, d), F32),
                *late.scratch,
            ],
        ),
        out_shape=[jax.ShapeDtypeStruct((n, d), BF), jax.ShapeDtypeStruct((2, 8, d), F32)],
        compiler_params=params(),
        cost_estimate=cost(6 * n * d * d, 8 * d * d + 16 * n * d),
        name="first_back",
    )(scal, *tri, *got, mod, *late.arrays, *wt.arrays)


def weight_grad(scal, terms, join, w, mine, geo, name, partial=None):
    n = terms[0][1][0].shape[-2] if not isinstance(terms[0][1][0], tuple) else terms[0][1][0][0].shape[-2]
    pr = geo.P * geo.R
    th = geo.Th
    half_n = geo.P // 2
    want = scal[1] if mine else 1 - scal[1]
    lefts = [term[0] for term in terms]
    if not geo.direct:
        lefts = [a[:n] for a in lefts]
    if not geo.direct:

        def pick(a):
            cols = a.reshape(n, geo.P, 2, geo.R)
            cols = jnp.where(want == 0, cols[:, :, 0], cols[:, :, 1])
            return cols.reshape(n, pr).T

        lefts = [pick(a) for a in lefts]
    ops, op_specs, counts = [], [], []
    for _, operands, _ in terms:
        counts.append(len(operands))
        for pair in operands:
            if isinstance(pair, tuple):
                tail = (0,) * (pair[0].ndim - 1)
                op_specs += two_halves((1,) + pair[0].shape[1:], th, tail)
                ops += pair
            else:
                op_specs.append(pl.BlockSpec((1,) + pair.shape[1:], lambda j, s: (j, 0, 0)))
                ops.append(pair)
    na, nb = len(lefts), len(ops)

    def kernel(s, *refs):
        a_refs, b_refs = refs[:na], refs[na : na + nb]
        rest = refs[na + nb :]
        got_ref = None
        if mine:
            got_ref, rest = rest[0], rest[1:]
        n_out = 4 if (mine and geo.direct) else 1
        outs, ats = rest[:n_out], rest[n_out:]
        j = pl.program_id(0)
        if geo.direct:

            @pl.when(j == 0)
            def _():
                pick_odd = (s[1] == 1) if mine else (s[1] == 0)
                for ref, at in zip(a_refs, ats):
                    flip = ref[...].T
                    for p in range(geo.P):
                        even = flip[2 * p * geo.R : (2 * p + 1) * geo.R]
                        odd = flip[(2 * p + 1) * geo.R : (2 * p + 2) * geo.R]
                        row = pl.multiple_of((s[0] ^ p) * geo.R, geo.R)
                        at[pl.ds(row, geo.R), :] = jnp.where(pick_odd, odd, even)
        else:
            ats = a_refs

        def store(half):
            at_op, parts = 0, []
            for at, (_, operands, build) in zip(ats, terms):
                blocks = []
                for pair in operands:
                    if isinstance(pair, tuple):
                        blocks.append(b_refs[at_op + half])
                        at_op += 2
                    else:
                        blocks.append(b_refs[at_op])
                        at_op += 1
                parts.append(dotg(at[...], build(*blocks), 1, 0))
            full = join(*parts)
            if not geo.direct:
                if mine:
                    full = full + got_ref[0, 0].astype(F32)
                outs[0][0, 0] = full.astype(BF)
                return
            if not mine:
                for rel in range(geo.P):
                    outs[0][0, rel] = full[rel * geo.R : (rel + 1) * geo.R].astype(BF)
                return
            for i, rel in enumerate(geo.order[half]):
                part = full[rel * geo.R : (rel + 1) * geo.R] + got_ref[0, rel].astype(F32)
                outs[2 * half + i // half_n][i % half_n, 0] = part.astype(BF)

        for half in range(2):

            @pl.when((j < th) if half == 0 else (j >= th))
            def _():
                store(half)

    in_specs = [whole((n, a.shape[1])) if geo.direct else whole(a.shape) for a in lefts] + op_specs
    rel_block = (1, geo.P, geo.R, w) if geo.direct else (1, 1, pr, w)
    rel_spec = pl.BlockSpec(rel_block, lambda j, s: (j, 0, 0, 0))
    rel_shape = jax.ShapeDtypeStruct((geo.T,) + rel_block[1:], BF)
    args = [*lefts, *ops]
    out_specs, shapes = [rel_spec], [rel_shape]
    if mine:
        in_specs.append(rel_spec)
        args.append(partial)
        if geo.direct:
            block = (half_n, 1, geo.R, w)
            first = pl.BlockSpec(block, lambda j, s: (0, jnp.minimum(j, th - 1), 0, 0))
            second = pl.BlockSpec(block, lambda j, s: (0, jnp.maximum(j - th, 0), 0, 0))
            out_specs = [first, first, second, second]
            shapes = [jax.ShapeDtypeStruct((half_n, th, geo.R, w), BF)] * 4
    scratch = [pltpu.VMEM((pr, n), BF)] * na if geo.direct else []
    got = pl.pallas_call(
        kernel,
        grid_spec=pltpu.PrefetchScalarGridSpec(
            num_scalar_prefetch=1,
            grid=(geo.T,),
            in_specs=in_specs,
            out_specs=out_specs,
            scratch_shapes=scratch,
        ),
        out_shape=shapes,
        compiler_params=params(62 << 20),
        cost_estimate=cost(2 * pr * n * w * geo.T, 2 * geo.T * w * (2 * pr + n)),
        name=name,
    )(scal, *args)
    if not mine:
        return got[0]
    if geo.direct:
        return got
    blocks = got[0].reshape(geo.T, geo.P, geo.R, w)
    out = []
    for half in range(2):
        part = blocks[half * th : (half + 1) * th]
        part = reorder(part, [scal[0] ^ rel for rel in geo.order[half]], 1)
        part = part.transpose(1, 0, 2, 3)
        out += [part[:half_n], part[half_n:]]
    return out


def body(
    latents,
    conditioning,
    mod_weight,
    mod_bias,
    in_weight,
    query_value_bias,
    out_weight,
    branch_bias,
    up_weight,
    up_bias,
    down_weight,
    cotangent,
):
    images, row_count, width = latents.shape
    geo = Geo(lax.axis_size("fsdp"), lax.axis_size("tensor"), width)
    F, T = geo.F, geo.T
    assert 2 * images == T
    highest = lax.Precision.HIGHEST
    fi = lax.axis_index("fsdp")
    ti = lax.axis_index("tensor")
    pair, core = fi // 2, fi % 2
    scal = jnp.stack([pair, core, ti]).astype(jnp.int32)
    cols = in_weight.shape[2]
    units = up_weight.shape[1]
    geo.windows(cols)

    def places(k):
        return [
            ((2 * p + c) * T + t, (2 * p + t // images) * T + c * images + (t % images + k) % images)
            for p in range(geo.P)
            for c in range(2)
            for t in range(T)
        ]

    def to_chip(arr):
        got = []
        for k in range(images):
            item = lax.dynamic_index_in_dim(arr, (ti + k) % images, 0, keepdims=False)
            got.append(lax.ppermute(item, BOTH, places(k)))
        return got

    def from_chip(arr):
        got = []
        for k in range(images):
            back = [(dst, src) for src, dst in places(k)]
            got.append(lax.ppermute(arr[k * row_count : (k + 1) * row_count], BOTH, back))
        return got

    def home(parts):
        return reorder(jnp.stack(parts), [(i - ti) % images for i in range(images)])

    def share(arr):
        sent = jnp.broadcast_to(arr[None], (F * T,) + arr.shape)
        return lax.all_to_all(sent, BOTH, 0, 0, tiled=True)

    now, opened = (), []

    def tie(value):
        return after(value, *now)

    def start(*chains):
        for way in chains:
            opened.extend(way.advance(*now))

    def begin(shard, make, *how):
        way = Chain(make(tie(shard), geo, *how))
        opened.extend(way.flight)
        return way

    def across(value):
        got = flip_core(tie(value), geo)
        opened.append(got)
        return got

    def close(*made):
        nonlocal now
        now = (*opened, *made)
        opened.clear()

    heads = cols // HEAD_DIM
    attn_shard = jnp.concatenate([in_weight[0], in_weight[1], in_weight[2], out_weight.T], axis=1)
    attn_way = begin(attn_shard, gather_steps, False)
    cond_all = after(conditioning, attn_shard)[None]
    bit = 1
    while bit < F:
        got = lax.ppermute(cond_all, "fsdp", [(i, i ^ bit) for i in range(F)])
        cond_all = jnp.concatenate([cond_all, got])
        bit *= 2
    cond_all = reorder(cond_all, [fi ^ f for f in range(F)]).reshape(F * images, width)
    silu_low = jax.nn.silu(cond_all.astype(F32)).astype(BF)
    silu_own = lax.dynamic_slice_in_dim(silu_low, fi * geo.R, geo.R, 1)
    mod_part = jnp.einsum("bd,dcj->bcj", silu_own, mod_weight, preferred_element_type=F32)
    bias_rows = jnp.concatenate([mod_bias, query_value_bias]).astype(F32)
    bias_rows = jnp.where(fi == 0, bias_rows, 0.0)
    mod_part = jnp.pad(mod_part, ((0, 0), (0, 2), (0, 0))) + bias_rows
    mod_part = mod_part.reshape(geo.P, 1, T, 8, cols)
    mod_part = jnp.broadcast_to(mod_part, (geo.P, 2, T, 8, cols)).reshape(F * T, 8, cols)
    close()
    start(attn_way)
    up_way = begin(up_weight, gather_steps, True, True)
    mod_part = lax.all_to_all(mod_part, BOTH, 0, 0, tiled=True)
    mod_part = mod_part.reshape(F, T, 8, cols).sum(axis=0)
    mod = mod_part[:, :6].transpose(1, 0, 2).reshape(6, width)
    qv_bias = mod_part[:, 6:]
    triple_bias = jnp.concatenate(
        [
            qv_bias[:, :1],
            jnp.zeros_like(qv_bias[:, :1]),
            qv_bias[:, 1:],
            jnp.zeros((T, 1, geo.n3 - 3 * cols), F32),
        ],
        axis=2,
    )
    bias_rows = branch_bias.astype(F32)
    close(mod)
    start(attn_way)
    x_parts = to_chip(tie(latents))
    opened.extend(x_parts)
    close()
    x = jnp.concatenate([*x_parts, jnp.zeros((ROWS, width), BF)])
    start(attn_way, up_way)
    h1 = norm_mod(tie(x), mod)
    close(h1)
    w_attn = Gathered(attn_way.finish(*now), geo, scal)
    start(up_way)

    q, kv, kvo = [None] * 2, [None] * 2, [None] * 2
    mixed, lse = [None] * 2, [None] * 2
    extras = []
    down_shard = jnp.concatenate(
        [down_weight.T, jnp.broadcast_to(up_bias, (16, units))]
    )
    down_way = begin(down_shard, gather_steps, True, False, extras)
    for half in range(2):
        q[half], kv[half] = in_proj(tie(scal), h1, w_attn, triple_bias, half, geo)
    close(q[0], q[1])
    kvo = [across(kv[0]), across(kv[1])]
    close()
    start(up_way, down_way)
    for half in range(2):
        mixed[half], lse[half] = attn_fwd(tie(q[half]), kv[half], kvo[half], geo)
    close(lse[0], lse[1])
    start(up_way, down_way)
    attn, resid, h2 = out_proj(tie(scal), mixed, x, mod, bias_rows[0:1], w_attn, geo)
    close(h2)
    w_up = Gathered(up_way.finish(*now), geo, scal)
    start(down_way)
    cot_parts = to_chip(tie(cotangent))
    opened.extend(cot_parts)
    unit_bias = jnp.stack([part[:1] for part in extras]).astype(F32)
    hidden, gp = up_proj(tie(scal), h2, unit_bias, w_up, geo)
    close(hidden)
    start(down_way)
    cot = jnp.concatenate(cot_parts)
    ffn_grad = (cot.astype(F32) * mod[5]).astype(BF)
    ffn_sum = jnp.sum(ffn_grad.astype(F32), axis=0)

    def block(ref):
        return ref[0]

    def alone(part):
        return part

    down_terms = [(ffn_grad, [hidden], block)]
    down_half = weight_grad(tie(scal), down_terms, alone, units, False, geo, "w_down_send")
    close(down_half)
    w_down = Gathered(down_way.finish(*now), geo, scal)
    down_got = across(down_half)
    block_rows, ffn_sums = down_proj(
        tie(scal), hidden, resid, cot, mod, bias_rows[1:2], w_down, geo
    )
    close(ffn_sums)

    down_parts = weight_grad(tie(scal), down_terms, alone, units, True, geo, "w_down", down_got)
    close(*down_parts)
    down_back = begin(down_parts, scatter_steps)
    block_back = from_chip(tie(block_rows))
    opened.extend(block_back)
    pre, unit_sum = pre_back(tie(scal), ffn_grad, gp, w_down, geo)
    up_terms = [(h2, [pre], block)]
    up_half = weight_grad(tie(scal), up_terms, alone, units, False, geo, "w_up_send")
    close(up_half)
    start(down_back)
    up_got = across(up_half)
    rg, ag, mid_sums = second_back(tie(scal), pre, resid, attn, cot, mod, w_up, geo)
    close(ag)
    start(down_back)
    up_parts = weight_grad(tie(scal), up_terms, alone, units, True, geo, "w_up", up_got)
    mg = mixed_back(tie(scal), ag, w_attn, geo)
    close(mg, *up_parts)
    start(down_back)
    up_back = begin(up_parts, scatter_steps)
    tri, tri_send, tri_sums, send_sums = [None] * 2, [None] * 2, [None] * 2, [None] * 2
    for half in range(2):
        tri[half], tri_send[half], tri_sums[half], send_sums[half] = attn_bwd(
            tie(q[half]), kv[half], kvo[half], mixed[half], mg, lse[half], half * geo.Th, geo
        )
    close(*tri_sums)
    tri_got = [across(tri_send[0]), across(tri_send[1])]
    tri_sum, send_sum = jnp.concatenate(tri_sums), jnp.concatenate(send_sums)
    pair_sums = jnp.concatenate(
        [
            tri_sum[:, :, :cols],
            tri_sum[:, :, 2 * cols : 3 * cols]
            + send_sum[:, :, geo.koff + cols : geo.koff + 2 * cols],
        ],
        axis=1,
    )
    close()
    start(up_back)
    down_back.finish(*now)

    def beside(first, second):
        shared = geo.n3 - geo.base
        middle = first[:, geo.base :] + second[:, :shared]
        return jnp.concatenate([first[:, : geo.base], middle, second[:, shared:]], axis=1)

    attn_terms = [
        (h1, [tuple(tri), tuple(tri_got)], lambda a, b: triple_grad(a, b, geo)),
        (ag, [tuple(mixed)], block),
    ]
    attn_half = weight_grad(tie(scal), attn_terms, beside, 4 * cols, False, geo, "w_attn_send")
    close(attn_half)
    start(up_back)
    attn_got = across(attn_half)
    latent_rows, first_sums = first_back(tie(scal), tri, tri_got, x, rg, mod, w_attn, geo)
    close(first_sums)
    start(up_back)
    mine = [i ^ ti for i in range(T)]
    rows = jnp.concatenate(
        [first_sums.sum(axis=1), mid_sums[:3].sum(axis=1), ffn_sums.sum(axis=0, keepdims=True)]
    )
    rows = tie(rows).reshape(6, T, cols).transpose(1, 0, 2).reshape(T, 6 * cols)
    branch_sums = jnp.stack([mid_sums[3].sum(axis=0), ffn_sum]).reshape(F, T, -1)
    unit_sums = reorder(unit_sum, mine).reshape(T, F, units // F).transpose(1, 0, 2)
    pair_sums = reorder(pair_sums, mine).reshape(T, F, 2 * cols // F).transpose(1, 0, 2)
    rows = jnp.broadcast_to(rows[None], (F,) + rows.shape)
    pack = jnp.concatenate([rows, branch_sums, unit_sums, pair_sums], axis=2)
    count = pack.shape[2]
    pack = jnp.pad(pack, ((0, 0), (0, 0), (0, -count % 1024))).reshape(F * T, -1, 128)
    pack = lax.all_to_all(pack, BOTH, 0, 0, tiled=True)
    attn_parts = weight_grad(
        tie(scal), attn_terms, beside, 4 * cols, True, geo, "w_attn", attn_got
    )
    close(pack, *attn_parts)
    attn_back = begin(attn_parts, scatter_steps, False)
    latent_back = from_chip(tie(latent_rows))
    opened.extend(latent_back)
    pack = tie(pack)
    slices = pack.sum(axis=0).reshape(-1)[6 * cols : count]
    tiles = -(-6 * cols // 128)
    mine_rows = pack[:, :tiles].reshape(geo.P, 2, T, tiles, 128).sum(axis=1)
    mine_rows = mine_rows.reshape(F * images, -1)[:, : 6 * cols].reshape(F * images, 6, cols)
    cond_part = jnp.einsum("bcj,dcj->bd", mine_rows, mod_weight.astype(F32), precision=highest)
    cond_part = cond_part.reshape(F, 1, images * geo.R)
    cond_part = jnp.broadcast_to(cond_part, (F, T, images * geo.R))
    kept = jnp.broadcast_to(slices[None, None], (F, T) + slices.shape)
    final = jnp.concatenate([cond_part, kept], axis=2).reshape(F * T, -1)
    final = jnp.pad(final, ((0, 0), (0, -final.shape[1] % 1024))).reshape(F * T, -1, 128)
    final = lax.all_to_all(final, BOTH, 0, 0, tiled=True)
    close(final)
    start(attn_back)
    close()
    start(attn_back)
    block_out, latent_grad = home(block_back), home(latent_back)
    down_grad, up_grad = down_back.finish(*now), up_back.finish(*now)
    attn_grad = attn_back.finish(*now)
    in_grad = attn_grad[:, : 3 * cols].reshape(geo.R, 3, cols).transpose(1, 0, 2)

    final = final.reshape(F, T, -1)
    at = images * geo.R
    cond_mine = final[:, :, :at].sum(axis=1).reshape(F, images, geo.R)
    step = 2 * width // (F * T)
    branch_grad = final[:, :, at : at + step].reshape(2, width)
    own = lax.dynamic_index_in_dim(final, ti, 1, keepdims=False)
    at += step
    unit_grad = own[:, at : at + units // F].reshape(units)
    at += units // F
    pair_grad = own[:, at : at + 2 * cols // F].reshape(2, cols)
    mod_weight_grad = jnp.einsum("bd,bcj->dcj", silu_own.astype(F32), mine_rows, precision=highest)
    mod_bias_grad = mine_rows.sum(axis=0)
    silu_grad = cond_mine.transpose(1, 0, 2).reshape(images, width)
    cond_f = conditioning.astype(F32)
    sig = jax.nn.sigmoid(cond_f)
    cond_grad = silu_grad * (sig * (1.0 + cond_f * (1.0 - sig)))

    return (
        block_out,
        latent_grad,
        cond_grad,
        mod_weight_grad,
        mod_bias_grad,
        in_grad,
        pair_grad,
        attn_grad[:, 3 * cols :].T,
        branch_grad,
        up_grad,
        unit_grad,
        down_grad.T,
    )


def solution(mesh):
    in_specs = (
        P("fsdp", "tensor", None),
        P("fsdp", None),
        P("fsdp", None, "tensor"),
        P(None, "tensor"),
        P(None, "fsdp", "tensor"),
        P(None, "tensor"),
        P("tensor", "fsdp"),
        P(),
        P("fsdp", "tensor"),
        P("tensor"),
        P("tensor", "fsdp"),
        P("fsdp", "tensor", None),
    )
    out_specs = (
        P("fsdp", "tensor", None),
        P("fsdp", "tensor", None),
        P("fsdp", None),
        P("fsdp", None, "tensor"),
        P(None, "tensor"),
        P(None, "fsdp", "tensor"),
        P(None, "tensor"),
        P("tensor", "fsdp"),
        P(),
        P("fsdp", "tensor"),
        P("tensor"),
        P("tensor", "fsdp"),
    )
    return jax.shard_map(body, mesh=mesh, in_specs=in_specs, out_specs=out_specs, check_vma=False)
```

```python
import functools

import jax
import jax.numpy as jnp
from jax import lax
from jax.experimental import pallas as pl
from jax.experimental.pallas import tpu as pltpu
from jax.sharding import PartitionSpec as P

HEAD_DIM = 72
EPS = 1e-06
TANH_C = 0.7978845608028654
CUBIC = 0.044715
LOG2E = 1.4426950408889634
VMEM_BYTES = 56 << 20
ROWS = 32
BF = jnp.bfloat16
F32 = jnp.float32
BOTH = ("fsdp", "tensor")


def dotg(a, b, ca, cb):
    return lax.dot_general(a, b, (((ca,), (cb,)), ((), ())), preferred_element_type=F32)


class Geo:
    def __init__(self, fsdp, tensor, dim):
        self.F, self.T, self.P = fsdp, tensor, fsdp // 2
        self.Th = tensor // 2
        self.D = dim
        self.R = dim // fsdp
        self.bits = [1 << b for b in range((self.P - 1).bit_length())]
        self.order = (self.orders(self.bits[::-1]), self.orders(self.bits))
        self.direct = self.R % 16 == 0

    def windows(self, w):
        self.w = w
        self.n3 = min(padded(3 * w), 4 * w)
        self.kbase = w // 128 * 128
        self.koff = w - self.kbase
        self.kvw = self.n3 - self.kbase
        self.base = 3 * w // 128 * 128
        self.off = 3 * w - self.base
        self.win = 4 * w - self.base

    @staticmethod
    def orders(msb_first):
        vals = [0]
        for bit in reversed(msb_first):
            vals = vals + [v | bit for v in vals]
        return vals


def reorder(x, index, axis=0):
    return jnp.stack([lax.dynamic_index_in_dim(x, i, axis, keepdims=False) for i in index], axis)


def flip_pair(x, bit, geo):
    return lax.ppermute(x, "fsdp", [(i, i ^ (2 * bit)) for i in range(geo.F)])


def flip_core(x, geo):
    return lax.ppermute(x, "fsdp", [(i, i ^ 1) for i in range(geo.F)])


def flip_tensor(x, k, geo):
    return lax.ppermute(x, "tensor", [(i, i ^ k) for i in range(geo.T)])


def after(value, *done):
    return lax.optimization_barrier((value, done))[0] if done else value


class Chain:
    def __init__(self, steps):
        self.steps = steps
        self.flight = next(steps)
        self.result = None

    def advance(self, *done):
        if self.result is not None:
            return []
        try:
            self.flight = self.steps.send(after(self.flight, *done))
        except StopIteration as end:
            self.flight, self.result = [], end.value
        return self.flight

    def finish(self, *done):
        while self.result is None:
            self.advance(*done)
        return self.result


def gather_steps(shard, geo, parted=True, joined=False, extras=None):
    if parted:
        late = [geo.Th] if extras is None else list(range(1, geo.Th + 1))
        most = [k for k in range(1, geo.T) if k not in late]
        got = dict(zip(most, (yield [flip_tensor(shard, k, geo) for k in most])))
        got.update(zip(late, (yield [flip_tensor(shard, k, geo) for k in late])))
        parts = [shard] + [got[k] for k in range(1, geo.T)]
    else:
        got = yield [flip_tensor(shard, k, geo) for k in range(1, geo.T)]
        parts = [shard] + got
    if extras is not None:
        extras += [part[geo.R :] for part in parts]
        parts = [part[: geo.R] for part in parts]
    bufs = [jnp.stack(parts[h * geo.Th : (h + 1) * geo.Th])[None] for h in range(2)]
    for at in range(len(geo.bits)):
        bits = (geo.bits[at], geo.bits[-1 - at])
        got = yield [flip_pair(bufs[h], bits[h], geo) for h in range(2)]
        if joined or at < len(geo.bits) - 1:
            bufs = [jnp.concatenate(pair) for pair in zip(bufs, got)]
    owns = [[buf] for buf in bufs] if joined else [list(pair) for pair in zip(bufs, got)]
    count = len(owns[0])
    others = yield [flip_core(a, geo) for own in owns for a in own]
    return [owns[h] + others[h * count : (h + 1) * count] for h in range(2)]


class Gathered:
    def __init__(self, halves, geo, scal):
        self.geo = geo
        if not geo.direct:
            fixed = []
            for half, arrays in enumerate(halves):
                at = [geo.order[half].index(rel) for rel in range(geo.P)]
                lookup = jnp.array(at, jnp.int32)
                blocks = jnp.concatenate(arrays)
                blocks = reorder(
                    blocks,
                    [
                        lookup[(f // 2) ^ scal[0]] + geo.P * ((f % 2) ^ scal[1])
                        for f in range(geo.F)
                    ],
                )
                _, th, r, w = blocks.shape
                fixed.append([blocks.transpose(1, 0, 2, 3).reshape(1, th, geo.D, w)])
            halves = fixed
        self.halves = halves
        self.arrays = halves[0] + halves[1]
        self.n = len(halves[0])
        self.width = self.arrays[0].shape[-1]

    def operands(self, half=None):
        return self.arrays if half is None else self.halves[half]

    def specs(self, half=None):
        return [pl.BlockSpec(memory_space=pl.ANY)] * len(self.operands(half))

    def scratch(self, lo=0, hi=None):
        hi = self.width if hi is None else hi
        if lo % 128 or hi % 128:
            lo, hi = 0, self.width
        self.lo, self.hi = lo, hi
        count = self.n * self.arrays[0].shape[0]
        return [
            pltpu.VMEM((2, self.geo.D, hi - lo), BF),
            pltpu.SemaphoreType.DMA((2, count)),
        ]

    def copies(self, group, slot, half, s_ref, refs, buf, sem):
        geo, out = self.geo, []
        for at, ref in enumerate(refs):
            n, _, rows, _ = ref.shape
            for i in range(n):
                row = 0
                if geo.direct:
                    place = at * n + i
                    rel = geo.order[half][place % geo.P]
                    row = 2 * (s_ref[0] ^ rel) + (s_ref[1] ^ (place // geo.P))
                    row = pl.multiple_of(row * rows, rows)
                out.append(
                    pltpu.make_async_copy(
                        ref.at[i, group, :, pl.ds(self.lo, self.hi - self.lo)],
                        buf.at[slot, pl.ds(row, rows), :],
                        sem.at[slot, at * n + i],
                    )
                )
        return out

    def stream(self, j, s_ref, refs, buf, sem, half=None):
        th = self.geo.Th

        def each(step, act):
            if half is not None:
                for copy in self.copies(step, step % 2, half, s_ref, refs, buf, sem):
                    act(copy)
                return
            for part in range(2):

                @pl.when((step < th) if part == 0 else (step >= th))
                def _():
                    mine = refs[part * self.n : (part + 1) * self.n]
                    for copy in self.copies(
                        step - part * th, step % 2, part, s_ref, mine, buf, sem
                    ):
                        act(copy)

        @pl.when(j == 0)
        def _():
            each(j, lambda copy: copy.start(priority=1))

        @pl.when(j + 1 < (self.geo.T if half is None else th))
        def _():
            each(j + 1, lambda copy: copy.start(priority=1))

        each(j, lambda copy: copy.wait())
        return buf.at[j % 2]


def scatter_steps(pieces, geo, parted=True):
    def add(a, b):
        return a.astype(F32) + b.astype(F32)

    keeps, sends = [pieces[0], pieces[2]], [pieces[1], pieces[3]]
    for at in range(len(geo.bits)):
        bits = (geo.bits[-1 - at], geo.bits[at])
        got = yield [flip_pair(sends[h], bits[h], geo) for h in range(2)]
        m = max(1, keeps[0].shape[0] // 2)
        if at < len(geo.bits) - 1:
            sends = [add(keeps[h][m:], got[h][m:]).astype(BF) for h in range(2)]
        keeps = [add(keeps[h][:m], got[h][:m]).astype(BF) for h in range(2)]
    units = [keep[0, k] for keep in keeps for k in range(geo.Th)]
    if parted:
        rest = [k for k in range(1, geo.T) if k != geo.Th]
        got = yield [flip_tensor(units[k], k, geo) for k in rest]
        got += yield [flip_tensor(units[geo.Th], geo.Th, geo)]
    else:
        got = yield [flip_tensor(units[k], k, geo) for k in range(1, geo.T)]
    total = units[0].astype(F32)
    for part in got:
        total = total + part.astype(F32)
    return total


def params(size=VMEM_BYTES):
    return pltpu.CompilerParams(vmem_limit_bytes=size)


def cost(flops, size):
    return pl.CostEstimate(flops=int(flops), bytes_accessed=int(size), transcendentals=0)


def whole(shape):
    zeros = (0,) * len(shape)
    return pl.BlockSpec(shape, lambda j, s: zeros)


def padded(w):
    return -(-w // 128) * 128


def pieces(total):
    step = 512 if total % 128 == 0 else total
    return [slice(at, min(at + step, total)) for at in range(0, total, step)]


def norm_of(v):
    centre = v - jnp.mean(v, axis=-1, keepdims=True)
    inv = lax.rsqrt(jnp.mean(centre * centre, axis=-1, keepdims=True) + EPS)
    return centre * inv, inv


def norm_back(norm, inv, g):
    return (
        g
        - jnp.mean(g, axis=-1, keepdims=True)
        - norm * jnp.mean(g * norm, axis=-1, keepdims=True)
    ) * inv


def fold_rows(v):
    return v.reshape(v.shape[0] // 8, 8, v.shape[1]).sum(axis=0)


class Late:
    def __init__(self, *arrays):
        self.arrays = arrays
        self.specs = [pl.BlockSpec(memory_space=pl.ANY)] * len(arrays)
        self.scratch = [pltpu.VMEM(a.shape, a.dtype) for a in arrays]
        self.scratch.append(pltpu.SemaphoreType.DMA((len(arrays),)))

    def copies(self, refs, scratch):
        sem = scratch[-1]
        return [
            pltpu.make_async_copy(ref, scratch[i], sem.at[i]) for i, ref in enumerate(refs)
        ]

    def start(self, j, refs, scratch):
        @pl.when(j == 0)
        def _():
            for copy in self.copies(refs, scratch):
                copy.start(priority=1)

    def wait(self, refs, scratch):
        for copy in self.copies(refs, scratch):
            copy.wait()
        return scratch[:-1]


def two_halves(block, th, tail):
    return [
        pl.BlockSpec(block, lambda j, s: (jnp.minimum(j, th - 1),) + tail),
        pl.BlockSpec(block, lambda j, s: (jnp.maximum(j - th, 0),) + tail),
    ]


def norm_mod(x, mod):
    n, d = x.shape[0] - ROWS, x.shape[1]

    def kernel(x_ref, m_ref, h_ref):
        @pl.loop(0, n // ROWS, unroll=4)
        def _(i):
            at = pl.ds(pl.multiple_of(i * ROWS, ROWS), ROWS)
            norm, _ = norm_of(x_ref[at, :].astype(F32))
            h_ref[at, :] = (norm * (1.0 + m_ref[1:2, :]) + m_ref[0:1, :]).astype(BF)

    return pl.pallas_call(
        kernel,
        out_shape=jax.ShapeDtypeStruct((n, d), BF),
        compiler_params=params(),
        cost_estimate=cost(20 * n * d, 4 * n * d),
        name="norm_mod",
    )(x, mod)


def in_proj(scal, h, wt, bias, half, geo):
    n, d = h.shape
    n3, wp = geo.n3, padded(geo.w)
    nw = wt.n

    def kernel(s, h_ref, b_ref, *refs):
        w_refs, (q_ref, kv_ref, wbuf, sem) = refs[:nw], refs[nw:]
        now = wt.stream(pl.program_id(0), s, w_refs, wbuf, sem, half)
        y = dotg(h_ref[...], now[:, :n3], 1, 0) + b_ref[0]
        y = y.astype(BF)
        q_ref[0] = y[:, :wp]
        kv_ref[0] = y[:, geo.kbase :]

    first = half * geo.Th
    return pl.pallas_call(
        kernel,
        grid_spec=pltpu.PrefetchScalarGridSpec(
            num_scalar_prefetch=1,
            grid=(geo.Th,),
            in_specs=[
                whole((n, d)),
                pl.BlockSpec((1, 1, n3), lambda j, s: (s[2] ^ (j + first), 0, 0)),
                *wt.specs(half),
            ],
            out_specs=[
                pl.BlockSpec((1, n, wp), lambda j, s: (j, 0, 0)),
                pl.BlockSpec((1, n, geo.kvw), lambda j, s: (j, 0, 0)),
            ],
            scratch_shapes=wt.scratch(0, n3),
        ),
        out_shape=[
            jax.ShapeDtypeStruct((geo.Th, n, wp), BF),
            jax.ShapeDtypeStruct((geo.Th, n, geo.kvw), BF),
        ],
        compiler_params=params(),
        cost_estimate=cost(2 * n * d * n3 * geo.Th, 8 * d * geo.w * geo.Th + 8 * n * d),
        name="in_proj",
    )(scal, h, bias, *wt.operands(half))


def head_lanes(geo, h):
    at = h * HEAD_DIM
    return [
        slice(start + at, start + at + HEAD_DIM)
        for start in (0, geo.koff, geo.koff + geo.w, geo.off)
    ]


def attn_fwd(q, kv, kvo, geo):
    z, n, wp = q.shape
    heads = geo.w // HEAD_DIM
    c = HEAD_DIM**-0.5 * LOG2E

    def kernel(q_ref, kv_ref, kvo_ref, o_ref, lse_ref):
        outs = [jnp.zeros((geo.off, n), F32)] if geo.off else []
        for h in range(heads):
            lq, lk, lv, _ = head_lanes(geo, h)
            qh = q_ref[0, :, lq]
            sa = dotg(kv_ref[0, :, lk], qh, 1, 1) * c
            sb = dotg(kvo_ref[0, :, lk], qh, 1, 1) * c
            top = jnp.maximum(
                jnp.max(sa, axis=0, keepdims=True), jnp.max(sb, axis=0, keepdims=True)
            )
            pa, pb = jnp.exp2(sa - top), jnp.exp2(sb - top)
            total = jnp.sum(pa, axis=0, keepdims=True) + jnp.sum(pb, axis=0, keepdims=True)
            o = dotg(kv_ref[0, :, lv], pa.astype(BF), 0, 0)
            o = o + dotg(kvo_ref[0, :, lv], pb.astype(BF), 0, 0)
            outs.append(o / total)
            lse_ref[0, h : h + 1, :] = top + jnp.log2(total)
        o_ref[0] = jnp.concatenate(outs, axis=0).T.astype(BF)

    def spec(width):
        return pl.BlockSpec((1, n, width), lambda j: (j, 0, 0))

    return pl.pallas_call(
        kernel,
        grid=(z,),
        in_specs=[spec(wp), spec(geo.kvw), spec(geo.kvw)],
        out_specs=[spec(geo.win), pl.BlockSpec((1, heads, n), lambda j: (j, 0, 0))],
        out_shape=[
            jax.ShapeDtypeStruct((z, n, geo.win), BF),
            jax.ShapeDtypeStruct((z, heads, n), F32),
        ],
        compiler_params=params(),
        cost_estimate=cost(3e9 * z, 10 * z * n * wp),
        name="attn_fwd",
    )(q, kv, kvo)


def attn_bwd(q, kv, kvo, o, do, lse, first, geo):
    z, n, wp = q.shape
    heads = lse.shape[1]
    scale = HEAD_DIM**-0.5
    c = scale * LOG2E

    def kernel(q_ref, kv_ref, kvo_ref, o_ref, do_ref, lse_ref, tri_ref, send_ref, ts_ref, ss_ref):
        both = (do_ref[0].astype(F32) * o_ref[0].astype(F32)).T
        dqs, parts = [], [[[], []], [[], []]]
        for h in range(heads):
            lq, lk, lv, lm = head_lanes(geo, h)
            qh, doh = q_ref[0, :, lq], do_ref[0, :, lm]
            delta = jnp.sum(both[lm], axis=0, keepdims=True)
            lse_h = lse_ref[0, h : h + 1, :]
            dq = None
            for i, ref in enumerate((kv_ref, kvo_ref)):
                k, v = ref[0, :, lk], ref[0, :, lv]
                p = jnp.exp2(dotg(k, qh, 1, 1) * c - lse_h)
                ds = (p * (dotg(v, doh, 1, 1) - delta)).astype(BF)
                parts[i][1].append(dotg(doh, p.astype(BF), 0, 1))
                parts[i][0].append(dotg(qh, ds, 0, 1) * scale)
                got = dotg(k, ds, 0, 0)
                dq = got if dq is None else dq + got
            dqs.append(dq * scale)

        def rows(count):
            return [jnp.zeros((count, n), F32)] if count else []

        pad = rows(geo.n3 - 3 * geo.w)
        own = jnp.concatenate(dqs + parts[0][0] + parts[0][1] + pad, axis=0).T
        other = jnp.concatenate(rows(geo.koff) + parts[1][0] + parts[1][1] + pad, axis=0).T
        tri_ref[0] = own.astype(BF)
        send_ref[0] = other.astype(BF)
        ts_ref[0] = jnp.sum(own, axis=0, keepdims=True)
        ss_ref[0] = jnp.sum(other, axis=0, keepdims=True)

    def spec(width, at=0, count=n):
        return pl.BlockSpec((1, count, width), lambda j: (j + at, 0, 0))

    return pl.pallas_call(
        kernel,
        grid=(z,),
        in_specs=[
            spec(wp),
            spec(geo.kvw),
            spec(geo.kvw),
            spec(geo.win),
            spec(geo.win, first),
            spec(n, 0, heads),
        ],
        out_specs=[spec(geo.n3), spec(geo.kvw), spec(geo.n3, 0, 1), spec(geo.kvw, 0, 1)],
        out_shape=[
            jax.ShapeDtypeStruct((z, n, geo.n3), BF),
            jax.ShapeDtypeStruct((z, n, geo.kvw), BF),
            jax.ShapeDtypeStruct((z, 1, geo.n3), F32),
            jax.ShapeDtypeStruct((z, 1, geo.kvw), F32),
        ],
        compiler_params=params(),
        cost_estimate=cost(5e9 * z, 16 * z * n * wp),
        name="attn_bwd",
    )(q, kv, kvo, o, do, lse)


def triple_grad(tri_ref, got_ref, geo):
    late = tri_ref[0, :, geo.kbase :].astype(F32) + got_ref[0].astype(F32)
    if not geo.kbase:
        return late.astype(BF)
    return jnp.concatenate([tri_ref[0, :, : geo.kbase], late.astype(BF)], axis=1)


def out_proj(scal, mixed, x, mod, bias, wt, geo):
    _, n, win = mixed[0].shape
    d = geo.D
    nw = len(wt.arrays)
    th = geo.Th

    late = Late(x)

    def kernel(s, ya_ref, yb_ref, m_ref, b_ref, *refs):
        late_in, refs = refs[:1], refs[1:]
        w_refs, (attn_out, resid_ref, h_ref, wbuf, sem, attn_ref, *late_buf) = refs[:nw], refs[nw:]
        j = pl.program_id(0)
        late.start(j, late_in, late_buf)
        now = wt.stream(j, s, w_refs, wbuf, sem)
        y = jnp.where(j < th, ya_ref[0], yb_ref[0])
        part = dotg(y, now[:, -win:], 1, 1)

        @pl.when(j == 0)
        def _():
            attn_ref[...] = part

        @pl.when(j > 0)
        def _():
            attn_ref[...] += part

        @pl.when(j == geo.T - 1)
        def _():
            (x_ref,) = late.wait(late_in, late_buf)

            @pl.loop(0, n // ROWS, unroll=4)
            def _(i):
                at = pl.ds(pl.multiple_of(i * ROWS, ROWS), ROWS)
                attn = attn_ref[at, :] + b_ref[...]
                attn_out[at, :] = attn.astype(BF)
                resid = x_ref[at, :].astype(F32) + m_ref[2:3, :] * attn
                resid_ref[at, :] = resid
                norm, _ = norm_of(resid)
                h_ref[at, :] = (norm * (1.0 + m_ref[4:5, :]) + m_ref[3:4, :]).astype(BF)

    return pl.pallas_call(
        kernel,
        grid_spec=pltpu.PrefetchScalarGridSpec(
            num_scalar_prefetch=1,
            grid=(geo.T,),
            in_specs=[
                *two_halves((1, n, win), th, (0, 0)),
                whole(mod.shape),
                whole((1, d)),
                *late.specs,
                *wt.specs(),
            ],
            out_specs=[whole((n, d))] * 3,
            scratch_shapes=[
                *wt.scratch(geo.base, 4 * geo.w),
                pltpu.VMEM((n, d), F32),
                *late.scratch,
            ],
        ),
        out_shape=[
            jax.ShapeDtypeStruct((n + ROWS, d), BF),
            jax.ShapeDtypeStruct((n, d), F32),
            jax.ShapeDtypeStruct((n + ROWS, d), BF),
        ],
        compiler_params=params(),
        cost_estimate=cost(2 * n * d * d, 8 * d * d + 14 * n * d),
        name="out_proj",
    )(scal, *mixed, mod, bias, *late.arrays, *wt.arrays)


def up_proj(scal, h, bias, wt, geo):
    n, d = h.shape[0] - ROWS, h.shape[1]
    w = wt.width
    nw = len(wt.arrays)

    def kernel(s, h_ref, b_ref, *refs):
        w_refs, (hid_ref, gp_ref, wbuf, sem) = refs[:nw], refs[nw:]
        j = pl.program_id(0)
        now = wt.stream(j, s, w_refs, wbuf, sem)
        for cols in pieces(w):
            u = dotg(h_ref[...], now[:, cols], 1, 0) + b_ref[0, :, cols]
            sq = u * u
            t = jnp.tanh(TANH_C * (u + CUBIC * sq * u))
            half = 0.5 * (1.0 + t)
            hid_ref[0, :, cols] = (u * half).astype(BF)
            slope = TANH_C * (1.0 + 3.0 * CUBIC * sq)
            gp_ref[0, :, cols] = (half + 0.5 * u * (1.0 - t * t) * slope).astype(BF)

    out = pl.BlockSpec((1, n, w), lambda j, s: (j, 0, 0))
    return pl.pallas_call(
        kernel,
        grid_spec=pltpu.PrefetchScalarGridSpec(
            num_scalar_prefetch=1,
            grid=(geo.T,),
            in_specs=[
                whole((n, d)),
                pl.BlockSpec((1, 1, w), lambda j, s: (j, 0, 0)),
                *wt.specs(),
            ],
            out_specs=[out, out],
            scratch_shapes=wt.scratch(),
        ),
        out_shape=[jax.ShapeDtypeStruct((geo.T, n, w), BF)] * 2,
        compiler_params=params(),
        cost_estimate=cost(2 * n * d * w * geo.T, 2 * geo.T * w * (d + 2 * n)),
        name="up_proj",
    )(scal, h, bias, *wt.arrays)


def down_proj(scal, hidden, resid, cot, mod, bias, wt, geo):
    _, n, w = hidden.shape
    d = geo.D
    nw = len(wt.arrays)

    late = Late(resid, cot)

    def kernel(s, y_ref, m_ref, b_ref, *refs):
        late_in, refs = refs[:2], refs[2:]
        w_refs, (out_ref, sum_ref, wbuf, sem, acc, *late_buf) = refs[:nw], refs[nw:]
        j = pl.program_id(0)
        late.start(j, late_in, late_buf)
        now = wt.stream(j, s, w_refs, wbuf, sem)
        part = dotg(y_ref[0], now[...], 1, 1)

        @pl.when(j == 0)
        def _():
            acc[...] = part
            sum_ref[...] = jnp.zeros_like(sum_ref)

        @pl.when(j > 0)
        def _():
            acc[...] += part

        @pl.when(j == geo.T - 1)
        def _():
            r_ref, c_ref = late.wait(late_in, late_buf)

            @pl.loop(0, n // ROWS, unroll=4)
            def _(i):
                at = pl.ds(pl.multiple_of(i * ROWS, ROWS), ROWS)
                ffn = acc[at, :] + b_ref[...]
                out_ref[at, :] = (r_ref[at, :] + m_ref[5:6, :] * ffn).astype(BF)
                sum_ref[...] += fold_rows(c_ref[at, :].astype(F32) * ffn)

    return pl.pallas_call(
        kernel,
        grid_spec=pltpu.PrefetchScalarGridSpec(
            num_scalar_prefetch=1,
            grid=(geo.T,),
            in_specs=[
                pl.BlockSpec((1, n, w), lambda j, s: (j, 0, 0)),
                whole(mod.shape),
                whole((1, d)),
                *late.specs,
                *wt.specs(),
            ],
            out_specs=[whole((n, d)), whole((8, d))],
            scratch_shapes=[*wt.scratch(), pltpu.VMEM((n, d), F32), *late.scratch],
        ),
        out_shape=[jax.ShapeDtypeStruct((n, d), BF), jax.ShapeDtypeStruct((8, d), F32)],
        compiler_params=params(),
        cost_estimate=cost(2 * n * d * w * geo.T, 2 * geo.T * w * (d + n) + 8 * n * d),
        name="down_proj",
    )(scal, hidden, mod, bias, *late.arrays, *wt.arrays)


def pre_back(scal, g, gp, wt, geo):
    n, d = g.shape
    w = wt.width
    nw = len(wt.arrays)

    def kernel(s, g_ref, gp_ref, *refs):
        w_refs, (out_ref, sum_ref, wbuf, sem) = refs[:nw], refs[nw:]
        j = pl.program_id(0)
        now = wt.stream(j, s, w_refs, wbuf, sem)
        for cols in pieces(w):
            y = dotg(g_ref[...], now[:, cols], 1, 0) * gp_ref[0, :, cols].astype(F32)
            out_ref[0, :, cols] = y.astype(BF)
            sum_ref[0, :, cols] = jnp.sum(y, axis=0, keepdims=True)

    out = pl.BlockSpec((1, n, w), lambda j, s: (j, 0, 0))
    return pl.pallas_call(
        kernel,
        grid_spec=pltpu.PrefetchScalarGridSpec(
            num_scalar_prefetch=1,
            grid=(geo.T,),
            in_specs=[whole((n, d)), out, *wt.specs()],
            out_specs=[out, pl.BlockSpec((1, 1, w), lambda j, s: (j, 0, 0))],
            scratch_shapes=wt.scratch(),
        ),
        out_shape=[
            jax.ShapeDtypeStruct((geo.T, n, w), BF),
            jax.ShapeDtypeStruct((geo.T, 1, w), F32),
        ],
        compiler_params=params(),
        cost_estimate=cost(2 * n * d * w * geo.T, 2 * geo.T * w * (d + 2 * n)),
        name="pre_back",
    )(scal, g, gp, *wt.arrays)


def second_back(scal, pre, resid, attn, cot, mod, wt, geo):
    _, n, w = pre.shape
    d = geo.D
    nw = len(wt.arrays)

    late = Late(resid, attn, cot)

    def kernel(s, y_ref, m_ref, *refs):
        late_in, refs = refs[:3], refs[3:]
        w_refs, (rg_ref, ag_ref, sum_ref, wbuf, sem, acc, *late_buf) = refs[:nw], refs[nw:]
        j = pl.program_id(0)
        late.start(j, late_in, late_buf)
        now = wt.stream(j, s, w_refs, wbuf, sem)
        part = dotg(y_ref[0], now[...], 1, 1)

        @pl.when(j == 0)
        def _():
            acc[...] = part
            sum_ref[...] = jnp.zeros_like(sum_ref)

        @pl.when(j > 0)
        def _():
            acc[...] += part

        @pl.when(j == geo.T - 1)
        def _():
            r_ref, a_ref, c_ref = late.wait(late_in, late_buf)

            @pl.loop(0, n // ROWS, unroll=4)
            def _(i):
                at = pl.ds(pl.multiple_of(i * ROWS, ROWS), ROWS)
                g = acc[at, :]
                norm, inv = norm_of(r_ref[at, :])
                rg = c_ref[at, :].astype(F32) + norm_back(norm, inv, g * (1.0 + m_ref[4:5, :]))
                rg_ref[at, :] = rg
                ag = rg * m_ref[2:3, :]
                ag_ref[at, :] = ag.astype(BF)
                sum_ref[0] += fold_rows(rg * a_ref[at, :].astype(F32))
                sum_ref[1] += fold_rows(g)
                sum_ref[2] += fold_rows(g * norm)
                sum_ref[3] += fold_rows(ag)

    return pl.pallas_call(
        kernel,
        grid_spec=pltpu.PrefetchScalarGridSpec(
            num_scalar_prefetch=1,
            grid=(geo.T,),
            in_specs=[
                pl.BlockSpec((1, n, w), lambda j, s: (j, 0, 0)),
                whole(mod.shape),
                *late.specs,
                *wt.specs(),
            ],
            out_specs=[whole((n, d)), whole((n, d)), whole((4, 8, d))],
            scratch_shapes=[*wt.scratch(), pltpu.VMEM((n, d), F32), *late.scratch],
        ),
        out_shape=[
            jax.ShapeDtypeStruct((n, d), F32),
            jax.ShapeDtypeStruct((n, d), BF),
            jax.ShapeDtypeStruct((4, 8, d), F32),
        ],
        compiler_params=params(),
        cost_estimate=cost(2 * n * d * w * geo.T, 2 * geo.T * w * (d + n) + 18 * n * d),
        name="second_back",
    )(scal, pre, mod, *late.arrays, *wt.arrays)


def mixed_back(scal, g, wt, geo):
    n, d = g.shape
    win = geo.win
    nw = len(wt.arrays)

    def kernel(s, g_ref, *refs):
        w_refs, (out_ref, wbuf, sem) = refs[:nw], refs[nw:]
        now = wt.stream(pl.program_id(0), s, w_refs, wbuf, sem)
        out_ref[0] = dotg(g_ref[...], now[:, -win:], 1, 0).astype(BF)

    return pl.pallas_call(
        kernel,
        grid_spec=pltpu.PrefetchScalarGridSpec(
            num_scalar_prefetch=1,
            grid=(geo.T,),
            in_specs=[whole((n, d)), *wt.specs()],
            out_specs=pl.BlockSpec((1, n, win), lambda j, s: (j, 0, 0)),
            scratch_shapes=wt.scratch(geo.base, 4 * geo.w),
        ),
        out_shape=jax.ShapeDtypeStruct((geo.T, n, win), BF),
        compiler_params=params(),
        cost_estimate=cost(2 * n * d * d, 8 * d * d + 4 * n * d),
        name="mixed_back",
    )(scal, g, *wt.arrays)


def first_back(scal, tri, got, x, rg, mod, wt, geo):
    _, n, n3 = tri[0].shape
    d = geo.D
    nw = len(wt.arrays)
    th = geo.Th

    late = Late(x, rg)

    def kernel(s, ta, tb, ga, gb, m_ref, *refs):
        late_in, refs = refs[:2], refs[2:]
        w_refs, (out_ref, sum_ref, wbuf, sem, lhs, acc, *late_buf) = refs[:nw], refs[nw:]
        j = pl.program_id(0)
        late.start(j, late_in, late_buf)
        now = wt.stream(j, s, w_refs, wbuf, sem)
        for half, (tri_ref, got_ref) in enumerate(((ta, ga), (tb, gb))):

            @pl.when((j < th) if half == 0 else (j >= th))
            def _():
                lhs[...] = triple_grad(tri_ref, got_ref, geo)

        part = dotg(lhs[...], now[:, :n3], 1, 1)

        @pl.when(j == 0)
        def _():
            acc[...] = part
            sum_ref[...] = jnp.zeros_like(sum_ref)

        @pl.when(j > 0)
        def _():
            acc[...] += part

        @pl.when(j == geo.T - 1)
        def _():
            x_ref, r_ref = late.wait(late_in, late_buf)

            @pl.loop(0, n // ROWS, unroll=4)
            def _(i):
                at = pl.ds(pl.multiple_of(i * ROWS, ROWS), ROWS)
                g = acc[at, :]
                norm, inv = norm_of(x_ref[at, :].astype(F32))
                back = norm_back(norm, inv, g * (1.0 + m_ref[1:2, :]))
                out_ref[at, :] = (r_ref[at, :] + back).astype(BF)
                sum_ref[0] += fold_rows(g)
                sum_ref[1] += fold_rows(g * norm)

    return pl.pallas_call(
        kernel,
        grid_spec=pltpu.PrefetchScalarGridSpec(
            num_scalar_prefetch=1,
            grid=(geo.T,),
            in_specs=[
                *two_halves((1, n, n3), th, (0, 0)),
                *two_halves((1, n, geo.kvw), th, (0, 0)),
                whole(mod.shape),
                *late.specs,
                *wt.specs(),
            ],
            out_specs=[whole((n, d)), whole((2, 8, d))],
            scratch_shapes=[
                *wt.scratch(0, n3),
                pltpu.VMEM((n, n3), BF),
                pltpu.VMEM((n, d), F32),
                *late.scratch,
            ],
        ),
        out_shape=[jax.ShapeDtypeStruct((n, d), BF), jax.ShapeDtypeStruct((2, 8, d), F32)],
        compiler_params=params(),
        cost_estimate=cost(6 * n * d * d, 8 * d * d + 16 * n * d),
        name="first_back",
    )(scal, *tri, *got, mod, *late.arrays, *wt.arrays)


def weight_grad(scal, terms, join, w, mine, geo, name, partial=None):
    n = terms[0][1][0].shape[-2] if not isinstance(terms[0][1][0], tuple) else terms[0][1][0][0].shape[-2]
    pr = geo.P * geo.R
    th = geo.Th
    half_n = geo.P // 2
    want = scal[1] if mine else 1 - scal[1]
    lefts = [term[0] for term in terms]
    if not geo.direct:
        lefts = [a[:n] for a in lefts]
    if not geo.direct:

        def pick(a):
            cols = a.reshape(n, geo.P, 2, geo.R)
            cols = jnp.where(want == 0, cols[:, :, 0], cols[:, :, 1])
            return cols.reshape(n, pr).T

        lefts = [pick(a) for a in lefts]
    ops, op_specs, counts = [], [], []
    for _, operands, _ in terms:
        counts.append(len(operands))
        for pair in operands:
            if isinstance(pair, tuple):
                tail = (0,) * (pair[0].ndim - 1)
                op_specs += two_halves((1,) + pair[0].shape[1:], th, tail)
                ops += pair
            else:
                op_specs.append(pl.BlockSpec((1,) + pair.shape[1:], lambda j, s: (j, 0, 0)))
                ops.append(pair)
    na, nb = len(lefts), len(ops)

    def kernel(s, *refs):
        a_refs, b_refs = refs[:na], refs[na : na + nb]
        rest = refs[na + nb :]
        got_ref = None
        if mine:
            got_ref, rest = rest[0], rest[1:]
        n_out = 4 if (mine and geo.direct) else 1
        outs, ats = rest[:n_out], rest[n_out:]
        j = pl.program_id(0)
        if geo.direct:

            @pl.when(j == 0)
            def _():
                pick_odd = (s[1] == 1) if mine else (s[1] == 0)
                for ref, at in zip(a_refs, ats):
                    flip = ref[...].T
                    for p in range(geo.P):
                        even = flip[2 * p * geo.R : (2 * p + 1) * geo.R]
                        odd = flip[(2 * p + 1) * geo.R : (2 * p + 2) * geo.R]
                        row = pl.multiple_of((s[0] ^ p) * geo.R, geo.R)
                        at[pl.ds(row, geo.R), :] = jnp.where(pick_odd, odd, even)
        else:
            ats = a_refs

        def store(half):
            at_op, parts = 0, []
            for at, (_, operands, build) in zip(ats, terms):
                blocks = []
                for pair in operands:
                    if isinstance(pair, tuple):
                        blocks.append(b_refs[at_op + half])
                        at_op += 2
                    else:
                        blocks.append(b_refs[at_op])
                        at_op += 1
                parts.append(dotg(at[...], build(*blocks), 1, 0))
            full = join(*parts)
            if not geo.direct:
                if mine:
                    full = full + got_ref[0, 0].astype(F32)
                outs[0][0, 0] = full.astype(BF)
                return
            if not mine:
                for rel in range(geo.P):
                    outs[0][0, rel] = full[rel * geo.R : (rel + 1) * geo.R].astype(BF)
                return
            for i, rel in enumerate(geo.order[half]):
                part = full[rel * geo.R : (rel + 1) * geo.R] + got_ref[0, rel].astype(F32)
                outs[2 * half + i // half_n][i % half_n, 0] = part.astype(BF)

        for half in range(2):

            @pl.when((j < th) if half == 0 else (j >= th))
            def _():
                store(half)

    in_specs = [whole((n, a.shape[1])) if geo.direct else whole(a.shape) for a in lefts] + op_specs
    rel_block = (1, geo.P, geo.R, w) if geo.direct else (1, 1, pr, w)
    rel_spec = pl.BlockSpec(rel_block, lambda j, s: (j, 0, 0, 0))
    rel_shape = jax.ShapeDtypeStruct((geo.T,) + rel_block[1:], BF)
    args = [*lefts, *ops]
    out_specs, shapes = [rel_spec], [rel_shape]
    if mine:
        in_specs.append(rel_spec)
        args.append(partial)
        if geo.direct:
            block = (half_n, 1, geo.R, w)
            first = pl.BlockSpec(block, lambda j, s: (0, jnp.minimum(j, th - 1), 0, 0))
            second = pl.BlockSpec(block, lambda j, s: (0, jnp.maximum(j - th, 0), 0, 0))
            out_specs = [first, first, second, second]
            shapes = [jax.ShapeDtypeStruct((half_n, th, geo.R, w), BF)] * 4
    scratch = [pltpu.VMEM((pr, n), BF)] * na if geo.direct else []
    got = pl.pallas_call(
        kernel,
        grid_spec=pltpu.PrefetchScalarGridSpec(
            num_scalar_prefetch=1,
            grid=(geo.T,),
            in_specs=in_specs,
            out_specs=out_specs,
            scratch_shapes=scratch,
        ),
        out_shape=shapes,
        compiler_params=params(62 << 20),
        cost_estimate=cost(2 * pr * n * w * geo.T, 2 * geo.T * w * (2 * pr + n)),
        name=name,
    )(scal, *args)
    if not mine:
        return got[0]
    if geo.direct:
        return got
    blocks = got[0].reshape(geo.T, geo.P, geo.R, w)
    out = []
    for half in range(2):
        part = blocks[half * th : (half + 1) * th]
        part = reorder(part, [scal[0] ^ rel for rel in geo.order[half]], 1)
        part = part.transpose(1, 0, 2, 3)
        out += [part[:half_n], part[half_n:]]
    return out


def body(
    latents,
    conditioning,
    mod_weight,
    mod_bias,
    in_weight,
    query_value_bias,
    out_weight,
    branch_bias,
    up_weight,
    up_bias,
    down_weight,
    cotangent,
):
    images, row_count, width = latents.shape
    geo = Geo(lax.axis_size("fsdp"), lax.axis_size("tensor"), width)
    F, T = geo.F, geo.T
    assert 2 * images == T
    highest = lax.Precision.HIGHEST
    fi = lax.axis_index("fsdp")
    ti = lax.axis_index("tensor")
    pair, core = fi // 2, fi % 2
    scal = jnp.stack([pair, core, ti]).astype(jnp.int32)
    cols = in_weight.shape[2]
    units = up_weight.shape[1]
    geo.windows(cols)

    def places(k):
        return [
            ((2 * p + c) * T + t, (2 * p + t // images) * T + c * images + (t % images + k) % images)
            for p in range(geo.P)
            for c in range(2)
            for t in range(T)
        ]

    def to_chip(arr):
        got = []
        for k in range(images):
            item = lax.dynamic_index_in_dim(arr, (ti + k) % images, 0, keepdims=False)
            got.append(lax.ppermute(item, BOTH, places(k)))
        return got

    def from_chip(arr):
        got = []
        for k in range(images):
            back = [(dst, src) for src, dst in places(k)]
            got.append(lax.ppermute(arr[k * row_count : (k + 1) * row_count], BOTH, back))
        return got

    def home(parts):
        return reorder(jnp.stack(parts), [(i - ti) % images for i in range(images)])

    def share(arr):
        sent = jnp.broadcast_to(arr[None], (F * T,) + arr.shape)
        return lax.all_to_all(sent, BOTH, 0, 0, tiled=True)

    now, opened = (), []

    def tie(value):
        return after(value, *now)

    def start(*chains):
        for way in chains:
            opened.extend(way.advance(*now))

    def begin(shard, make, *how):
        way = Chain(make(tie(shard), geo, *how))
        opened.extend(way.flight)
        return way

    def across(value):
        got = flip_core(tie(value), geo)
        opened.append(got)
        return got

    def close(*made):
        nonlocal now
        now = (*opened, *made)
        opened.clear()

    heads = cols // HEAD_DIM
    attn_shard = jnp.concatenate([in_weight[0], in_weight[1], in_weight[2], out_weight.T], axis=1)
    attn_way = begin(attn_shard, gather_steps, False)
    cond_all = after(conditioning, attn_shard)[None]
    bit = 1
    while bit < F:
        got = lax.ppermute(cond_all, "fsdp", [(i, i ^ bit) for i in range(F)])
        cond_all = jnp.concatenate([cond_all, got])
        bit *= 2
    cond_all = reorder(cond_all, [fi ^ f for f in range(F)]).reshape(F * images, width)
    silu_low = jax.nn.silu(cond_all.astype(F32)).astype(BF)
    silu_own = lax.dynamic_slice_in_dim(silu_low, fi * geo.R, geo.R, 1)
    mod_part = jnp.einsum("bd,dcj->bcj", silu_own, mod_weight, preferred_element_type=F32)
    bias_rows = jnp.concatenate([mod_bias, query_value_bias]).astype(F32)
    bias_rows = jnp.where(fi == 0, bias_rows, 0.0)
    mod_part = jnp.pad(mod_part, ((0, 0), (0, 2), (0, 0))) + bias_rows
    mod_part = mod_part.reshape(geo.P, 1, T, 8, cols)
    mod_part = jnp.broadcast_to(mod_part, (geo.P, 2, T, 8, cols)).reshape(F * T, 8, cols)
    close()
    start(attn_way)
    up_way = begin(up_weight, gather_steps, True, True)
    mod_part = lax.all_to_all(mod_part, BOTH, 0, 0, tiled=True)
    mod_part = mod_part.reshape(F, T, 8, cols).sum(axis=0)
    mod = mod_part[:, :6].transpose(1, 0, 2).reshape(6, width)
    qv_bias = mod_part[:, 6:]
    triple_bias = jnp.concatenate(
        [
            qv_bias[:, :1],
            jnp.zeros_like(qv_bias[:, :1]),
            qv_bias[:, 1:],
            jnp.zeros((T, 1, geo.n3 - 3 * cols), F32),
        ],
        axis=2,
    )
    bias_rows = branch_bias.astype(F32)
    close(mod)
    start(attn_way)
    x_parts = to_chip(tie(latents))
    opened.extend(x_parts)
    close()
    x = jnp.concatenate([*x_parts, jnp.zeros((ROWS, width), BF)])
    start(attn_way, up_way)
    h1 = norm_mod(tie(x), mod)
    close(h1)
    w_attn = Gathered(attn_way.finish(*now), geo, scal)
    start(up_way)

    q, kv, kvo = [None] * 2, [None] * 2, [None] * 2
    mixed, lse = [None] * 2, [None] * 2
    extras = []
    down_shard = jnp.concatenate(
        [down_weight.T, jnp.broadcast_to(up_bias, (16, units))]
    )
    down_way = begin(down_shard, gather_steps, True, False, extras)
    for half in range(2):
        q[half], kv[half] = in_proj(tie(scal), h1, w_attn, triple_bias, half, geo)
    close(q[0], q[1])
    kvo = [across(kv[0]), across(kv[1])]
    close()
    start(up_way, down_way)
    for half in range(2):
        mixed[half], lse[half] = attn_fwd(tie(q[half]), kv[half], kvo[half], geo)
    close(lse[0], lse[1])
    start(up_way, down_way)
    attn, resid, h2 = out_proj(tie(scal), mixed, x, mod, bias_rows[0:1], w_attn, geo)
    close(h2)
    w_up = Gathered(up_way.finish(*now), geo, scal)
    start(down_way)
    cot_parts = to_chip(tie(cotangent))
    opened.extend(cot_parts)
    unit_bias = jnp.stack([part[:1] for part in extras]).astype(F32)
    hidden, gp = up_proj(tie(scal), h2, unit_bias, w_up, geo)
    close(hidden)
    start(down_way)
    cot = jnp.concatenate(cot_parts)
    ffn_grad = (cot.astype(F32) * mod[5]).astype(BF)

    def block(ref):
        return ref[0]

    def alone(part):
        return part

    down_terms = [(ffn_grad, [hidden], block)]
    down_half = weight_grad(tie(scal), down_terms, alone, units, False, geo, "w_down_send")
    close(down_half)
    w_down = Gathered(down_way.finish(*now), geo, scal)
    down_got = across(down_half)
    block_rows, ffn_sums = down_proj(
        tie(scal), hidden, resid, cot, mod, bias_rows[1:2], w_down, geo
    )
    close(ffn_sums)

    down_parts = weight_grad(tie(scal), down_terms, alone, units, True, geo, "w_down", down_got)
    close(*down_parts)
    down_back = begin(down_parts, scatter_steps)
    block_back = from_chip(tie(block_rows))
    opened.extend(block_back)
    pre, unit_sum = pre_back(tie(scal), ffn_grad, gp, w_down, geo)
    up_terms = [(h2, [pre], block)]
    up_half = weight_grad(tie(scal), up_terms, alone, units, False, geo, "w_up_send")
    close(up_half)
    start(down_back)
    up_got = across(up_half)
    rg, ag, mid_sums = second_back(tie(scal), pre, resid, attn, cot, mod, w_up, geo)
    close(ag)
    start(down_back)
    up_parts = weight_grad(tie(scal), up_terms, alone, units, True, geo, "w_up", up_got)
    mg = mixed_back(tie(scal), ag, w_attn, geo)
    close(mg, *up_parts)
    start(down_back)
    up_back = begin(up_parts, scatter_steps)
    tri, tri_send, tri_sums, send_sums = [None] * 2, [None] * 2, [None] * 2, [None] * 2
    for half in range(2):
        tri[half], tri_send[half], tri_sums[half], send_sums[half] = attn_bwd(
            tie(q[half]), kv[half], kvo[half], mixed[half], mg, lse[half], half * geo.Th, geo
        )
    close(*tri_sums)
    tri_got = [across(tri_send[0]), across(tri_send[1])]
    ffn_sum = jnp.sum(tie(ffn_grad).astype(F32), axis=0)
    tri_sum, send_sum = jnp.concatenate(tri_sums), jnp.concatenate(send_sums)
    pair_sums = jnp.concatenate(
        [
            tri_sum[:, :, :cols],
            tri_sum[:, :, 2 * cols : 3 * cols]
            + send_sum[:, :, geo.koff + cols : geo.koff + 2 * cols],
        ],
        axis=1,
    )
    close()
    start(up_back)

    def beside(first, second):
        shared = geo.n3 - geo.base
        middle = first[:, geo.base :] + second[:, :shared]
        return jnp.concatenate([first[:, : geo.base], middle, second[:, shared:]], axis=1)

    attn_terms = [
        (h1, [tuple(tri), tuple(tri_got)], lambda a, b: triple_grad(a, b, geo)),
        (ag, [tuple(mixed)], block),
    ]
    attn_half = weight_grad(tie(scal), attn_terms, beside, 4 * cols, False, geo, "w_attn_send")
    close(attn_half)
    start(up_back)
    attn_got = across(attn_half)
    latent_rows, first_sums = first_back(tie(scal), tri, tri_got, x, rg, mod, w_attn, geo)
    close(first_sums)
    start(up_back)
    mine = [i ^ ti for i in range(T)]
    rows = jnp.concatenate(
        [first_sums.sum(axis=1), mid_sums[:3].sum(axis=1), ffn_sums.sum(axis=0, keepdims=True)]
    )
    rows = tie(rows).reshape(6, T, cols).transpose(1, 0, 2).reshape(T, 6 * cols)
    branch_sums = jnp.stack([mid_sums[3].sum(axis=0), ffn_sum]).reshape(F, T, -1)
    unit_sums = reorder(unit_sum, mine).reshape(T, F, units // F).transpose(1, 0, 2)
    pair_sums = reorder(pair_sums, mine).reshape(T, F, 2 * cols // F).transpose(1, 0, 2)
    rows = jnp.broadcast_to(rows[None], (F,) + rows.shape)
    pack = jnp.concatenate([rows, branch_sums, unit_sums, pair_sums], axis=2)
    count = pack.shape[2]
    pack = jnp.pad(pack, ((0, 0), (0, 0), (0, -count % 1024))).reshape(F * T, -1, 128)
    pack = lax.all_to_all(pack, BOTH, 0, 0, tiled=True)
    attn_parts = weight_grad(
        tie(scal), attn_terms, beside, 4 * cols, True, geo, "w_attn", attn_got
    )
    close(pack, *attn_parts)
    attn_back = begin(attn_parts, scatter_steps, False)
    block_back = [tie(part) for part in block_back]
    down_shard = down_back.finish(*now)
    latent_back = from_chip(tie(latent_rows))
    opened.extend(latent_back)
    pack = tie(pack)
    slices = pack.sum(axis=0).reshape(-1)[6 * cols : count]
    tiles = -(-6 * cols // 128)
    mine_rows = pack[:, :tiles].reshape(geo.P, 2, T, tiles, 128).sum(axis=1)
    mine_rows = mine_rows.reshape(F * images, -1)[:, : 6 * cols].reshape(F * images, 6, cols)
    cond_part = jnp.einsum("bcj,dcj->bd", mine_rows, mod_weight.astype(F32), precision=highest)
    cond_part = cond_part.reshape(F, 1, images * geo.R)
    cond_part = jnp.broadcast_to(cond_part, (F, T, images * geo.R))
    kept = jnp.broadcast_to(slices[None, None], (F, T) + slices.shape)
    final = jnp.concatenate([cond_part, kept], axis=2).reshape(F * T, -1)
    final = jnp.pad(final, ((0, 0), (0, -final.shape[1] % 1024))).reshape(F * T, -1, 128)
    final = lax.all_to_all(final, BOTH, 0, 0, tiled=True)
    close(final)
    start(attn_back)
    close()
    start(attn_back)
    block_out, latent_grad = home(block_back), home(latent_back)
    down_grad, up_grad = down_shard, up_back.finish(*now)
    attn_grad = attn_back.finish(*now)
    in_grad = attn_grad[:, : 3 * cols].reshape(geo.R, 3, cols).transpose(1, 0, 2)

    final = final.reshape(F, T, -1)
    at = images * geo.R
    cond_mine = final[:, :, :at].sum(axis=1).reshape(F, images, geo.R)
    step = 2 * width // (F * T)
    branch_grad = final[:, :, at : at + step].reshape(2, width)
    own = lax.dynamic_index_in_dim(final, ti, 1, keepdims=False)
    at += step
    unit_grad = own[:, at : at + units // F].reshape(units)
    at += units // F
    pair_grad = own[:, at : at + 2 * cols // F].reshape(2, cols)
    mod_weight_grad = jnp.einsum("bd,bcj->dcj", silu_own.astype(F32), mine_rows, precision=highest)
    mod_bias_grad = mine_rows.sum(axis=0)
    silu_grad = cond_mine.transpose(1, 0, 2).reshape(images, width)
    cond_f = conditioning.astype(F32)
    sig = jax.nn.sigmoid(cond_f)
    cond_grad = silu_grad * (sig * (1.0 + cond_f * (1.0 - sig)))

    return (
        block_out,
        latent_grad,
        cond_grad,
        mod_weight_grad,
        mod_bias_grad,
        in_grad,
        pair_grad,
        attn_grad[:, 3 * cols :].T,
        branch_grad,
        up_grad,
        unit_grad,
        down_grad.T,
    )


def solution(mesh):
    in_specs = (
        P("fsdp", "tensor", None),
        P("fsdp", None),
        P("fsdp", None, "tensor"),
        P(None, "tensor"),
        P(None, "fsdp", "tensor"),
        P(None, "tensor"),
        P("tensor", "fsdp"),
        P(),
        P("fsdp", "tensor"),
        P("tensor"),
        P("tensor", "fsdp"),
        P("fsdp", "tensor", None),
    )
    out_specs = (
        P("fsdp", "tensor", None),
        P("fsdp", "tensor", None),
        P("fsdp", None),
        P("fsdp", None, "tensor"),
        P(None, "tensor"),
        P(None, "fsdp", "tensor"),
        P(None, "tensor"),
        P("tensor", "fsdp"),
        P(),
        P("fsdp", "tensor"),
        P("tensor"),
        P("tensor", "fsdp"),
    )
    return jax.shard_map(body, mesh=mesh, in_specs=in_specs, out_specs=out_specs, check_vma=False)
```

```python
import functools

import jax
import jax.numpy as jnp
from jax import lax
from jax.experimental import pallas as pl
from jax.experimental.pallas import tpu as pltpu
from jax.sharding import PartitionSpec as P

HEAD_DIM = 72
EPS = 1e-06
TANH_C = 0.7978845608028654
CUBIC = 0.044715
LOG2E = 1.4426950408889634
VMEM_BYTES = 56 << 20
ROWS = 32
BF = jnp.bfloat16
F32 = jnp.float32
BOTH = ("fsdp", "tensor")


def dotg(a, b, ca, cb):
    return lax.dot_general(a, b, (((ca,), (cb,)), ((), ())), preferred_element_type=F32)


class Geo:
    def __init__(self, fsdp, tensor, dim):
        self.F, self.T, self.P = fsdp, tensor, fsdp // 2
        self.Th = tensor // 2
        self.D = dim
        self.R = dim // fsdp
        self.bits = [1 << b for b in range((self.P - 1).bit_length())]
        self.order = (self.orders(self.bits[::-1]), self.orders(self.bits))
        self.direct = self.R % 16 == 0

    def windows(self, w):
        self.w = w
        self.n3 = min(padded(3 * w), 4 * w)
        self.kbase = w // 128 * 128
        self.koff = w - self.kbase
        self.kvw = self.n3 - self.kbase
        self.base = 3 * w // 128 * 128
        self.off = 3 * w - self.base
        self.win = 4 * w - self.base

    @staticmethod
    def orders(msb_first):
        vals = [0]
        for bit in reversed(msb_first):
            vals = vals + [v | bit for v in vals]
        return vals


def reorder(x, index, axis=0):
    return jnp.stack([lax.dynamic_index_in_dim(x, i, axis, keepdims=False) for i in index], axis)


def flip_pair(x, bit, geo):
    return lax.ppermute(x, "fsdp", [(i, i ^ (2 * bit)) for i in range(geo.F)])


def flip_core(x, geo):
    return lax.ppermute(x, "fsdp", [(i, i ^ 1) for i in range(geo.F)])


def flip_tensor(x, k, geo):
    return lax.ppermute(x, "tensor", [(i, i ^ k) for i in range(geo.T)])


def after(value, *done):
    return lax.optimization_barrier((value, done))[0] if done else value


class Chain:
    def __init__(self, steps):
        self.steps = steps
        self.flight = next(steps)
        self.result = None

    def advance(self, *done):
        if self.result is not None:
            return []
        try:
            self.flight = self.steps.send(after(self.flight, *done))
        except StopIteration as end:
            self.flight, self.result = [], end.value
        return self.flight

    def finish(self, *done):
        while self.result is None:
            self.advance(*done)
        return self.result


def gather_steps(shard, geo, parted=True, joined=False, extras=None):
    if parted:
        late = [geo.Th] if extras is None else list(range(1, geo.Th + 1))
        most = [k for k in range(1, geo.T) if k not in late]
        got = dict(zip(most, (yield [flip_tensor(shard, k, geo) for k in most])))
        got.update(zip(late, (yield [flip_tensor(shard, k, geo) for k in late])))
        parts = [shard] + [got[k] for k in range(1, geo.T)]
    else:
        got = yield [flip_tensor(shard, k, geo) for k in range(1, geo.T)]
        parts = [shard] + got
    if extras is not None:
        extras += [part[geo.R :] for part in parts]
        parts = [part[: geo.R] for part in parts]
    bufs = [jnp.stack(parts[h * geo.Th : (h + 1) * geo.Th])[None] for h in range(2)]
    for at in range(len(geo.bits)):
        bits = (geo.bits[at], geo.bits[-1 - at])
        got = yield [flip_pair(bufs[h], bits[h], geo) for h in range(2)]
        if joined or at < len(geo.bits) - 1:
            bufs = [jnp.concatenate(pair) for pair in zip(bufs, got)]
    owns = [[buf] for buf in bufs] if joined else [list(pair) for pair in zip(bufs, got)]
    count = len(owns[0])
    others = yield [flip_core(a, geo) for own in owns for a in own]
    return [owns[h] + others[h * count : (h + 1) * count] for h in range(2)]


class Gathered:
    def __init__(self, halves, geo, scal):
        self.geo = geo
        if not geo.direct:
            fixed = []
            for half, arrays in enumerate(halves):
                at = [geo.order[half].index(rel) for rel in range(geo.P)]
                lookup = jnp.array(at, jnp.int32)
                blocks = jnp.concatenate(arrays)
                blocks = reorder(
                    blocks,
                    [
                        lookup[(f // 2) ^ scal[0]] + geo.P * ((f % 2) ^ scal[1])
                        for f in range(geo.F)
                    ],
                )
                _, th, r, w = blocks.shape
                fixed.append([blocks.transpose(1, 0, 2, 3).reshape(1, th, geo.D, w)])
            halves = fixed
        self.halves = halves
        self.arrays = halves[0] + halves[1]
        self.n = len(halves[0])
        self.width = self.arrays[0].shape[-1]

    def operands(self, half=None):
        return self.arrays if half is None else self.halves[half]

    def specs(self, half=None):
        return [pl.BlockSpec(memory_space=pl.ANY)] * len(self.operands(half))

    def scratch(self, lo=0, hi=None):
        hi = self.width if hi is None else hi
        if lo % 128 or hi % 128:
            lo, hi = 0, self.width
        self.lo, self.hi = lo, hi
        count = self.n * self.arrays[0].shape[0]
        return [
            pltpu.VMEM((2, self.geo.D, hi - lo), BF),
            pltpu.SemaphoreType.DMA((2, count)),
        ]

    def copies(self, group, slot, half, s_ref, refs, buf, sem):
        geo, out = self.geo, []
        for at, ref in enumerate(refs):
            n, _, rows, _ = ref.shape
            for i in range(n):
                row = 0
                if geo.direct:
                    place = at * n + i
                    rel = geo.order[half][place % geo.P]
                    row = 2 * (s_ref[0] ^ rel) + (s_ref[1] ^ (place // geo.P))
                    row = pl.multiple_of(row * rows, rows)
                out.append(
                    pltpu.make_async_copy(
                        ref.at[i, group, :, pl.ds(self.lo, self.hi - self.lo)],
                        buf.at[slot, pl.ds(row, rows), :],
                        sem.at[slot, at * n + i],
                    )
                )
        return out

    def stream(self, j, s_ref, refs, buf, sem, half=None):
        th = self.geo.Th

        def each(step, act):
            if half is not None:
                for copy in self.copies(step, step % 2, half, s_ref, refs, buf, sem):
                    act(copy)
                return
            for part in range(2):

                @pl.when((step < th) if part == 0 else (step >= th))
                def _():
                    mine = refs[part * self.n : (part + 1) * self.n]
                    for copy in self.copies(
                        step - part * th, step % 2, part, s_ref, mine, buf, sem
                    ):
                        act(copy)

        @pl.when(j == 0)
        def _():
            each(j, lambda copy: copy.start(priority=1))

        @pl.when(j + 1 < (self.geo.T if half is None else th))
        def _():
            each(j + 1, lambda copy: copy.start(priority=1))

        each(j, lambda copy: copy.wait())
        return buf.at[j % 2]


def scatter_steps(pieces, geo, parted=True):
    def add(a, b):
        return a.astype(F32) + b.astype(F32)

    keeps, sends = [pieces[0], pieces[2]], [pieces[1], pieces[3]]
    for at in range(len(geo.bits)):
        bits = (geo.bits[-1 - at], geo.bits[at])
        got = yield [flip_pair(sends[h], bits[h], geo) for h in range(2)]
        m = max(1, keeps[0].shape[0] // 2)
        if at < len(geo.bits) - 1:
            sends = [add(keeps[h][m:], got[h][m:]).astype(BF) for h in range(2)]
        keeps = [add(keeps[h][:m], got[h][:m]).astype(BF) for h in range(2)]
    units = [keep[0, k] for keep in keeps for k in range(geo.Th)]
    if parted:
        rest = [k for k in range(1, geo.T) if k != geo.Th]
        got = yield [flip_tensor(units[k], k, geo) for k in rest]
        got += yield [flip_tensor(units[geo.Th], geo.Th, geo)]
    else:
        got = yield [flip_tensor(units[k], k, geo) for k in range(1, geo.T)]
    total = units[0].astype(F32)
    for part in got:
        total = total + part.astype(F32)
    return total


def params(size=VMEM_BYTES):
    return pltpu.CompilerParams(vmem_limit_bytes=size)


def cost(flops, size):
    return pl.CostEstimate(flops=int(flops), bytes_accessed=int(size), transcendentals=0)


def whole(shape):
    zeros = (0,) * len(shape)
    return pl.BlockSpec(shape, lambda j, s: zeros)


def padded(w):
    return -(-w // 128) * 128


def pieces(total):
    step = 512 if total % 128 == 0 else total
    return [slice(at, min(at + step, total)) for at in range(0, total, step)]


def norm_of(v):
    centre = v - jnp.mean(v, axis=-1, keepdims=True)
    inv = lax.rsqrt(jnp.mean(centre * centre, axis=-1, keepdims=True) + EPS)
    return centre * inv, inv


def norm_back(norm, inv, g):
    return (
        g
        - jnp.mean(g, axis=-1, keepdims=True)
        - norm * jnp.mean(g * norm, axis=-1, keepdims=True)
    ) * inv


def fold_rows(v):
    return v.reshape(v.shape[0] // 8, 8, v.shape[1]).sum(axis=0)


class Late:
    def __init__(self, *arrays):
        self.arrays = arrays
        self.specs = [pl.BlockSpec(memory_space=pl.ANY)] * len(arrays)
        self.scratch = [pltpu.VMEM(a.shape, a.dtype) for a in arrays]
        self.scratch.append(pltpu.SemaphoreType.DMA((len(arrays),)))

    def copies(self, refs, scratch):
        sem = scratch[-1]
        return [
            pltpu.make_async_copy(ref, scratch[i], sem.at[i]) for i, ref in enumerate(refs)
        ]

    def start(self, j, refs, scratch):
        @pl.when(j == 0)
        def _():
            for copy in self.copies(refs, scratch):
                copy.start(priority=1)

    def wait(self, refs, scratch):
        for copy in self.copies(refs, scratch):
            copy.wait()
        return scratch[:-1]


def two_halves(block, th, tail):
    return [
        pl.BlockSpec(block, lambda j, s: (jnp.minimum(j, th - 1),) + tail),
        pl.BlockSpec(block, lambda j, s: (jnp.maximum(j - th, 0),) + tail),
    ]


def norm_mod(x, mod):
    n, d = x.shape[0] - ROWS, x.shape[1]

    def kernel(x_ref, m_ref, h_ref):
        @pl.loop(0, n // ROWS, unroll=4)
        def _(i):
            at = pl.ds(pl.multiple_of(i * ROWS, ROWS), ROWS)
            norm, _ = norm_of(x_ref[at, :].astype(F32))
            h_ref[at, :] = (norm * (1.0 + m_ref[1:2, :]) + m_ref[0:1, :]).astype(BF)

    return pl.pallas_call(
        kernel,
        out_shape=jax.ShapeDtypeStruct((n, d), BF),
        compiler_params=params(),
        cost_estimate=cost(20 * n * d, 4 * n * d),
        name="norm_mod",
    )(x, mod)


def in_proj(scal, h, wt, bias, half, geo):
    n, d = h.shape
    n3, wp = geo.n3, padded(geo.w)
    nw = wt.n

    def kernel(s, h_ref, b_ref, *refs):
        w_refs, (q_ref, kv_ref, wbuf, sem) = refs[:nw], refs[nw:]
        now = wt.stream(pl.program_id(0), s, w_refs, wbuf, sem, half)
        y = dotg(h_ref[...], now[:, :n3], 1, 0) + b_ref[0]
        y = y.astype(BF)
        q_ref[0] = y[:, :wp]
        kv_ref[0] = y[:, geo.kbase :]

    first = half * geo.Th
    return pl.pallas_call(
        kernel,
        grid_spec=pltpu.PrefetchScalarGridSpec(
            num_scalar_prefetch=1,
            grid=(geo.Th,),
            in_specs=[
                whole((n, d)),
                pl.BlockSpec((1, 1, n3), lambda j, s: (s[2] ^ (j + first), 0, 0)),
                *wt.specs(half),
            ],
            out_specs=[
                pl.BlockSpec((1, n, wp), lambda j, s: (j, 0, 0)),
                pl.BlockSpec((1, n, geo.kvw), lambda j, s: (j, 0, 0)),
            ],
            scratch_shapes=wt.scratch(0, n3),
        ),
        out_shape=[
            jax.ShapeDtypeStruct((geo.Th, n, wp), BF),
            jax.ShapeDtypeStruct((geo.Th, n, geo.kvw), BF),
        ],
        compiler_params=params(),
        cost_estimate=cost(2 * n * d * n3 * geo.Th, 8 * d * geo.w * geo.Th + 8 * n * d),
        name="in_proj",
    )(scal, h, bias, *wt.operands(half))


def head_lanes(geo, h):
    at = h * HEAD_DIM
    return [
        slice(start + at, start + at + HEAD_DIM)
        for start in (0, geo.koff, geo.koff + geo.w, geo.off)
    ]


def attn_fwd(q, kv, kvo, geo):
    z, n, wp = q.shape
    heads = geo.w // HEAD_DIM
    c = HEAD_DIM**-0.5 * LOG2E

    def kernel(q_ref, kv_ref, kvo_ref, o_ref, lse_ref):
        outs = [jnp.zeros((geo.off, n), F32)] if geo.off else []
        for h in range(heads):
            lq, lk, lv, _ = head_lanes(geo, h)
            qh = q_ref[0, :, lq]
            sa = dotg(kv_ref[0, :, lk], qh, 1, 1) * c
            sb = dotg(kvo_ref[0, :, lk], qh, 1, 1) * c
            top = jnp.maximum(
                jnp.max(sa, axis=0, keepdims=True), jnp.max(sb, axis=0, keepdims=True)
            )
            pa, pb = jnp.exp2(sa - top), jnp.exp2(sb - top)
            total = jnp.sum(pa, axis=0, keepdims=True) + jnp.sum(pb, axis=0, keepdims=True)
            o = dotg(kv_ref[0, :, lv], pa.astype(BF), 0, 0)
            o = o + dotg(kvo_ref[0, :, lv], pb.astype(BF), 0, 0)
            outs.append(o / total)
            lse_ref[0, h : h + 1, :] = top + jnp.log2(total)
        o_ref[0] = jnp.concatenate(outs, axis=0).T.astype(BF)

    def spec(width):
        return pl.BlockSpec((1, n, width), lambda j: (j, 0, 0))

    return pl.pallas_call(
        kernel,
        grid=(z,),
        in_specs=[spec(wp), spec(geo.kvw), spec(geo.kvw)],
        out_specs=[spec(geo.win), pl.BlockSpec((1, heads, n), lambda j: (j, 0, 0))],
        out_shape=[
            jax.ShapeDtypeStruct((z, n, geo.win), BF),
            jax.ShapeDtypeStruct((z, heads, n), F32),
        ],
        compiler_params=params(),
        cost_estimate=cost(3e9 * z, 10 * z * n * wp),
        name="attn_fwd",
    )(q, kv, kvo)


def attn_bwd(q, kv, kvo, o, do, lse, first, geo):
    z, n, wp = q.shape
    heads = lse.shape[1]
    scale = HEAD_DIM**-0.5
    c = scale * LOG2E

    def kernel(q_ref, kv_ref, kvo_ref, o_ref, do_ref, lse_ref, tri_ref, send_ref, ts_ref, ss_ref):
        both = (do_ref[0].astype(F32) * o_ref[0].astype(F32)).T
        dqs, parts = [], [[[], []], [[], []]]
        for h in range(heads):
            lq, lk, lv, lm = head_lanes(geo, h)
            qh, doh = q_ref[0, :, lq], do_ref[0, :, lm]
            delta = jnp.sum(both[lm], axis=0, keepdims=True)
            lse_h = lse_ref[0, h : h + 1, :]
            dq = None
            for i, ref in enumerate((kv_ref, kvo_ref)):
                k, v = ref[0, :, lk], ref[0, :, lv]
                p = jnp.exp2(dotg(k, qh, 1, 1) * c - lse_h)
                ds = (p * (dotg(v, doh, 1, 1) - delta)).astype(BF)
                parts[i][1].append(dotg(doh, p.astype(BF), 0, 1))
                parts[i][0].append(dotg(qh, ds, 0, 1) * scale)
                got = dotg(k, ds, 0, 0)
                dq = got if dq is None else dq + got
            dqs.append(dq * scale)

        def rows(count):
            return [jnp.zeros((count, n), F32)] if count else []

        pad = rows(geo.n3 - 3 * geo.w)
        own = jnp.concatenate(dqs + parts[0][0] + parts[0][1] + pad, axis=0).T
        other = jnp.concatenate(rows(geo.koff) + parts[1][0] + parts[1][1] + pad, axis=0).T
        tri_ref[0] = own.astype(BF)
        send_ref[0] = other.astype(BF)
        ts_ref[0] = jnp.sum(own, axis=0, keepdims=True)
        ss_ref[0] = jnp.sum(other, axis=0, keepdims=True)

    def spec(width, at=0, count=n):
        return pl.BlockSpec((1, count, width), lambda j: (j + at, 0, 0))

    return pl.pallas_call(
        kernel,
        grid=(z,),
        in_specs=[
            spec(wp),
            spec(geo.kvw),
            spec(geo.kvw),
            spec(geo.win),
            spec(geo.win, first),
            spec(n, 0, heads),
        ],
        out_specs=[spec(geo.n3), spec(geo.kvw), spec(geo.n3, 0, 1), spec(geo.kvw, 0, 1)],
        out_shape=[
            jax.ShapeDtypeStruct((z, n, geo.n3), BF),
            jax.ShapeDtypeStruct((z, n, geo.kvw), BF),
            jax.ShapeDtypeStruct((z, 1, geo.n3), F32),
            jax.ShapeDtypeStruct((z, 1, geo.kvw), F32),
        ],
        compiler_params=params(),
        cost_estimate=cost(5e9 * z, 16 * z * n * wp),
        name="attn_bwd",
    )(q, kv, kvo, o, do, lse)


def triple_grad(tri_ref, got_ref, geo):
    late = tri_ref[0, :, geo.kbase :].astype(F32) + got_ref[0].astype(F32)
    if not geo.kbase:
        return late.astype(BF)
    return jnp.concatenate([tri_ref[0, :, : geo.kbase], late.astype(BF)], axis=1)


def out_proj(scal, mixed, x, mod, bias, wt, geo):
    _, n, win = mixed[0].shape
    d = geo.D
    nw = len(wt.arrays)
    th = geo.Th

    late = Late(x)

    def kernel(s, ya_ref, yb_ref, m_ref, b_ref, *refs):
        late_in, refs = refs[:1], refs[1:]
        w_refs, (attn_out, resid_ref, h_ref, wbuf, sem, attn_ref, *late_buf) = refs[:nw], refs[nw:]
        j = pl.program_id(0)
        late.start(j, late_in, late_buf)
        now = wt.stream(j, s, w_refs, wbuf, sem)
        y = jnp.where(j < th, ya_ref[0], yb_ref[0])
        part = dotg(y, now[:, -win:], 1, 1)

        @pl.when(j == 0)
        def _():
            attn_ref[...] = part

        @pl.when(j > 0)
        def _():
            attn_ref[...] += part

        @pl.when(j == geo.T - 1)
        def _():
            (x_ref,) = late.wait(late_in, late_buf)

            @pl.loop(0, n // ROWS, unroll=4)
            def _(i):
                at = pl.ds(pl.multiple_of(i * ROWS, ROWS), ROWS)
                attn = attn_ref[at, :] + b_ref[...]
                attn_out[at, :] = attn.astype(BF)
                resid = x_ref[at, :].astype(F32) + m_ref[2:3, :] * attn
                resid_ref[at, :] = resid
                norm, _ = norm_of(resid)
                h_ref[at, :] = (norm * (1.0 + m_ref[4:5, :]) + m_ref[3:4, :]).astype(BF)

    return pl.pallas_call(
        kernel,
        grid_spec=pltpu.PrefetchScalarGridSpec(
            num_scalar_prefetch=1,
            grid=(geo.T,),
            in_specs=[
                *two_halves((1, n, win), th, (0, 0)),
                whole(mod.shape),
                whole((1, d)),
                *late.specs,
                *wt.specs(),
            ],
            out_specs=[whole((n, d))] * 3,
            scratch_shapes=[
                *wt.scratch(geo.base, 4 * geo.w),
                pltpu.VMEM((n, d), F32),
                *late.scratch,
            ],
        ),
        out_shape=[
            jax.ShapeDtypeStruct((n + ROWS, d), BF),
            jax.ShapeDtypeStruct((n, d), F32),
            jax.ShapeDtypeStruct((n + ROWS, d), BF),
        ],
        compiler_params=params(),
        cost_estimate=cost(2 * n * d * d, 8 * d * d + 14 * n * d),
        name="out_proj",
    )(scal, *mixed, mod, bias, *late.arrays, *wt.arrays)


def up_proj(scal, h, bias, wt, geo):
    n, d = h.shape[0] - ROWS, h.shape[1]
    w = wt.width
    nw = len(wt.arrays)

    def kernel(s, h_ref, b_ref, *refs):
        w_refs, (hid_ref, gp_ref, wbuf, sem) = refs[:nw], refs[nw:]
        j = pl.program_id(0)
        now = wt.stream(j, s, w_refs, wbuf, sem)
        for cols in pieces(w):
            u = dotg(h_ref[...], now[:, cols], 1, 0) + b_ref[0, :, cols]
            sq = u * u
            t = jnp.tanh(TANH_C * (u + CUBIC * sq * u))
            half = 0.5 * (1.0 + t)
            hid_ref[0, :, cols] = (u * half).astype(BF)
            slope = TANH_C * (1.0 + 3.0 * CUBIC * sq)
            gp_ref[0, :, cols] = (half + 0.5 * u * (1.0 - t * t) * slope).astype(BF)

    out = pl.BlockSpec((1, n, w), lambda j, s: (j, 0, 0))
    return pl.pallas_call(
        kernel,
        grid_spec=pltpu.PrefetchScalarGridSpec(
            num_scalar_prefetch=1,
            grid=(geo.T,),
            in_specs=[
                whole((n, d)),
                pl.BlockSpec((1, 1, w), lambda j, s: (j, 0, 0)),
                *wt.specs(),
            ],
            out_specs=[out, out],
            scratch_shapes=wt.scratch(),
        ),
        out_shape=[jax.ShapeDtypeStruct((geo.T, n, w), BF)] * 2,
        compiler_params=params(),
        cost_estimate=cost(2 * n * d * w * geo.T, 2 * geo.T * w * (d + 2 * n)),
        name="up_proj",
    )(scal, h, bias, *wt.arrays)


def down_proj(scal, hidden, resid, cot, mod, bias, wt, geo):
    _, n, w = hidden.shape
    d = geo.D
    nw = len(wt.arrays)

    late = Late(resid, cot)

    def kernel(s, y_ref, m_ref, b_ref, *refs):
        late_in, refs = refs[:2], refs[2:]
        w_refs, (out_ref, sum_ref, wbuf, sem, acc, *late_buf) = refs[:nw], refs[nw:]
        j = pl.program_id(0)
        late.start(j, late_in, late_buf)
        now = wt.stream(j, s, w_refs, wbuf, sem)
        part = dotg(y_ref[0], now[...], 1, 1)

        @pl.when(j == 0)
        def _():
            acc[...] = part
            sum_ref[...] = jnp.zeros_like(sum_ref)

        @pl.when(j > 0)
        def _():
            acc[...] += part

        @pl.when(j == geo.T - 1)
        def _():
            r_ref, c_ref = late.wait(late_in, late_buf)

            @pl.loop(0, n // ROWS, unroll=4)
            def _(i):
                at = pl.ds(pl.multiple_of(i * ROWS, ROWS), ROWS)
                ffn = acc[at, :] + b_ref[...]
                out_ref[at, :] = (r_ref[at, :] + m_ref[5:6, :] * ffn).astype(BF)
                sum_ref[...] += fold_rows(c_ref[at, :].astype(F32) * ffn)

    return pl.pallas_call(
        kernel,
        grid_spec=pltpu.PrefetchScalarGridSpec(
            num_scalar_prefetch=1,
            grid=(geo.T,),
            in_specs=[
                pl.BlockSpec((1, n, w), lambda j, s: (j, 0, 0)),
                whole(mod.shape),
                whole((1, d)),
                *late.specs,
                *wt.specs(),
            ],
            out_specs=[whole((n, d)), whole((8, d))],
            scratch_shapes=[*wt.scratch(), pltpu.VMEM((n, d), F32), *late.scratch],
        ),
        out_shape=[jax.ShapeDtypeStruct((n, d), BF), jax.ShapeDtypeStruct((8, d), F32)],
        compiler_params=params(),
        cost_estimate=cost(2 * n * d * w * geo.T, 2 * geo.T * w * (d + n) + 8 * n * d),
        name="down_proj",
    )(scal, hidden, mod, bias, *late.arrays, *wt.arrays)


def pre_back(scal, g, gp, wt, geo):
    n, d = g.shape
    w = wt.width
    nw = len(wt.arrays)

    def kernel(s, g_ref, gp_ref, *refs):
        w_refs, (out_ref, sum_ref, wbuf, sem) = refs[:nw], refs[nw:]
        j = pl.program_id(0)
        now = wt.stream(j, s, w_refs, wbuf, sem)
        for cols in pieces(w):
            y = dotg(g_ref[...], now[:, cols], 1, 0) * gp_ref[0, :, cols].astype(F32)
            out_ref[0, :, cols] = y.astype(BF)
            sum_ref[0, :, cols] = jnp.sum(y, axis=0, keepdims=True)

    out = pl.BlockSpec((1, n, w), lambda j, s: (j, 0, 0))
    return pl.pallas_call(
        kernel,
        grid_spec=pltpu.PrefetchScalarGridSpec(
            num_scalar_prefetch=1,
            grid=(geo.T,),
            in_specs=[whole((n, d)), out, *wt.specs()],
            out_specs=[out, pl.BlockSpec((1, 1, w), lambda j, s: (j, 0, 0))],
            scratch_shapes=wt.scratch(),
        ),
        out_shape=[
            jax.ShapeDtypeStruct((geo.T, n, w), BF),
            jax.ShapeDtypeStruct((geo.T, 1, w), F32),
        ],
        compiler_params=params(),
        cost_estimate=cost(2 * n * d * w * geo.T, 2 * geo.T * w * (d + 2 * n)),
        name="pre_back",
    )(scal, g, gp, *wt.arrays)


def second_back(scal, pre, resid, attn, cot, mod, wt, geo):
    _, n, w = pre.shape
    d = geo.D
    nw = len(wt.arrays)

    late = Late(resid, attn, cot)

    def kernel(s, y_ref, m_ref, *refs):
        late_in, refs = refs[:3], refs[3:]
        w_refs, (rg_ref, ag_ref, sum_ref, wbuf, sem, acc, *late_buf) = refs[:nw], refs[nw:]
        j = pl.program_id(0)
        late.start(j, late_in, late_buf)
        now = wt.stream(j, s, w_refs, wbuf, sem)
        part = dotg(y_ref[0], now[...], 1, 1)

        @pl.when(j == 0)
        def _():
            acc[...] = part
            sum_ref[...] = jnp.zeros_like(sum_ref)

        @pl.when(j > 0)
        def _():
            acc[...] += part

        @pl.when(j == geo.T - 1)
        def _():
            r_ref, a_ref, c_ref = late.wait(late_in, late_buf)

            @pl.loop(0, n // ROWS, unroll=4)
            def _(i):
                at = pl.ds(pl.multiple_of(i * ROWS, ROWS), ROWS)
                g = acc[at, :]
                norm, inv = norm_of(r_ref[at, :])
                rg = c_ref[at, :].astype(F32) + norm_back(norm, inv, g * (1.0 + m_ref[4:5, :]))
                rg_ref[at, :] = rg
                ag = rg * m_ref[2:3, :]
                ag_ref[at, :] = ag.astype(BF)
                sum_ref[0] += fold_rows(rg * a_ref[at, :].astype(F32))
                sum_ref[1] += fold_rows(g)
                sum_ref[2] += fold_rows(g * norm)
                sum_ref[3] += fold_rows(ag)

    return pl.pallas_call(
        kernel,
        grid_spec=pltpu.PrefetchScalarGridSpec(
            num_scalar_prefetch=1,
            grid=(geo.T,),
            in_specs=[
                pl.BlockSpec((1, n, w), lambda j, s: (j, 0, 0)),
                whole(mod.shape),
                *late.specs,
                *wt.specs(),
            ],
            out_specs=[whole((n, d)), whole((n, d)), whole((4, 8, d))],
            scratch_shapes=[*wt.scratch(), pltpu.VMEM((n, d), F32), *late.scratch],
        ),
        out_shape=[
            jax.ShapeDtypeStruct((n, d), F32),
            jax.ShapeDtypeStruct((n, d), BF),
            jax.ShapeDtypeStruct((4, 8, d), F32),
        ],
        compiler_params=params(),
        cost_estimate=cost(2 * n * d * w * geo.T, 2 * geo.T * w * (d + n) + 18 * n * d),
        name="second_back",
    )(scal, pre, mod, *late.arrays, *wt.arrays)


def mixed_back(scal, g, wt, geo):
    n, d = g.shape
    win = geo.win
    nw = len(wt.arrays)

    def kernel(s, g_ref, *refs):
        w_refs, (out_ref, wbuf, sem) = refs[:nw], refs[nw:]
        now = wt.stream(pl.program_id(0), s, w_refs, wbuf, sem)
        out_ref[0] = dotg(g_ref[...], now[:, -win:], 1, 0).astype(BF)

    return pl.pallas_call(
        kernel,
        grid_spec=pltpu.PrefetchScalarGridSpec(
            num_scalar_prefetch=1,
            grid=(geo.T,),
            in_specs=[whole((n, d)), *wt.specs()],
            out_specs=pl.BlockSpec((1, n, win), lambda j, s: (j, 0, 0)),
            scratch_shapes=wt.scratch(geo.base, 4 * geo.w),
        ),
        out_shape=jax.ShapeDtypeStruct((geo.T, n, win), BF),
        compiler_params=params(),
        cost_estimate=cost(2 * n * d * d, 8 * d * d + 4 * n * d),
        name="mixed_back",
    )(scal, g, *wt.arrays)


def first_back(scal, tri, got, x, rg, mod, wt, geo):
    _, n, n3 = tri[0].shape
    d = geo.D
    nw = len(wt.arrays)
    th = geo.Th

    late = Late(x, rg)

    def kernel(s, ta, tb, ga, gb, m_ref, *refs):
        late_in, refs = refs[:2], refs[2:]
        w_refs, (out_ref, sum_ref, wbuf, sem, lhs, acc, *late_buf) = refs[:nw], refs[nw:]
        j = pl.program_id(0)
        late.start(j, late_in, late_buf)
        now = wt.stream(j, s, w_refs, wbuf, sem)
        for half, (tri_ref, got_ref) in enumerate(((ta, ga), (tb, gb))):

            @pl.when((j < th) if half == 0 else (j >= th))
            def _():
                lhs[...] = triple_grad(tri_ref, got_ref, geo)

        part = dotg(lhs[...], now[:, :n3], 1, 1)

        @pl.when(j == 0)
        def _():
            acc[...] = part
            sum_ref[...] = jnp.zeros_like(sum_ref)

        @pl.when(j > 0)
        def _():
            acc[...] += part

        @pl.when(j == geo.T - 1)
        def _():
            x_ref, r_ref = late.wait(late_in, late_buf)

            @pl.loop(0, n // ROWS, unroll=4)
            def _(i):
                at = pl.ds(pl.multiple_of(i * ROWS, ROWS), ROWS)
                g = acc[at, :]
                norm, inv = norm_of(x_ref[at, :].astype(F32))
                back = norm_back(norm, inv, g * (1.0 + m_ref[1:2, :]))
                out_ref[at, :] = (r_ref[at, :] + back).astype(BF)
                sum_ref[0] += fold_rows(g)
                sum_ref[1] += fold_rows(g * norm)

    return pl.pallas_call(
        kernel,
        grid_spec=pltpu.PrefetchScalarGridSpec(
            num_scalar_prefetch=1,
            grid=(geo.T,),
            in_specs=[
                *two_halves((1, n, n3), th, (0, 0)),
                *two_halves((1, n, geo.kvw), th, (0, 0)),
                whole(mod.shape),
                *late.specs,
                *wt.specs(),
            ],
            out_specs=[whole((n, d)), whole((2, 8, d))],
            scratch_shapes=[
                *wt.scratch(0, n3),
                pltpu.VMEM((n, n3), BF),
                pltpu.VMEM((n, d), F32),
                *late.scratch,
            ],
        ),
        out_shape=[jax.ShapeDtypeStruct((n, d), BF), jax.ShapeDtypeStruct((2, 8, d), F32)],
        compiler_params=params(),
        cost_estimate=cost(6 * n * d * d, 8 * d * d + 16 * n * d),
        name="first_back",
    )(scal, *tri, *got, mod, *late.arrays, *wt.arrays)


def weight_grad(scal, terms, join, w, mine, geo, name, partial=None):
    n = terms[0][1][0].shape[-2] if not isinstance(terms[0][1][0], tuple) else terms[0][1][0][0].shape[-2]
    pr = geo.P * geo.R
    th = geo.Th
    half_n = geo.P // 2
    want = scal[1] if mine else 1 - scal[1]
    lefts = [term[0] for term in terms]
    if not geo.direct:
        lefts = [a[:n] for a in lefts]
    if not geo.direct:

        def pick(a):
            cols = a.reshape(n, geo.P, 2, geo.R)
            cols = jnp.where(want == 0, cols[:, :, 0], cols[:, :, 1])
            return cols.reshape(n, pr).T

        lefts = [pick(a) for a in lefts]
    ops, op_specs, counts = [], [], []
    for _, operands, _ in terms:
        counts.append(len(operands))
        for pair in operands:
            if isinstance(pair, tuple):
                tail = (0,) * (pair[0].ndim - 1)
                op_specs += two_halves((1,) + pair[0].shape[1:], th, tail)
                ops += pair
            else:
                op_specs.append(pl.BlockSpec((1,) + pair.shape[1:], lambda j, s: (j, 0, 0)))
                ops.append(pair)
    na, nb = len(lefts), len(ops)

    def kernel(s, *refs):
        a_refs, b_refs = refs[:na], refs[na : na + nb]
        rest = refs[na + nb :]
        got_ref = None
        if mine:
            got_ref, rest = rest[0], rest[1:]
        n_out = 4 if (mine and geo.direct) else 1
        outs, ats = rest[:n_out], rest[n_out:]
        j = pl.program_id(0)
        if geo.direct:

            @pl.when(j == 0)
            def _():
                pick_odd = (s[1] == 1) if mine else (s[1] == 0)
                for ref, at in zip(a_refs, ats):
                    flip = ref[...].T
                    for p in range(geo.P):
                        even = flip[2 * p * geo.R : (2 * p + 1) * geo.R]
                        odd = flip[(2 * p + 1) * geo.R : (2 * p + 2) * geo.R]
                        row = pl.multiple_of((s[0] ^ p) * geo.R, geo.R)
                        at[pl.ds(row, geo.R), :] = jnp.where(pick_odd, odd, even)
        else:
            ats = a_refs

        def store(half):
            at_op, parts = 0, []
            for at, (_, operands, build) in zip(ats, terms):
                blocks = []
                for pair in operands:
                    if isinstance(pair, tuple):
                        blocks.append(b_refs[at_op + half])
                        at_op += 2
                    else:
                        blocks.append(b_refs[at_op])
                        at_op += 1
                parts.append(dotg(at[...], build(*blocks), 1, 0))
            full = join(*parts)
            if not geo.direct:
                if mine:
                    full = full + got_ref[0, 0].astype(F32)
                outs[0][0, 0] = full.astype(BF)
                return
            if not mine:
                for rel in range(geo.P):
                    outs[0][0, rel] = full[rel * geo.R : (rel + 1) * geo.R].astype(BF)
                return
            for i, rel in enumerate(geo.order[half]):
                part = full[rel * geo.R : (rel + 1) * geo.R] + got_ref[0, rel].astype(F32)
                outs[2 * half + i // half_n][i % half_n, 0] = part.astype(BF)

        for half in range(2):

            @pl.when((j < th) if half == 0 else (j >= th))
            def _():
                store(half)

    in_specs = [whole((n, a.shape[1])) if geo.direct else whole(a.shape) for a in lefts] + op_specs
    rel_block = (1, geo.P, geo.R, w) if geo.direct else (1, 1, pr, w)
    rel_spec = pl.BlockSpec(rel_block, lambda j, s: (j, 0, 0, 0))
    rel_shape = jax.ShapeDtypeStruct((geo.T,) + rel_block[1:], BF)
    args = [*lefts, *ops]
    out_specs, shapes = [rel_spec], [rel_shape]
    if mine:
        in_specs.append(rel_spec)
        args.append(partial)
        if geo.direct:
            block = (half_n, 1, geo.R, w)
            first = pl.BlockSpec(block, lambda j, s: (0, jnp.minimum(j, th - 1), 0, 0))
            second = pl.BlockSpec(block, lambda j, s: (0, jnp.maximum(j - th, 0), 0, 0))
            out_specs = [first, first, second, second]
            shapes = [jax.ShapeDtypeStruct((half_n, th, geo.R, w), BF)] * 4
    scratch = [pltpu.VMEM((pr, n), BF)] * na if geo.direct else []
    got = pl.pallas_call(
        kernel,
        grid_spec=pltpu.PrefetchScalarGridSpec(
            num_scalar_prefetch=1,
            grid=(geo.T,),
            in_specs=in_specs,
            out_specs=out_specs,
            scratch_shapes=scratch,
        ),
        out_shape=shapes,
        compiler_params=params(62 << 20),
        cost_estimate=cost(2 * pr * n * w * geo.T, 2 * geo.T * w * (2 * pr + n)),
        name=name,
    )(scal, *args)
    if not mine:
        return got[0]
    if geo.direct:
        return got
    blocks = got[0].reshape(geo.T, geo.P, geo.R, w)
    out = []
    for half in range(2):
        part = blocks[half * th : (half + 1) * th]
        part = reorder(part, [scal[0] ^ rel for rel in geo.order[half]], 1)
        part = part.transpose(1, 0, 2, 3)
        out += [part[:half_n], part[half_n:]]
    return out


def body(
    latents,
    conditioning,
    mod_weight,
    mod_bias,
    in_weight,
    query_value_bias,
    out_weight,
    branch_bias,
    up_weight,
    up_bias,
    down_weight,
    cotangent,
):
    images, row_count, width = latents.shape
    geo = Geo(lax.axis_size("fsdp"), lax.axis_size("tensor"), width)
    F, T = geo.F, geo.T
    assert 2 * images == T
    highest = lax.Precision.HIGHEST
    fi = lax.axis_index("fsdp")
    ti = lax.axis_index("tensor")
    pair, core = fi // 2, fi % 2
    scal = jnp.stack([pair, core, ti]).astype(jnp.int32)
    cols = in_weight.shape[2]
    units = up_weight.shape[1]
    geo.windows(cols)

    def places(k):
        return [
            ((2 * p + c) * T + t, (2 * p + t // images) * T + c * images + (t % images + k) % images)
            for p in range(geo.P)
            for c in range(2)
            for t in range(T)
        ]

    def to_chip(arr):
        got = []
        for k in range(images):
            item = lax.dynamic_index_in_dim(arr, (ti + k) % images, 0, keepdims=False)
            got.append(lax.ppermute(item, BOTH, places(k)))
        return got

    def from_chip(arr):
        got = []
        for k in range(images):
            back = [(dst, src) for src, dst in places(k)]
            got.append(lax.ppermute(arr[k * row_count : (k + 1) * row_count], BOTH, back))
        return got

    def home(parts):
        return reorder(jnp.stack(parts), [(i - ti) % images for i in range(images)])

    def share(arr):
        sent = jnp.broadcast_to(arr[None], (F * T,) + arr.shape)
        return lax.all_to_all(sent, BOTH, 0, 0, tiled=True)

    now, opened = (), []

    def tie(value):
        return after(value, *now)

    def start(*chains):
        for way in chains:
            opened.extend(way.advance(*now))

    def begin(shard, make, *how):
        way = Chain(make(tie(shard), geo, *how))
        opened.extend(way.flight)
        return way

    def across(value):
        got = flip_core(tie(value), geo)
        opened.append(got)
        return got

    def close(*made):
        nonlocal now
        now = (*opened, *made)
        opened.clear()

    heads = cols // HEAD_DIM
    attn_shard = jnp.concatenate([in_weight[0], in_weight[1], in_weight[2], out_weight.T], axis=1)
    attn_way = begin(attn_shard, gather_steps, False)
    cond_all = after(conditioning, attn_shard)[None]
    bit = 1
    while bit < F:
        got = lax.ppermute(cond_all, "fsdp", [(i, i ^ bit) for i in range(F)])
        cond_all = jnp.concatenate([cond_all, got])
        bit *= 2
    cond_all = reorder(cond_all, [fi ^ f for f in range(F)]).reshape(F * images, width)
    silu_low = jax.nn.silu(cond_all.astype(F32)).astype(BF)
    silu_own = lax.dynamic_slice_in_dim(silu_low, fi * geo.R, geo.R, 1)
    mod_part = jnp.einsum("bd,dcj->bcj", silu_own, mod_weight, preferred_element_type=F32)
    bias_rows = jnp.concatenate([mod_bias, query_value_bias]).astype(F32)
    bias_rows = jnp.where(fi == 0, bias_rows, 0.0)
    mod_part = jnp.pad(mod_part, ((0, 0), (0, 2), (0, 0))) + bias_rows
    mod_part = mod_part.reshape(geo.P, 1, T, 8, cols)
    mod_part = jnp.broadcast_to(mod_part, (geo.P, 2, T, 8, cols)).reshape(F * T, 8, cols)
    close()
    start(attn_way)
    up_way = begin(up_weight, gather_steps, True, True)
    mod_part = lax.all_to_all(mod_part, BOTH, 0, 0, tiled=True)
    mod_part = mod_part.reshape(F, T, 8, cols).sum(axis=0)
    mod = mod_part[:, :6].transpose(1, 0, 2).reshape(6, width)
    qv_bias = mod_part[:, 6:]
    triple_bias = jnp.concatenate(
        [
            qv_bias[:, :1],
            jnp.zeros_like(qv_bias[:, :1]),
            qv_bias[:, 1:],
            jnp.zeros((T, 1, geo.n3 - 3 * cols), F32),
        ],
        axis=2,
    )
    bias_rows = branch_bias.astype(F32)
    close(mod)
    start(attn_way)
    x_parts = to_chip(tie(latents))
    opened.extend(x_parts)
    close()
    x = jnp.concatenate([*x_parts, jnp.zeros((ROWS, width), BF)])
    start(attn_way, up_way)
    h1 = norm_mod(tie(x), mod)
    close(h1)
    w_attn = Gathered(attn_way.finish(*now), geo, scal)
    start(up_way)

    q, kv, kvo = [None] * 2, [None] * 2, [None] * 2
    mixed, lse = [None] * 2, [None] * 2
    extras = []
    down_shard = jnp.concatenate(
        [down_weight.T, jnp.broadcast_to(up_bias, (16, units))]
    )
    down_way = begin(down_shard, gather_steps, True, False, extras)
    for half in range(2):
        q[half], kv[half] = in_proj(tie(scal), h1, w_attn, triple_bias, half, geo)
    close(q[0], q[1])
    kvo = [across(kv[0]), across(kv[1])]
    close()
    start(up_way, down_way)
    for half in range(2):
        mixed[half], lse[half] = attn_fwd(tie(q[half]), kv[half], kvo[half], geo)
    close(lse[0], lse[1])
    start(up_way, down_way)
    attn, resid, h2 = out_proj(tie(scal), mixed, x, mod, bias_rows[0:1], w_attn, geo)
    close(h2)
    w_up = Gathered(up_way.finish(*now), geo, scal)
    start(down_way)
    cot_parts = to_chip(tie(cotangent))
    opened.extend(cot_parts)
    unit_bias = jnp.stack([part[:1] for part in extras]).astype(F32)
    hidden, gp = up_proj(tie(scal), h2, unit_bias, w_up, geo)
    close(hidden)
    start(down_way)
    cot = jnp.concatenate(cot_parts)
    ffn_grad = (cot.astype(F32) * mod[5]).astype(BF)

    def block(ref):
        return ref[0]

    def alone(part):
        return part

    down_terms = [(ffn_grad, [hidden], block)]
    down_half = weight_grad(tie(scal), down_terms, alone, units, False, geo, "w_down_send")
    close(down_half)
    w_down = Gathered(down_way.finish(*now), geo, scal)
    down_got = across(down_half)
    block_rows, ffn_sums = down_proj(
        tie(scal), hidden, resid, cot, mod, bias_rows[1:2], w_down, geo
    )
    close(ffn_sums)

    down_parts = weight_grad(tie(scal), down_terms, alone, units, True, geo, "w_down", down_got)
    close(*down_parts)
    down_back = begin(down_parts, scatter_steps)
    block_back = from_chip(tie(block_rows))
    opened.extend(block_back)
    pre, unit_sum = pre_back(tie(scal), ffn_grad, gp, w_down, geo)
    up_terms = [(h2, [pre], block)]
    up_half = weight_grad(tie(scal), up_terms, alone, units, False, geo, "w_up_send")
    close(up_half)
    start(down_back)
    up_got = across(up_half)
    rg, ag, mid_sums = second_back(tie(scal), pre, resid, attn, cot, mod, w_up, geo)
    close(ag)
    start(down_back)
    up_parts = weight_grad(tie(scal), up_terms, alone, units, True, geo, "w_up", up_got)
    mg = mixed_back(tie(scal), ag, w_attn, geo)
    close(mg, *up_parts)
    start(down_back)
    up_back = begin(up_parts, scatter_steps)
    tri, tri_send, tri_sums, send_sums = [None] * 2, [None] * 2, [None] * 2, [None] * 2
    for half in range(2):
        tri[half], tri_send[half], tri_sums[half], send_sums[half] = attn_bwd(
            tie(q[half]), kv[half], kvo[half], mixed[half], mg, lse[half], half * geo.Th, geo
        )
    close(*tri_sums)
    tri_got = [across(tri_send[0]), across(tri_send[1])]
    ffn_sum = jnp.sum(tie(ffn_grad).astype(F32), axis=0)
    tri_sum, send_sum = jnp.concatenate(tri_sums), jnp.concatenate(send_sums)
    pair_sums = jnp.concatenate(
        [
            tri_sum[:, :, :cols],
            tri_sum[:, :, 2 * cols : 3 * cols]
            + send_sum[:, :, geo.koff + cols : geo.koff + 2 * cols],
        ],
        axis=1,
    )
    close()
    start(up_back)
    down_back.finish(*now)

    def beside(first, second):
        shared = geo.n3 - geo.base
        middle = first[:, geo.base :] + second[:, :shared]
        return jnp.concatenate([first[:, : geo.base], middle, second[:, shared:]], axis=1)

    attn_terms = [
        (h1, [tuple(tri), tuple(tri_got)], lambda a, b: triple_grad(a, b, geo)),
        (ag, [tuple(mixed)], block),
    ]
    attn_half = weight_grad(tie(scal), attn_terms, beside, 4 * cols, False, geo, "w_attn_send")
    close(attn_half)
    start(up_back)
    attn_got = across(attn_half)
    latent_rows, first_sums = first_back(tie(scal), tri, tri_got, x, rg, mod, w_attn, geo)
    close(first_sums)
    start(up_back)
    mine = [i ^ ti for i in range(T)]
    rows = jnp.concatenate(
        [first_sums.sum(axis=1), mid_sums[:3].sum(axis=1), ffn_sums.sum(axis=0, keepdims=True)]
    )
    rows = tie(rows).reshape(6, T, cols).transpose(1, 0, 2).reshape(T, 6 * cols)
    branch_sums = jnp.stack([mid_sums[3].sum(axis=0), ffn_sum]).reshape(F, T, -1)
    unit_sums = reorder(unit_sum, mine).reshape(T, F, units // F).transpose(1, 0, 2)
    pair_sums = reorder(pair_sums, mine).reshape(T, F, 2 * cols // F).transpose(1, 0, 2)
    rows = jnp.broadcast_to(rows[None], (F,) + rows.shape)
    pack = jnp.concatenate([rows, branch_sums, unit_sums, pair_sums], axis=2)
    count = pack.shape[2]
    pack = jnp.pad(pack, ((0, 0), (0, 0), (0, -count % 1024))).reshape(F * T, -1, 128)
    pack = lax.all_to_all(pack, BOTH, 0, 0, tiled=True)
    attn_parts = weight_grad(
        tie(scal), attn_terms, beside, 4 * cols, True, geo, "w_attn", attn_got
    )
    close(pack, *attn_parts)
    attn_back = begin(attn_parts, scatter_steps, False)
    block_back = [tie(part) for part in block_back]
    down_shard = tie(down_back.finish())
    latent_back = from_chip(tie(latent_rows))
    opened.extend(latent_back)
    pack = tie(pack)
    slices = pack.sum(axis=0).reshape(-1)[6 * cols : count]
    tiles = -(-6 * cols // 128)
    mine_rows = pack[:, :tiles].reshape(geo.P, 2, T, tiles, 128).sum(axis=1)
    mine_rows = mine_rows.reshape(F * images, -1)[:, : 6 * cols].reshape(F * images, 6, cols)
    cond_part = jnp.einsum("bcj,dcj->bd", mine_rows, mod_weight.astype(F32), precision=highest)
    cond_part = cond_part.reshape(F, 1, images * geo.R)
    cond_part = jnp.broadcast_to(cond_part, (F, T, images * geo.R))
    kept = jnp.broadcast_to(slices[None, None], (F, T) + slices.shape)
    final = jnp.concatenate([cond_part, kept], axis=2).reshape(F * T, -1)
    final = jnp.pad(final, ((0, 0), (0, -final.shape[1] % 1024))).reshape(F * T, -1, 128)
    final = lax.all_to_all(final, BOTH, 0, 0, tiled=True)
    close(final)
    start(attn_back)
    close()
    start(attn_back)
    block_out, latent_grad = home(block_back), home(latent_back)
    down_grad, up_grad = down_shard, up_back.finish(*now)
    attn_grad = attn_back.finish(*now)
    in_grad = attn_grad[:, : 3 * cols].reshape(geo.R, 3, cols).transpose(1, 0, 2)

    final = final.reshape(F, T, -1)
    at = images * geo.R
    cond_mine = final[:, :, :at].sum(axis=1).reshape(F, images, geo.R)
    step = 2 * width // (F * T)
    branch_grad = final[:, :, at : at + step].reshape(2, width)
    own = lax.dynamic_index_in_dim(final, ti, 1, keepdims=False)
    at += step
    unit_grad = own[:, at : at + units // F].reshape(units)
    at += units // F
    pair_grad = own[:, at : at + 2 * cols // F].reshape(2, cols)
    mod_weight_grad = jnp.einsum("bd,bcj->dcj", silu_own.astype(F32), mine_rows, precision=highest)
    mod_bias_grad = mine_rows.sum(axis=0)
    silu_grad = cond_mine.transpose(1, 0, 2).reshape(images, width)
    cond_f = conditioning.astype(F32)
    sig = jax.nn.sigmoid(cond_f)
    cond_grad = silu_grad * (sig * (1.0 + cond_f * (1.0 - sig)))

    return (
        block_out,
        latent_grad,
        cond_grad,
        mod_weight_grad,
        mod_bias_grad,
        in_grad,
        pair_grad,
        attn_grad[:, 3 * cols :].T,
        branch_grad,
        up_grad,
        unit_grad,
        down_grad.T,
    )


def solution(mesh):
    in_specs = (
        P("fsdp", "tensor", None),
        P("fsdp", None),
        P("fsdp", None, "tensor"),
        P(None, "tensor"),
        P(None, "fsdp", "tensor"),
        P(None, "tensor"),
        P("tensor", "fsdp"),
        P(),
        P("fsdp", "tensor"),
        P("tensor"),
        P("tensor", "fsdp"),
        P("fsdp", "tensor", None),
    )
    out_specs = (
        P("fsdp", "tensor", None),
        P("fsdp", "tensor", None),
        P("fsdp", None),
        P("fsdp", None, "tensor"),
        P(None, "tensor"),
        P(None, "fsdp", "tensor"),
        P(None, "tensor"),
        P("tensor", "fsdp"),
        P(),
        P("fsdp", "tensor"),
        P("tensor"),
        P("tensor", "fsdp"),
    )
    return jax.shard_map(body, mesh=mesh, in_specs=in_specs, out_specs=out_specs, check_vma=False)
```

```python
import functools

import jax
import jax.numpy as jnp
from jax import lax
from jax.experimental import pallas as pl
from jax.experimental.pallas import tpu as pltpu
from jax.sharding import PartitionSpec as P

HEAD_DIM = 72
EPS = 1e-06
TANH_C = 0.7978845608028654
CUBIC = 0.044715
LOG2E = 1.4426950408889634
VMEM_BYTES = 56 << 20
ROWS = 32
BF = jnp.bfloat16
F32 = jnp.float32
BOTH = ("fsdp", "tensor")


def dotg(a, b, ca, cb):
    return lax.dot_general(a, b, (((ca,), (cb,)), ((), ())), preferred_element_type=F32)


class Geo:
    def __init__(self, fsdp, tensor, dim):
        self.F, self.T, self.P = fsdp, tensor, fsdp // 2
        self.Th = tensor // 2
        self.D = dim
        self.R = dim // fsdp
        self.bits = [1 << b for b in range((self.P - 1).bit_length())]
        self.order = (self.orders(self.bits[::-1]), self.orders(self.bits))
        self.direct = self.R % 16 == 0

    def windows(self, w):
        self.w = w
        self.n3 = min(padded(3 * w), 4 * w)
        self.kbase = w // 128 * 128
        self.koff = w - self.kbase
        self.kvw = self.n3 - self.kbase
        self.base = 3 * w // 128 * 128
        self.off = 3 * w - self.base
        self.win = 4 * w - self.base

    @staticmethod
    def orders(msb_first):
        vals = [0]
        for bit in reversed(msb_first):
            vals = vals + [v | bit for v in vals]
        return vals


def reorder(x, index, axis=0):
    return jnp.stack([lax.dynamic_index_in_dim(x, i, axis, keepdims=False) for i in index], axis)


def flip_pair(x, bit, geo):
    return lax.ppermute(x, "fsdp", [(i, i ^ (2 * bit)) for i in range(geo.F)])


def flip_core(x, geo):
    return lax.ppermute(x, "fsdp", [(i, i ^ 1) for i in range(geo.F)])


def flip_tensor(x, k, geo):
    return lax.ppermute(x, "tensor", [(i, i ^ k) for i in range(geo.T)])


def after(value, *done):
    return lax.optimization_barrier((value, done))[0] if done else value


class Chain:
    def __init__(self, steps):
        self.steps = steps
        self.flight = next(steps)
        self.result = None

    def advance(self, *done):
        if self.result is not None:
            return []
        try:
            self.flight = self.steps.send(after(self.flight, *done))
        except StopIteration as end:
            self.flight, self.result = [], end.value
        return self.flight

    def finish(self, *done):
        while self.result is None:
            self.advance(*done)
        return self.result


def gather_steps(shard, geo, parted=True, joined=False, extras=None):
    if parted:
        late = [geo.Th] if extras is None else list(range(1, geo.Th + 1))
        most = [k for k in range(1, geo.T) if k not in late]
        got = dict(zip(most, (yield [flip_tensor(shard, k, geo) for k in most])))
        got.update(zip(late, (yield [flip_tensor(shard, k, geo) for k in late])))
        parts = [shard] + [got[k] for k in range(1, geo.T)]
    else:
        got = yield [flip_tensor(shard, k, geo) for k in range(1, geo.T)]
        parts = [shard] + got
    if extras is not None:
        extras += [part[geo.R :] for part in parts]
        parts = [part[: geo.R] for part in parts]
    bufs = [jnp.stack(parts[h * geo.Th : (h + 1) * geo.Th])[None] for h in range(2)]
    for at in range(len(geo.bits)):
        bits = (geo.bits[at], geo.bits[-1 - at])
        got = yield [flip_pair(bufs[h], bits[h], geo) for h in range(2)]
        if joined or at < len(geo.bits) - 1:
            bufs = [jnp.concatenate(pair) for pair in zip(bufs, got)]
    owns = [[buf] for buf in bufs] if joined else [list(pair) for pair in zip(bufs, got)]
    count = len(owns[0])
    others = yield [flip_core(a, geo) for own in owns for a in own]
    return [owns[h] + others[h * count : (h + 1) * count] for h in range(2)]


class Gathered:
    def __init__(self, halves, geo, scal):
        self.geo = geo
        if not geo.direct:
            fixed = []
            for half, arrays in enumerate(halves):
                at = [geo.order[half].index(rel) for rel in range(geo.P)]
                lookup = jnp.array(at, jnp.int32)
                blocks = jnp.concatenate(arrays)
                blocks = reorder(
                    blocks,
                    [
                        lookup[(f // 2) ^ scal[0]] + geo.P * ((f % 2) ^ scal[1])
                        for f in range(geo.F)
                    ],
                )
                _, th, r, w = blocks.shape
                fixed.append([blocks.transpose(1, 0, 2, 3).reshape(1, th, geo.D, w)])
            halves = fixed
        self.halves = halves
        self.arrays = halves[0] + halves[1]
        self.n = len(halves[0])
        self.width = self.arrays[0].shape[-1]

    def operands(self, half=None):
        return self.arrays if half is None else self.halves[half]

    def specs(self, half=None):
        return [pl.BlockSpec(memory_space=pl.ANY)] * len(self.operands(half))

    def scratch(self, lo=0, hi=None):
        hi = self.width if hi is None else hi
        if lo % 128 or hi % 128:
            lo, hi = 0, self.width
        self.lo, self.hi = lo, hi
        count = self.n * self.arrays[0].shape[0]
        return [
            pltpu.VMEM((2, self.geo.D, hi - lo), BF),
            pltpu.SemaphoreType.DMA((2, count)),
        ]

    def copies(self, group, slot, half, s_ref, refs, buf, sem):
        geo, out = self.geo, []
        for at, ref in enumerate(refs):
            n, _, rows, _ = ref.shape
            for i in range(n):
                row = 0
                if geo.direct:
                    place = at * n + i
                    rel = geo.order[half][place % geo.P]
                    row = 2 * (s_ref[0] ^ rel) + (s_ref[1] ^ (place // geo.P))
                    row = pl.multiple_of(row * rows, rows)
                out.append(
                    pltpu.make_async_copy(
                        ref.at[i, group, :, pl.ds(self.lo, self.hi - self.lo)],
                        buf.at[slot, pl.ds(row, rows), :],
                        sem.at[slot, at * n + i],
                    )
                )
        return out

    def stream(self, j, s_ref, refs, buf, sem, half=None):
        th = self.geo.Th

        def each(step, act):
            if half is not None:
                for copy in self.copies(step, step % 2, half, s_ref, refs, buf, sem):
                    act(copy)
                return
            for part in range(2):

                @pl.when((step < th) if part == 0 else (step >= th))
                def _():
                    mine = refs[part * self.n : (part + 1) * self.n]
                    for copy in self.copies(
                        step - part * th, step % 2, part, s_ref, mine, buf, sem
                    ):
                        act(copy)

        @pl.when(j == 0)
        def _():
            each(j, lambda copy: copy.start(priority=1))

        @pl.when(j + 1 < (self.geo.T if half is None else th))
        def _():
            each(j + 1, lambda copy: copy.start(priority=1))

        each(j, lambda copy: copy.wait())
        return buf.at[j % 2]


def scatter_steps(pieces, geo, parted=True):
    def add(a, b):
        return a.astype(F32) + b.astype(F32)

    keeps, sends = [pieces[0], pieces[2]], [pieces[1], pieces[3]]
    for at in range(len(geo.bits)):
        bits = (geo.bits[-1 - at], geo.bits[at])
        got = yield [flip_pair(sends[h], bits[h], geo) for h in range(2)]
        m = max(1, keeps[0].shape[0] // 2)
        if at < len(geo.bits) - 1:
            sends = [add(keeps[h][m:], got[h][m:]).astype(BF) for h in range(2)]
        keeps = [add(keeps[h][:m], got[h][:m]).astype(BF) for h in range(2)]
    units = [keep[0, k] for keep in keeps for k in range(geo.Th)]
    if parted:
        rest = [k for k in range(1, geo.T) if k != geo.Th]
        got = yield [flip_tensor(units[k], k, geo) for k in rest]
        got += yield [flip_tensor(units[geo.Th], geo.Th, geo)]
    else:
        got = yield [flip_tensor(units[k], k, geo) for k in range(1, geo.T)]
    total = units[0].astype(F32)
    for part in got:
        total = total + part.astype(F32)
    return total


def params(size=VMEM_BYTES):
    return pltpu.CompilerParams(vmem_limit_bytes=size)


def cost(flops, size):
    return pl.CostEstimate(flops=int(flops), bytes_accessed=int(size), transcendentals=0)


def whole(shape):
    zeros = (0,) * len(shape)
    return pl.BlockSpec(shape, lambda j, s: zeros)


def padded(w):
    return -(-w // 128) * 128


def pieces(total):
    step = 512 if total % 128 == 0 else total
    return [slice(at, min(at + step, total)) for at in range(0, total, step)]


def norm_of(v):
    centre = v - jnp.mean(v, axis=-1, keepdims=True)
    inv = lax.rsqrt(jnp.mean(centre * centre, axis=-1, keepdims=True) + EPS)
    return centre * inv, inv


def norm_back(norm, inv, g):
    return (
        g
        - jnp.mean(g, axis=-1, keepdims=True)
        - norm * jnp.mean(g * norm, axis=-1, keepdims=True)
    ) * inv


def fold_rows(v):
    return v.reshape(v.shape[0] // 8, 8, v.shape[1]).sum(axis=0)


class Late:
    def __init__(self, *arrays):
        self.arrays = arrays
        self.specs = [pl.BlockSpec(memory_space=pl.ANY)] * len(arrays)
        self.scratch = [pltpu.VMEM(a.shape, a.dtype) for a in arrays]
        self.scratch.append(pltpu.SemaphoreType.DMA((len(arrays),)))

    def copies(self, refs, scratch):
        sem = scratch[-1]
        return [
            pltpu.make_async_copy(ref, scratch[i], sem.at[i]) for i, ref in enumerate(refs)
        ]

    def start(self, j, refs, scratch):
        @pl.when(j == 0)
        def _():
            for copy in self.copies(refs, scratch):
                copy.start(priority=1)

    def wait(self, refs, scratch):
        for copy in self.copies(refs, scratch):
            copy.wait()
        return scratch[:-1]


def two_halves(block, th, tail):
    return [
        pl.BlockSpec(block, lambda j, s: (jnp.minimum(j, th - 1),) + tail),
        pl.BlockSpec(block, lambda j, s: (jnp.maximum(j - th, 0),) + tail),
    ]


def norm_mod(x, mod):
    n, d = x.shape[0] - ROWS, x.shape[1]

    def kernel(x_ref, m_ref, h_ref):
        @pl.loop(0, n // ROWS, unroll=4)
        def _(i):
            at = pl.ds(pl.multiple_of(i * ROWS, ROWS), ROWS)
            norm, _ = norm_of(x_ref[at, :].astype(F32))
            h_ref[at, :] = (norm * (1.0 + m_ref[1:2, :]) + m_ref[0:1, :]).astype(BF)

    return pl.pallas_call(
        kernel,
        out_shape=jax.ShapeDtypeStruct((n, d), BF),
        compiler_params=params(),
        cost_estimate=cost(20 * n * d, 4 * n * d),
        name="norm_mod",
    )(x, mod)


def in_proj(scal, h, wt, bias, half, geo):
    n, d = h.shape
    n3, wp = geo.n3, padded(geo.w)
    nw = wt.n

    def kernel(s, h_ref, b_ref, *refs):
        w_refs, (q_ref, kv_ref, wbuf, sem) = refs[:nw], refs[nw:]
        now = wt.stream(pl.program_id(0), s, w_refs, wbuf, sem, half)
        y = dotg(h_ref[...], now[:, :n3], 1, 0) + b_ref[0]
        y = y.astype(BF)
        q_ref[0] = y[:, :wp]
        kv_ref[0] = y[:, geo.kbase :]

    first = half * geo.Th
    return pl.pallas_call(
        kernel,
        grid_spec=pltpu.PrefetchScalarGridSpec(
            num_scalar_prefetch=1,
            grid=(geo.Th,),
            in_specs=[
                whole((n, d)),
                pl.BlockSpec((1, 1, n3), lambda j, s: (s[2] ^ (j + first), 0, 0)),
                *wt.specs(half),
            ],
            out_specs=[
                pl.BlockSpec((1, n, wp), lambda j, s: (j, 0, 0)),
                pl.BlockSpec((1, n, geo.kvw), lambda j, s: (j, 0, 0)),
            ],
            scratch_shapes=wt.scratch(0, n3),
        ),
        out_shape=[
            jax.ShapeDtypeStruct((geo.Th, n, wp), BF),
            jax.ShapeDtypeStruct((geo.Th, n, geo.kvw), BF),
        ],
        compiler_params=params(),
        cost_estimate=cost(2 * n * d * n3 * geo.Th, 8 * d * geo.w * geo.Th + 8 * n * d),
        name="in_proj",
    )(scal, h, bias, *wt.operands(half))


def head_lanes(geo, h):
    at = h * HEAD_DIM
    return [
        slice(start + at, start + at + HEAD_DIM)
        for start in (0, geo.koff, geo.koff + geo.w, geo.off)
    ]


def attn_fwd(q, kv, kvo, geo):
    z, n, wp = q.shape
    heads = geo.w // HEAD_DIM
    c = HEAD_DIM**-0.5 * LOG2E

    def kernel(q_ref, kv_ref, kvo_ref, o_ref, lse_ref):
        outs = [jnp.zeros((geo.off, n), F32)] if geo.off else []
        for h in range(heads):
            lq, lk, lv, _ = head_lanes(geo, h)
            qh = q_ref[0, :, lq]
            sa = dotg(kv_ref[0, :, lk], qh, 1, 1) * c
            sb = dotg(kvo_ref[0, :, lk], qh, 1, 1) * c
            top = jnp.maximum(
                jnp.max(sa, axis=0, keepdims=True), jnp.max(sb, axis=0, keepdims=True)
            )
            pa, pb = jnp.exp2(sa - top), jnp.exp2(sb - top)
            total = jnp.sum(pa, axis=0, keepdims=True) + jnp.sum(pb, axis=0, keepdims=True)
            o = dotg(kv_ref[0, :, lv], pa.astype(BF), 0, 0)
            o = o + dotg(kvo_ref[0, :, lv], pb.astype(BF), 0, 0)
            outs.append(o / total)
            lse_ref[0, h : h + 1, :] = top + jnp.log2(total)
        o_ref[0] = jnp.concatenate(outs, axis=0).T.astype(BF)

    def spec(width):
        return pl.BlockSpec((1, n, width), lambda j: (j, 0, 0))

    return pl.pallas_call(
        kernel,
        grid=(z,),
        in_specs=[spec(wp), spec(geo.kvw), spec(geo.kvw)],
        out_specs=[spec(geo.win), pl.BlockSpec((1, heads, n), lambda j: (j, 0, 0))],
        out_shape=[
            jax.ShapeDtypeStruct((z, n, geo.win), BF),
            jax.ShapeDtypeStruct((z, heads, n), F32),
        ],
        compiler_params=params(),
        cost_estimate=cost(3e9 * z, 10 * z * n * wp),
        name="attn_fwd",
    )(q, kv, kvo)


def attn_bwd(q, kv, kvo, o, do, lse, first, geo):
    z, n, wp = q.shape
    heads = lse.shape[1]
    scale = HEAD_DIM**-0.5
    c = scale * LOG2E

    def kernel(q_ref, kv_ref, kvo_ref, o_ref, do_ref, lse_ref, tri_ref, send_ref, ts_ref, ss_ref):
        both = (do_ref[0].astype(F32) * o_ref[0].astype(F32)).T
        dqs, parts = [], [[[], []], [[], []]]
        for h in range(heads):
            lq, lk, lv, lm = head_lanes(geo, h)
            qh, doh = q_ref[0, :, lq], do_ref[0, :, lm]
            delta = jnp.sum(both[lm], axis=0, keepdims=True)
            lse_h = lse_ref[0, h : h + 1, :]
            dq = None
            for i, ref in enumerate((kv_ref, kvo_ref)):
                k, v = ref[0, :, lk], ref[0, :, lv]
                p = jnp.exp2(dotg(k, qh, 1, 1) * c - lse_h)
                ds = (p * (dotg(v, doh, 1, 1) - delta)).astype(BF)
                parts[i][1].append(dotg(doh, p.astype(BF), 0, 1))
                parts[i][0].append(dotg(qh, ds, 0, 1) * scale)
                got = dotg(k, ds, 0, 0)
                dq = got if dq is None else dq + got
            dqs.append(dq * scale)

        def rows(count):
            return [jnp.zeros((count, n), F32)] if count else []

        pad = rows(geo.n3 - 3 * geo.w)
        own = jnp.concatenate(dqs + parts[0][0] + parts[0][1] + pad, axis=0).T
        other = jnp.concatenate(rows(geo.koff) + parts[1][0] + parts[1][1] + pad, axis=0).T
        tri_ref[0] = own.astype(BF)
        send_ref[0] = other.astype(BF)
        ts_ref[0] = jnp.sum(own, axis=0, keepdims=True)
        ss_ref[0] = jnp.sum(other, axis=0, keepdims=True)

    def spec(width, at=0, count=n):
        return pl.BlockSpec((1, count, width), lambda j: (j + at, 0, 0))

    return pl.pallas_call(
        kernel,
        grid=(z,),
        in_specs=[
            spec(wp),
            spec(geo.kvw),
            spec(geo.kvw),
            spec(geo.win),
            spec(geo.win, first),
            spec(n, 0, heads),
        ],
        out_specs=[spec(geo.n3), spec(geo.kvw), spec(geo.n3, 0, 1), spec(geo.kvw, 0, 1)],
        out_shape=[
            jax.ShapeDtypeStruct((z, n, geo.n3), BF),
            jax.ShapeDtypeStruct((z, n, geo.kvw), BF),
            jax.ShapeDtypeStruct((z, 1, geo.n3), F32),
            jax.ShapeDtypeStruct((z, 1, geo.kvw), F32),
        ],
        compiler_params=params(),
        cost_estimate=cost(5e9 * z, 16 * z * n * wp),
        name="attn_bwd",
    )(q, kv, kvo, o, do, lse)


def triple_grad(tri_ref, got_ref, geo):
    late = tri_ref[0, :, geo.kbase :].astype(F32) + got_ref[0].astype(F32)
    if not geo.kbase:
        return late.astype(BF)
    return jnp.concatenate([tri_ref[0, :, : geo.kbase], late.astype(BF)], axis=1)


def out_proj(scal, mixed, x, mod, bias, wt, geo):
    _, n, win = mixed[0].shape
    d = geo.D
    nw = len(wt.arrays)
    th = geo.Th

    late = Late(x)

    def kernel(s, ya_ref, yb_ref, m_ref, b_ref, *refs):
        late_in, refs = refs[:1], refs[1:]
        w_refs, (attn_out, resid_ref, h_ref, wbuf, sem, attn_ref, *late_buf) = refs[:nw], refs[nw:]
        j = pl.program_id(0)
        late.start(j, late_in, late_buf)
        now = wt.stream(j, s, w_refs, wbuf, sem)
        y = jnp.where(j < th, ya_ref[0], yb_ref[0])
        part = dotg(y, now[:, -win:], 1, 1)

        @pl.when(j == 0)
        def _():
            attn_ref[...] = part

        @pl.when(j > 0)
        def _():
            attn_ref[...] += part

        @pl.when(j == geo.T - 1)
        def _():
            (x_ref,) = late.wait(late_in, late_buf)

            @pl.loop(0, n // ROWS, unroll=4)
            def _(i):
                at = pl.ds(pl.multiple_of(i * ROWS, ROWS), ROWS)
                attn = attn_ref[at, :] + b_ref[...]
                attn_out[at, :] = attn.astype(BF)
                resid = x_ref[at, :].astype(F32) + m_ref[2:3, :] * attn
                resid_ref[at, :] = resid
                norm, _ = norm_of(resid)
                h_ref[at, :] = (norm * (1.0 + m_ref[4:5, :]) + m_ref[3:4, :]).astype(BF)

    return pl.pallas_call(
        kernel,
        grid_spec=pltpu.PrefetchScalarGridSpec(
            num_scalar_prefetch=1,
            grid=(geo.T,),
            in_specs=[
                *two_halves((1, n, win), th, (0, 0)),
                whole(mod.shape),
                whole((1, d)),
                *late.specs,
                *wt.specs(),
            ],
            out_specs=[whole((n, d))] * 3,
            scratch_shapes=[
                *wt.scratch(geo.base, 4 * geo.w),
                pltpu.VMEM((n, d), F32),
                *late.scratch,
            ],
        ),
        out_shape=[
            jax.ShapeDtypeStruct((n + ROWS, d), BF),
            jax.ShapeDtypeStruct((n, d), F32),
            jax.ShapeDtypeStruct((n + ROWS, d), BF),
        ],
        compiler_params=params(),
        cost_estimate=cost(2 * n * d * d, 8 * d * d + 14 * n * d),
        name="out_proj",
    )(scal, *mixed, mod, bias, *late.arrays, *wt.arrays)


def up_proj(scal, h, bias, wt, geo):
    n, d = h.shape[0] - ROWS, h.shape[1]
    w = wt.width
    nw = len(wt.arrays)

    def kernel(s, h_ref, b_ref, *refs):
        w_refs, (hid_ref, gp_ref, wbuf, sem) = refs[:nw], refs[nw:]
        j = pl.program_id(0)
        now = wt.stream(j, s, w_refs, wbuf, sem)
        for cols in pieces(w):
            u = dotg(h_ref[...], now[:, cols], 1, 0) + b_ref[0, :, cols]
            sq = u * u
            t = jnp.tanh(TANH_C * (u + CUBIC * sq * u))
            half = 0.5 * (1.0 + t)
            hid_ref[0, :, cols] = (u * half).astype(BF)
            slope = TANH_C * (1.0 + 3.0 * CUBIC * sq)
            gp_ref[0, :, cols] = (half + 0.5 * u * (1.0 - t * t) * slope).astype(BF)

    out = pl.BlockSpec((1, n, w), lambda j, s: (j, 0, 0))
    return pl.pallas_call(
        kernel,
        grid_spec=pltpu.PrefetchScalarGridSpec(
            num_scalar_prefetch=1,
            grid=(geo.T,),
            in_specs=[
                whole((n, d)),
                pl.BlockSpec((1, 1, w), lambda j, s: (j, 0, 0)),
                *wt.specs(),
            ],
            out_specs=[out, out],
            scratch_shapes=wt.scratch(),
        ),
        out_shape=[jax.ShapeDtypeStruct((geo.T, n, w), BF)] * 2,
        compiler_params=params(),
        cost_estimate=cost(2 * n * d * w * geo.T, 2 * geo.T * w * (d + 2 * n)),
        name="up_proj",
    )(scal, h, bias, *wt.arrays)


def down_proj(scal, hidden, resid, cot, mod, bias, wt, blocks, geo):
    _, n, w = hidden.shape
    d = geo.D
    nw = len(wt.arrays)

    late = Late(resid, cot)
    rows = n // blocks

    def kernel(s, y_ref, m_ref, b_ref, *refs):
        late_in, refs = refs[:2], refs[2:]
        w_refs, outs, refs = refs[:nw], refs[nw : nw + blocks], refs[nw + blocks :]
        sum_ref, wbuf, sem, acc, *late_buf = refs
        j = pl.program_id(0)
        late.start(j, late_in, late_buf)
        now = wt.stream(j, s, w_refs, wbuf, sem)
        part = dotg(y_ref[0], now[...], 1, 1)

        @pl.when(j == 0)
        def _():
            acc[...] = part
            sum_ref[...] = jnp.zeros_like(sum_ref)

        @pl.when(j > 0)
        def _():
            acc[...] += part

        @pl.when(j == geo.T - 1)
        def _():
            r_ref, c_ref = late.wait(late_in, late_buf)

            for part, out_ref in enumerate(outs):

                @pl.loop(0, rows // ROWS, unroll=4)
                def _(i):
                    here = pl.ds(pl.multiple_of(i * ROWS, ROWS), ROWS)
                    at = pl.ds(pl.multiple_of(part * rows + i * ROWS, ROWS), ROWS)
                    ffn = acc[at, :] + b_ref[...]
                    out_ref[here, :] = (r_ref[at, :] + m_ref[5:6, :] * ffn).astype(BF)
                    sum_ref[...] += fold_rows(c_ref[at, :].astype(F32) * ffn)

    return pl.pallas_call(
        kernel,
        grid_spec=pltpu.PrefetchScalarGridSpec(
            num_scalar_prefetch=1,
            grid=(geo.T,),
            in_specs=[
                pl.BlockSpec((1, n, w), lambda j, s: (j, 0, 0)),
                whole(mod.shape),
                whole((1, d)),
                *late.specs,
                *wt.specs(),
            ],
            out_specs=[*[whole((rows, d))] * blocks, whole((8, d))],
            scratch_shapes=[*wt.scratch(), pltpu.VMEM((n, d), F32), *late.scratch],
        ),
        out_shape=[
            *[jax.ShapeDtypeStruct((rows, d), BF)] * blocks,
            jax.ShapeDtypeStruct((8, d), F32),
        ],
        compiler_params=params(),
        cost_estimate=cost(2 * n * d * w * geo.T, 2 * geo.T * w * (d + n) + 8 * n * d),
        name="down_proj",
    )(scal, hidden, mod, bias, *late.arrays, *wt.arrays)


def pre_back(scal, g, gp, wt, geo):
    n, d = g.shape
    w = wt.width
    nw = len(wt.arrays)

    def kernel(s, g_ref, gp_ref, *refs):
        w_refs, (out_ref, sum_ref, wbuf, sem) = refs[:nw], refs[nw:]
        j = pl.program_id(0)
        now = wt.stream(j, s, w_refs, wbuf, sem)
        for cols in pieces(w):
            y = dotg(g_ref[...], now[:, cols], 1, 0) * gp_ref[0, :, cols].astype(F32)
            out_ref[0, :, cols] = y.astype(BF)
            sum_ref[0, :, cols] = jnp.sum(y, axis=0, keepdims=True)

    out = pl.BlockSpec((1, n, w), lambda j, s: (j, 0, 0))
    return pl.pallas_call(
        kernel,
        grid_spec=pltpu.PrefetchScalarGridSpec(
            num_scalar_prefetch=1,
            grid=(geo.T,),
            in_specs=[whole((n, d)), out, *wt.specs()],
            out_specs=[out, pl.BlockSpec((1, 1, w), lambda j, s: (j, 0, 0))],
            scratch_shapes=wt.scratch(),
        ),
        out_shape=[
            jax.ShapeDtypeStruct((geo.T, n, w), BF),
            jax.ShapeDtypeStruct((geo.T, 1, w), F32),
        ],
        compiler_params=params(),
        cost_estimate=cost(2 * n * d * w * geo.T, 2 * geo.T * w * (d + 2 * n)),
        name="pre_back",
    )(scal, g, gp, *wt.arrays)


def second_back(scal, pre, resid, attn, cot, mod, wt, geo):
    _, n, w = pre.shape
    d = geo.D
    nw = len(wt.arrays)

    late = Late(resid, attn, cot)

    def kernel(s, y_ref, m_ref, *refs):
        late_in, refs = refs[:3], refs[3:]
        w_refs, (rg_ref, ag_ref, sum_ref, wbuf, sem, acc, *late_buf) = refs[:nw], refs[nw:]
        j = pl.program_id(0)
        late.start(j, late_in, late_buf)
        now = wt.stream(j, s, w_refs, wbuf, sem)
        part = dotg(y_ref[0], now[...], 1, 1)

        @pl.when(j == 0)
        def _():
            acc[...] = part
            sum_ref[...] = jnp.zeros_like(sum_ref)

        @pl.when(j > 0)
        def _():
            acc[...] += part

        @pl.when(j == geo.T - 1)
        def _():
            r_ref, a_ref, c_ref = late.wait(late_in, late_buf)

            @pl.loop(0, n // ROWS, unroll=4)
            def _(i):
                at = pl.ds(pl.multiple_of(i * ROWS, ROWS), ROWS)
                g = acc[at, :]
                norm, inv = norm_of(r_ref[at, :])
                rg = c_ref[at, :].astype(F32) + norm_back(norm, inv, g * (1.0 + m_ref[4:5, :]))
                rg_ref[at, :] = rg
                ag = rg * m_ref[2:3, :]
                ag_ref[at, :] = ag.astype(BF)
                sum_ref[0] += fold_rows(rg * a_ref[at, :].astype(F32))
                sum_ref[1] += fold_rows(g)
                sum_ref[2] += fold_rows(g * norm)
                sum_ref[3] += fold_rows(ag)

    return pl.pallas_call(
        kernel,
        grid_spec=pltpu.PrefetchScalarGridSpec(
            num_scalar_prefetch=1,
            grid=(geo.T,),
            in_specs=[
                pl.BlockSpec((1, n, w), lambda j, s: (j, 0, 0)),
                whole(mod.shape),
                *late.specs,
                *wt.specs(),
            ],
            out_specs=[whole((n, d)), whole((n, d)), whole((4, 8, d))],
            scratch_shapes=[*wt.scratch(), pltpu.VMEM((n, d), F32), *late.scratch],
        ),
        out_shape=[
            jax.ShapeDtypeStruct((n, d), F32),
            jax.ShapeDtypeStruct((n, d), BF),
            jax.ShapeDtypeStruct((4, 8, d), F32),
        ],
        compiler_params=params(),
        cost_estimate=cost(2 * n * d * w * geo.T, 2 * geo.T * w * (d + n) + 18 * n * d),
        name="second_back",
    )(scal, pre, mod, *late.arrays, *wt.arrays)


def mixed_back(scal, g, wt, geo):
    n, d = g.shape
    win = geo.win
    nw = len(wt.arrays)

    def kernel(s, g_ref, *refs):
        w_refs, (out_ref, wbuf, sem) = refs[:nw], refs[nw:]
        now = wt.stream(pl.program_id(0), s, w_refs, wbuf, sem)
        out_ref[0] = dotg(g_ref[...], now[:, -win:], 1, 0).astype(BF)

    return pl.pallas_call(
        kernel,
        grid_spec=pltpu.PrefetchScalarGridSpec(
            num_scalar_prefetch=1,
            grid=(geo.T,),
            in_specs=[whole((n, d)), *wt.specs()],
            out_specs=pl.BlockSpec((1, n, win), lambda j, s: (j, 0, 0)),
            scratch_shapes=wt.scratch(geo.base, 4 * geo.w),
        ),
        out_shape=jax.ShapeDtypeStruct((geo.T, n, win), BF),
        compiler_params=params(),
        cost_estimate=cost(2 * n * d * d, 8 * d * d + 4 * n * d),
        name="mixed_back",
    )(scal, g, *wt.arrays)


def first_back(scal, tri, got, x, rg, mod, wt, geo):
    _, n, n3 = tri[0].shape
    d = geo.D
    nw = len(wt.arrays)
    th = geo.Th

    late = Late(x, rg)

    def kernel(s, ta, tb, ga, gb, m_ref, *refs):
        late_in, refs = refs[:2], refs[2:]
        w_refs, (out_ref, sum_ref, wbuf, sem, lhs, acc, *late_buf) = refs[:nw], refs[nw:]
        j = pl.program_id(0)
        late.start(j, late_in, late_buf)
        now = wt.stream(j, s, w_refs, wbuf, sem)
        for half, (tri_ref, got_ref) in enumerate(((ta, ga), (tb, gb))):

            @pl.when((j < th) if half == 0 else (j >= th))
            def _():
                lhs[...] = triple_grad(tri_ref, got_ref, geo)

        part = dotg(lhs[...], now[:, :n3], 1, 1)

        @pl.when(j == 0)
        def _():
            acc[...] = part
            sum_ref[...] = jnp.zeros_like(sum_ref)

        @pl.when(j > 0)
        def _():
            acc[...] += part

        @pl.when(j == geo.T - 1)
        def _():
            x_ref, r_ref = late.wait(late_in, late_buf)

            @pl.loop(0, n // ROWS, unroll=4)
            def _(i):
                at = pl.ds(pl.multiple_of(i * ROWS, ROWS), ROWS)
                g = acc[at, :]
                norm, inv = norm_of(x_ref[at, :].astype(F32))
                back = norm_back(norm, inv, g * (1.0 + m_ref[1:2, :]))
                out_ref[at, :] = (r_ref[at, :] + back).astype(BF)
                sum_ref[0] += fold_rows(g)
                sum_ref[1] += fold_rows(g * norm)

    return pl.pallas_call(
        kernel,
        grid_spec=pltpu.PrefetchScalarGridSpec(
            num_scalar_prefetch=1,
            grid=(geo.T,),
            in_specs=[
                *two_halves((1, n, n3), th, (0, 0)),
                *two_halves((1, n, geo.kvw), th, (0, 0)),
                whole(mod.shape),
                *late.specs,
                *wt.specs(),
            ],
            out_specs=[whole((n, d)), whole((2, 8, d))],
            scratch_shapes=[
                *wt.scratch(0, n3),
                pltpu.VMEM((n, n3), BF),
                pltpu.VMEM((n, d), F32),
                *late.scratch,
            ],
        ),
        out_shape=[jax.ShapeDtypeStruct((n, d), BF), jax.ShapeDtypeStruct((2, 8, d), F32)],
        compiler_params=params(),
        cost_estimate=cost(6 * n * d * d, 8 * d * d + 16 * n * d),
        name="first_back",
    )(scal, *tri, *got, mod, *late.arrays, *wt.arrays)


def weight_grad(scal, terms, join, w, mine, geo, name, partial=None):
    n = terms[0][1][0].shape[-2] if not isinstance(terms[0][1][0], tuple) else terms[0][1][0][0].shape[-2]
    pr = geo.P * geo.R
    th = geo.Th
    half_n = geo.P // 2
    want = scal[1] if mine else 1 - scal[1]
    lefts = [term[0] for term in terms]
    if not geo.direct:
        lefts = [a[:n] for a in lefts]
    if not geo.direct:

        def pick(a):
            cols = a.reshape(n, geo.P, 2, geo.R)
            cols = jnp.where(want == 0, cols[:, :, 0], cols[:, :, 1])
            return cols.reshape(n, pr).T

        lefts = [pick(a) for a in lefts]
    ops, op_specs, counts = [], [], []
    for _, operands, _ in terms:
        counts.append(len(operands))
        for pair in operands:
            if isinstance(pair, tuple):
                tail = (0,) * (pair[0].ndim - 1)
                op_specs += two_halves((1,) + pair[0].shape[1:], th, tail)
                ops += pair
            else:
                op_specs.append(pl.BlockSpec((1,) + pair.shape[1:], lambda j, s: (j, 0, 0)))
                ops.append(pair)
    na, nb = len(lefts), len(ops)

    def kernel(s, *refs):
        a_refs, b_refs = refs[:na], refs[na : na + nb]
        rest = refs[na + nb :]
        got_ref = None
        if mine:
            got_ref, rest = rest[0], rest[1:]
        n_out = 4 if (mine and geo.direct) else 1
        outs, ats = rest[:n_out], rest[n_out:]
        j = pl.program_id(0)
        if geo.direct:

            @pl.when(j == 0)
            def _():
                pick_odd = (s[1] == 1) if mine else (s[1] == 0)
                for ref, at in zip(a_refs, ats):
                    flip = ref[...].T
                    for p in range(geo.P):
                        even = flip[2 * p * geo.R : (2 * p + 1) * geo.R]
                        odd = flip[(2 * p + 1) * geo.R : (2 * p + 2) * geo.R]
                        row = pl.multiple_of((s[0] ^ p) * geo.R, geo.R)
                        at[pl.ds(row, geo.R), :] = jnp.where(pick_odd, odd, even)
        else:
            ats = a_refs

        def store(half):
            at_op, parts = 0, []
            for at, (_, operands, build) in zip(ats, terms):
                blocks = []
                for pair in operands:
                    if isinstance(pair, tuple):
                        blocks.append(b_refs[at_op + half])
                        at_op += 2
                    else:
                        blocks.append(b_refs[at_op])
                        at_op += 1
                parts.append(dotg(at[...], build(*blocks), 1, 0))
            full = join(*parts)
            if not geo.direct:
                if mine:
                    full = full + got_ref[0, 0].astype(F32)
                outs[0][0, 0] = full.astype(BF)
                return
            if not mine:
                for rel in range(geo.P):
                    outs[0][0, rel] = full[rel * geo.R : (rel + 1) * geo.R].astype(BF)
                return
            for i, rel in enumerate(geo.order[half]):
                part = full[rel * geo.R : (rel + 1) * geo.R] + got_ref[0, rel].astype(F32)
                outs[2 * half + i // half_n][i % half_n, 0] = part.astype(BF)

        for half in range(2):

            @pl.when((j < th) if half == 0 else (j >= th))
            def _():
                store(half)

    in_specs = [whole((n, a.shape[1])) if geo.direct else whole(a.shape) for a in lefts] + op_specs
    rel_block = (1, geo.P, geo.R, w) if geo.direct else (1, 1, pr, w)
    rel_spec = pl.BlockSpec(rel_block, lambda j, s: (j, 0, 0, 0))
    rel_shape = jax.ShapeDtypeStruct((geo.T,) + rel_block[1:], BF)
    args = [*lefts, *ops]
    out_specs, shapes = [rel_spec], [rel_shape]
    if mine:
        in_specs.append(rel_spec)
        args.append(partial)
        if geo.direct:
            block = (half_n, 1, geo.R, w)
            first = pl.BlockSpec(block, lambda j, s: (0, jnp.minimum(j, th - 1), 0, 0))
            second = pl.BlockSpec(block, lambda j, s: (0, jnp.maximum(j - th, 0), 0, 0))
            out_specs = [first, first, second, second]
            shapes = [jax.ShapeDtypeStruct((half_n, th, geo.R, w), BF)] * 4
    scratch = [pltpu.VMEM((pr, n), BF)] * na if geo.direct else []
    got = pl.pallas_call(
        kernel,
        grid_spec=pltpu.PrefetchScalarGridSpec(
            num_scalar_prefetch=1,
            grid=(geo.T,),
            in_specs=in_specs,
            out_specs=out_specs,
            scratch_shapes=scratch,
        ),
        out_shape=shapes,
        compiler_params=params(62 << 20),
        cost_estimate=cost(2 * pr * n * w * geo.T, 2 * geo.T * w * (2 * pr + n)),
        name=name,
    )(scal, *args)
    if not mine:
        return got[0]
    if geo.direct:
        return got
    blocks = got[0].reshape(geo.T, geo.P, geo.R, w)
    out = []
    for half in range(2):
        part = blocks[half * th : (half + 1) * th]
        part = reorder(part, [scal[0] ^ rel for rel in geo.order[half]], 1)
        part = part.transpose(1, 0, 2, 3)
        out += [part[:half_n], part[half_n:]]
    return out


def body(
    latents,
    conditioning,
    mod_weight,
    mod_bias,
    in_weight,
    query_value_bias,
    out_weight,
    branch_bias,
    up_weight,
    up_bias,
    down_weight,
    cotangent,
):
    images, row_count, width = latents.shape
    geo = Geo(lax.axis_size("fsdp"), lax.axis_size("tensor"), width)
    F, T = geo.F, geo.T
    assert 2 * images == T
    highest = lax.Precision.HIGHEST
    fi = lax.axis_index("fsdp")
    ti = lax.axis_index("tensor")
    pair, core = fi // 2, fi % 2
    scal = jnp.stack([pair, core, ti]).astype(jnp.int32)
    cols = in_weight.shape[2]
    units = up_weight.shape[1]
    geo.windows(cols)

    def places(k):
        return [
            ((2 * p + c) * T + t, (2 * p + t // images) * T + c * images + (t % images + k) % images)
            for p in range(geo.P)
            for c in range(2)
            for t in range(T)
        ]

    def to_chip(arr):
        got = []
        for k in range(images):
            item = lax.dynamic_index_in_dim(arr, (ti + k) % images, 0, keepdims=False)
            got.append(lax.ppermute(item, BOTH, places(k)))
        return got

    def from_chip(arr):
        got = []
        for k in range(images):
            back = [(dst, src) for src, dst in places(k)]
            got.append(lax.ppermute(arr[k], BOTH, back))
        return got

    def home(parts):
        return reorder(jnp.stack(parts), [(i - ti) % images for i in range(images)])

    def share(arr):
        sent = jnp.broadcast_to(arr[None], (F * T,) + arr.shape)
        return lax.all_to_all(sent, BOTH, 0, 0, tiled=True)

    now, opened = (), []

    def tie(value):
        return after(value, *now)

    def start(*chains):
        for way in chains:
            opened.extend(way.advance(*now))

    def begin(shard, make, *how):
        way = Chain(make(tie(shard), geo, *how))
        opened.extend(way.flight)
        return way

    def across(value):
        got = flip_core(tie(value), geo)
        opened.append(got)
        return got

    def close(*made):
        nonlocal now
        now = (*opened, *made)
        opened.clear()

    heads = cols // HEAD_DIM
    attn_shard = jnp.concatenate([in_weight[0], in_weight[1], in_weight[2], out_weight.T], axis=1)
    attn_way = begin(attn_shard, gather_steps, False)
    cond_all = after(conditioning, attn_shard)[None]
    bit = 1
    while bit < F:
        got = lax.ppermute(cond_all, "fsdp", [(i, i ^ bit) for i in range(F)])
        cond_all = jnp.concatenate([cond_all, got])
        bit *= 2
    cond_all = reorder(cond_all, [fi ^ f for f in range(F)]).reshape(F * images, width)
    silu_low = jax.nn.silu(cond_all.astype(F32)).astype(BF)
    silu_own = lax.dynamic_slice_in_dim(silu_low, fi * geo.R, geo.R, 1)
    mod_part = jnp.einsum("bd,dcj->bcj", silu_own, mod_weight, preferred_element_type=F32)
    bias_rows = jnp.concatenate([mod_bias, query_value_bias]).astype(F32)
    bias_rows = jnp.where(fi == 0, bias_rows, 0.0)
    mod_part = jnp.pad(mod_part, ((0, 0), (0, 2), (0, 0))) + bias_rows
    mod_part = mod_part.reshape(geo.P, 1, T, 8, cols)
    mod_part = jnp.broadcast_to(mod_part, (geo.P, 2, T, 8, cols)).reshape(F * T, 8, cols)
    close()
    start(attn_way)
    up_way = begin(up_weight, gather_steps, True, True)
    mod_part = lax.all_to_all(mod_part, BOTH, 0, 0, tiled=True)
    mod_part = mod_part.reshape(F, T, 8, cols).sum(axis=0)
    mod = mod_part[:, :6].transpose(1, 0, 2).reshape(6, width)
    qv_bias = mod_part[:, 6:]
    triple_bias = jnp.concatenate(
        [
            qv_bias[:, :1],
            jnp.zeros_like(qv_bias[:, :1]),
            qv_bias[:, 1:],
            jnp.zeros((T, 1, geo.n3 - 3 * cols), F32),
        ],
        axis=2,
    )
    bias_rows = branch_bias.astype(F32)
    close(mod)
    start(attn_way)
    x_parts = to_chip(tie(latents))
    opened.extend(x_parts)
    close()
    x = jnp.concatenate([*x_parts, jnp.zeros((ROWS, width), BF)])
    start(attn_way, up_way)
    h1 = norm_mod(tie(x), mod)
    close(h1)
    w_attn = Gathered(attn_way.finish(*now), geo, scal)
    start(up_way)

    q, kv, kvo = [None] * 2, [None] * 2, [None] * 2
    mixed, lse = [None] * 2, [None] * 2
    extras = []
    down_shard = jnp.concatenate(
        [down_weight.T, jnp.broadcast_to(up_bias, (16, units))]
    )
    down_way = begin(down_shard, gather_steps, True, False, extras)
    for half in range(2):
        q[half], kv[half] = in_proj(tie(scal), h1, w_attn, triple_bias, half, geo)
    close(q[0], q[1])
    kvo = [across(kv[0]), across(kv[1])]
    close()
    start(up_way, down_way)
    for half in range(2):
        mixed[half], lse[half] = attn_fwd(tie(q[half]), kv[half], kvo[half], geo)
    close(lse[0], lse[1])
    start(up_way, down_way)
    attn, resid, h2 = out_proj(tie(scal), mixed, x, mod, bias_rows[0:1], w_attn, geo)
    close(h2)
    w_up = Gathered(up_way.finish(*now), geo, scal)
    start(down_way)
    cot_parts = to_chip(tie(cotangent))
    opened.extend(cot_parts)
    unit_bias = jnp.stack([part[:1] for part in extras]).astype(F32)
    hidden, gp = up_proj(tie(scal), h2, unit_bias, w_up, geo)
    close(hidden)
    start(down_way)
    cot = jnp.concatenate(cot_parts)
    ffn_grad = (cot.astype(F32) * mod[5]).astype(BF)

    def block(ref):
        return ref[0]

    def alone(part):
        return part

    down_terms = [(ffn_grad, [hidden], block)]
    down_half = weight_grad(tie(scal), down_terms, alone, units, False, geo, "w_down_send")
    close(down_half)
    w_down = Gathered(down_way.finish(*now), geo, scal)
    down_got = across(down_half)
    *block_rows, ffn_sums = down_proj(
        tie(scal), hidden, resid, cot, mod, bias_rows[1:2], w_down, images, geo
    )
    close(ffn_sums)

    down_parts = weight_grad(tie(scal), down_terms, alone, units, True, geo, "w_down", down_got)
    close(*down_parts)
    down_back = begin(down_parts, scatter_steps)
    block_back = from_chip(tie(block_rows))
    opened.extend(block_back)
    pre, unit_sum = pre_back(tie(scal), ffn_grad, gp, w_down, geo)
    up_terms = [(h2, [pre], block)]
    up_half = weight_grad(tie(scal), up_terms, alone, units, False, geo, "w_up_send")
    close(up_half)
    start(down_back)
    up_got = across(up_half)
    rg, ag, mid_sums = second_back(tie(scal), pre, resid, attn, cot, mod, w_up, geo)
    close(ag)
    start(down_back)
    up_parts = weight_grad(tie(scal), up_terms, alone, units, True, geo, "w_up", up_got)
    mg = mixed_back(tie(scal), ag, w_attn, geo)
    close(mg, *up_parts)
    start(down_back)
    up_back = begin(up_parts, scatter_steps)
    tri, tri_send, tri_sums, send_sums = [None] * 2, [None] * 2, [None] * 2, [None] * 2
    for half in range(2):
        tri[half], tri_send[half], tri_sums[half], send_sums[half] = attn_bwd(
            tie(q[half]), kv[half], kvo[half], mixed[half], mg, lse[half], half * geo.Th, geo
        )
    close(*tri_sums)
    tri_got = [across(tri_send[0]), across(tri_send[1])]
    ffn_sum = jnp.sum(tie(ffn_grad).astype(F32), axis=0)
    tri_sum, send_sum = jnp.concatenate(tri_sums), jnp.concatenate(send_sums)
    pair_sums = jnp.concatenate(
        [
            tri_sum[:, :, :cols],
            tri_sum[:, :, 2 * cols : 3 * cols]
            + send_sum[:, :, geo.koff + cols : geo.koff + 2 * cols],
        ],
        axis=1,
    )
    close()
    start(up_back)
    down_back.finish(*now)

    def beside(first, second):
        shared = geo.n3 - geo.base
        middle = first[:, geo.base :] + second[:, :shared]
        return jnp.concatenate([first[:, : geo.base], middle, second[:, shared:]], axis=1)

    attn_terms = [
        (h1, [tuple(tri), tuple(tri_got)], lambda a, b: triple_grad(a, b, geo)),
        (ag, [tuple(mixed)], block),
    ]
    attn_half = weight_grad(tie(scal), attn_terms, beside, 4 * cols, False, geo, "w_attn_send")
    close(attn_half)
    start(up_back)
    attn_got = across(attn_half)
    latent_rows, first_sums = first_back(tie(scal), tri, tri_got, x, rg, mod, w_attn, geo)
    close(first_sums)
    start(up_back)
    mine = [i ^ ti for i in range(T)]
    rows = jnp.concatenate(
        [first_sums.sum(axis=1), mid_sums[:3].sum(axis=1), ffn_sums.sum(axis=0, keepdims=True)]
    )
    rows = tie(rows).reshape(6, T, cols).transpose(1, 0, 2).reshape(T, 6 * cols)
    branch_sums = jnp.stack([mid_sums[3].sum(axis=0), ffn_sum]).reshape(F, T, -1)
    unit_sums = reorder(unit_sum, mine).reshape(T, F, units // F).transpose(1, 0, 2)
    pair_sums = reorder(pair_sums, mine).reshape(T, F, 2 * cols // F).transpose(1, 0, 2)
    rows = jnp.broadcast_to(rows[None], (F,) + rows.shape)
    pack = jnp.concatenate([rows, branch_sums, unit_sums, pair_sums], axis=2)
    count = pack.shape[2]
    pack = jnp.pad(pack, ((0, 0), (0, 0), (0, -count % 1024))).reshape(F * T, -1, 128)
    pack = lax.all_to_all(pack, BOTH, 0, 0, tiled=True)
    attn_parts = weight_grad(
        tie(scal), attn_terms, beside, 4 * cols, True, geo, "w_attn", attn_got
    )
    close(pack, *attn_parts)
    attn_back = begin(attn_parts, scatter_steps, False)
    block_back = [tie(part) for part in block_back]
    down_shard = tie(down_back.finish())
    latent_back = from_chip(tie(latent_rows).reshape(images, row_count, width))
    opened.extend(latent_back)
    pack = tie(pack)
    slices = pack.sum(axis=0).reshape(-1)[6 * cols : count]
    tiles = -(-6 * cols // 128)
    mine_rows = pack[:, :tiles].reshape(geo.P, 2, T, tiles, 128).sum(axis=1)
    mine_rows = mine_rows.reshape(F * images, -1)[:, : 6 * cols].reshape(F * images, 6, cols)
    cond_part = jnp.einsum("bcj,dcj->bd", mine_rows, mod_weight.astype(F32), precision=highest)
    cond_part = cond_part.reshape(F, 1, images * geo.R)
    cond_part = jnp.broadcast_to(cond_part, (F, T, images * geo.R))
    kept = jnp.broadcast_to(slices[None, None], (F, T) + slices.shape)
    final = jnp.concatenate([cond_part, kept], axis=2).reshape(F * T, -1)
    final = jnp.pad(final, ((0, 0), (0, -final.shape[1] % 1024))).reshape(F * T, -1, 128)
    final = lax.all_to_all(final, BOTH, 0, 0, tiled=True)
    close(final)
    start(attn_back)
    close()
    start(attn_back)
    block_out, latent_grad = home(block_back), home(latent_back)
    down_grad, up_grad = down_shard, up_back.finish(*now)
    attn_grad = attn_back.finish(*now)
    in_grad = attn_grad[:, : 3 * cols].reshape(geo.R, 3, cols).transpose(1, 0, 2)

    final = final.reshape(F, T, -1)
    at = images * geo.R
    cond_mine = final[:, :, :at].sum(axis=1).reshape(F, images, geo.R)
    step = 2 * width // (F * T)
    branch_grad = final[:, :, at : at + step].reshape(2, width)
    own = lax.dynamic_index_in_dim(final, ti, 1, keepdims=False)
    at += step
    unit_grad = own[:, at : at + units // F].reshape(units)
    at += units // F
    pair_grad = own[:, at : at + 2 * cols // F].reshape(2, cols)
    mod_weight_grad = jnp.einsum("bd,bcj->dcj", silu_own.astype(F32), mine_rows, precision=highest)
    mod_bias_grad = mine_rows.sum(axis=0)
    silu_grad = cond_mine.transpose(1, 0, 2).reshape(images, width)
    cond_f = conditioning.astype(F32)
    sig = jax.nn.sigmoid(cond_f)
    cond_grad = silu_grad * (sig * (1.0 + cond_f * (1.0 - sig)))

    return (
        block_out,
        latent_grad,
        cond_grad,
        mod_weight_grad,
        mod_bias_grad,
        in_grad,
        pair_grad,
        attn_grad[:, 3 * cols :].T,
        branch_grad,
        up_grad,
        unit_grad,
        down_grad.T,
    )


def solution(mesh):
    in_specs = (
        P("fsdp", "tensor", None),
        P("fsdp", None),
        P("fsdp", None, "tensor"),
        P(None, "tensor"),
        P(None, "fsdp", "tensor"),
        P(None, "tensor"),
        P("tensor", "fsdp"),
        P(),
        P("fsdp", "tensor"),
        P("tensor"),
        P("tensor", "fsdp"),
        P("fsdp", "tensor", None),
    )
    out_specs = (
        P("fsdp", "tensor", None),
        P("fsdp", "tensor", None),
        P("fsdp", None),
        P("fsdp", None, "tensor"),
        P(None, "tensor"),
        P(None, "fsdp", "tensor"),
        P(None, "tensor"),
        P("tensor", "fsdp"),
        P(),
        P("fsdp", "tensor"),
        P("tensor"),
        P("tensor", "fsdp"),
    )
    return jax.shard_map(body, mesh=mesh, in_specs=in_specs, out_specs=out_specs, check_vma=False)
```
